32 devices in a mesh: dp: 2 (over x), row: 4 (over y, core), col: 4 (over z).
Axes of the slice: x: 2, y: 2, z: 4, core: 2. Of those that a mesh axis runs over, the one named last changes fastest.
Arguments:
- tokens: bfloat16 [5120, 2048], P(('dp', 'col'), 'row'), may hold values from -6 to 6
- cotangent: bfloat16 [5120, 2048], P(('dp', 'col'), 'row'), may hold values from -6 to 6
- seg_ids: int32 [5120], P('dp'), may hold values from 0 to 12, as said below
- positions: int32 [5120], P('dp'), may hold values from 0 to 1279, as said below
- parents: int32 [2, 13], P('dp'), may hold values from 0 to 4, as said below
- tree_sets: int32 [2], P('dp'), may hold values from 0 to 7
- gain_q: float32 [2048], P('col'), may hold values from 0.25 to 1.75
- gain_k: float32 [2048], P('col'), may hold values from 0.25 to 1.75
- gain_attn: float32 [2048], P('row'), may hold values from 0.25 to 1.75
- gain_ffn: float32 [2048], P('row'), may hold values from 0.25 to 1.75
- query_key_value_weight: bfloat16 [2048, 3, 2048], P('row', None, 'col'), may hold values from -0.125 to 0.125
- output_weight: bfloat16 [2048, 2048], P('col', 'row'), may hold values from -0.125 to 0.125
- gate_up_weight: bfloat16 [2048, 2, 8192], P('row', None, 'col'), may hold values from -0.125 to 0.125
- down_weight: bfloat16 [8192, 2048], P('col', 'row'), may hold values from -0.0625 to 0.0625
- query_key_value_adapter_first: float32 [3, 8, 16, 2048], P(None, None, None, 'row'), may hold values from -0.125 to 0.125
- query_key_value_adapter_second: float32 [3, 8, 16, 2048], P(None, None, None, 'col'), may hold values from -0.5 to 0.5
- output_adapter_first: float32 [8, 16, 2048], P(None, None, 'col'), may hold values from -0.125 to 0.125
- output_adapter_second: float32 [8, 16, 2048], P(None, None, 'row'), may hold values from -0.5 to 0.5
- gate_up_adapter_first: float32 [2, 8, 16, 2048], P(None, None, None, 'row'), may hold values from -0.125 to 0.125
- gate_up_adapter_second: float32 [2, 8, 16, 8192], P(None, None, None, 'col'), may hold values from -0.5 to 0.5
- down_adapter_first: float32 [8, 16, 8192], P(None, None, 'col'), may hold values from -0.0625 to 0.0625
- down_adapter_second: float32 [8, 16, 2048], P(None, None, 'row'), may hold values from -0.5 to 0.5
Outputs:
- layer_out: bfloat16 [5120, 2048], P(('dp', 'col'), 'row')
- input_grad: float32 [5120, 2048], P(('dp', 'col'), 'row')
- grad_a_qkv: float32 [3, 8, 16, 2048], P(None, 'dp', 'col', 'row')
- grad_b_qkv: float32 [3, 8, 16, 2048], P(None, 'dp', 'row', 'col')
- grad_a_out: float32 [8, 16, 2048], P('dp', 'row', 'col')
- grad_b_out: float32 [8, 16, 2048], P('dp', 'col', 'row')
- grad_a_gu: float32 [2, 8, 16, 2048], P(None, 'dp', 'col', 'row')
- grad_b_gu: float32 [2, 8, 16, 8192], P(None, 'dp', 'row', 'col')
- grad_a_down: float32 [8, 16, 8192], P('dp', 'row', 'col')
- grad_b_down: float32 [8, 16, 2048], P('dp', 'col', 'row')
The draws below stay inside these ranges and needn't reach their ends.
Inputs may be any that keep to these rules, and one draw needn't show every extreme that they name: `seg_ids`: in each tree the first 1024 tokens are segment 0, the trunk; the other 12 segments of 128 tokens each follow in any order: branches are 1 to 4, leaves the higher numbers. The trunk's tokens have positions 0 to 1023 in order, a branch's 1024 onward, a leaf's 1024 + 128 onward. `parents`: the trunk and the branches have parent 0; each leaf has a branch as parent, and each branch has 2 leaves.
All inputs are finite; a program needn't handle non-finite values.
Results may differ from the reference program's by a relative error of at most 0.025.
Values may be sent and summed in bfloat16 or wider, within the bound.
A program may use at most 320 MiB of HBM per device.

```python
import jax
import jax.numpy as jnp
from jax import lax

D = 2048
HEADS = 16
HEAD = 128
FF = 8192
RANK = 16
SETS = 8
TRUNK = 1024
SEG = 128
BRANCHES = 4
LEAVES = 2
TREE_TOK = 2560
QBLOCK = 640
TREES = 2
TOKENS = 5120


def tree_layout(key):
    tree_keys = jax.random.split(jax.random.fold_in(key, 7), TREES)

    def one_tree(tree_key):
        first_key, second_key = jax.random.split(tree_key)
        others = BRANCHES + BRANCHES * LEAVES
        slots = 1 + jax.random.permutation(first_key, others).astype(jnp.int32)
        owners = jax.random.permutation(second_key, BRANCHES * LEAVES).astype(jnp.int32) // LEAVES + 1
        parent_row = jnp.concatenate([jnp.zeros((1 + BRANCHES,), jnp.int32), owners])
        seg_rest = jnp.repeat(slots, SEG)
        seg_all = jnp.concatenate([jnp.zeros((TRUNK,), jnp.int32), seg_rest])
        leaf_flag = (seg_rest > BRANCHES).astype(jnp.int32)
        inside = jnp.tile(jnp.arange(SEG, dtype=jnp.int32), others)
        pos_rest = TRUNK + leaf_flag * SEG + inside
        pos_all = jnp.concatenate([jnp.arange(TRUNK, dtype=jnp.int32), pos_rest])
        return (seg_all, pos_all, parent_row)
    return jax.vmap(one_tree)(tree_keys)


def draw_seg_ids(key, part):
    seg_all, pos_all, parent_rows = tree_layout(key)
    return seg_all.reshape(TOKENS)


def draw_positions(key, part):
    seg_all, pos_all, parent_rows = tree_layout(key)
    return pos_all.reshape(TOKENS)


def draw_parents(key, part):
    seg_all, pos_all, parent_rows = tree_layout(key)
    return parent_rows


def block_scale(stream_key, shape, cuts, least, high):
    def one(dim, blocks):
        heights = jax.random.uniform(jax.random.fold_in(jax.random.fold_in(stream_key, 6), dim), (blocks,), jnp.float32, least / len(cuts), high / len(cuts))
        return jnp.repeat(jnp.exp(heights), shape[dim] // blocks).reshape((-1,) + (1,) * (len(shape) - dim - 1))

    factor_of = one(*cuts[0])
    for cut in cuts[1:]:
        factor_of = factor_of * one(*cut)
    return factor_of


def gaussian(key, dims, width, bound, cuts=(), kind=jnp.bfloat16):
    drawn = width * jax.random.normal(key, dims, jnp.float32)
    if cuts:
        drawn = drawn * block_scale(key, dims, cuts, -0.22, 0.18)
    return jnp.clip(drawn, -bound, bound).astype(kind)


def setup_inputs(seed: int = 0) -> dict:
    key_list = jax.random.split(jax.random.key(seed), 23)
    return {
        "tokens": gaussian(key_list[0], (TOKENS, D), 1.0, 6.0, ((0, 8), (1, 4))),
        "cotangent": gaussian(key_list[1], (TOKENS, D), 1.0, 6.0, ((0, 8), (1, 4))),
        "seg_ids": draw_seg_ids(jax.random.fold_in(key_list[22], 71), 0),
        "positions": draw_positions(jax.random.fold_in(key_list[22], 71), 0),
        "parents": draw_parents(jax.random.fold_in(key_list[22], 71), 0),
        "tree_sets": jax.random.randint(key_list[5], (TREES,), 0, SETS).astype(jnp.int32),
        "gain_q": jnp.clip(1.0 + 0.15 * jax.random.normal(key_list[6], (D,), jnp.float32), 0.25, 1.75),
        "gain_k": jnp.clip(1.0 + 0.15 * jax.random.normal(key_list[7], (D,), jnp.float32), 0.25, 1.75),
        "gain_attn": jnp.clip(1.0 + 0.15 * jax.random.normal(key_list[8], (D,), jnp.float32), 0.25, 1.75),
        "gain_ffn": jnp.clip(1.0 + 0.15 * jax.random.normal(key_list[9], (D,), jnp.float32), 0.25, 1.75),
        "query_key_value_weight": gaussian(key_list[10], (D, 3, D), D ** -0.5, 0.125, ((0, 4), (2, 4))),
        "output_weight": gaussian(key_list[11], (D, D), D ** -0.5, 0.125, ((0, 4), (1, 4))),
        "gate_up_weight": gaussian(key_list[12], (D, 2, FF), D ** -0.5, 0.125, ((0, 4), (2, 4))),
        "down_weight": gaussian(key_list[13], (FF, D), FF ** -0.5, 0.0625, ((0, 4), (1, 4))),
        "query_key_value_adapter_first": gaussian(key_list[14], (3, SETS, RANK, D), D ** -0.5, 0.125, ((3, 4),), jnp.float32),
        "query_key_value_adapter_second": gaussian(key_list[15], (3, SETS, RANK, D), 0.08, 0.5, ((3, 4),), jnp.float32),
        "output_adapter_first": gaussian(key_list[16], (SETS, RANK, D), D ** -0.5, 0.125, ((2, 4),), jnp.float32),
        "output_adapter_second": gaussian(key_list[17], (SETS, RANK, D), 0.08, 0.5, ((2, 4),), jnp.float32),
        "gate_up_adapter_first": gaussian(key_list[18], (2, SETS, RANK, D), D ** -0.5, 0.125, ((3, 4),), jnp.float32),
        "gate_up_adapter_second": gaussian(key_list[19], (2, SETS, RANK, FF), 0.08, 0.5, ((3, 4),), jnp.float32),
        "down_adapter_first": gaussian(key_list[20], (SETS, RANK, FF), FF ** -0.5, 0.0625, ((2, 4),), jnp.float32),
        "down_adapter_second": gaussian(key_list[21], (SETS, RANK, D), 0.08, 0.5, ((2, 4),), jnp.float32),
    }


precise = lax.Precision.HIGHEST
epsilon = 1e-06
rope_base = 500000.0
masked_out = -1e+30

@jax.custom_vjp
def low(v):
    return lax.optimization_barrier(v.astype(jnp.bfloat16)).astype(jnp.float32)

@jax.custom_vjp
def low_back(v):
    return v

def low_keep(v):
    return (low(v), None)

def low_pass(kept, grad):
    return (grad,)

def back_keep(v):
    return (v, None)

def back_low(kept, grad):
    return (low(grad),)
low.defvjp(low_keep, low_pass)
low_back.defvjp(back_keep, back_low)

def matrix_product_exact(left_term, right_term):
    return jnp.dot(left_term, right_term, precision=precise)

def rms_norm(values, gain):
    factor = lax.rsqrt(lax.optimization_barrier(jnp.mean(values * values, axis=-1, keepdims=True)) + epsilon)
    return values * factor * gain

def angles(positions):
    half_width = HEAD // 2
    frequency = rope_base ** (-(jnp.arange(half_width, dtype=jnp.float32) * 2.0) / HEAD)
    angle_table = positions.astype(jnp.float32)[:, None] * frequency[None, :]
    return (jnp.cos(angle_table)[:, None, :], jnp.sin(angle_table)[:, None, :])

def rotate(values, cosine, sine):
    half_width = values.shape[-1] // 2
    first_half = values[..., :half_width]
    second_half = values[..., half_width:]
    return jnp.concatenate([first_half * cosine - second_half * sine, second_half * cosine + first_half * sine], axis=-1)

def adapter_contribution(input_values, down_lookup, up_lookup):
    return matrix_product_exact(matrix_product_exact(input_values, down_lookup.T), up_lookup)

def tree_forward(frozen, adapters, token_features, seg_tree, pos_tree, parent_tree, set_selection):
    gain_q, gain_k, gain_attn, gain_ffn, query_key_value_weight, output_weight, gate_up_weight, down_weight = frozen
    query_key_value_adapter_first, query_key_value_adapter_second, output_adapter_first, output_adapter_second, gate_up_adapter_first, gate_up_adapter_second, down_adapter_first, down_adapter_second = adapters
    length = token_features.shape[0]
    unscaled_pieces_list = [matrix_product_exact(token_features, query_key_value_weight[:, selector_index, :]) + adapter_contribution(token_features, query_key_value_adapter_first[selector_index, set_selection], query_key_value_adapter_second[selector_index, set_selection]) for selector_index in range(3)]
    query_raw = low_back(unscaled_pieces_list[0])
    key_raw = low_back(unscaled_pieces_list[1])
    value_low = low(low_back(unscaled_pieces_list[2])).reshape(length, HEADS, HEAD)
    cosine, sine = angles(pos_tree)
    query_low = low(rotate(rms_norm(query_raw, gain_q).reshape(length, HEADS, HEAD), cosine, sine))
    key_low = low(rotate(rms_norm(key_raw, gain_k).reshape(length, HEADS, HEAD), cosine, sine))
    parent_tok = parent_tree[seg_tree]
    grand_tok = parent_tree[parent_tok]
    score_scale = HEAD ** (-0.5)

    def attend_block(pieces):
        query_blk, seg_query, pos_query, parent_query, grand_query = pieces
        scores = low_back(jnp.einsum('qhd,khd->hqk', query_blk, key_low, precision=precise) * score_scale)
        on_path = (seg_tree[None, :] == seg_query[:, None]) | (seg_tree[None, :] == parent_query[:, None]) | (seg_tree[None, :] == grand_query[:, None])
        visible = on_path & (pos_tree[None, :] <= pos_query[:, None])
        scores = jnp.where(visible[None, :, :], scores, masked_out)
        weights_p = jax.nn.softmax(scores, axis=-1)
        return jnp.einsum('hqk,khd->qhd', low(weights_p), value_low, precision=precise)
    blocks = length // QBLOCK
    attended = lax.map(jax.checkpoint(attend_block), (query_low.reshape(blocks, QBLOCK, HEADS, HEAD), seg_tree.reshape(blocks, QBLOCK), pos_tree.reshape(blocks, QBLOCK), parent_tok.reshape(blocks, QBLOCK), grand_tok.reshape(blocks, QBLOCK)))
    attention_reduced = low(low_back(attended.reshape(length, D)))
    attention_unscaled = low_back(matrix_product_exact(attention_reduced, output_weight) + adapter_contribution(attention_reduced, output_adapter_first[set_selection], output_adapter_second[set_selection]))
    hidden_in = token_features + rms_norm(attention_unscaled, gain_attn)
    hidden_reduced = low(hidden_in)
    gate_unscaled = low_back(matrix_product_exact(hidden_reduced, gate_up_weight[:, 0, :]) + adapter_contribution(hidden_reduced, gate_up_adapter_first[0, set_selection], gate_up_adapter_second[0, set_selection]))
    up_unscaled = low_back(matrix_product_exact(hidden_reduced, gate_up_weight[:, 1, :]) + adapter_contribution(hidden_reduced, gate_up_adapter_first[1, set_selection], gate_up_adapter_second[1, set_selection]))
    product_reduced = low(jax.nn.silu(gate_unscaled) * up_unscaled)
    down_unscaled = low_back(matrix_product_exact(product_reduced, down_weight) + adapter_contribution(product_reduced, down_adapter_first[set_selection], down_adapter_second[set_selection]))
    return hidden_in + rms_norm(down_unscaled, gain_ffn)

def reference(tokens, cotangent, seg_ids, positions, parents, tree_sets, gain_q, gain_k, gain_attn, gain_ffn, query_key_value_weight, output_weight, gate_up_weight, down_weight, query_key_value_adapter_first, query_key_value_adapter_second, output_adapter_first, output_adapter_second, gate_up_adapter_first, gate_up_adapter_second, down_adapter_first, down_adapter_second):
    frozen = tuple((weight.astype(jnp.float32) for weight in (gain_q, gain_k, gain_attn, gain_ffn, query_key_value_weight, output_weight, gate_up_weight, down_weight)))
    adapters = tuple((table.astype(jnp.float32) for table in (query_key_value_adapter_first, query_key_value_adapter_second, output_adapter_first, output_adapter_second, gate_up_adapter_first, gate_up_adapter_second, down_adapter_first, down_adapter_second)))
    inputs_f = tokens.astype(jnp.float32).reshape(TREES, TREE_TOK, D)
    upstream = cotangent.astype(jnp.float32).reshape(TREES, TREE_TOK, D)

    def per_tree(totals, pieces):
        token_features, grad_out, seg_tree, pos_tree, parent_tree, set_selection = pieces

        def forward(inputs_x, tables):
            return tree_forward(frozen, tables, inputs_x, seg_tree, pos_tree, parent_tree, set_selection)
        result, pullback = jax.vjp(forward, token_features, adapters)
        input_part, table_grads = pullback(grad_out)
        totals = jax.tree.map(jnp.add, totals, table_grads)
        return (totals, (result.astype(jnp.bfloat16), input_part))
    start_totals = jax.tree.map(jnp.zeros_like, adapters)
    totals, (outputs, input_parts) = lax.scan(per_tree, start_totals, (inputs_f, upstream, seg_ids.reshape(TREES, TREE_TOK), positions.reshape(TREES, TREE_TOK), parents, tree_sets))
    return (outputs.reshape(TOKENS, D), input_parts.reshape(TOKENS, D), totals[0], totals[1], totals[2], totals[3], totals[4], totals[5], totals[6], totals[7])
```

```python
import jax
import jax.numpy as jnp
from jax import lax
from jax.sharding import PartitionSpec as P

D = 2048
HEAD = 128
RANK = 16

epsilon = 1e-06
rope_base = 500000.0
masked_out = -1e30
low = jnp.bfloat16
wide = jnp.float32
last_last = (((1,), (1,)), ((), ()))
first_first = (((0,), (0,)), ((), ()))


def dot(left, right):
    return jnp.dot(left, right, preferred_element_type=wide)


def dot_t(left, right):
    return lax.dot_general(left, right, last_last, preferred_element_type=wide)


def t_dot(left, right):
    return lax.dot_general(left, right, first_first, preferred_element_type=wide)


def angles(positions):
    half_width = HEAD // 2
    frequency = rope_base ** (-(jnp.arange(half_width, dtype=wide) * 2.0) / HEAD)
    angle_table = positions.astype(wide)[:, None] * frequency[None, :]
    return (jnp.cos(angle_table)[:, None, :], jnp.sin(angle_table)[:, None, :])


def rotate(values, cosine, sine):
    half_width = values.shape[-1] // 2
    first_half = values[..., :half_width]
    second_half = values[..., half_width:]
    return jnp.concatenate(
        [first_half * cosine - second_half * sine, second_half * cosine + first_half * sine],
        axis=-1,
    )


def norm_factor(square_sum):
    return lax.rsqrt(square_sum / D + epsilon)


def norm_back(scaled, flat, factor, cross_sum):
    return factor[:, None] * (scaled - flat * (cross_sum / D)[:, None])


def tree_mask(seg_ids, positions, parents):
    parent_row = parents[0]
    labels = jnp.arange(parent_row.shape[0], dtype=jnp.int32)
    parent_tok = jnp.sum(jnp.where(seg_ids[:, None] == labels[None, :], parent_row[None, :], 0), axis=1)
    grand_tok = jnp.sum(jnp.where(parent_tok[:, None] == labels[None, :], parent_row[None, :], 0), axis=1)
    on_path = (
        (seg_ids[None, :] == seg_ids[:, None])
        | (seg_ids[None, :] == parent_tok[:, None])
        | (seg_ids[None, :] == grand_tok[:, None])
    )
    return on_path & (positions[None, :] <= positions[:, None])


def per_device(
    tokens,
    cotangent,
    seg_ids,
    positions,
    parents,
    tree_sets,
    gain_q,
    gain_k,
    gain_attn,
    gain_ffn,
    query_key_value_weight,
    output_weight,
    gate_up_weight,
    down_weight,
    query_key_value_adapter_first,
    query_key_value_adapter_second,
    output_adapter_first,
    output_adapter_second,
    gate_up_adapter_first,
    gate_up_adapter_second,
    down_adapter_first,
    down_adapter_second,
):
    dp_count = lax.axis_size("dp")
    row_count = lax.axis_size("row")
    col_count = lax.axis_size("col")
    row_at = lax.axis_index("row")
    tree_tokens = seg_ids.shape[0]
    assert tree_sets.shape[0] == 1
    set_count = output_adapter_first.shape[0]
    own = tokens.shape[0] // row_count
    group = own * col_count
    width_row = tokens.shape[1]
    width_col = gain_q.shape[0]
    hidden_col = down_weight.shape[0]
    heads_col = width_col // HEAD
    score_scale = HEAD ** (-0.5)
    tree_set = tree_sets[0]

    def pick(table, axis):
        return lax.dynamic_index_in_dim(table, tree_set, axis, keepdims=False)

    narrow = jnp.concatenate(
        [
            pick(query_key_value_adapter_first, 1),
            pick(gate_up_adapter_first, 1),
            pick(output_adapter_second, 0)[None],
            pick(down_adapter_second, 0)[None],
        ],
        axis=0,
    ).astype(low)
    narrow_all = lax.all_gather(narrow, "row", axis=2, tiled=True)
    a_qkv = narrow_all[:3].reshape(3 * RANK, D)
    a_gu = narrow_all[3:5].reshape(2 * RANK, D)
    b_out = narrow_all[5]
    b_down = narrow_all[6]
    b_qkv = pick(query_key_value_adapter_second, 1).astype(low)
    b_gu = pick(gate_up_adapter_second, 1).astype(low)
    a_out = pick(output_adapter_first, 0).astype(low)
    a_down = pick(down_adapter_first, 0).astype(low)
    gains = lax.all_gather(jnp.stack([gain_attn, gain_ffn]), "row", axis=1, tiled=True)

    w_qkv = lax.all_gather(query_key_value_weight, "row", axis=0, tiled=True).reshape(D, 3 * width_col)
    w_out = lax.all_gather(output_weight, "row", axis=1, tiled=True)
    w_gu = lax.all_gather(gate_up_weight, "row", axis=0, tiled=True).reshape(D, 2 * hidden_col)
    w_down = lax.all_gather(down_weight, "row", axis=1, tiled=True)

    def to_tokens(values):
        return lax.all_to_all(values, "row", split_axis=0, concat_axis=1, tiled=True)

    def to_width(values):
        return lax.all_to_all(values, "row", split_axis=1, concat_axis=0, tiled=True)

    def gather_col(values):
        return lax.all_gather(values, "col", axis=0, tiled=True)

    def scatter_col(values):
        return lax.psum_scatter(values.astype(low), "col", scatter_dimension=0, tiled=True).astype(wide)

    def to_heads(values, parts):
        by_head = values.reshape(group, parts, heads_col, HEAD).transpose(2, 0, 1, 3).reshape(heads_col, group, parts * HEAD)
        moved = lax.all_to_all(by_head, "row", split_axis=0, concat_axis=0, tiled=True)
        return (
            moved.reshape(row_count, col_count, own, parts * HEAD)
            .transpose(1, 0, 2, 3)
            .reshape(tree_tokens, parts * HEAD)
        )

    def from_heads(values, parts):
        by_row = (
            values.reshape(col_count, row_count, own, parts * HEAD)
            .transpose(1, 0, 2, 3)
            .reshape(row_count, group, parts * HEAD)
        )
        moved = lax.all_to_all(by_row, "row", split_axis=0, concat_axis=0, tiled=True)
        return moved.reshape(heads_col, group, parts, HEAD).transpose(1, 2, 0, 3).reshape(group, parts * width_col)

    x_own = to_tokens(tokens)
    x = gather_col(x_own)
    red_qkv = dot_t(x, a_qkv).astype(low)
    raw = dot(x, w_qkv)
    extra = jnp.concatenate([dot(red_qkv[:, RANK * j : RANK * (j + 1)], b_qkv[j]) for j in range(3)], axis=1)
    raw = raw + extra
    q_raw = raw[:, :width_col]
    k_raw = raw[:, width_col : 2 * width_col]
    v_raw = raw[:, 2 * width_col :]
    square_qk = lax.psum(jnp.stack([jnp.sum(q_raw * q_raw, axis=1), jnp.sum(k_raw * k_raw, axis=1)]), "col")
    q_factor = norm_factor(square_qk[0])
    k_factor = norm_factor(square_qk[1])
    q_flat = q_raw * q_factor[:, None]
    k_flat = k_raw * k_factor[:, None]
    pos_own = lax.dynamic_index_in_dim(
        positions.reshape(col_count, row_count, own), row_at, 1, keepdims=False
    ).reshape(group)
    cos_own, sin_own = angles(pos_own)

    def turn(values, sine):
        return rotate(values.reshape(group, heads_col, HEAD), cos_own, sine).reshape(group, width_col)

    q_low = turn(q_flat * gain_q, sin_own).astype(low)
    k_low = turn(k_flat * gain_k, sin_own).astype(low)
    qkv_head = to_heads(jnp.concatenate([q_low, k_low, v_raw.astype(low)], axis=1), 3)
    q_head = qkv_head[:, :HEAD]
    k_head = qkv_head[:, HEAD : 2 * HEAD]
    v_head = qkv_head[:, 2 * HEAD :]
    visible = tree_mask(seg_ids, positions, parents)
    scores = jnp.where(visible, dot_t(q_head, k_head) * score_scale, masked_out)
    highest = jnp.max(scores, axis=1, keepdims=True)
    raised = jnp.exp(scores - highest)
    probs = raised / jnp.sum(raised, axis=1, keepdims=True)
    probs_low = probs.astype(low)
    attn_head = dot(probs_low, v_head).astype(low)
    attn = from_heads(attn_head, 1)

    red_out = dot_t(attn, a_out).astype(low)
    a_raw = scatter_col(dot(attn, w_out) + dot(red_out, b_out))
    a_factor = norm_factor(jnp.sum(a_raw * a_raw, axis=1))
    a_flat = a_raw * a_factor[:, None]
    h_own = x_own.astype(wide) + a_flat * gains[0]
    h = gather_col(h_own.astype(low))

    red_gu = dot_t(h, a_gu).astype(low)
    gate = dot(h, w_gu[:, :hidden_col]) + dot(red_gu[:, :RANK], b_gu[0])
    up = dot(h, w_gu[:, hidden_col:]) + dot(red_gu[:, RANK:], b_gu[1])
    sigma = jax.nn.sigmoid(gate)
    hidden = (gate * sigma * up).astype(low)
    red_down = dot_t(hidden, a_down).astype(low)
    f_raw = scatter_col(dot(hidden, w_down) + dot(red_down, b_down))
    f_factor = norm_factor(jnp.sum(f_raw * f_raw, axis=1))
    f_flat = f_raw * f_factor[:, None]
    out_own = (h_own + f_flat * gains[1]).astype(low)
    layer_out = to_width(out_own)

    g_own = to_tokens(cotangent).astype(wide)
    scaled_f = g_own * gains[1]
    d_f_own = norm_back(scaled_f, f_flat, f_factor, jnp.sum(scaled_f * f_flat, axis=1)).astype(low)
    d_f = gather_col(d_f_own)
    back_down = dot_t(d_f, b_down).astype(low)
    d_hidden = dot_t(d_f, w_down) + dot(back_down, a_down)
    d_gate = (d_hidden * up * sigma * (1.0 + gate * (1.0 - sigma))).astype(low)
    d_up = (d_hidden * (gate * sigma)).astype(low)
    back_gate = dot_t(d_gate, b_gu[0]).astype(low)
    back_up = dot_t(d_up, b_gu[1]).astype(low)
    back_gu = jnp.concatenate([back_gate, back_up], axis=1)
    d_h = g_own + scatter_col(
        dot_t(d_gate, w_gu[:, :hidden_col]) + dot_t(d_up, w_gu[:, hidden_col:]) + dot(back_gu, a_gu)
    )
    scaled_a = d_h * gains[0]
    d_a_own = norm_back(scaled_a, a_flat, a_factor, jnp.sum(scaled_a * a_flat, axis=1)).astype(low)
    d_a = gather_col(d_a_own)
    back_out = dot_t(d_a, b_out).astype(low)
    d_attn = (dot_t(d_a, w_out) + dot(back_out, a_out)).astype(low)

    d_attn_head = to_heads(d_attn, 1)
    d_probs = dot_t(d_attn_head, v_head)
    inner = jnp.sum(probs * d_probs, axis=1, keepdims=True)
    d_scores = (probs * (d_probs - inner)).astype(low)
    dq_head = (dot(d_scores, k_head) * score_scale).astype(low)
    dk_head = (t_dot(d_scores, q_head) * score_scale).astype(low)
    dv_head = t_dot(probs_low, d_attn_head).astype(low)
    d_qkv = from_heads(jnp.concatenate([dq_head, dk_head, dv_head], axis=1), 3)
    dq_n = turn(d_qkv[:, :width_col].astype(wide), -sin_own) * gain_q
    dk_n = turn(d_qkv[:, width_col : 2 * width_col].astype(wide), -sin_own) * gain_k
    cross_qk = lax.psum(jnp.stack([jnp.sum(dq_n * q_flat, axis=1), jnp.sum(dk_n * k_flat, axis=1)]), "col")
    d_q = norm_back(dq_n, q_flat, q_factor, cross_qk[0]).astype(low)
    d_k = norm_back(dk_n, k_flat, k_factor, cross_qk[1]).astype(low)
    d_v = d_qkv[:, 2 * width_col :]
    d_raw = jnp.concatenate([d_q, d_k, d_v], axis=1)
    back_qkv = jnp.concatenate(
        [dot_t(d, b) for d, b in zip((d_q, d_k, d_v), (b_qkv[0], b_qkv[1], b_qkv[2]))], axis=1
    ).astype(low)
    in_own = d_h + scatter_col(dot_t(d_raw, w_qkv) + dot(back_qkv, a_qkv))
    input_grad = to_width(in_own.astype(low)).astype(wide)

    full_width = jnp.concatenate(
        [t_dot(back_qkv, x), t_dot(back_gu, h), t_dot(red_out, d_a), t_dot(red_down, d_f)], axis=0
    ).astype(low)
    full_width = lax.psum_scatter(full_width, "row", scatter_dimension=1, tiled=True)
    full_width = full_width.reshape(7, col_count, RANK // col_count, width_row).transpose(1, 0, 2, 3)
    full_width = lax.psum_scatter(full_width, "col", scatter_dimension=0, tiled=False)
    col_width = jnp.concatenate(
        [t_dot(red_qkv[:, RANK * j : RANK * (j + 1)], d) for j, d in enumerate((d_q, d_k, d_v))]
        + [t_dot(back_out, attn), t_dot(red_gu[:, :RANK], d_gate), t_dot(red_gu[:, RANK:], d_up), t_dot(back_down, hidden)],
        axis=1,
    ).astype(low)
    col_width = lax.psum_scatter(col_width, "row", scatter_dimension=0, tiled=True)
    onehot = (tree_set == jnp.arange(set_count, dtype=jnp.int32)).astype(wide)
    owner = jnp.concatenate([full_width.reshape(-1), col_width.reshape(-1)])
    owner_all = lax.all_gather(owner, "dp", axis=0, tiled=False).astype(wide)
    onehot_all = lax.all_gather(onehot, "dp", axis=0, tiled=False)
    sets_own = set_count // dp_count
    onehot_own = lax.dynamic_slice_in_dim(onehot_all, lax.axis_index("dp") * sets_own, sets_own, 1)
    per_set = jnp.sum(onehot_own[:, :, None] * owner_all[:, None, :], axis=0)
    split_at = full_width.size
    full_sets = per_set[:, :split_at].reshape(sets_own, 7, RANK // col_count, width_row)
    col_sets = per_set[:, split_at:].reshape(sets_own, RANK // row_count, -1)
    grad_a_qkv = full_sets[:, :3].transpose(1, 0, 2, 3)
    grad_a_gu = full_sets[:, 3:5].transpose(1, 0, 2, 3)
    grad_b_out = full_sets[:, 5]
    grad_b_down = full_sets[:, 6]
    grad_b_qkv = jnp.stack([col_sets[..., width_col * j : width_col * (j + 1)] for j in range(3)])
    grad_a_out = col_sets[..., 3 * width_col : 4 * width_col]
    gu_at = 4 * width_col
    grad_b_gu = jnp.stack([col_sets[..., gu_at + hidden_col * j : gu_at + hidden_col * (j + 1)] for j in range(2)])
    grad_a_down = col_sets[..., gu_at + 2 * hidden_col :]
    return (
        layer_out,
        input_grad,
        grad_a_qkv,
        grad_b_qkv,
        grad_a_out,
        grad_b_out,
        grad_a_gu,
        grad_b_gu,
        grad_a_down,
        grad_b_down,
    )


def solution(mesh):
    in_specs = (
        P(("dp", "col"), "row"),
        P(("dp", "col"), "row"),
        P("dp"),
        P("dp"),
        P("dp", None),
        P("dp"),
        P("col"),
        P("col"),
        P("row"),
        P("row"),
        P("row", None, "col"),
        P("col", "row"),
        P("row", None, "col"),
        P("col", "row"),
        P(None, None, None, "row"),
        P(None, None, None, "col"),
        P(None, None, "col"),
        P(None, None, "row"),
        P(None, None, None, "row"),
        P(None, None, None, "col"),
        P(None, None, "col"),
        P(None, None, "row"),
    )
    out_specs = (
        P(("dp", "col"), "row"),
        P(("dp", "col"), "row"),
        P(None, "dp", "col", "row"),
        P(None, "dp", "row", "col"),
        P("dp", "row", "col"),
        P("dp", "col", "row"),
        P(None, "dp", "col", "row"),
        P(None, "dp", "row", "col"),
        P("dp", "row", "col"),
        P("dp", "col", "row"),
    )
    return jax.shard_map(
        per_device, mesh=mesh, in_specs=in_specs, out_specs=out_specs, check_vma=False
    )
```

```python
import functools

import jax
import jax.numpy as jnp
from jax import lax
from jax.experimental import pallas as pl
from jax.experimental.pallas import tpu as pltpu
from jax.sharding import PartitionSpec as P

D = 2048
HEAD = 128
RANK = 16
SEG = 128
TRUNK = 1024
QT = 256
MESH = pl.DeviceIdType.MESH
VM = pl.BlockSpec(memory_space=pltpu.VMEM)

epsilon = 1e-06
rope_base = 500000.0
masked_out = -1e30
low = jnp.bfloat16
wide = jnp.float32
last_last = (((1,), (1,)), ((), ()))
first_first = (((0,), (0,)), ((), ()))


def dot(left, right):
    return jnp.dot(left, right, preferred_element_type=wide)


def dot_t(left, right):
    return lax.dot_general(left, right, last_last, preferred_element_type=wide)


def t_dot(left, right):
    return lax.dot_general(left, right, first_first, preferred_element_type=wide)


def angles(positions):
    half_width = HEAD // 2
    frequency = rope_base ** (-(jnp.arange(half_width, dtype=wide) * 2.0) / HEAD)
    angle_table = positions.astype(wide)[:, None] * frequency[None, :]
    return (jnp.cos(angle_table)[:, None, :], jnp.sin(angle_table)[:, None, :])


def rotate(values, cosine, sine):
    half_width = values.shape[-1] // 2
    first_half = values[..., :half_width]
    second_half = values[..., half_width:]
    return jnp.concatenate(
        [first_half * cosine - second_half * sine, second_half * cosine + first_half * sine],
        axis=-1,
    )


def norm_factor(square_sum):
    return lax.rsqrt(square_sum * (1.0 / D) + epsilon)


def norm_back(scaled, flat, factor, cross_sum):
    return factor[:, None] * (scaled - flat * (cross_sum / D)[:, None])


def tail_scores(q, k_ref, own_at, parent_at, has_parent, pos_q, pos_k):
    scale = HEAD ** -0.5
    s_trunk = dot_t(q, k_ref[:TRUNK, :]) * scale
    s_par = dot_t(q, k_ref[pl.ds(parent_at, SEG), :]) * scale
    s_par = jnp.where(has_parent > 0, s_par, masked_out)
    s_own = dot_t(q, k_ref[pl.ds(own_at, SEG), :]) * scale
    s_own = jnp.where(pos_k <= pos_q, s_own, masked_out)
    return s_trunk, s_par, s_own

def trunk_scores(q, k_ref, pos_q, pos_k):
    s = dot_t(q, k_ref[:TRUNK, :]) * HEAD ** -0.5
    return jnp.where(pos_k <= pos_q, s, masked_out)

def fwd_kernel(parent_ref, flag_ref, q_ref, k_ref, v_ref, posq_ref, posk_ref, o_ref, lse_ref):
    tails = (q_ref.shape[0] - TRUNK) // SEG
    @pl.loop(0, TRUNK // QT)
    def _(i):
        at = pl.multiple_of(i * QT, QT)
        s = trunk_scores(q_ref[pl.ds(at, QT), :], k_ref, posq_ref[pl.ds(at, QT), :], posk_ref[:, :TRUNK])
        top = jnp.max(s, axis=1, keepdims=True)
        e = jnp.exp(s - top)
        total = jnp.sum(e, axis=1, keepdims=True)
        p = (e * (1.0 / total)).astype(low)
        o_ref[pl.ds(at, QT), :] = dot(p, v_ref[:TRUNK, :]).astype(low)
        lse_ref[pl.ds(at, QT), :] = top + jnp.log(total)
    @pl.loop(0, tails)
    def _(j):
        at = pl.multiple_of(TRUNK + j * SEG, SEG)
        par = pl.multiple_of(parent_ref[j] * SEG, SEG)
        s1, s2, s3 = tail_scores(q_ref[pl.ds(at, SEG), :], k_ref, at, par, flag_ref[j],
                                 posq_ref[pl.ds(at, SEG), :], posk_ref[:, pl.ds(at, SEG)])
        top = jnp.maximum(jnp.maximum(jnp.max(s1, axis=1, keepdims=True), jnp.max(s2, axis=1, keepdims=True)),
                          jnp.max(s3, axis=1, keepdims=True))
        e1 = jnp.exp(s1 - top); e2 = jnp.exp(s2 - top); e3 = jnp.exp(s3 - top)
        total = jnp.sum(e1, axis=1, keepdims=True) + jnp.sum(e2, axis=1, keepdims=True) + jnp.sum(e3, axis=1, keepdims=True)
        inv = 1.0 / total
        o = dot((e1 * inv).astype(low), v_ref[:TRUNK, :])
        o += dot((e2 * inv).astype(low), v_ref[pl.ds(par, SEG), :])
        o += dot((e3 * inv).astype(low), v_ref[pl.ds(at, SEG), :])
        o_ref[pl.ds(at, SEG), :] = o.astype(low)
        lse_ref[pl.ds(at, SEG), :] = top + jnp.log(total)

def bwd_kernel(parent_ref, flag_ref, q_ref, k_ref, v_ref, do_ref, posq_ref, posk_ref, lse_ref, d_ref, dk_acc, dv_acc):
    scale = HEAD ** -0.5
    tails = (q_ref.shape[0] - TRUNK) // SEG
    dk_acc[...] = jnp.zeros_like(dk_acc)
    dv_acc[...] = jnp.zeros_like(dv_acc)
    @pl.loop(0, TRUNK // QT)
    def _(i):
        at = pl.multiple_of(i * QT, QT)
        q = q_ref[pl.ds(at, QT), :]
        do = do_ref[pl.ds(at, QT), :]
        s = trunk_scores(q, k_ref, posq_ref[pl.ds(at, QT), :], posk_ref[:, :TRUNK])
        p = jnp.exp(s - lse_ref[pl.ds(at, QT), :])
        dp = dot_t(do, v_ref[:TRUNK, :])
        inner = jnp.sum(p * dp, axis=1, keepdims=True)
        ds = (p * (dp - inner)).astype(low)
        d_ref[pl.ds(at, QT), :HEAD] = (dot(ds, k_ref[:TRUNK, :]) * scale).astype(low)
        dk_acc[:TRUNK, :] += t_dot(ds, q)
        dv_acc[:TRUNK, :] += t_dot(p.astype(low), do)
    @pl.loop(0, tails)
    def _(j):
        at = pl.multiple_of(TRUNK + j * SEG, SEG)
        par = pl.multiple_of(parent_ref[j] * SEG, SEG)
        q = q_ref[pl.ds(at, SEG), :]
        do = do_ref[pl.ds(at, SEG), :]
        lse = lse_ref[pl.ds(at, SEG), :]
        s1, s2, s3 = tail_scores(q, k_ref, at, par, flag_ref[j],
                                 posq_ref[pl.ds(at, SEG), :], posk_ref[:, pl.ds(at, SEG)])
        p1 = jnp.exp(s1 - lse); p2 = jnp.exp(s2 - lse); p3 = jnp.exp(s3 - lse)
        d1 = dot_t(do, v_ref[:TRUNK, :])
        d2 = dot_t(do, v_ref[pl.ds(par, SEG), :])
        d3 = dot_t(do, v_ref[pl.ds(at, SEG), :])
        inner = jnp.sum(p1 * d1, axis=1, keepdims=True) + jnp.sum(p2 * d2, axis=1, keepdims=True) + jnp.sum(p3 * d3, axis=1, keepdims=True)
        g1 = (p1 * (d1 - inner)).astype(low)
        g2 = (p2 * (d2 - inner)).astype(low)
        g3 = (p3 * (d3 - inner)).astype(low)
        dq = dot(g1, k_ref[:TRUNK, :]) + dot(g2, k_ref[pl.ds(par, SEG), :]) + dot(g3, k_ref[pl.ds(at, SEG), :])
        d_ref[pl.ds(at, SEG), :HEAD] = (dq * scale).astype(low)
        dk_acc[:TRUNK, :] += t_dot(g1, q)
        dv_acc[:TRUNK, :] += t_dot(p1.astype(low), do)
        dk_acc[pl.ds(par, SEG), :] += t_dot(g2, q)
        dv_acc[pl.ds(par, SEG), :] += t_dot(p2.astype(low), do)
        dk_acc[pl.ds(at, SEG), :] += t_dot(g3, q)
        dv_acc[pl.ds(at, SEG), :] += t_dot(p3.astype(low), do)
    d_ref[:, HEAD:2 * HEAD] = (dk_acc[...] * scale).astype(low)
    d_ref[:, 2 * HEAD:] = dv_acc[...].astype(low)

def whole(shape, at=0):
    return pl.BlockSpec(shape, lambda i, *_: (0, at))

def attend(qkv, parent_at, flag, posq, posk):
    n = qkv.shape[0]
    return pl.pallas_call(
        fwd_kernel,
        grid_spec=pltpu.PrefetchScalarGridSpec(
            num_scalar_prefetch=2, grid=(1,),
            in_specs=[whole((n, HEAD), 0), whole((n, HEAD), 1), whole((n, HEAD), 2), whole((n, 1)), whole((1, n))],
            out_specs=[whole((n, HEAD)), whole((n, 1))]),
        out_shape=[jax.ShapeDtypeStruct((n, HEAD), low), jax.ShapeDtypeStruct((n, 1), wide)],
        name="attend",
    )(parent_at, flag, qkv, qkv, qkv, posq, posk)

def attend_back(qkv, d_o, parent_at, flag, posq, posk, lse):
    n = qkv.shape[0]
    return pl.pallas_call(
        bwd_kernel,
        grid_spec=pltpu.PrefetchScalarGridSpec(
            num_scalar_prefetch=2, grid=(1,),
            in_specs=[whole((n, HEAD), 0), whole((n, HEAD), 1), whole((n, HEAD), 2), whole((n, HEAD)), whole((n, 1)), whole((1, n)), whole((n, 1))],
            out_specs=whole((n, 3 * HEAD)),
            scratch_shapes=[pltpu.VMEM((n, HEAD), wide), pltpu.VMEM((n, HEAD), wide)]),
        out_shape=jax.ShapeDtypeStruct((n, 3 * HEAD), low),
        name="attend_back",
    )(parent_at, flag, qkv, qkv, qkv, d_o, posq, posk, lse)

def tree_tables(seg_ids, parents):
    tail_seg = seg_ids[TRUNK::SEG]
    labels = jnp.arange(parents.shape[1], dtype=jnp.int32)
    tail_parent = jnp.sum(jnp.where(tail_seg[:, None] == labels[None, :], parents[0][None, :], 0), axis=1)
    hit = (tail_seg[None, :] == tail_parent[:, None])
    at = jnp.arange(tail_seg.shape[0], dtype=jnp.int32) + TRUNK // SEG
    parent_at = jnp.sum(jnp.where(hit, at[None, :], 0), axis=1)
    flag = (tail_parent > 0).astype(jnp.int32)
    return parent_at, flag


def row_sum(v): return jnp.sum(v, axis=1, keepdims=True)

def owner_step(mode, total, rows_all, rows_own, ins, outs):
    if mode == "attn":
        x_ref, gain_ref = ins
        (raw_ref,) = outs
        raw_ref[rows_own, :] = total
        flat = total * norm_factor(row_sum(total * total))
        return (x_ref[rows_all, :].astype(wide) + flat * gain_ref[0:1, :]).astype(low)
    if mode == "ffn":
        x_ref, gain_ref, raw_ref, cot_ref = ins
        (out_ref,) = outs
        raw = raw_ref[rows_own, :]
        h = x_ref[rows_all, :].astype(wide) + raw * norm_factor(row_sum(raw * raw)) * gain_ref[0:1, :]
        factor = norm_factor(row_sum(total * total))
        flat = total * factor
        gain = gain_ref[1:2, :]
        out_ref[rows_own, :] = (h + flat * gain).astype(low)
        scaled = cot_ref[rows_own, :].astype(wide) * gain
        return (factor * (scaled - flat * (row_sum(scaled * flat) * (1.0 / D)))).astype(low)
    gain_ref, raw_ref, cot_ref = ins
    (grad_ref,) = outs
    grad = cot_ref[rows_own, :].astype(wide) + total
    grad_ref[rows_own, :] = grad
    raw = raw_ref[rows_own, :]
    factor = norm_factor(row_sum(raw * raw))
    flat = raw * factor
    scaled = grad * gain_ref[0:1, :]
    return (factor * (scaled - flat * (row_sum(scaled * flat) * (1.0 / D)))).astype(low)

def relay_kernel(mode, n, m, hop, n_in, part_ref, *refs):
    ins = refs[:n_in]
    all_ref = refs[n_in]
    outs = refs[n_in + 1:n_in + 2]
    recv_right, recv_left, send_right, send_left, sems_send, sems_recv = refs[n_in + 2:]
    c = lax.axis_index("col")
    half = part_ref.shape[0] // 2
    chunks = half // m
    left = {"col": jnp.maximum(c - 1, 0)}
    right = {"col": jnp.minimum(c + 1, n - 1)}
    first = c == 0
    last = c == n - 1
    inner = jnp.logical_and(c > 0, c < n - 1)

    def rows(j, base=0):
        return pl.ds(pl.multiple_of(base + j * m, m), m)

    def send(kind, j, src, dst, to):
        return pltpu.make_async_remote_copy(src_ref=src, dst_ref=dst, send_sem=sems_send.at[kind, j],
                                            recv_sem=sems_recv.at[kind, j], device_id=to, device_id_type=MESH)

    def reduce_right(j):
        return send(0, j, part_ref.at[rows(j, half)], recv_right.at[rows(j)], right)
    def reduce_right_mid(j):
        return send(0, j, send_right.at[rows(j)], recv_right.at[rows(j)], right)
    def reduce_left(j):
        return send(1, j, part_ref.at[rows(j)], recv_left.at[rows(j)], left)
    def reduce_left_mid(j):
        return send(1, j, send_left.at[rows(j)], recv_left.at[rows(j)], left)
    def spread_left(j):
        return send(2, j, all_ref.at[rows(j, half)], all_ref.at[rows(j, half)], left)
    def spread_right(j):
        return send(3, j, all_ref.at[rows(j)], all_ref.at[rows(j)], right)

    barrier = pltpu.get_barrier_semaphore()
    @pl.when(c > 0)
    def _():
        pl.semaphore_signal(barrier, inc=1, device_id=left, device_id_type=MESH)
    @pl.when(c < n - 1)
    def _():
        pl.semaphore_signal(barrier, inc=1, device_id=right, device_id_type=MESH)
    @pl.when(inner)
    def _():
        pl.semaphore_wait(barrier, 2)
    @pl.when(jnp.logical_not(inner))
    def _():
        pl.semaphore_wait(barrier, 1)

    @pl.loop(0, chunks + hop * 2 * (n - 1))
    def _(i):
        def on(offset, who, run):
            j = i - offset
            @pl.when(jnp.logical_and(who, jnp.logical_and(j >= 0, j < chunks)))
            def _():
                run(j)

        def first_right(j):
            reduce_right(j).start()
        def mid_right(j):
            reduce_right_mid(j).wait_recv()
            send_right[rows(j), :] = (part_ref[rows(j, half), :].astype(wide) + recv_right[rows(j), :].astype(wide)).astype(low)
            reduce_right_mid(j).start()
        def end_right(j):
            reduce_right_mid(j).wait_recv()
            total = part_ref[rows(j, half), :].astype(wide) + recv_right[rows(j), :].astype(wide)
            all_ref[rows(j, half), :] = owner_step(mode, total, rows(j, half), rows(j), ins, outs)
            spread_left(j).start()
        def first_left(j):
            reduce_left(j).start()
        def mid_left(j):
            reduce_left_mid(j).wait_recv()
            send_left[rows(j), :] = (part_ref[rows(j), :].astype(wide) + recv_left[rows(j), :].astype(wide)).astype(low)
            reduce_left_mid(j).start()
        def end_left(j):
            reduce_left_mid(j).wait_recv()
            total = part_ref[rows(j), :].astype(wide) + recv_left[rows(j), :].astype(wide)
            all_ref[rows(j), :] = owner_step(mode, total, rows(j), rows(j), ins, outs)
            spread_right(j).start()
        def pass_left(j):
            spread_left(j).wait_recv()
            spread_left(j).start()
        def pass_right(j):
            spread_right(j).wait_recv()
            spread_right(j).start()

        on(0, first, first_right)
        on(0, last, first_left)
        on(hop * c, inner, mid_right)
        on(hop * (n - 1 - c), inner, mid_left)
        on(hop * (n - 1), last, end_right)
        on(hop * (n - 1), first, end_left)
        on(hop * (2 * (n - 1) - c), inner, pass_left)
        on(hop * (n - 1 + c), inner, pass_right)

    @pl.loop(0, chunks)
    def _(j):
        @pl.when(first)
        def _():
            reduce_right(j).wait_send()
            spread_right(j).wait_send()
            spread_left(j).wait_recv()
        @pl.when(last)
        def _():
            reduce_left(j).wait_send()
            spread_left(j).wait_send()
            spread_right(j).wait_recv()
        @pl.when(inner)
        def _():
            reduce_right_mid(j).wait_send()
            reduce_left_mid(j).wait_send()
            spread_left(j).wait_send()
            spread_right(j).wait_send()

kinds = {"attn": 0, "ffn": 1, "back": 2}

def relay(mode, part, ins, n, m=16, hop=2):
    group, width = part.shape
    half = group // 2
    chunks = half // m
    saved = jax.ShapeDtypeStruct((half, width), low if mode == "ffn" else wide)
    return pl.pallas_call(
        functools.partial(relay_kernel, mode, n, m, hop, len(ins)),
        out_shape=[jax.ShapeDtypeStruct((group, width), low), saved],
        in_specs=[VM] * (1 + len(ins)),
        out_specs=[VM] * 2,
        scratch_shapes=[pltpu.VMEM((half, width), low)] * 4
        + [pltpu.SemaphoreType.DMA((4, chunks))] * 2,
        compiler_params=pltpu.CompilerParams(collective_id=kinds[mode], has_side_effects=True, vmem_limit_bytes=60 << 20),
        name="relay_" + mode,
    )(part, *ins)


def per_device(
    tokens,
    cotangent,
    seg_ids,
    positions,
    parents,
    tree_sets,
    gain_q,
    gain_k,
    gain_attn,
    gain_ffn,
    query_key_value_weight,
    output_weight,
    gate_up_weight,
    down_weight,
    query_key_value_adapter_first,
    query_key_value_adapter_second,
    output_adapter_first,
    output_adapter_second,
    gate_up_adapter_first,
    gate_up_adapter_second,
    down_adapter_first,
    down_adapter_second,
):
    dp_count = lax.axis_size("dp")
    row_count = lax.axis_size("row")
    col_count = lax.axis_size("col")
    row_at = lax.axis_index("row")
    tree_tokens = seg_ids.shape[0]
    assert tree_sets.shape[0] == 1 and col_count == 4
    set_count = output_adapter_first.shape[0]
    own = tokens.shape[0] // row_count
    group = own * col_count
    width_row = tokens.shape[1]
    width_col = gain_q.shape[0]
    hidden_col = down_weight.shape[0]
    heads_col = width_col // HEAD
    tree_set = tree_sets[0]

    def pick(table, axis):
        return lax.dynamic_index_in_dim(table, tree_set, axis, keepdims=False)

    narrow = jnp.concatenate(
        [
            pick(query_key_value_adapter_first, 1),
            pick(gate_up_adapter_first, 1),
            pick(output_adapter_second, 0)[None],
            pick(down_adapter_second, 0)[None],
        ],
        axis=0,
    ).astype(low)
    narrow_all = lax.all_gather(narrow, "row", axis=2, tiled=True)
    a_qkv = narrow_all[:3].reshape(3 * RANK, D)
    a_gu = narrow_all[3:5].reshape(2 * RANK, D)
    b_out = narrow_all[5]
    b_down = narrow_all[6]
    b_qkv = pick(query_key_value_adapter_second, 1).astype(low)
    b_gu = pick(gate_up_adapter_second, 1).astype(low)
    a_out = pick(output_adapter_first, 0).astype(low)
    a_down = pick(down_adapter_first, 0).astype(low)
    gains = lax.all_gather(jnp.stack([gain_attn, gain_ffn]), "row", axis=1, tiled=True)

    w_qkv = lax.all_gather(query_key_value_weight, "row", axis=0, tiled=True).reshape(D, 3 * width_col)
    w_out = lax.all_gather(output_weight, "row", axis=1, tiled=True)
    w_gu = lax.all_gather(gate_up_weight, "row", axis=0, tiled=True).reshape(D, 2 * hidden_col)
    w_down = lax.all_gather(down_weight, "row", axis=1, tiled=True)

    def to_tokens(values):
        return lax.all_to_all(values, "row", split_axis=0, concat_axis=1, tiled=True)

    def to_width(values):
        return lax.all_to_all(values, "row", split_axis=1, concat_axis=0, tiled=True)

    def gather_col(values):
        return lax.all_gather(values, "col", axis=0, tiled=True)

    def scatter_col(values):
        return lax.psum_scatter(values.astype(low), "col", scatter_dimension=0, tiled=True).astype(wide)

    def to_heads(values, parts):
        by_head = values.reshape(group, parts, heads_col, HEAD).transpose(2, 0, 1, 3).reshape(heads_col, group, parts * HEAD)
        moved = lax.all_to_all(by_head, "row", split_axis=0, concat_axis=0, tiled=True)
        return (
            moved.reshape(row_count, col_count, own, parts * HEAD)
            .transpose(1, 0, 2, 3)
            .reshape(tree_tokens, parts * HEAD)
        )

    def from_heads(values, parts):
        by_row = (
            values.reshape(col_count, row_count, own, parts * HEAD)
            .transpose(1, 0, 2, 3)
            .reshape(row_count, group, parts * HEAD)
        )
        moved = lax.all_to_all(by_row, "row", split_axis=0, concat_axis=0, tiled=True)
        return moved.reshape(heads_col, group, parts, HEAD).transpose(1, 2, 0, 3).reshape(group, parts * width_col)

    first = lax.axis_index("col") == 0
    final = lax.axis_index("col") == col_count - 1
    x_own = to_tokens(tokens)
    g_own = to_tokens(cotangent)
    g_moved = lax.ppermute(g_own, "col", [(1, 0), (col_count - 2, col_count - 1)])
    g_half = jnp.concatenate([jnp.where(first, g_own, g_moved), jnp.where(first, g_moved, g_own)], axis=0)
    x = gather_col(x_own)
    red_qkv = dot_t(x, a_qkv).astype(low)
    raw = dot(x, w_qkv)
    extra = jnp.concatenate([dot(red_qkv[:, RANK * j : RANK * (j + 1)], b_qkv[j]) for j in range(3)], axis=1)
    raw = raw + extra
    q_raw = raw[:, :width_col]
    k_raw = raw[:, width_col : 2 * width_col]
    v_raw = raw[:, 2 * width_col :]
    square_qk = lax.psum(jnp.stack([jnp.sum(q_raw * q_raw, axis=1), jnp.sum(k_raw * k_raw, axis=1)]), "col")
    q_factor = norm_factor(square_qk[0])
    k_factor = norm_factor(square_qk[1])
    q_flat = q_raw * q_factor[:, None]
    k_flat = k_raw * k_factor[:, None]
    pos_own = lax.dynamic_index_in_dim(
        positions.reshape(col_count, row_count, own), row_at, 1, keepdims=False
    ).reshape(group)
    cos_own, sin_own = angles(pos_own)

    def turn(values, sine):
        return rotate(values.reshape(group, heads_col, HEAD), cos_own, sine).reshape(group, width_col)

    q_low = turn(q_flat * gain_q, sin_own).astype(low)
    k_low = turn(k_flat * gain_k, sin_own).astype(low)
    qkv_head = to_heads(jnp.concatenate([q_low, k_low, v_raw.astype(low)], axis=1), 3)
    parent_at, branch_flag = tree_tables(seg_ids, parents)
    pos_down, pos_across = positions[:, None], positions[None, :]
    attn_head, lse = attend(qkv_head, parent_at, branch_flag, pos_down, pos_across)
    attn = from_heads(attn_head, 1)

    red_out = dot_t(attn, a_out).astype(low)
    part_a = (dot(attn, w_out) + dot(red_out, b_out)).astype(low)
    h, a_raw = relay("attn", part_a, (x, gains), col_count)

    red_gu = dot_t(h, a_gu).astype(low)
    gate = dot(h, w_gu[:, :hidden_col]) + dot(red_gu[:, :RANK], b_gu[0])
    up = dot(h, w_gu[:, hidden_col:]) + dot(red_gu[:, RANK:], b_gu[1])
    sigma = jax.nn.sigmoid(gate)
    hidden = (gate * sigma * up).astype(low)
    red_down = dot_t(hidden, a_down).astype(low)
    part_f = (dot(hidden, w_down) + dot(red_down, b_down)).astype(low)
    d_f, out_half = relay("ffn", part_f, (x, gains, a_raw, g_half), col_count)
    out_moved = lax.ppermute(
        jnp.where(first, out_half[own:], out_half[:own]), "col", [(0, 1), (col_count - 1, col_count - 2)]
    )
    out_own = jnp.where(first, out_half[:own], jnp.where(final, out_half[own:], out_moved))
    layer_out = to_width(out_own)

    back_down = dot_t(d_f, b_down).astype(low)
    d_hidden = dot_t(d_f, w_down) + dot(back_down, a_down)
    d_gate = (d_hidden * up * sigma * (1.0 + gate * (1.0 - sigma))).astype(low)
    d_up = (d_hidden * (gate * sigma)).astype(low)
    back_gate = dot_t(d_gate, b_gu[0]).astype(low)
    back_up = dot_t(d_up, b_gu[1]).astype(low)
    back_gu = jnp.concatenate([back_gate, back_up], axis=1)
    part_h = (
        dot_t(d_gate, w_gu[:, :hidden_col]) + dot_t(d_up, w_gu[:, hidden_col:]) + dot(back_gu, a_gu)
    ).astype(low)
    d_a, d_h_half = relay("back", part_h, (gains, a_raw, g_half), col_count)
    back_out = dot_t(d_a, b_out).astype(low)
    d_attn = (dot_t(d_a, w_out) + dot(back_out, a_out)).astype(low)

    d_attn_head = to_heads(d_attn, 1)
    d_qkv_head = attend_back(
        qkv_head, d_attn_head, parent_at, branch_flag, pos_down, pos_across, lse
    )
    d_qkv = from_heads(d_qkv_head, 3)
    dq_n = turn(d_qkv[:, :width_col].astype(wide), -sin_own) * gain_q
    dk_n = turn(d_qkv[:, width_col : 2 * width_col].astype(wide), -sin_own) * gain_k
    cross_qk = lax.psum(jnp.stack([jnp.sum(dq_n * q_flat, axis=1), jnp.sum(dk_n * k_flat, axis=1)]), "col")
    d_q = norm_back(dq_n, q_flat, q_factor, cross_qk[0]).astype(low)
    d_k = norm_back(dk_n, k_flat, k_factor, cross_qk[1]).astype(low)
    d_v = d_qkv[:, 2 * width_col :]
    d_raw = jnp.concatenate([d_q, d_k, d_v], axis=1)
    back_qkv = jnp.concatenate(
        [dot_t(d, b) for d, b in zip((d_q, d_k, d_v), (b_qkv[0], b_qkv[1], b_qkv[2]))], axis=1
    ).astype(low)
    d_h_all = jnp.concatenate([jnp.where(first, d_h_half, 0.0), jnp.where(final, d_h_half, 0.0)], axis=0)
    in_own = scatter_col(dot_t(d_raw, w_qkv) + dot(back_qkv, a_qkv) + d_h_all)
    input_grad = to_width(in_own.astype(low)).astype(wide)

    full_width = jnp.concatenate(
        [t_dot(back_qkv, x), t_dot(back_gu, h), t_dot(red_out, d_a), t_dot(red_down, d_f)], axis=0
    ).astype(low)
    full_width = lax.psum_scatter(full_width, "row", scatter_dimension=1, tiled=True)
    full_width = full_width.reshape(7, col_count, RANK // col_count, width_row).transpose(1, 0, 2, 3)
    full_width = lax.psum_scatter(full_width, "col", scatter_dimension=0, tiled=False)
    col_width = jnp.concatenate(
        [t_dot(red_qkv[:, RANK * j : RANK * (j + 1)], d) for j, d in enumerate((d_q, d_k, d_v))]
        + [t_dot(back_out, attn), t_dot(red_gu[:, :RANK], d_gate), t_dot(red_gu[:, RANK:], d_up), t_dot(back_down, hidden)],
        axis=1,
    ).astype(low)
    col_width = lax.psum_scatter(col_width, "row", scatter_dimension=0, tiled=True)
    onehot = (tree_set == jnp.arange(set_count, dtype=jnp.int32)).astype(wide)
    owner = jnp.concatenate([full_width.reshape(-1), col_width.reshape(-1)])
    owner_all = lax.all_gather(owner, "dp", axis=0, tiled=False).astype(wide)
    onehot_all = lax.all_gather(onehot, "dp", axis=0, tiled=False)
    sets_own = set_count // dp_count
    onehot_own = lax.dynamic_slice_in_dim(onehot_all, lax.axis_index("dp") * sets_own, sets_own, 1)
    per_set = jnp.sum(onehot_own[:, :, None] * owner_all[:, None, :], axis=0)
    split_at = full_width.size
    full_sets = per_set[:, :split_at].reshape(sets_own, 7, RANK // col_count, width_row)
    col_sets = per_set[:, split_at:].reshape(sets_own, RANK // row_count, -1)
    grad_a_qkv = full_sets[:, :3].transpose(1, 0, 2, 3)
    grad_a_gu = full_sets[:, 3:5].transpose(1, 0, 2, 3)
    grad_b_out = full_sets[:, 5]
    grad_b_down = full_sets[:, 6]
    grad_b_qkv = jnp.stack([col_sets[..., width_col * j : width_col * (j + 1)] for j in range(3)])
    grad_a_out = col_sets[..., 3 * width_col : 4 * width_col]
    gu_at = 4 * width_col
    grad_b_gu = jnp.stack([col_sets[..., gu_at + hidden_col * j : gu_at + hidden_col * (j + 1)] for j in range(2)])
    grad_a_down = col_sets[..., gu_at + 2 * hidden_col :]
    return (
        layer_out,
        input_grad,
        grad_a_qkv,
        grad_b_qkv,
        grad_a_out,
        grad_b_out,
        grad_a_gu,
        grad_b_gu,
        grad_a_down,
        grad_b_down,
    )


def solution(mesh):
    in_specs = (
        P(("dp", "col"), "row"),
        P(("dp", "col"), "row"),
        P("dp"),
        P("dp"),
        P("dp", None),
        P("dp"),
        P("col"),
        P("col"),
        P("row"),
        P("row"),
        P("row", None, "col"),
        P("col", "row"),
        P("row", None, "col"),
        P("col", "row"),
        P(None, None, None, "row"),
        P(None, None, None, "col"),
        P(None, None, "col"),
        P(None, None, "row"),
        P(None, None, None, "row"),
        P(None, None, None, "col"),
        P(None, None, "col"),
        P(None, None, "row"),
    )
    out_specs = (
        P(("dp", "col"), "row"),
        P(("dp", "col"), "row"),
        P(None, "dp", "col", "row"),
        P(None, "dp", "row", "col"),
        P("dp", "row", "col"),
        P("dp", "col", "row"),
        P(None, "dp", "col", "row"),
        P(None, "dp", "row", "col"),
        P("dp", "row", "col"),
        P("dp", "col", "row"),
    )
    return jax.shard_map(
        per_device, mesh=mesh, in_specs=in_specs, out_specs=out_specs, check_vma=False
    )
```

```python
import functools

import jax
import jax.numpy as jnp
from jax import lax
from jax.experimental import pallas as pl
from jax.experimental.pallas import tpu as pltpu
from jax.sharding import PartitionSpec as P

D = 2048
HEAD = 128
RANK = 16
SEG = 128
TRUNK = 1024
QT = 256
MESH = pl.DeviceIdType.MESH
VM = pl.BlockSpec(memory_space=pltpu.VMEM)
precise = lax.Precision.HIGHEST

epsilon = 1e-06
rope_base = 500000.0
masked_out = -1e30
low = jnp.bfloat16
wide = jnp.float32
last_last = (((1,), (1,)), ((), ()))
first_first = (((0,), (0,)), ((), ()))


def dot(left, right):
    return jnp.dot(left, right, preferred_element_type=wide)


def dot_t(left, right):
    return lax.dot_general(left, right, last_last, preferred_element_type=wide)


def t_dot(left, right):
    return lax.dot_general(left, right, first_first, preferred_element_type=wide)


def angles(positions):
    half_width = HEAD // 2
    frequency = rope_base ** (-(jnp.arange(half_width, dtype=wide) * 2.0) / HEAD)
    angle_table = positions.astype(wide)[:, None] * frequency[None, :]
    return (jnp.cos(angle_table), jnp.sin(angle_table))


def norm_factor(square_sum):
    return lax.rsqrt(square_sum * (1.0 / D) + epsilon)


def tail_scores(q, k_ref, own_at, parent_at, has_parent, pos_q, pos_k):
    scale = HEAD ** -0.5
    s_trunk = dot_t(q, k_ref[:TRUNK, :]) * scale
    s_par = dot_t(q, k_ref[pl.ds(parent_at, SEG), :]) * scale
    s_par = jnp.where(has_parent > 0, s_par, masked_out)
    s_own = dot_t(q, k_ref[pl.ds(own_at, SEG), :]) * scale
    s_own = jnp.where(pos_k <= pos_q, s_own, masked_out)
    return s_trunk, s_par, s_own

def trunk_scores(q, k_ref, pos_q, pos_k):
    s = dot_t(q, k_ref[:TRUNK, :]) * HEAD ** -0.5
    return jnp.where(pos_k <= pos_q, s, masked_out)

def fwd_kernel(parent_ref, flag_ref, q_ref, k_ref, v_ref, posq_ref, posk_ref, o_ref, lse_ref):
    tails = (q_ref.shape[0] - TRUNK) // SEG
    @pl.loop(0, TRUNK // QT)
    def _(i):
        at = pl.multiple_of(i * QT, QT)
        s = trunk_scores(q_ref[pl.ds(at, QT), :], k_ref, posq_ref[pl.ds(at, QT), :], posk_ref[:, :TRUNK])
        top = jnp.max(s, axis=1, keepdims=True)
        e = jnp.exp(s - top)
        total = jnp.sum(e, axis=1, keepdims=True)
        p = (e * (1.0 / total)).astype(low)
        o_ref[pl.ds(at, QT), :] = dot(p, v_ref[:TRUNK, :]).astype(low)
        lse_ref[pl.ds(at, QT), :] = top + jnp.log(total)
    @pl.loop(0, tails)
    def _(j):
        at = pl.multiple_of(TRUNK + j * SEG, SEG)
        par = pl.multiple_of(parent_ref[j] * SEG, SEG)
        s1, s2, s3 = tail_scores(q_ref[pl.ds(at, SEG), :], k_ref, at, par, flag_ref[j],
                                 posq_ref[pl.ds(at, SEG), :], posk_ref[:, pl.ds(at, SEG)])
        top = jnp.maximum(jnp.maximum(jnp.max(s1, axis=1, keepdims=True), jnp.max(s2, axis=1, keepdims=True)),
                          jnp.max(s3, axis=1, keepdims=True))
        e1 = jnp.exp(s1 - top); e2 = jnp.exp(s2 - top); e3 = jnp.exp(s3 - top)
        total = jnp.sum(e1, axis=1, keepdims=True) + jnp.sum(e2, axis=1, keepdims=True) + jnp.sum(e3, axis=1, keepdims=True)
        inv = 1.0 / total
        o = dot((e1 * inv).astype(low), v_ref[:TRUNK, :])
        o += dot((e2 * inv).astype(low), v_ref[pl.ds(par, SEG), :])
        o += dot((e3 * inv).astype(low), v_ref[pl.ds(at, SEG), :])
        o_ref[pl.ds(at, SEG), :] = o.astype(low)
        lse_ref[pl.ds(at, SEG), :] = top + jnp.log(total)

def bwd_kernel(parent_ref, flag_ref, q_ref, k_ref, v_ref, do_ref, posq_ref, posk_ref, lse_ref, d_ref, dk_acc, dv_acc):
    scale = HEAD ** -0.5
    tails = (q_ref.shape[0] - TRUNK) // SEG
    dk_acc[...] = jnp.zeros_like(dk_acc)
    dv_acc[...] = jnp.zeros_like(dv_acc)
    @pl.loop(0, TRUNK // QT)
    def _(i):
        at = pl.multiple_of(i * QT, QT)
        q = q_ref[pl.ds(at, QT), :]
        do = do_ref[pl.ds(at, QT), :]
        s = trunk_scores(q, k_ref, posq_ref[pl.ds(at, QT), :], posk_ref[:, :TRUNK])
        p = jnp.exp(s - lse_ref[pl.ds(at, QT), :])
        dp = dot_t(do, v_ref[:TRUNK, :])
        inner = jnp.sum(p * dp, axis=1, keepdims=True)
        ds = (p * (dp - inner)).astype(low)
        d_ref[pl.ds(at, QT), :HEAD] = (dot(ds, k_ref[:TRUNK, :]) * scale).astype(low)
        dk_acc[:TRUNK, :] += t_dot(ds, q)
        dv_acc[:TRUNK, :] += t_dot(p.astype(low), do)
    @pl.loop(0, tails)
    def _(j):
        at = pl.multiple_of(TRUNK + j * SEG, SEG)
        par = pl.multiple_of(parent_ref[j] * SEG, SEG)
        q = q_ref[pl.ds(at, SEG), :]
        do = do_ref[pl.ds(at, SEG), :]
        lse = lse_ref[pl.ds(at, SEG), :]
        s1, s2, s3 = tail_scores(q, k_ref, at, par, flag_ref[j],
                                 posq_ref[pl.ds(at, SEG), :], posk_ref[:, pl.ds(at, SEG)])
        p1 = jnp.exp(s1 - lse); p2 = jnp.exp(s2 - lse); p3 = jnp.exp(s3 - lse)
        d1 = dot_t(do, v_ref[:TRUNK, :])
        d2 = dot_t(do, v_ref[pl.ds(par, SEG), :])
        d3 = dot_t(do, v_ref[pl.ds(at, SEG), :])
        inner = jnp.sum(p1 * d1, axis=1, keepdims=True) + jnp.sum(p2 * d2, axis=1, keepdims=True) + jnp.sum(p3 * d3, axis=1, keepdims=True)
        g1 = (p1 * (d1 - inner)).astype(low)
        g2 = (p2 * (d2 - inner)).astype(low)
        g3 = (p3 * (d3 - inner)).astype(low)
        dq = dot(g1, k_ref[:TRUNK, :]) + dot(g2, k_ref[pl.ds(par, SEG), :]) + dot(g3, k_ref[pl.ds(at, SEG), :])
        d_ref[pl.ds(at, SEG), :HEAD] = (dq * scale).astype(low)
        dk_acc[:TRUNK, :] += t_dot(g1, q)
        dv_acc[:TRUNK, :] += t_dot(p1.astype(low), do)
        dk_acc[pl.ds(par, SEG), :] += t_dot(g2, q)
        dv_acc[pl.ds(par, SEG), :] += t_dot(p2.astype(low), do)
        dk_acc[pl.ds(at, SEG), :] += t_dot(g3, q)
        dv_acc[pl.ds(at, SEG), :] += t_dot(p3.astype(low), do)
    d_ref[:, HEAD:2 * HEAD] = (dk_acc[...] * scale).astype(low)
    d_ref[:, 2 * HEAD:] = dv_acc[...].astype(low)

def whole(shape, at=0):
    return pl.BlockSpec(shape, lambda i, *_: (0, at))

def attend(qkv, parent_at, flag, posq, posk):
    n = qkv.shape[0]
    return pl.pallas_call(
        fwd_kernel,
        grid_spec=pltpu.PrefetchScalarGridSpec(
            num_scalar_prefetch=2, grid=(1,),
            in_specs=[whole((n, HEAD), 0), whole((n, HEAD), 1), whole((n, HEAD), 2), whole((n, 1)), whole((1, n))],
            out_specs=[whole((n, HEAD)), whole((n, 1))]),
        out_shape=[jax.ShapeDtypeStruct((n, HEAD), low), jax.ShapeDtypeStruct((n, 1), wide)],
        name="attend",
    )(parent_at, flag, qkv, qkv, qkv, posq, posk)

def attend_back(qkv, d_o, parent_at, flag, posq, posk, lse):
    n = qkv.shape[0]
    return pl.pallas_call(
        bwd_kernel,
        grid_spec=pltpu.PrefetchScalarGridSpec(
            num_scalar_prefetch=2, grid=(1,),
            in_specs=[whole((n, HEAD), 0), whole((n, HEAD), 1), whole((n, HEAD), 2), whole((n, HEAD)), whole((n, 1)), whole((1, n)), whole((n, 1))],
            out_specs=whole((n, 3 * HEAD)),
            scratch_shapes=[pltpu.VMEM((n, HEAD), wide), pltpu.VMEM((n, HEAD), wide)]),
        out_shape=jax.ShapeDtypeStruct((n, 3 * HEAD), low),
        name="attend_back",
    )(parent_at, flag, qkv, qkv, qkv, d_o, posq, posk, lse)

def tree_tables(seg_ids, parents):
    tail_seg = seg_ids[TRUNK::SEG]
    labels = jnp.arange(parents.shape[1], dtype=jnp.int32)
    tail_parent = jnp.sum(jnp.where(tail_seg[:, None] == labels[None, :], parents[0][None, :], 0), axis=1)
    hit = (tail_seg[None, :] == tail_parent[:, None])
    at = jnp.arange(tail_seg.shape[0], dtype=jnp.int32) + TRUNK // SEG
    parent_at = jnp.sum(jnp.where(hit, at[None, :], 0), axis=1)
    flag = (tail_parent > 0).astype(jnp.int32)
    return parent_at, flag


def row_sum(v): return jnp.sum(v, axis=1, keepdims=True)

def owner_step(mode, total, rows_all, rows_own, ins, outs):
    if mode == "attn":
        x_ref, gain_ref = ins
        (raw_ref,) = outs
        raw_ref[rows_own, :] = total
        flat = total * norm_factor(row_sum(total * total))
        return (x_ref[rows_all, :].astype(wide) + flat * gain_ref[0:1, :]).astype(low)
    if mode == "ffn":
        x_ref, gain_ref, raw_ref, cot_ref = ins
        (out_ref,) = outs
        raw = raw_ref[rows_own, :]
        h = x_ref[rows_all, :].astype(wide) + raw * norm_factor(row_sum(raw * raw)) * gain_ref[0:1, :]
        factor = norm_factor(row_sum(total * total))
        flat = total * factor
        gain = gain_ref[1:2, :]
        out_ref[rows_own, :] = (h + flat * gain).astype(low)
        scaled = cot_ref[rows_own, :].astype(wide) * gain
        return (factor * (scaled - flat * (row_sum(scaled * flat) * (1.0 / D)))).astype(low)
    gain_ref, raw_ref, cot_ref = ins
    (grad_ref,) = outs
    grad = cot_ref[rows_own, :].astype(wide) + total
    grad_ref[rows_own, :] = grad
    raw = raw_ref[rows_own, :]
    factor = norm_factor(row_sum(raw * raw))
    flat = raw * factor
    scaled = grad * gain_ref[0:1, :]
    return (factor * (scaled - flat * (row_sum(scaled * flat) * (1.0 / D)))).astype(low)

def relay_kernel(mode, n, m, hop, n_in, part_ref, *refs):
    ins = refs[:n_in]
    all_ref = refs[n_in]
    outs = refs[n_in + 1:n_in + 2]
    recv_right, recv_left, send_right, send_left, sems_send, sems_recv = refs[n_in + 2:]
    c = lax.axis_index("col")
    half = part_ref.shape[0] // 2
    chunks = half // m
    left = {"col": jnp.maximum(c - 1, 0)}
    right = {"col": jnp.minimum(c + 1, n - 1)}
    first = c == 0
    last = c == n - 1
    inner = jnp.logical_and(c > 0, c < n - 1)

    def rows(j, base=0):
        return pl.ds(pl.multiple_of(base + j * m, m), m)

    def send(kind, j, src, dst, to):
        return pltpu.make_async_remote_copy(src_ref=src, dst_ref=dst, send_sem=sems_send.at[kind, j],
                                            recv_sem=sems_recv.at[kind, j], device_id=to, device_id_type=MESH)

    def reduce_right(j):
        return send(0, j, part_ref.at[rows(j, half)], recv_right.at[rows(j)], right)
    def reduce_right_mid(j):
        return send(0, j, send_right.at[rows(j)], recv_right.at[rows(j)], right)
    def reduce_left(j):
        return send(1, j, part_ref.at[rows(j)], recv_left.at[rows(j)], left)
    def reduce_left_mid(j):
        return send(1, j, send_left.at[rows(j)], recv_left.at[rows(j)], left)
    def spread_left(j):
        return send(2, j, all_ref.at[rows(j, half)], all_ref.at[rows(j, half)], left)
    def spread_right(j):
        return send(3, j, all_ref.at[rows(j)], all_ref.at[rows(j)], right)

    barrier = pltpu.get_barrier_semaphore()
    @pl.when(c > 0)
    def _():
        pl.semaphore_signal(barrier, inc=1, device_id=left, device_id_type=MESH)
    @pl.when(c < n - 1)
    def _():
        pl.semaphore_signal(barrier, inc=1, device_id=right, device_id_type=MESH)
    @pl.when(inner)
    def _():
        pl.semaphore_wait(barrier, 2)
    @pl.when(jnp.logical_not(inner))
    def _():
        pl.semaphore_wait(barrier, 1)

    @pl.loop(0, chunks + hop * 2 * (n - 1))
    def _(i):
        def on(offset, who, run):
            j = i - offset
            @pl.when(jnp.logical_and(who, jnp.logical_and(j >= 0, j < chunks)))
            def _():
                run(j)

        def first_right(j):
            reduce_right(j).start()
        def mid_right(j):
            reduce_right_mid(j).wait_recv()
            send_right[rows(j), :] = (part_ref[rows(j, half), :].astype(wide) + recv_right[rows(j), :].astype(wide)).astype(low)
            reduce_right_mid(j).start()
        def end_right(j):
            reduce_right_mid(j).wait_recv()
            total = part_ref[rows(j, half), :].astype(wide) + recv_right[rows(j), :].astype(wide)
            all_ref[rows(j, half), :] = owner_step(mode, total, rows(j, half), rows(j), ins, outs)
            spread_left(j).start()
        def first_left(j):
            reduce_left(j).start()
        def mid_left(j):
            reduce_left_mid(j).wait_recv()
            send_left[rows(j), :] = (part_ref[rows(j), :].astype(wide) + recv_left[rows(j), :].astype(wide)).astype(low)
            reduce_left_mid(j).start()
        def end_left(j):
            reduce_left_mid(j).wait_recv()
            total = part_ref[rows(j), :].astype(wide) + recv_left[rows(j), :].astype(wide)
            all_ref[rows(j), :] = owner_step(mode, total, rows(j), rows(j), ins, outs)
            spread_right(j).start()
        def pass_left(j):
            spread_left(j).wait_recv()
            spread_left(j).start()
        def pass_right(j):
            spread_right(j).wait_recv()
            spread_right(j).start()

        on(0, first, first_right)
        on(0, last, first_left)
        on(hop * c, inner, mid_right)
        on(hop * (n - 1 - c), inner, mid_left)
        on(hop * (n - 1), last, end_right)
        on(hop * (n - 1), first, end_left)
        on(hop * (2 * (n - 1) - c), inner, pass_left)
        on(hop * (n - 1 + c), inner, pass_right)

    @pl.loop(0, chunks)
    def _(j):
        @pl.when(first)
        def _():
            reduce_right(j).wait_send()
            spread_right(j).wait_send()
            spread_left(j).wait_recv()
        @pl.when(last)
        def _():
            reduce_left(j).wait_send()
            spread_left(j).wait_send()
            spread_right(j).wait_recv()
        @pl.when(inner)
        def _():
            reduce_right_mid(j).wait_send()
            reduce_left_mid(j).wait_send()
            spread_left(j).wait_send()
            spread_right(j).wait_send()

kinds = {"attn": 0, "ffn": 1, "back": 2}

def relay(mode, part, ins, n, m=16, hop=2):
    group, width = part.shape
    half = group // 2
    chunks = half // m
    saved = jax.ShapeDtypeStruct((half, width), low if mode == "ffn" else wide)
    return pl.pallas_call(
        functools.partial(relay_kernel, mode, n, m, hop, len(ins)),
        out_shape=[jax.ShapeDtypeStruct((group, width), low), saved],
        in_specs=[VM] * (1 + len(ins)),
        out_specs=[VM] * 2,
        scratch_shapes=[pltpu.VMEM((half, width), low)] * 4
        + [pltpu.SemaphoreType.DMA((4, chunks))] * 2,
        compiler_params=pltpu.CompilerParams(collective_id=kinds[mode], has_side_effects=True, vmem_limit_bytes=60 << 20),
        name="relay_" + mode,
    )(part, *ins)


def params(collective):
    return pltpu.CompilerParams(collective_id=collective, has_side_effects=True, vmem_limit_bytes=60 << 20)


def span(at, size):
    return pl.ds(pl.multiple_of(at, size), size)


def remote(src, dst, send_sem, recv_sem, to):
    return pltpu.make_async_remote_copy(
        src_ref=src, dst_ref=dst, send_sem=send_sem, recv_sem=recv_sem, device_id=to, device_id_type=MESH
    )


def greet(n, nr):
    r, c = lax.axis_index("row"), lax.axis_index("col")
    me = r * n + c
    barrier = pltpu.get_barrier_semaphore()

    @pl.loop(1, n * nr)
    def _(d):
        peer = lax.rem(me + d, n * nr)
        pl.semaphore_signal(barrier, inc=1, device_id={"row": peer // n, "col": lax.rem(peer, n)}, device_id_type=MESH)

    pl.semaphore_wait(barrier, n * nr - 1)


def enter_kernel(n, nr, m, tok_ref, x_ref, send_a, recv_a, send_z, recv_z, local_sem):
    r, c = lax.axis_index("row"), lax.axis_index("col")
    own = tok_ref.shape[0] // nr
    width = tok_ref.shape[1]
    chunks = own // m
    left = {"col": jnp.maximum(c - 1, 0)}
    right = {"col": jnp.minimum(c + 1, n - 1)}

    def piece(d, j):
        peer = lax.rem(r + d, nr)
        return remote(
            tok_ref.at[span(peer * own + j * m, m)],
            x_ref.at[span(c * own + j * m, m), span(r * width, width)],
            send_a.at[d - 1, j], recv_a.at[d - 1, j], {"row": peer},
        )

    def block(kind, s, at, j, to):
        rows = span(at * own + j * m, m)
        return remote(x_ref.at[rows], x_ref.at[rows], send_z.at[kind, s, j], recv_z.at[kind, s, j], to)

    keep = pltpu.make_async_copy(
        tok_ref.at[span(r * own, own)], x_ref.at[span(c * own, own), span(r * width, width)], local_sem
    )
    keep.start()
    barrier = pltpu.get_barrier_semaphore()
    for d in range(1, nr):
        pl.semaphore_signal(barrier, inc=1, device_id={"row": lax.rem(r + d, nr)}, device_id_type=MESH)

    @pl.when(c > 0)
    def _():
        pl.semaphore_signal(barrier, inc=1, device_id=left, device_id_type=MESH)

    @pl.when(c < n - 1)
    def _():
        pl.semaphore_signal(barrier, inc=1, device_id=right, device_id_type=MESH)

    inner = jnp.logical_and(c > 0, c < n - 1)

    @pl.when(inner)
    def _():
        pl.semaphore_wait(barrier, nr + 1)

    @pl.when(jnp.logical_not(inner))
    def _():
        pl.semaphore_wait(barrier, nr)

    @pl.loop(0, chunks)
    def _(j):
        for d in range(1, nr):
            piece(d, j).start()

    keep.wait()

    for s in range(n):
        @pl.loop(0, chunks)
        def _(j):
            if s == 0:
                for d in range(1, nr):
                    piece(d, j).wait_recv()

            @pl.when(c - s >= 0)
            def _():
                if s > 0:
                    block(0, s - 1, jnp.maximum(c - s, 0), j, right).wait_recv()
                if s < n - 1:
                    @pl.when(c < n - 1)
                    def _():
                        block(0, s, jnp.maximum(c - s, 0), j, right).start()

            @pl.when(c + s <= n - 1)
            def _():
                if s > 0:
                    block(1, s - 1, jnp.minimum(c + s, n - 1), j, left).wait_recv()
                if s < n - 1:
                    @pl.when(c > 0)
                    def _():
                        block(1, s, jnp.minimum(c + s, n - 1), j, left).start()

    @pl.loop(0, chunks)
    def _(j):
        for d in range(1, nr):
            piece(d, j).wait_send()
        for s in range(n - 1):
            @pl.when(jnp.logical_and(c - s >= 0, c < n - 1))
            def _():
                block(0, s, jnp.maximum(c - s, 0), j, right).wait_send()

            @pl.when(jnp.logical_and(c + s <= n - 1, c > 0))
            def _():
                block(1, s, jnp.minimum(c + s, n - 1), j, left).wait_send()


def enter(tokens, n, nr, m=32):
    own = tokens.shape[0] // nr
    chunks = own // m
    dma = pltpu.SemaphoreType.DMA
    return pl.pallas_call(
        functools.partial(enter_kernel, n, nr, m),
        out_shape=jax.ShapeDtypeStruct((own * n, tokens.shape[1] * nr), tokens.dtype),
        in_specs=[VM],
        out_specs=VM,
        scratch_shapes=[dma((nr - 1, chunks)), dma((nr - 1, chunks)), dma((2, n - 1, chunks)), dma((2, n - 1, chunks)), dma],
        compiler_params=params(3),
        name="enter",
    )(tokens)


def row_sums(first, second):
    ones = jnp.ones((8, first.shape[1]), wide)
    at = lax.broadcasted_iota(jnp.int32, (8, first.shape[0]), 0)
    sum_first = lax.dot_general(ones, first, last_last, preferred_element_type=wide, precision=precise)
    sum_second = lax.dot_general(ones, second, last_last, preferred_element_type=wide, precision=precise)
    return jnp.where(at < 4, sum_first, sum_second)


def down_columns(values, at):
    pick = (lax.broadcasted_iota(jnp.int32, (8, HEAD), 0) == at).astype(wide)
    return lax.dot_general(values, pick, first_first, preferred_element_type=wide, precision=precise)


def swap_stats(stats, n, send_sem, recv_sem):
    c = lax.axis_index("col")

    def copy(d):
        peer = lax.rem(c + d, n)
        return remote(stats.at[c], stats.at[c], send_sem.at[d - 1], recv_sem.at[d - 1], {"col": peer})

    for d in range(1, n):
        copy(d).start()
    for d in range(1, n):
        copy(d).wait()


def heads_kernel(n, nr, m, raw_ref, gq_ref, gk_ref, cos_ref, sin_ref, cot_ref, out_ref, factor_ref, half_ref,
                 stats, buf, fq, fk, send_s, recv_s, send_h, recv_h, send_g, recv_g, local_sem, local_g):
    r, c = lax.axis_index("row"), lax.axis_index("col")
    rows_all = raw_ref.shape[0]
    own = rows_all // n
    width = gq_ref.shape[1]
    heads = width // HEAD
    tree_part = own * nr
    q_all = raw_ref[:, :width]
    k_all = raw_ref[:, width:2 * width]
    stats[c] = row_sums(q_all * q_all, k_all * k_all)
    greet(n, nr)
    middle = n // 2
    owner = jnp.where(c < middle, 0, n - 1)
    at_owner = jnp.where(c < middle, c, c - middle)
    cot_width = cot_ref.shape[1]

    def cot_piece(d):
        peer = lax.rem(r + d, nr)
        return remote(
            cot_ref.at[span(peer * own, own)],
            half_ref.at[span(at_owner * own, own), span(r * cot_width, cot_width)],
            send_g.at[d], recv_g.at[at_owner, d], {"row": peer, "col": owner},
        )

    def cot_local():
        return pltpu.make_async_copy(
            cot_ref.at[span(r * own, own)],
            half_ref.at[span(at_owner * own, own), span(r * cot_width, cot_width)], local_g
        )

    swap_stats(stats, n, send_s, recv_s)
    for d in range(1, nr):
        cot_piece(d).start()

    @pl.when(owner == c)
    def _():
        cot_local().start()

    @pl.when(owner != c)
    def _():
        cot_piece(0).start()

    total = stats[0]
    for s in range(1, n):
        total = total + stats[s]
    factor = lax.rsqrt(total * (1.0 / D) + epsilon)
    factor_ref[...] = factor
    fq[...] = down_columns(factor, 0)
    fk[...] = down_columns(factor, 4)

    def piece(d, i, at):
        peer = lax.rem(r + d, nr)
        block = i // (own // m)
        inside = lax.rem(i, own // m)
        return remote(
            buf.at[peer, span(i * m, m)],
            out_ref.at[span(block * tree_part + r * own + inside * m, m)],
            send_h.at[d - 1, i], recv_h.at[d - 1, i], {"row": peer},
        )

    def local(i):
        block = i // (own // m)
        inside = lax.rem(i, own // m)
        return pltpu.make_async_copy(
            buf.at[r, span(i * m, m)], out_ref.at[span(block * tree_part + r * own + inside * m, m)], local_sem.at[i]
        )

    steps = rows_all // m

    @pl.loop(0, steps)
    def _(i):
        rows = span(i * m, m)
        cosine = cos_ref[rows, :]
        sine = sin_ref[rows, :]
        for h in range(heads):
            lanes = slice(h * HEAD, (h + 1) * HEAD)
            u = raw_ref[rows, lanes] * fq[rows, :] * gq_ref[:, lanes]
            buf[h, rows, :HEAD] = (u * cosine + pltpu.roll(u, HEAD // 2, 1) * sine).astype(low)
            k_lanes = slice(width + h * HEAD, width + (h + 1) * HEAD)
            u = raw_ref[rows, k_lanes] * fk[rows, :] * gk_ref[:, lanes]
            buf[h, rows, HEAD:2 * HEAD] = (u * cosine + pltpu.roll(u, HEAD // 2, 1) * sine).astype(low)
            v_lanes = slice(2 * width + h * HEAD, 2 * width + (h + 1) * HEAD)
            buf[h, rows, 2 * HEAD:] = raw_ref[rows, v_lanes].astype(low)
        for d in range(1, nr):
            piece(d, i, 0).start()
        local(i).start()

    @pl.loop(0, steps)
    def _(i):
        for d in range(1, nr):
            piece(d, i, 0).wait()
        local(i).wait()

    for d in range(1, nr):
        cot_piece(d).wait_send()

    @pl.when(owner != c)
    def _():
        cot_piece(0).wait_send()

    @pl.when(owner == c)
    def _():
        cot_local().wait()
        for b in range(middle):
            for d in range(nr):
                def take():
                    remote(
                        cot_ref.at[span(r * own, own)],
                        half_ref.at[span(b * own, own), span(0, cot_width)],
                        send_g.at[d], recv_g.at[b, d], {"row": r, "col": c},
                    ).wait_recv()
                if d == 0:
                    pl.when(b != at_owner)(take)
                else:
                    take()


def to_heads_call(raw, gain_q, gain_k, cos2, sin2, cot, n, nr, m=80):
    rows_all, wide3 = raw.shape
    width = wide3 // 3
    own = rows_all // n
    dma = pltpu.SemaphoreType.DMA
    steps = rows_all // m
    return pl.pallas_call(
        functools.partial(heads_kernel, n, nr, m),
        out_shape=[
            jax.ShapeDtypeStruct((own * n * nr, 3 * HEAD), low),
            jax.ShapeDtypeStruct((8, rows_all), wide),
            jax.ShapeDtypeStruct((own * n // 2, cot.shape[1] * nr), low),
        ],
        in_specs=[VM] * 6,
        out_specs=[VM] * 3,
        scratch_shapes=[
            pltpu.VMEM((n, 8, rows_all), wide),
            pltpu.VMEM((width // HEAD, rows_all, 3 * HEAD), low),
            pltpu.VMEM((rows_all, HEAD), wide),
            pltpu.VMEM((rows_all, HEAD), wide),
            dma((n - 1,)), dma((n - 1,)), dma((nr - 1, steps)), dma((nr - 1, steps)),
            dma((nr,)), dma((n // 2, nr)), dma((steps,)), dma,
        ],
        compiler_params=params(4),
        name="to_heads",
    )(raw, gain_q, gain_k, cos2, sin2, cot)


def unheads_kernel(n, nr, d_ref, raw_ref, factor_ref, gq_ref, gk_ref, cos_ref, sin_ref, res_ref, out_ref, res_out,
                   stats, buf, nq, nk, pq, pk, fq, fk, send_s, recv_s, send_h, recv_h, send_o, recv_o, local_sem, local_o):
    r, c = lax.axis_index("row"), lax.axis_index("col")
    rows_all = raw_ref.shape[0]
    own = rows_all // n
    width = gq_ref.shape[1]
    heads = width // HEAD
    tree_part = own * nr
    middle = n // 2
    out_width = res_out.shape[1]

    def piece(d, b):
        peer = lax.rem(r + d, nr)
        return remote(
            d_ref.at[span(b * tree_part + peer * own, own)],
            buf.at[r, span(b * own, own)],
            send_h.at[d - 1, b], recv_h.at[d - 1, b], {"row": peer},
        )

    def local(b):
        return pltpu.make_async_copy(
            d_ref.at[span(b * tree_part + r * own, own)], buf.at[r, span(b * own, own)], local_sem.at[b]
        )

    is_owner = jnp.logical_or(c == 0, c == n - 1)
    base = jnp.where(c == 0, 0, middle)

    def result_piece(b, d):
        peer = lax.rem(r + d, nr)
        return remote(
            res_ref.at[span(b * own, own), span(peer * out_width, out_width)],
            res_out.at[span(r * own, own)],
            send_o.at[b, d], recv_o.at[d], {"row": peer, "col": base + b},
        )

    def result_local(b):
        return pltpu.make_async_copy(
            res_ref.at[span(b * own, own), span(r * out_width, out_width)], res_out.at[span(r * own, own)], local_o
        )

    for b in range(n):
        local(b).start()
    greet(n, nr)
    for b in range(n):
        for d in range(1, nr):
            piece(d, b).start()

    @pl.when(is_owner)
    def _():
        for b in range(middle):
            for d in range(nr):
                if d == 0:
                    @pl.when(base + b == c)
                    def _():
                        result_local(b).start()

                    @pl.when(base + b != c)
                    def _():
                        result_piece(b, d).start()
                else:
                    result_piece(b, d).start()

    fq[...] = down_columns(factor_ref[...], 0)
    fk[...] = down_columns(factor_ref[...], 4)
    for b in range(n):
        for d in range(1, nr):
            piece(d, b).wait_recv()
        local(b).wait()
        rows = slice(b * own, (b + 1) * own)
        cosine = cos_ref[rows, :]
        sine = sin_ref[rows, :]
        for h in range(heads):
            lanes = slice(h * HEAD, (h + 1) * HEAD)
            u = buf[h, rows, :HEAD].astype(wide)
            u = (u * cosine - pltpu.roll(u, HEAD // 2, 1) * sine) * gq_ref[:, lanes]
            nq[rows, lanes] = u
            pq[rows, lanes] = u * raw_ref[rows, lanes] * fq[rows, :]
            u = buf[h, rows, HEAD:2 * HEAD].astype(wide)
            u = (u * cosine - pltpu.roll(u, HEAD // 2, 1) * sine) * gk_ref[:, lanes]
            nk[rows, lanes] = u
            pk[rows, lanes] = u * raw_ref[rows, slice(width + h * HEAD, width + (h + 1) * HEAD)] * fk[rows, :]
            out_ref[rows, slice(2 * width + h * HEAD, 2 * width + (h + 1) * HEAD)] = buf[h, rows, 2 * HEAD:]
    stats[c] = row_sums(pq[...], pk[...])
    swap_stats(stats, n, send_s, recv_s)
    total = stats[0]
    for s in range(1, n):
        total = total + stats[s]
    mean = total * (1.0 / D) * factor_ref[...]
    pq[:, :HEAD] = down_columns(mean, 0)
    pk[:, :HEAD] = down_columns(mean, 4)
    for b in range(n):
        rows = slice(b * own, (b + 1) * own)
        for h in range(heads):
            lanes = slice(h * HEAD, (h + 1) * HEAD)
            k_lanes = slice(width + h * HEAD, width + (h + 1) * HEAD)
            out_ref[rows, lanes] = (fq[rows, :] * (nq[rows, lanes] - raw_ref[rows, lanes] * pq[rows, :HEAD])).astype(low)
            out_ref[rows, k_lanes] = (fk[rows, :] * (nk[rows, lanes] - raw_ref[rows, k_lanes] * pk[rows, :HEAD])).astype(low)
    for b in range(n):
        for d in range(1, nr):
            piece(d, b).wait_send()

    @pl.when(is_owner)
    def _():
        for b in range(middle):
            for d in range(nr):
                if d == 0:
                    @pl.when(base + b == c)
                    def _():
                        result_local(b).wait()

                    @pl.when(base + b != c)
                    def _():
                        result_piece(b, d).wait_send()
                else:
                    result_piece(b, d).wait_send()

    for d in range(nr):
        def take():
            remote(
                res_ref.at[span(0, own), span(0, out_width)], res_out.at[span(r * own, own)],
                send_o.at[0, d], recv_o.at[d], {"row": r, "col": c},
            ).wait_recv()
        if d == 0:
            pl.when(jnp.logical_not(is_owner))(take)
        else:
            take()


def from_heads_call(d_head, raw, factor, gain_q, gain_k, cos2, sin2, result, n, nr):
    rows_all, wide3 = raw.shape
    width = wide3 // 3
    dma = pltpu.SemaphoreType.DMA
    square = pltpu.VMEM((rows_all, width), wide)
    return pl.pallas_call(
        functools.partial(unheads_kernel, n, nr),
        out_shape=[
            jax.ShapeDtypeStruct((rows_all, wide3), low),
            jax.ShapeDtypeStruct((rows_all // n * nr, result.shape[1] // nr), low),
        ],
        in_specs=[VM] * 8,
        out_specs=[VM] * 2,
        scratch_shapes=[
            pltpu.VMEM((n, 8, rows_all), wide),
            pltpu.VMEM((nr, rows_all, 3 * HEAD), low),
            square, square, square, square,
            pltpu.VMEM((rows_all, HEAD), wide),
            pltpu.VMEM((rows_all, HEAD), wide),
            dma((n - 1,)), dma((n - 1,)), dma((nr - 1, n)), dma((nr - 1, n)),
            dma((n // 2, nr)), dma((nr,)), dma((n,)), dma,
        ],
        compiler_params=params(5),
        name="from_heads",
    )(d_head, raw, factor, gain_q, gain_k, cos2, sin2, result)


def finish_kernel(n, nr, ndp, m, part_ref, full_ref, col_ref, hot_ref, grad_ref, sets_ref,
                  recv_right, recv_left, send_right, send_left, own_buf, in_buf, full_recv, full_sum, full_last,
                  col_recv, owned, hot_all,
                  send_z, recv_z, send_w, recv_w, local_w, send_f, recv_f, send_c, recv_c, send_l, recv_l,
                  send_d, recv_d, send_k, recv_k):
    g, r, c = lax.axis_index("dp"), lax.axis_index("row"), lax.axis_index("col")
    own = part_ref.shape[0] // n
    width = in_buf.shape[1]
    chunks = own // m
    left = {"col": jnp.maximum(c - 1, 0)}
    right = {"col": jnp.minimum(c + 1, n - 1)}
    full_rows = full_last.shape[1]
    col_rows = col_recv.shape[1]

    def full_piece(d):
        peer = lax.rem(r + d, nr)
        return remote(full_ref.at[:, span(peer * width, width)], full_recv.at[r], send_f.at[d - 1], recv_f.at[d - 1], {"row": peer})

    def col_piece(d):
        peer = lax.rem(r + d, nr)
        return remote(col_ref.at[span(peer * col_rows, col_rows)], col_recv.at[r], send_c.at[d - 1], recv_c.at[d - 1], {"row": peer})

    def last_piece(d):
        peer = lax.rem(c + d, n)
        return remote(full_sum.at[span(peer * full_rows, full_rows)], full_last.at[c], send_l.at[d - 1], recv_l.at[d - 1], {"col": peer})

    def tree_piece(d):
        peer = lax.rem(g + d, ndp)
        return remote(owned.at[g], owned.at[g], send_d.at[d - 1], recv_d.at[d - 1], {"dp": peer})

    def hot_piece(d):
        peer = lax.rem(g + d, ndp)
        return remote(hot_all.at[g], hot_all.at[g], send_k.at[d - 1], recv_k.at[d - 1], {"dp": peer})

    def reduce(kind, b, j, src):
        rows = span(b * own + j * m, m)
        dst, to = ((recv_right, right), (recv_left, left))[kind]
        return remote(src.at[rows], dst.at[rows], send_z.at[kind, b, j], recv_z.at[kind, b, j], to)

    def width_piece(d, j):
        peer = lax.rem(r + d, nr)
        return remote(
            own_buf.at[span(j * m, m), span(peer * width, width)], in_buf.at[span(r * own + j * m, m)],
            send_w.at[d - 1, j], recv_w.at[d - 1, j], {"row": peer},
        )

    def width_local(j):
        return pltpu.make_async_copy(
            own_buf.at[span(j * m, m), span(r * width, width)], in_buf.at[span(r * own + j * m, m)], local_w.at[j]
        )

    me = r * n + c
    barrier = pltpu.get_barrier_semaphore()
    for d in range(1, ndp):
        pl.semaphore_signal(barrier, inc=1, device_id={"dp": lax.rem(g + d, ndp)}, device_id_type=MESH)

    @pl.loop(1, n * nr)
    def _(d):
        peer = lax.rem(me + d, n * nr)
        pl.semaphore_signal(barrier, inc=1, device_id={"row": peer // n, "col": lax.rem(peer, n)}, device_id_type=MESH)

    pl.semaphore_wait(barrier, n * nr - 1 + ndp - 1)
    hot_all[g] = hot_ref[...]
    for d in range(1, nr):
        full_piece(d).start()
        col_piece(d).start()

    def stage(s):
        @pl.loop(0, chunks)
        def _(j):
            for kind, b, go, edge, acc, got in (
                (0, n - 1 - s, n - 1 - s > c, c == 0, send_right, recv_right),
                (1, s, s < c, c == n - 1, send_left, recv_left),
            ):
                @pl.when(go)
                def _():
                    @pl.when(edge)
                    def _():
                        reduce(kind, b, j, part_ref).start()

                    @pl.when(jnp.logical_not(edge))
                    def _():
                        rows = span(b * own + j * m, m)
                        reduce(kind, b, j, acc).wait_recv()
                        acc[rows, :] = (part_ref[rows, :].astype(wide) + got[rows, :].astype(wide)).astype(low)
                        reduce(kind, b, j, acc).start()

    stage(0)
    for d in range(1, nr):
        full_piece(d).wait_recv()
        col_piece(d).wait_recv()
    total = full_ref[:, span(r * width, width)].astype(wide)
    col_total = col_ref[span(r * col_rows, col_rows), :].astype(wide)
    for d in range(1, nr):
        peer = lax.rem(r + d, nr)
        total = total + full_recv[peer].astype(wide)
        col_total = col_total + col_recv[peer].astype(wide)
    full_sum[...] = total.astype(low)
    owned[g, full_rows:, :] = col_total.astype(low)
    for d in range(1, n):
        last_piece(d).start()
    stage(1)
    for d in range(1, n):
        last_piece(d).wait_recv()
    last = full_sum[span(c * full_rows, full_rows), :].astype(wide)
    for d in range(1, n):
        last = last + full_last[lax.rem(c + d, n)].astype(wide)
    owned[g, :full_rows, :] = last.astype(low)
    for d in range(1, ndp):
        tree_piece(d).start()
        hot_piece(d).start()
    for s in range(2, n - 1):
        stage(s)

    rows_own = c * own

    @pl.loop(0, chunks)
    def _(j):
        rows = span(rows_own + j * m, m)
        at = span(j * m, m)

        @pl.when(c == 0)
        def _():
            reduce(1, c, j, send_left).wait_recv()
            own_buf[at, :] = (part_ref[rows, :].astype(wide) + recv_left[rows, :].astype(wide)).astype(low)

        @pl.when(c == n - 1)
        def _():
            reduce(0, c, j, send_right).wait_recv()
            own_buf[at, :] = (part_ref[rows, :].astype(wide) + recv_right[rows, :].astype(wide)).astype(low)

        @pl.when(jnp.logical_and(c > 0, c < n - 1))
        def _():
            reduce(0, c, j, send_right).wait_recv()
            reduce(1, c, j, send_left).wait_recv()
            own_buf[at, :] = (
                part_ref[rows, :].astype(wide) + recv_right[rows, :].astype(wide) + recv_left[rows, :].astype(wide)
            ).astype(low)

        for d in range(1, nr):
            width_piece(d, j).start()
        width_local(j).start()

    for d in range(1, ndp):
        tree_piece(d).wait_recv()
        hot_piece(d).wait_recv()
    sets_own = sets_ref.shape[0]
    for s in range(sets_own):
        total = owned[0].astype(wide) * hot_all[0, pl.ds(g * sets_own + s, 1), :]
        for t in range(1, ndp):
            total = total + owned[t].astype(wide) * hot_all[t, pl.ds(g * sets_own + s, 1), :]
        sets_ref[s] = total

    @pl.loop(0, chunks)
    def _(j):
        for d in range(1, nr):
            width_piece(d, j).wait()
        width_local(j).wait()

    grad_ref[...] = in_buf[...].astype(wide)
    for d in range(1, nr):
        full_piece(d).wait_send()
        col_piece(d).wait_send()
    for d in range(1, n):
        last_piece(d).wait_send()
    for d in range(1, ndp):
        tree_piece(d).wait_send()
        hot_piece(d).wait_send()
    for s in range(n - 1):
        @pl.loop(0, chunks)
        def _(j):
            @pl.when(n - 1 - s > c)
            def _():
                reduce(0, n - 1 - s, j, send_right).wait_send()

            @pl.when(s < c)
            def _():
                reduce(1, s, j, send_left).wait_send()


def finish(part, full, cols, hot, sets_own, n, nr, ndp, m=32):
    rows_all, width_all = part.shape
    own = rows_all // n
    width = width_all // nr
    chunks = own // m
    full_rows = full.shape[0] // n
    col_rows = cols.shape[0] // nr
    dma = pltpu.SemaphoreType.DMA
    big = pltpu.VMEM((rows_all, width_all), low)
    return pl.pallas_call(
        functools.partial(finish_kernel, n, nr, ndp, m),
        out_shape=[
            jax.ShapeDtypeStruct((own * nr, width), wide),
            jax.ShapeDtypeStruct((sets_own, full_rows + col_rows, width), wide),
        ],
        in_specs=[VM] * 4,
        out_specs=[VM] * 2,
        scratch_shapes=[
            big, big, big, big,
            pltpu.VMEM((own, width_all), low),
            pltpu.VMEM((own * nr, width), low),
            pltpu.VMEM((nr, full.shape[0], width), low),
            pltpu.VMEM((full.shape[0], width), low),
            pltpu.VMEM((n, full_rows, width), low),
            pltpu.VMEM((nr, col_rows, width), low),
            pltpu.VMEM((ndp, full_rows + col_rows, width), low),
            pltpu.VMEM((ndp,) + hot.shape, wide),
            dma((2, n, chunks)), dma((2, n, chunks)), dma((nr - 1, chunks)), dma((nr - 1, chunks)), dma((chunks,)),
            dma((nr - 1,)), dma((nr - 1,)), dma((nr - 1,)), dma((nr - 1,)), dma((n - 1,)), dma((n - 1,)),
            dma((ndp - 1,)), dma((ndp - 1,)), dma((ndp - 1,)), dma((ndp - 1,)),
        ],
        compiler_params=params(6),
        name="finish",
    )(part, full, cols, hot)


def per_device(
    tokens,
    cotangent,
    seg_ids,
    positions,
    parents,
    tree_sets,
    gain_q,
    gain_k,
    gain_attn,
    gain_ffn,
    query_key_value_weight,
    output_weight,
    gate_up_weight,
    down_weight,
    query_key_value_adapter_first,
    query_key_value_adapter_second,
    output_adapter_first,
    output_adapter_second,
    gate_up_adapter_first,
    gate_up_adapter_second,
    down_adapter_first,
    down_adapter_second,
):
    dp_count = lax.axis_size("dp")
    row_count = lax.axis_size("row")
    col_count = lax.axis_size("col")
    row_at = lax.axis_index("row")
    tree_tokens = seg_ids.shape[0]
    assert tree_sets.shape[0] == 1 and col_count == 4
    set_count = output_adapter_first.shape[0]
    own = tokens.shape[0] // row_count
    group = own * col_count
    width_row = tokens.shape[1]
    width_col = gain_q.shape[0]
    hidden_col = down_weight.shape[0]
    heads_col = width_col // HEAD
    tree_set = tree_sets[0]

    def pick(table, axis):
        return lax.dynamic_index_in_dim(table, tree_set, axis, keepdims=False)

    narrow = jnp.concatenate(
        [
            pick(query_key_value_adapter_first, 1),
            pick(gate_up_adapter_first, 1),
            pick(output_adapter_second, 0)[None],
            pick(down_adapter_second, 0)[None],
        ],
        axis=0,
    ).astype(low)
    narrow_all = lax.all_gather(narrow, "row", axis=2, tiled=True)
    a_qkv = narrow_all[:3].reshape(3 * RANK, D)
    a_gu = narrow_all[3:5].reshape(2 * RANK, D)
    b_out = narrow_all[5]
    b_down = narrow_all[6]
    b_qkv = pick(query_key_value_adapter_second, 1).astype(low)
    b_gu = pick(gate_up_adapter_second, 1).astype(low)
    a_out = pick(output_adapter_first, 0).astype(low)
    a_down = pick(down_adapter_first, 0).astype(low)
    gains = lax.all_gather(jnp.stack([gain_attn, gain_ffn]), "row", axis=1, tiled=True)

    w_qkv = lax.all_gather(query_key_value_weight, "row", axis=0, tiled=True).reshape(D, 3 * width_col)
    w_out = lax.all_gather(output_weight, "row", axis=1, tiled=True)
    w_gu = lax.all_gather(gate_up_weight, "row", axis=0, tiled=True).reshape(D, 2 * hidden_col)
    w_down = lax.all_gather(down_weight, "row", axis=1, tiled=True)

    def to_heads(values, parts):
        by_head = values.reshape(group, parts, heads_col, HEAD).transpose(2, 0, 1, 3).reshape(heads_col, group, parts * HEAD)
        moved = lax.all_to_all(by_head, "row", split_axis=0, concat_axis=0, tiled=True)
        return (
            moved.reshape(row_count, col_count, own, parts * HEAD)
            .transpose(1, 0, 2, 3)
            .reshape(tree_tokens, parts * HEAD)
        )

    def from_heads(values, parts):
        by_row = (
            values.reshape(col_count, row_count, own, parts * HEAD)
            .transpose(1, 0, 2, 3)
            .reshape(row_count, group, parts * HEAD)
        )
        moved = lax.all_to_all(by_row, "row", split_axis=0, concat_axis=0, tiled=True)
        return moved.reshape(heads_col, group, parts, HEAD).transpose(1, 2, 0, 3).reshape(group, parts * width_col)

    first = lax.axis_index("col") == 0
    final = lax.axis_index("col") == col_count - 1
    x = enter(tokens, col_count, row_count)
    red_qkv = dot_t(x, a_qkv).astype(low)
    raw = dot(x, w_qkv)
    extra = jnp.concatenate([dot(red_qkv[:, RANK * j : RANK * (j + 1)], b_qkv[j]) for j in range(3)], axis=1)
    raw = raw + extra
    pos_own = lax.dynamic_index_in_dim(
        positions.reshape(col_count, row_count, own), row_at, 1, keepdims=False
    ).reshape(group)
    cosine, sine = angles(pos_own)
    cos2 = jnp.concatenate([cosine, cosine], axis=1)
    sin2 = jnp.concatenate([-sine, sine], axis=1)
    gq, gk = gain_q[None, :], gain_k[None, :]
    qkv_head, factors, g_half = to_heads_call(raw, gq, gk, cos2, sin2, cotangent, col_count, row_count)
    parent_at, branch_flag = tree_tables(seg_ids, parents)
    pos_down, pos_across = positions[:, None], positions[None, :]
    attn_head, lse = attend(qkv_head, parent_at, branch_flag, pos_down, pos_across)
    attn = from_heads(attn_head, 1)

    red_out = dot_t(attn, a_out).astype(low)
    part_a = (dot(attn, w_out) + dot(red_out, b_out)).astype(low)
    h, a_raw = relay("attn", part_a, (x, gains), col_count)

    red_gu = dot_t(h, a_gu).astype(low)
    gate = dot(h, w_gu[:, :hidden_col]) + dot(red_gu[:, :RANK], b_gu[0])
    up = dot(h, w_gu[:, hidden_col:]) + dot(red_gu[:, RANK:], b_gu[1])
    sigma = jax.nn.sigmoid(gate)
    hidden = (gate * sigma * up).astype(low)
    red_down = dot_t(hidden, a_down).astype(low)
    part_f = (dot(hidden, w_down) + dot(red_down, b_down)).astype(low)
    d_f, out_half = relay("ffn", part_f, (x, gains, a_raw, g_half), col_count)
    back_down = dot_t(d_f, b_down).astype(low)
    d_hidden = dot_t(d_f, w_down) + dot(back_down, a_down)
    d_gate = (d_hidden * up * sigma * (1.0 + gate * (1.0 - sigma))).astype(low)
    d_up = (d_hidden * (gate * sigma)).astype(low)
    back_gate = dot_t(d_gate, b_gu[0]).astype(low)
    back_up = dot_t(d_up, b_gu[1]).astype(low)
    back_gu = jnp.concatenate([back_gate, back_up], axis=1)
    part_h = (
        dot_t(d_gate, w_gu[:, :hidden_col]) + dot_t(d_up, w_gu[:, hidden_col:]) + dot(back_gu, a_gu)
    ).astype(low)
    d_a, d_h_half = relay("back", part_h, (gains, a_raw, g_half), col_count)
    back_out = dot_t(d_a, b_out).astype(low)
    d_attn = (dot_t(d_a, w_out) + dot(back_out, a_out)).astype(low)

    d_attn_head = to_heads(d_attn, 1)
    d_qkv_head = attend_back(
        qkv_head, d_attn_head, parent_at, branch_flag, pos_down, pos_across, lse
    )
    d_raw, layer_out = from_heads_call(
        d_qkv_head, raw, factors, gq, gk, cos2, sin2, out_half, col_count, row_count
    )
    d_q, d_k, d_v = (d_raw[:, width_col * j : width_col * (j + 1)] for j in range(3))
    back_qkv = jnp.concatenate(
        [dot_t(d, b) for d, b in zip((d_q, d_k, d_v), (b_qkv[0], b_qkv[1], b_qkv[2]))], axis=1
    ).astype(low)
    d_h_all = jnp.concatenate([jnp.where(first, d_h_half, 0.0), jnp.where(final, d_h_half, 0.0)], axis=0)
    part_in = (dot_t(d_raw, w_qkv) + dot(back_qkv, a_qkv) + d_h_all).astype(low)

    rank_own = RANK // col_count
    full = jnp.concatenate(
        [t_dot(back_qkv, x), t_dot(back_gu, h), t_dot(red_out, d_a), t_dot(red_down, d_f)], axis=0
    ).astype(low)
    full = full.reshape(7, col_count, rank_own, D).transpose(1, 0, 2, 3).reshape(col_count, 7 * rank_own, D)
    full = jnp.pad(full, ((0, 0), (0, rank_own), (0, 0))).reshape(col_count * 8 * rank_own, D)
    cols = jnp.concatenate(
        [t_dot(red_qkv[:, RANK * j : RANK * (j + 1)], d) for j, d in enumerate((d_q, d_k, d_v))]
        + [t_dot(back_out, attn), t_dot(red_gu[:, :RANK], d_gate), t_dot(red_gu[:, RANK:], d_up), t_dot(back_down, hidden)],
        axis=1,
    ).astype(low)
    cols = cols.reshape(RANK * 16, width_row)
    hot = (tree_set == lax.broadcasted_iota(jnp.int32, (set_count, width_row), 0)).astype(wide)
    sets_own = set_count // dp_count
    input_grad, sets = finish(part_in, full, cols, hot, sets_own, col_count, row_count, dp_count)
    full_sets = sets[:, : 7 * rank_own].reshape(sets_own, 7, rank_own, width_row)
    col_sets = sets[:, 8 * rank_own :].reshape(sets_own, RANK // row_count, 16 * width_row)
    grad_a_qkv = full_sets[:, :3].transpose(1, 0, 2, 3)
    grad_a_gu = full_sets[:, 3:5].transpose(1, 0, 2, 3)
    grad_b_out = full_sets[:, 5]
    grad_b_down = full_sets[:, 6]
    grad_b_qkv = jnp.stack([col_sets[..., width_col * j : width_col * (j + 1)] for j in range(3)])
    grad_a_out = col_sets[..., 3 * width_col : 4 * width_col]
    gu_at = 4 * width_col
    grad_b_gu = jnp.stack([col_sets[..., gu_at + hidden_col * j : gu_at + hidden_col * (j + 1)] for j in range(2)])
    grad_a_down = col_sets[..., gu_at + 2 * hidden_col :]
    return (
        layer_out,
        input_grad,
        grad_a_qkv,
        grad_b_qkv,
        grad_a_out,
        grad_b_out,
        grad_a_gu,
        grad_b_gu,
        grad_a_down,
        grad_b_down,
    )


def solution(mesh):
    in_specs = (
        P(("dp", "col"), "row"),
        P(("dp", "col"), "row"),
        P("dp"),
        P("dp"),
        P("dp", None),
        P("dp"),
        P("col"),
        P("col"),
        P("row"),
        P("row"),
        P("row", None, "col"),
        P("col", "row"),
        P("row", None, "col"),
        P("col", "row"),
        P(None, None, None, "row"),
        P(None, None, None, "col"),
        P(None, None, "col"),
        P(None, None, "row"),
        P(None, None, None, "row"),
        P(None, None, None, "col"),
        P(None, None, "col"),
        P(None, None, "row"),
    )
    out_specs = (
        P(("dp", "col"), "row"),
        P(("dp", "col"), "row"),
        P(None, "dp", "col", "row"),
        P(None, "dp", "row", "col"),
        P("dp", "row", "col"),
        P("dp", "col", "row"),
        P(None, "dp", "col", "row"),
        P(None, "dp", "row", "col"),
        P("dp", "row", "col"),
        P("dp", "col", "row"),
    )
    return jax.shard_map(
        per_device, mesh=mesh, in_specs=in_specs, out_specs=out_specs, check_vma=False
    )
```

```python
import functools

import jax
import jax.numpy as jnp
from jax import lax
from jax.experimental import pallas as pl
from jax.experimental.pallas import tpu as pltpu
from jax.sharding import PartitionSpec as P

D = 2048
HEAD = 128
RANK = 16
SEG = 128
TRUNK = 1024
QT = 256
MESH = pl.DeviceIdType.MESH
VM = pl.BlockSpec(memory_space=pltpu.VMEM)
precise = lax.Precision.HIGHEST

epsilon = 1e-06
rope_base = 500000.0
masked_out = -1e30
low = jnp.bfloat16
wide = jnp.float32
last_last = (((1,), (1,)), ((), ()))
first_first = (((0,), (0,)), ((), ()))


def dot(left, right):
    return jnp.dot(left, right, preferred_element_type=wide)


def dot_t(left, right):
    return lax.dot_general(left, right, last_last, preferred_element_type=wide)


def t_dot(left, right):
    return lax.dot_general(left, right, first_first, preferred_element_type=wide)


def angles(positions):
    half_width = HEAD // 2
    frequency = rope_base ** (-(jnp.arange(half_width, dtype=wide) * 2.0) / HEAD)
    angle_table = positions.astype(wide)[:, None] * frequency[None, :]
    return (jnp.cos(angle_table), jnp.sin(angle_table))


def norm_factor(square_sum):
    return lax.rsqrt(square_sum * (1.0 / D) + epsilon)


def tail_scores(q, k_ref, own_at, parent_at, has_parent, pos_q, pos_k):
    scale = HEAD ** -0.5
    s_trunk = dot_t(q, k_ref[:TRUNK, :]) * scale
    s_par = dot_t(q, k_ref[pl.ds(parent_at, SEG), :]) * scale
    s_par = jnp.where(has_parent > 0, s_par, masked_out)
    s_own = dot_t(q, k_ref[pl.ds(own_at, SEG), :]) * scale
    s_own = jnp.where(pos_k <= pos_q, s_own, masked_out)
    return s_trunk, s_par, s_own

def trunk_scores(q, k_ref, pos_q, pos_k):
    s = dot_t(q, k_ref[:TRUNK, :]) * HEAD ** -0.5
    return jnp.where(pos_k <= pos_q, s, masked_out)

def fwd_kernel(parent_ref, flag_ref, q_ref, k_ref, v_ref, posq_ref, posk_ref, o_ref, lse_ref):
    tails = (q_ref.shape[0] - TRUNK) // SEG
    @pl.loop(0, TRUNK // QT)
    def _(i):
        at = pl.multiple_of(i * QT, QT)
        s = trunk_scores(q_ref[pl.ds(at, QT), :], k_ref, posq_ref[pl.ds(at, QT), :], posk_ref[:, :TRUNK])
        top = jnp.max(s, axis=1, keepdims=True)
        e = jnp.exp(s - top)
        total = jnp.sum(e, axis=1, keepdims=True)
        p = (e * (1.0 / total)).astype(low)
        o_ref[pl.ds(at, QT), :] = dot(p, v_ref[:TRUNK, :]).astype(low)
        lse_ref[pl.ds(at, QT), :] = top + jnp.log(total)
    @pl.loop(0, tails)
    def _(j):
        at = pl.multiple_of(TRUNK + j * SEG, SEG)
        par = pl.multiple_of(parent_ref[j] * SEG, SEG)
        s1, s2, s3 = tail_scores(q_ref[pl.ds(at, SEG), :], k_ref, at, par, flag_ref[j],
                                 posq_ref[pl.ds(at, SEG), :], posk_ref[:, pl.ds(at, SEG)])
        top = jnp.maximum(jnp.maximum(jnp.max(s1, axis=1, keepdims=True), jnp.max(s2, axis=1, keepdims=True)),
                          jnp.max(s3, axis=1, keepdims=True))
        e1 = jnp.exp(s1 - top); e2 = jnp.exp(s2 - top); e3 = jnp.exp(s3 - top)
        total = jnp.sum(e1, axis=1, keepdims=True) + jnp.sum(e2, axis=1, keepdims=True) + jnp.sum(e3, axis=1, keepdims=True)
        inv = 1.0 / total
        o = dot((e1 * inv).astype(low), v_ref[:TRUNK, :])
        o += dot((e2 * inv).astype(low), v_ref[pl.ds(par, SEG), :])
        o += dot((e3 * inv).astype(low), v_ref[pl.ds(at, SEG), :])
        o_ref[pl.ds(at, SEG), :] = o.astype(low)
        lse_ref[pl.ds(at, SEG), :] = top + jnp.log(total)

def bwd_kernel(parent_ref, flag_ref, q_ref, k_ref, v_ref, do_ref, posq_ref, posk_ref, lse_ref, d_ref, dk_acc, dv_acc):
    scale = HEAD ** -0.5
    tails = (q_ref.shape[0] - TRUNK) // SEG
    dk_acc[...] = jnp.zeros_like(dk_acc)
    dv_acc[...] = jnp.zeros_like(dv_acc)
    @pl.loop(0, TRUNK // QT)
    def _(i):
        at = pl.multiple_of(i * QT, QT)
        q = q_ref[pl.ds(at, QT), :]
        do = do_ref[pl.ds(at, QT), :]
        s = trunk_scores(q, k_ref, posq_ref[pl.ds(at, QT), :], posk_ref[:, :TRUNK])
        p = jnp.exp(s - lse_ref[pl.ds(at, QT), :])
        dp = dot_t(do, v_ref[:TRUNK, :])
        inner = jnp.sum(p * dp, axis=1, keepdims=True)
        ds = (p * (dp - inner)).astype(low)
        d_ref[pl.ds(at, QT), :HEAD] = (dot(ds, k_ref[:TRUNK, :]) * scale).astype(low)
        dk_acc[:TRUNK, :] += t_dot(ds, q)
        dv_acc[:TRUNK, :] += t_dot(p.astype(low), do)
    @pl.loop(0, tails)
    def _(j):
        at = pl.multiple_of(TRUNK + j * SEG, SEG)
        par = pl.multiple_of(parent_ref[j] * SEG, SEG)
        q = q_ref[pl.ds(at, SEG), :]
        do = do_ref[pl.ds(at, SEG), :]
        lse = lse_ref[pl.ds(at, SEG), :]
        s1, s2, s3 = tail_scores(q, k_ref, at, par, flag_ref[j],
                                 posq_ref[pl.ds(at, SEG), :], posk_ref[:, pl.ds(at, SEG)])
        p1 = jnp.exp(s1 - lse); p2 = jnp.exp(s2 - lse); p3 = jnp.exp(s3 - lse)
        d1 = dot_t(do, v_ref[:TRUNK, :])
        d2 = dot_t(do, v_ref[pl.ds(par, SEG), :])
        d3 = dot_t(do, v_ref[pl.ds(at, SEG), :])
        inner = jnp.sum(p1 * d1, axis=1, keepdims=True) + jnp.sum(p2 * d2, axis=1, keepdims=True) + jnp.sum(p3 * d3, axis=1, keepdims=True)
        g1 = (p1 * (d1 - inner)).astype(low)
        g2 = (p2 * (d2 - inner)).astype(low)
        g3 = (p3 * (d3 - inner)).astype(low)
        dq = dot(g1, k_ref[:TRUNK, :]) + dot(g2, k_ref[pl.ds(par, SEG), :]) + dot(g3, k_ref[pl.ds(at, SEG), :])
        d_ref[pl.ds(at, SEG), :HEAD] = (dq * scale).astype(low)
        dk_acc[:TRUNK, :] += t_dot(g1, q)
        dv_acc[:TRUNK, :] += t_dot(p1.astype(low), do)
        dk_acc[pl.ds(par, SEG), :] += t_dot(g2, q)
        dv_acc[pl.ds(par, SEG), :] += t_dot(p2.astype(low), do)
        dk_acc[pl.ds(at, SEG), :] += t_dot(g3, q)
        dv_acc[pl.ds(at, SEG), :] += t_dot(p3.astype(low), do)
    d_ref[:, HEAD:2 * HEAD] = (dk_acc[...] * scale).astype(low)
    d_ref[:, 2 * HEAD:] = dv_acc[...].astype(low)

def whole(shape, at=0):
    return pl.BlockSpec(shape, lambda i, *_: (0, at))

def attend(qkv, parent_at, flag, posq, posk):
    n = qkv.shape[0]
    return pl.pallas_call(
        fwd_kernel,
        grid_spec=pltpu.PrefetchScalarGridSpec(
            num_scalar_prefetch=2, grid=(1,),
            in_specs=[whole((n, HEAD), 0), whole((n, HEAD), 1), whole((n, HEAD), 2), whole((n, 1)), whole((1, n))],
            out_specs=[whole((n, HEAD)), whole((n, 1))]),
        out_shape=[jax.ShapeDtypeStruct((n, HEAD), low), jax.ShapeDtypeStruct((n, 1), wide)],
        name="attend",
    )(parent_at, flag, qkv, qkv, qkv, posq, posk)

def attend_back(qkv, d_o, parent_at, flag, posq, posk, lse):
    n = qkv.shape[0]
    return pl.pallas_call(
        bwd_kernel,
        grid_spec=pltpu.PrefetchScalarGridSpec(
            num_scalar_prefetch=2, grid=(1,),
            in_specs=[whole((n, HEAD), 0), whole((n, HEAD), 1), whole((n, HEAD), 2), whole((n, HEAD)), whole((n, 1)), whole((1, n)), whole((n, 1))],
            out_specs=whole((n, 3 * HEAD)),
            scratch_shapes=[pltpu.VMEM((n, HEAD), wide), pltpu.VMEM((n, HEAD), wide)]),
        out_shape=jax.ShapeDtypeStruct((n, 3 * HEAD), low),
        name="attend_back",
    )(parent_at, flag, qkv, qkv, qkv, d_o, posq, posk, lse)

def tree_tables(seg_ids, parents):
    tail_seg = seg_ids[TRUNK::SEG]
    labels = jnp.arange(parents.shape[1], dtype=jnp.int32)
    tail_parent = jnp.sum(jnp.where(tail_seg[:, None] == labels[None, :], parents[0][None, :], 0), axis=1)
    hit = (tail_seg[None, :] == tail_parent[:, None])
    at = jnp.arange(tail_seg.shape[0], dtype=jnp.int32) + TRUNK // SEG
    parent_at = jnp.sum(jnp.where(hit, at[None, :], 0), axis=1)
    flag = (tail_parent > 0).astype(jnp.int32)
    return parent_at, flag


def row_sum(v): return jnp.sum(v, axis=1, keepdims=True)

def params(collective):
    return pltpu.CompilerParams(collective_id=collective, has_side_effects=True, vmem_limit_bytes=60 << 20)


def span(at, size):
    return pl.ds(pl.multiple_of(at, size), size)


def remote(src, dst, send_sem, recv_sem, to):
    return pltpu.make_async_remote_copy(
        src_ref=src, dst_ref=dst, send_sem=send_sem, recv_sem=recv_sem, device_id=to, device_id_type=MESH
    )


def greet(n, nr):
    r, c = lax.axis_index("row"), lax.axis_index("col")
    me = r * n + c
    barrier = pltpu.get_barrier_semaphore()

    @pl.loop(1, n * nr)
    def _(d):
        peer = lax.rem(me + d, n * nr)
        pl.semaphore_signal(barrier, inc=1, device_id={"row": peer // n, "col": lax.rem(peer, n)}, device_id_type=MESH)

    pl.semaphore_wait(barrier, n * nr - 1)


def enter_kernel(n, nr, m, tok_ref, table_ref, gain_ref, x_ref, table_all, gain_all,
                 send_a, recv_a, send_z, recv_z, send_t, recv_t, local_sem):
    r, c = lax.axis_index("row"), lax.axis_index("col")
    own = tok_ref.shape[0] // nr
    width = tok_ref.shape[1]
    chunks = own // m
    left = {"col": jnp.maximum(c - 1, 0)}
    right = {"col": jnp.minimum(c + 1, n - 1)}

    def piece(d, j):
        peer = lax.rem(r + d, nr)
        return remote(
            tok_ref.at[span(peer * own + j * m, m)],
            x_ref.at[span(c * own + j * m, m), span(r * width, width)],
            send_a.at[d - 1, j], recv_a.at[d - 1, j], {"row": peer},
        )

    def block(kind, s, at, j, to):
        rows = span(at * own + j * m, m)
        return remote(x_ref.at[rows], x_ref.at[rows], send_z.at[kind, s, j], recv_z.at[kind, s, j], to)

    def table_piece(d, kind):
        src, dst = ((table_ref, table_all), (gain_ref, gain_all))[kind]
        to = {"row": lax.rem(r + d, nr)}
        return remote(src, dst.at[:, span(r * width, width)], send_t.at[kind, d - 1], recv_t.at[kind, d - 1], to)

    keep = pltpu.make_async_copy(
        tok_ref.at[span(r * own, own)], x_ref.at[span(c * own, own), span(r * width, width)], local_sem.at[0]
    )
    keep_table = pltpu.make_async_copy(table_ref, table_all.at[:, span(r * width, width)], local_sem.at[1])
    keep_gain = pltpu.make_async_copy(gain_ref, gain_all.at[:, span(r * width, width)], local_sem.at[2])
    keep.start()
    keep_table.start()
    keep_gain.start()
    barrier = pltpu.get_barrier_semaphore()
    for d in range(1, nr):
        pl.semaphore_signal(barrier, inc=1, device_id={"row": lax.rem(r + d, nr)}, device_id_type=MESH)

    @pl.when(c > 0)
    def _():
        pl.semaphore_signal(barrier, inc=1, device_id=left, device_id_type=MESH)

    @pl.when(c < n - 1)
    def _():
        pl.semaphore_signal(barrier, inc=1, device_id=right, device_id_type=MESH)

    inner = jnp.logical_and(c > 0, c < n - 1)

    @pl.when(inner)
    def _():
        pl.semaphore_wait(barrier, nr + 1)

    @pl.when(jnp.logical_not(inner))
    def _():
        pl.semaphore_wait(barrier, nr)

    @pl.loop(0, chunks)
    def _(j):
        for d in range(1, nr):
            piece(d, j).start()

    for d in range(1, nr):
        table_piece(d, 0).start()
        table_piece(d, 1).start()
    keep.wait()
    keep_table.wait()
    keep_gain.wait()

    for s in range(n):
        @pl.loop(0, chunks)
        def _(j):
            if s == 0:
                for d in range(1, nr):
                    piece(d, j).wait_recv()

            @pl.when(c - s >= 0)
            def _():
                if s > 0:
                    block(0, s - 1, jnp.maximum(c - s, 0), j, right).wait_recv()
                if s < n - 1:
                    @pl.when(c < n - 1)
                    def _():
                        block(0, s, jnp.maximum(c - s, 0), j, right).start()

            @pl.when(c + s <= n - 1)
            def _():
                if s > 0:
                    block(1, s - 1, jnp.minimum(c + s, n - 1), j, left).wait_recv()
                if s < n - 1:
                    @pl.when(c > 0)
                    def _():
                        block(1, s, jnp.minimum(c + s, n - 1), j, left).start()

    for d in range(1, nr):
        table_piece(d, 0).wait()
        table_piece(d, 1).wait()

    @pl.loop(0, chunks)
    def _(j):
        for d in range(1, nr):
            piece(d, j).wait_send()
        for s in range(n - 1):
            @pl.when(jnp.logical_and(c - s >= 0, c < n - 1))
            def _():
                block(0, s, jnp.maximum(c - s, 0), j, right).wait_send()

            @pl.when(jnp.logical_and(c + s <= n - 1, c > 0))
            def _():
                block(1, s, jnp.minimum(c + s, n - 1), j, left).wait_send()


def enter(tokens, table, gain, n, nr, m=32):
    own = tokens.shape[0] // nr
    chunks = own // m
    dma = pltpu.SemaphoreType.DMA
    return pl.pallas_call(
        functools.partial(enter_kernel, n, nr, m),
        out_shape=[
            jax.ShapeDtypeStruct((own * n, tokens.shape[1] * nr), tokens.dtype),
            jax.ShapeDtypeStruct((table.shape[0], table.shape[1] * nr), table.dtype),
            jax.ShapeDtypeStruct((gain.shape[0], gain.shape[1] * nr), gain.dtype),
        ],
        in_specs=[VM] * 3,
        out_specs=[VM] * 3,
        scratch_shapes=[
            dma((nr - 1, chunks)), dma((nr - 1, chunks)), dma((2, n - 1, chunks)), dma((2, n - 1, chunks)),
            dma((2, nr - 1)), dma((2, nr - 1)), dma((3,)),
        ],
        compiler_params=params(3),
        name="enter",
    )(tokens, table, gain)


def row_sums(first, second):
    ones = jnp.ones((8, first.shape[1]), wide)
    at = lax.broadcasted_iota(jnp.int32, (8, first.shape[0]), 0)
    sum_first = lax.dot_general(ones, first, last_last, preferred_element_type=wide, precision=precise)
    sum_second = lax.dot_general(ones, second, last_last, preferred_element_type=wide, precision=precise)
    return jnp.where(at < 4, sum_first, sum_second)


def down_columns(values, at):
    pick = (lax.broadcasted_iota(jnp.int32, (8, HEAD), 0) == at).astype(wide)
    return lax.dot_general(values, pick, first_first, preferred_element_type=wide, precision=precise)


def swap_stats(stats, n, send_sem, recv_sem):
    c = lax.axis_index("col")

    def copy(d):
        peer = lax.rem(c + d, n)
        return remote(stats.at[c], stats.at[c], send_sem.at[d - 1], recv_sem.at[d - 1], {"col": peer})

    for d in range(1, n):
        copy(d).start()
    for d in range(1, n):
        copy(d).wait()


def heads_kernel(n, nr, m, raw_ref, gq_ref, gk_ref, cos_ref, sin_ref, cot_ref, out_ref, factor_ref, half_ref,
                 stats, buf, fq, fk, send_s, recv_s, send_h, recv_h, send_g, recv_g, local_sem, local_g):
    r, c = lax.axis_index("row"), lax.axis_index("col")
    rows_all = raw_ref.shape[0]
    own = rows_all // n
    width = gq_ref.shape[1]
    heads = width // HEAD
    tree_part = own * nr
    q_all = raw_ref[:, :width]
    k_all = raw_ref[:, width:2 * width]
    stats[c] = row_sums(q_all * q_all, k_all * k_all)
    greet(n, nr)
    middle = n // 2
    owner = jnp.where(c < middle, 0, n - 1)
    at_owner = jnp.where(c < middle, c, c - middle)
    cot_width = cot_ref.shape[1]

    def cot_piece(d):
        peer = lax.rem(r + d, nr)
        return remote(
            cot_ref.at[span(peer * own, own)],
            half_ref.at[span(at_owner * own, own), span(r * cot_width, cot_width)],
            send_g.at[d], recv_g.at[at_owner, d], {"row": peer, "col": owner},
        )

    def cot_local():
        return pltpu.make_async_copy(
            cot_ref.at[span(r * own, own)],
            half_ref.at[span(at_owner * own, own), span(r * cot_width, cot_width)], local_g
        )

    swap_stats(stats, n, send_s, recv_s)
    for d in range(1, nr):
        cot_piece(d).start()

    @pl.when(owner == c)
    def _():
        cot_local().start()

    @pl.when(owner != c)
    def _():
        cot_piece(0).start()

    total = stats[0]
    for s in range(1, n):
        total = total + stats[s]
    factor = lax.rsqrt(total * (1.0 / D) + epsilon)
    factor_ref[...] = factor
    fq[...] = down_columns(factor, 0)
    fk[...] = down_columns(factor, 4)

    def piece(d, i, at):
        peer = lax.rem(r + d, nr)
        block = i // (own // m)
        inside = lax.rem(i, own // m)
        return remote(
            buf.at[peer, span(i * m, m)],
            out_ref.at[span(block * tree_part + r * own + inside * m, m)],
            send_h.at[d - 1, i], recv_h.at[d - 1, i], {"row": peer},
        )

    def local(i):
        block = i // (own // m)
        inside = lax.rem(i, own // m)
        return pltpu.make_async_copy(
            buf.at[r, span(i * m, m)], out_ref.at[span(block * tree_part + r * own + inside * m, m)], local_sem.at[i]
        )

    steps = rows_all // m

    @pl.loop(0, steps)
    def _(i):
        rows = span(i * m, m)
        cosine = cos_ref[rows, :]
        sine = sin_ref[rows, :]
        for h in range(heads):
            lanes = slice(h * HEAD, (h + 1) * HEAD)
            u = raw_ref[rows, lanes] * fq[rows, :] * gq_ref[:, lanes]
            buf[h, rows, :HEAD] = (u * cosine + pltpu.roll(u, HEAD // 2, 1) * sine).astype(low)
            k_lanes = slice(width + h * HEAD, width + (h + 1) * HEAD)
            u = raw_ref[rows, k_lanes] * fk[rows, :] * gk_ref[:, lanes]
            buf[h, rows, HEAD:2 * HEAD] = (u * cosine + pltpu.roll(u, HEAD // 2, 1) * sine).astype(low)
            v_lanes = slice(2 * width + h * HEAD, 2 * width + (h + 1) * HEAD)
            buf[h, rows, 2 * HEAD:] = raw_ref[rows, v_lanes].astype(low)
        for d in range(1, nr):
            piece(d, i, 0).start()
        local(i).start()

    @pl.loop(0, steps)
    def _(i):
        for d in range(1, nr):
            piece(d, i, 0).wait()
        local(i).wait()

    for d in range(1, nr):
        cot_piece(d).wait_send()

    @pl.when(owner != c)
    def _():
        cot_piece(0).wait_send()

    @pl.when(owner == c)
    def _():
        cot_local().wait()
        for b in range(middle):
            for d in range(nr):
                def take():
                    remote(
                        cot_ref.at[span(r * own, own)],
                        half_ref.at[span(b * own, own), span(0, cot_width)],
                        send_g.at[d], recv_g.at[b, d], {"row": r, "col": c},
                    ).wait_recv()
                if d == 0:
                    pl.when(b != at_owner)(take)
                else:
                    take()


def to_heads_call(raw, gain_q, gain_k, cos2, sin2, cot, n, nr, m=80):
    rows_all, wide3 = raw.shape
    width = wide3 // 3
    own = rows_all // n
    dma = pltpu.SemaphoreType.DMA
    steps = rows_all // m
    return pl.pallas_call(
        functools.partial(heads_kernel, n, nr, m),
        out_shape=[
            jax.ShapeDtypeStruct((own * n * nr, 3 * HEAD), low),
            jax.ShapeDtypeStruct((8, rows_all), wide),
            jax.ShapeDtypeStruct((own * n // 2, cot.shape[1] * nr), low),
        ],
        in_specs=[VM] * 6,
        out_specs=[VM] * 3,
        scratch_shapes=[
            pltpu.VMEM((n, 8, rows_all), wide),
            pltpu.VMEM((width // HEAD, rows_all, 3 * HEAD), low),
            pltpu.VMEM((rows_all, HEAD), wide),
            pltpu.VMEM((rows_all, HEAD), wide),
            dma((n - 1,)), dma((n - 1,)), dma((nr - 1, steps)), dma((nr - 1, steps)),
            dma((nr,)), dma((n // 2, nr)), dma((steps,)), dma,
        ],
        compiler_params=params(4),
        name="to_heads",
    )(raw, gain_q, gain_k, cos2, sin2, cot)


def unheads_kernel(n, nr, d_ref, raw_ref, factor_ref, gq_ref, gk_ref, cos_ref, sin_ref, res_ref, out_ref, res_out,
                   stats, buf, nq, nk, pq, pk, fq, fk, send_s, recv_s, send_h, recv_h, send_o, recv_o, local_sem, local_o):
    r, c = lax.axis_index("row"), lax.axis_index("col")
    rows_all = raw_ref.shape[0]
    own = rows_all // n
    width = gq_ref.shape[1]
    heads = width // HEAD
    tree_part = own * nr
    middle = n // 2
    out_width = res_out.shape[1]

    def piece(d, b):
        peer = lax.rem(r + d, nr)
        return remote(
            d_ref.at[span(b * tree_part + peer * own, own)],
            buf.at[r, span(b * own, own)],
            send_h.at[d - 1, b], recv_h.at[d - 1, b], {"row": peer},
        )

    def local(b):
        return pltpu.make_async_copy(
            d_ref.at[span(b * tree_part + r * own, own)], buf.at[r, span(b * own, own)], local_sem.at[b]
        )

    is_owner = jnp.logical_or(c == 0, c == n - 1)
    base = jnp.where(c == 0, 0, middle)

    def result_piece(b, d):
        peer = lax.rem(r + d, nr)
        return remote(
            res_ref.at[span(b * own, own), span(peer * out_width, out_width)],
            res_out.at[span(r * own, own)],
            send_o.at[b, d], recv_o.at[d], {"row": peer, "col": base + b},
        )

    def result_local(b):
        return pltpu.make_async_copy(
            res_ref.at[span(b * own, own), span(r * out_width, out_width)], res_out.at[span(r * own, own)], local_o
        )

    for b in range(n):
        local(b).start()
    greet(n, nr)
    for b in range(n):
        for d in range(1, nr):
            piece(d, b).start()

    @pl.when(is_owner)
    def _():
        for b in range(middle):
            for d in range(nr):
                if d == 0:
                    @pl.when(base + b == c)
                    def _():
                        result_local(b).start()

                    @pl.when(base + b != c)
                    def _():
                        result_piece(b, d).start()
                else:
                    result_piece(b, d).start()

    fq[...] = down_columns(factor_ref[...], 0)
    fk[...] = down_columns(factor_ref[...], 4)
    for b in range(n):
        for d in range(1, nr):
            piece(d, b).wait_recv()
        local(b).wait()
        rows = slice(b * own, (b + 1) * own)
        cosine = cos_ref[rows, :]
        sine = sin_ref[rows, :]
        for h in range(heads):
            lanes = slice(h * HEAD, (h + 1) * HEAD)
            u = buf[h, rows, :HEAD].astype(wide)
            u = (u * cosine - pltpu.roll(u, HEAD // 2, 1) * sine) * gq_ref[:, lanes]
            nq[rows, lanes] = u
            pq[rows, lanes] = u * raw_ref[rows, lanes] * fq[rows, :]
            u = buf[h, rows, HEAD:2 * HEAD].astype(wide)
            u = (u * cosine - pltpu.roll(u, HEAD // 2, 1) * sine) * gk_ref[:, lanes]
            nk[rows, lanes] = u
            pk[rows, lanes] = u * raw_ref[rows, slice(width + h * HEAD, width + (h + 1) * HEAD)] * fk[rows, :]
            out_ref[rows, slice(2 * width + h * HEAD, 2 * width + (h + 1) * HEAD)] = buf[h, rows, 2 * HEAD:]
    stats[c] = row_sums(pq[...], pk[...])
    swap_stats(stats, n, send_s, recv_s)
    total = stats[0]
    for s in range(1, n):
        total = total + stats[s]
    mean = total * (1.0 / D) * factor_ref[...]
    pq[:, :HEAD] = down_columns(mean, 0)
    pk[:, :HEAD] = down_columns(mean, 4)
    for b in range(n):
        rows = slice(b * own, (b + 1) * own)
        for h in range(heads):
            lanes = slice(h * HEAD, (h + 1) * HEAD)
            k_lanes = slice(width + h * HEAD, width + (h + 1) * HEAD)
            out_ref[rows, lanes] = (fq[rows, :] * (nq[rows, lanes] - raw_ref[rows, lanes] * pq[rows, :HEAD])).astype(low)
            out_ref[rows, k_lanes] = (fk[rows, :] * (nk[rows, lanes] - raw_ref[rows, k_lanes] * pk[rows, :HEAD])).astype(low)
    for b in range(n):
        for d in range(1, nr):
            piece(d, b).wait_send()

    @pl.when(is_owner)
    def _():
        for b in range(middle):
            for d in range(nr):
                if d == 0:
                    @pl.when(base + b == c)
                    def _():
                        result_local(b).wait()

                    @pl.when(base + b != c)
                    def _():
                        result_piece(b, d).wait_send()
                else:
                    result_piece(b, d).wait_send()

    for d in range(nr):
        def take():
            remote(
                res_ref.at[span(0, own), span(0, out_width)], res_out.at[span(r * own, own)],
                send_o.at[0, d], recv_o.at[d], {"row": r, "col": c},
            ).wait_recv()
        if d == 0:
            pl.when(jnp.logical_not(is_owner))(take)
        else:
            take()


def from_heads_call(d_head, raw, factor, gain_q, gain_k, cos2, sin2, result, n, nr):
    rows_all, wide3 = raw.shape
    width = wide3 // 3
    dma = pltpu.SemaphoreType.DMA
    square = pltpu.VMEM((rows_all, width), wide)
    return pl.pallas_call(
        functools.partial(unheads_kernel, n, nr),
        out_shape=[
            jax.ShapeDtypeStruct((rows_all, wide3), low),
            jax.ShapeDtypeStruct((rows_all // n * nr, result.shape[1] // nr), low),
        ],
        in_specs=[VM] * 8,
        out_specs=[VM] * 2,
        scratch_shapes=[
            pltpu.VMEM((n, 8, rows_all), wide),
            pltpu.VMEM((nr, rows_all, 3 * HEAD), low),
            square, square, square, square,
            pltpu.VMEM((rows_all, HEAD), wide),
            pltpu.VMEM((rows_all, HEAD), wide),
            dma((n - 1,)), dma((n - 1,)), dma((nr - 1, n)), dma((nr - 1, n)),
            dma((n // 2, nr)), dma((nr,)), dma((n,)), dma,
        ],
        compiler_params=params(5),
        name="from_heads",
    )(d_head, raw, factor, gain_q, gain_k, cos2, sin2, result)


def finish_kernel(n, nr, ndp, m, part_ref, full_ref, col_ref, hot_ref, grad_ref, sets_ref,
                  recv_right, recv_left, send_right, send_left, own_buf, in_buf, full_recv, full_sum, full_last,
                  col_recv, owned, hot_all,
                  send_z, recv_z, send_w, recv_w, local_w, send_f, recv_f, send_c, recv_c, send_l, recv_l,
                  send_d, recv_d, send_k, recv_k):
    g, r, c = lax.axis_index("dp"), lax.axis_index("row"), lax.axis_index("col")
    own = part_ref.shape[0] // n
    width = in_buf.shape[1]
    chunks = own // m
    left = {"col": jnp.maximum(c - 1, 0)}
    right = {"col": jnp.minimum(c + 1, n - 1)}
    full_rows = full_last.shape[1]
    col_rows = col_recv.shape[1]

    def full_piece(d):
        peer = lax.rem(r + d, nr)
        return remote(full_ref.at[:, span(peer * width, width)], full_recv.at[r], send_f.at[d - 1], recv_f.at[d - 1], {"row": peer})

    def col_piece(d):
        peer = lax.rem(r + d, nr)
        return remote(col_ref.at[span(peer * col_rows, col_rows)], col_recv.at[r], send_c.at[d - 1], recv_c.at[d - 1], {"row": peer})

    def last_piece(d):
        peer = lax.rem(c + d, n)
        return remote(full_sum.at[span(peer * full_rows, full_rows)], full_last.at[c], send_l.at[d - 1], recv_l.at[d - 1], {"col": peer})

    def tree_piece(d):
        peer = lax.rem(g + d, ndp)
        return remote(owned.at[g], owned.at[g], send_d.at[d - 1], recv_d.at[d - 1], {"dp": peer})

    def hot_piece(d):
        peer = lax.rem(g + d, ndp)
        return remote(hot_all.at[g], hot_all.at[g], send_k.at[d - 1], recv_k.at[d - 1], {"dp": peer})

    def reduce(kind, b, j, src):
        rows = span(b * own + j * m, m)
        dst, to = ((recv_right, right), (recv_left, left))[kind]
        return remote(src.at[rows], dst.at[rows], send_z.at[kind, b, j], recv_z.at[kind, b, j], to)

    def width_piece(d, j):
        peer = lax.rem(r + d, nr)
        return remote(
            own_buf.at[span(j * m, m), span(peer * width, width)], in_buf.at[span(r * own + j * m, m)],
            send_w.at[d - 1, j], recv_w.at[d - 1, j], {"row": peer},
        )

    def width_local(j):
        return pltpu.make_async_copy(
            own_buf.at[span(j * m, m), span(r * width, width)], in_buf.at[span(r * own + j * m, m)], local_w.at[j]
        )

    me = r * n + c
    barrier = pltpu.get_barrier_semaphore()
    for d in range(1, ndp):
        pl.semaphore_signal(barrier, inc=1, device_id={"dp": lax.rem(g + d, ndp)}, device_id_type=MESH)

    @pl.loop(1, n * nr)
    def _(d):
        peer = lax.rem(me + d, n * nr)
        pl.semaphore_signal(barrier, inc=1, device_id={"row": peer // n, "col": lax.rem(peer, n)}, device_id_type=MESH)

    pl.semaphore_wait(barrier, n * nr - 1 + ndp - 1)
    hot_all[g] = hot_ref[...]
    for d in range(1, nr):
        full_piece(d).start()
        col_piece(d).start()

    def stage(s):
        @pl.loop(0, chunks)
        def _(j):
            for kind, b, go, edge, acc, got in (
                (0, n - 1 - s, n - 1 - s > c, c == 0, send_right, recv_right),
                (1, s, s < c, c == n - 1, send_left, recv_left),
            ):
                @pl.when(go)
                def _():
                    @pl.when(edge)
                    def _():
                        reduce(kind, b, j, part_ref).start()

                    @pl.when(jnp.logical_not(edge))
                    def _():
                        rows = span(b * own + j * m, m)
                        reduce(kind, b, j, acc).wait_recv()
                        acc[rows, :] = (part_ref[rows, :].astype(wide) + got[rows, :].astype(wide)).astype(low)
                        reduce(kind, b, j, acc).start()

    stage(0)
    for d in range(1, nr):
        full_piece(d).wait_recv()
        col_piece(d).wait_recv()
    total = full_ref[:, span(r * width, width)].astype(wide)
    col_total = col_ref[span(r * col_rows, col_rows), :].astype(wide)
    for d in range(1, nr):
        peer = lax.rem(r + d, nr)
        total = total + full_recv[peer].astype(wide)
        col_total = col_total + col_recv[peer].astype(wide)
    full_sum[...] = total.astype(low)
    owned[g, full_rows:, :] = col_total.astype(low)
    for d in range(1, n):
        last_piece(d).start()
    stage(1)
    for d in range(1, n):
        last_piece(d).wait_recv()
    last = full_sum[span(c * full_rows, full_rows), :].astype(wide)
    for d in range(1, n):
        last = last + full_last[lax.rem(c + d, n)].astype(wide)
    owned[g, :full_rows, :] = last.astype(low)
    for d in range(1, ndp):
        tree_piece(d).start()
        hot_piece(d).start()
    for s in range(2, n - 1):
        stage(s)

    rows_own = c * own

    @pl.loop(0, chunks)
    def _(j):
        rows = span(rows_own + j * m, m)
        at = span(j * m, m)

        @pl.when(c == 0)
        def _():
            reduce(1, c, j, send_left).wait_recv()
            own_buf[at, :] = (part_ref[rows, :].astype(wide) + recv_left[rows, :].astype(wide)).astype(low)

        @pl.when(c == n - 1)
        def _():
            reduce(0, c, j, send_right).wait_recv()
            own_buf[at, :] = (part_ref[rows, :].astype(wide) + recv_right[rows, :].astype(wide)).astype(low)

        @pl.when(jnp.logical_and(c > 0, c < n - 1))
        def _():
            reduce(0, c, j, send_right).wait_recv()
            reduce(1, c, j, send_left).wait_recv()
            own_buf[at, :] = (
                part_ref[rows, :].astype(wide) + recv_right[rows, :].astype(wide) + recv_left[rows, :].astype(wide)
            ).astype(low)

        for d in range(1, nr):
            width_piece(d, j).start()
        width_local(j).start()

    for d in range(1, ndp):
        tree_piece(d).wait_recv()
        hot_piece(d).wait_recv()
    sets_own = sets_ref.shape[0]
    for s in range(sets_own):
        total = owned[0].astype(wide) * hot_all[0, pl.ds(g * sets_own + s, 1), :]
        for t in range(1, ndp):
            total = total + owned[t].astype(wide) * hot_all[t, pl.ds(g * sets_own + s, 1), :]
        sets_ref[s] = total

    @pl.loop(0, chunks)
    def _(j):
        for d in range(1, nr):
            width_piece(d, j).wait()
        width_local(j).wait()

    grad_ref[...] = in_buf[...].astype(wide)
    for d in range(1, nr):
        full_piece(d).wait_send()
        col_piece(d).wait_send()
    for d in range(1, n):
        last_piece(d).wait_send()
    for d in range(1, ndp):
        tree_piece(d).wait_send()
        hot_piece(d).wait_send()
    for s in range(n - 1):
        @pl.loop(0, chunks)
        def _(j):
            @pl.when(n - 1 - s > c)
            def _():
                reduce(0, n - 1 - s, j, send_right).wait_send()

            @pl.when(s < c)
            def _():
                reduce(1, s, j, send_left).wait_send()


def finish(part, full, cols, hot, sets_own, n, nr, ndp, m=32):
    rows_all, width_all = part.shape
    own = rows_all // n
    width = width_all // nr
    chunks = own // m
    full_rows = full.shape[0] // n
    col_rows = cols.shape[0] // nr
    dma = pltpu.SemaphoreType.DMA
    big = pltpu.VMEM((rows_all, width_all), low)
    return pl.pallas_call(
        functools.partial(finish_kernel, n, nr, ndp, m),
        out_shape=[
            jax.ShapeDtypeStruct((own * nr, width), wide),
            jax.ShapeDtypeStruct((sets_own, full_rows + col_rows, width), wide),
        ],
        in_specs=[VM] * 4,
        out_specs=[VM] * 2,
        scratch_shapes=[
            big, big, big, big,
            pltpu.VMEM((own, width_all), low),
            pltpu.VMEM((own * nr, width), low),
            pltpu.VMEM((nr, full.shape[0], width), low),
            pltpu.VMEM((full.shape[0], width), low),
            pltpu.VMEM((n, full_rows, width), low),
            pltpu.VMEM((nr, col_rows, width), low),
            pltpu.VMEM((ndp, full_rows + col_rows, width), low),
            pltpu.VMEM((ndp,) + hot.shape, wide),
            dma((2, n, chunks)), dma((2, n, chunks)), dma((nr - 1, chunks)), dma((nr - 1, chunks)), dma((chunks,)),
            dma((nr - 1,)), dma((nr - 1,)), dma((nr - 1,)), dma((nr - 1,)), dma((n - 1,)), dma((n - 1,)),
            dma((ndp - 1,)), dma((ndp - 1,)), dma((ndp - 1,)), dma((ndp - 1,)),
        ],
        compiler_params=params(6),
        name="finish",
    )(part, full, cols, hot)


def middle_kernel(n, nr, m, hop, head_ref, x_hbm, cot_hbm, gain_ref, wo_hbm, wg_hbm, wd_hbm,
                  ao_ref, bo_ref, ag_ref, bg_ref, ad_ref, bd_ref,
                  dhead_ref, out_half, grad_half, full_ref, co_ref, cg_ref, cd_ref,
                  wo, wg, wd, x_half, cot_half, raw, attn, d_attn, h_all, df_all, da_all, gu, part,
                  recv_right, recv_left, hid, red_gu, red_down, back_gu, back_down,
                  sems_send, sems_recv, send_in, recv_in, send_out, recv_out, local_in, local_out, load, load_w):
    r, c = lax.axis_index("row"), lax.axis_index("col")
    rows_all, width_all = part.shape
    half = rows_all // 2
    own = rows_all // n
    tree_part = own * nr
    chunks = half // m
    blocks = 4
    band = half // blocks
    hidden = ad_ref.shape[1]
    width = width_all // nr
    left = {"col": jnp.maximum(c - 1, 0)}
    right = {"col": jnp.minimum(c + 1, n - 1)}
    first = c == 0
    last = c == n - 1
    inner = jnp.logical_and(c > 0, c < n - 1)

    base = jnp.where(last, half, 0)
    a_cut = hidden // 4
    loads = [pltpu.make_async_copy(wo_hbm, wo, load.at[0])]
    loads_a = []
    for k in range(4):
        lanes = slice(k * a_cut, (k + 1) * a_cut)
        up_lanes = slice(hidden + k * a_cut, hidden + (k + 1) * a_cut)
        loads_a.append(pltpu.make_async_copy(wg_hbm.at[:, lanes], wg.at[:, lanes], load_w.at[2 * k]))
        loads_a.append(pltpu.make_async_copy(wg_hbm.at[:, up_lanes], wg.at[:, up_lanes], load_w.at[2 * k + 1]))
    load_x = pltpu.make_async_copy(x_hbm.at[span(base, half)], x_half, load.at[1])
    load_cot = pltpu.make_async_copy(cot_hbm, cot_half, load.at[2])
    load_d = pltpu.make_async_copy(wd_hbm, wd, load.at[3])
    loads[0].start()

    def piece_in(d, b):
        peer = lax.rem(r + d, nr)
        return remote(
            head_ref.at[span(b * tree_part + peer * own, own)],
            attn.at[span(b * own, own), span(r * HEAD, HEAD)],
            send_in.at[d - 1, b], recv_in.at[d - 1, b], {"row": peer},
        )

    def local_piece_in(b):
        return pltpu.make_async_copy(
            head_ref.at[span(b * tree_part + r * own, own)],
            attn.at[span(b * own, own), span(r * HEAD, HEAD)], local_in.at[b]
        )

    def piece_out(d, b):
        peer = lax.rem(r + d, nr)
        return remote(
            d_attn.at[span(b * own, own), span(peer * HEAD, HEAD)],
            dhead_ref.at[span(b * tree_part + r * own, own)],
            send_out.at[d - 1, b], recv_out.at[d - 1, b], {"row": peer},
        )

    def local_piece_out(b):
        return pltpu.make_async_copy(
            d_attn.at[span(b * own, own), span(r * HEAD, HEAD)],
            dhead_ref.at[span(b * tree_part + r * own, own)], local_out.at[b]
        )

    for b in range(n):
        local_piece_in(b).start()
    barrier = pltpu.get_barrier_semaphore()
    for d in range(1, nr):
        pl.semaphore_signal(barrier, inc=1, device_id={"row": lax.rem(r + d, nr)}, device_id_type=MESH)

    @pl.when(c > 0)
    def _():
        pl.semaphore_signal(barrier, inc=1, device_id=left, device_id_type=MESH)

    @pl.when(c < n - 1)
    def _():
        pl.semaphore_signal(barrier, inc=1, device_id=right, device_id_type=MESH)

    full_ref[...] = jnp.zeros_like(full_ref)
    co_ref[...] = jnp.zeros_like(co_ref)
    cg_ref[...] = jnp.zeros_like(cg_ref)
    cd_ref[...] = jnp.zeros_like(cd_ref)

    @pl.when(inner)
    def _():
        pl.semaphore_wait(barrier, nr + 1)

    @pl.when(jnp.logical_not(inner))
    def _():
        pl.semaphore_wait(barrier, nr)

    middle = n // 2
    for b in range(middle):
        for block in (b, middle + b):
            for d in range(1, nr):
                piece_in(d, block).start()
    for copy in loads_a:
        copy.start()
    load_x.start()
    load_d.start()
    load_cot.start()

    def rows(j, start=0):
        return span(start + j * m, m)

    def band_rows(b):
        return span(b * band, band), span(half + b * band, band)

    def take(ref, b):
        low_rows, high_rows = band_rows(b)
        return jnp.concatenate([ref[low_rows, :], ref[high_rows, :]], axis=0)

    def put(b, lanes, value):
        low_rows, high_rows = band_rows(b)
        part[low_rows, lanes] = value[:band].astype(low)
        part[high_rows, lanes] = value[band:].astype(low)

    def relay_stage(stage, per, work, owner_step, all_ref):
        def send(kind, j, src, dst, to):
            return remote(src, dst, sems_send.at[stage, kind, j], sems_recv.at[stage, kind, j], to)

        def reduce_right(j):
            return send(0, j, part.at[rows(j, half)], recv_right.at[rows(j)], right)

        def reduce_left(j):
            return send(1, j, part.at[rows(j)], recv_left.at[rows(j)], left)

        def spread_left(j):
            return send(2, j, all_ref.at[rows(j, half)], all_ref.at[rows(j, half)], left)

        def spread_right(j):
            return send(3, j, all_ref.at[rows(j)], all_ref.at[rows(j)], right)

        total_slices = per * blocks
        each = chunks // blocks

        def slices_before(i):
            late = per + (jnp.maximum(i - per, 0) * per) // each
            return jnp.minimum(jnp.where(i < per, i, late), total_slices)

        @pl.loop(0, per + chunks + hop * 2 * (n - 1))
        def _(ii):
            i = ii - per

            def on(offset, who, run):
                j = i - offset

                @pl.when(jnp.logical_and(who, jnp.logical_and(j >= 0, j < chunks)))
                def _():
                    run(j)

            def mid_right(j):
                reduce_right(j).wait_recv()
                at = rows(j, half)
                part[at, :] = (part[at, :].astype(wide) + recv_right[rows(j), :].astype(wide)).astype(low)
                reduce_right(j).start()

            def mid_left(j):
                reduce_left(j).wait_recv()
                at = rows(j)
                part[at, :] = (part[at, :].astype(wide) + recv_left[at, :].astype(wide)).astype(low)
                reduce_left(j).start()

            def end_right(j):
                reduce_right(j).wait_recv()
                total = part[rows(j, half), :].astype(wide) + recv_right[rows(j), :].astype(wide)
                all_ref[rows(j, half), :] = owner_step(total, rows(j))
                spread_left(j).start()

            def end_left(j):
                reduce_left(j).wait_recv()
                total = part[rows(j), :].astype(wide) + recv_left[rows(j), :].astype(wide)
                all_ref[rows(j), :] = owner_step(total, rows(j))
                spread_right(j).start()

            def pass_left(j):
                spread_left(j).wait_recv()
                spread_left(j).start()

            def pass_right(j):
                spread_right(j).wait_recv()
                spread_right(j).start()

            on(0, first, lambda j: reduce_right(j).start())
            on(0, last, lambda j: reduce_left(j).start())
            on(hop * c, inner, mid_right)
            on(hop * (n - 1 - c), inner, mid_left)
            on(hop * (n - 1), last, end_right)
            on(hop * (n - 1), first, end_left)
            on(hop * (2 * (n - 1) - c), inner, pass_left)
            on(hop * (n - 1 + c), inner, pass_right)

            @pl.loop(slices_before(ii), slices_before(ii + 1))
            def _(t):
                work(t // per, lax.rem(t, per))

        @pl.loop(0, chunks)
        def _(j):
            @pl.when(first)
            def _():
                reduce_right(j).wait_send()
                spread_right(j).wait_send()
                spread_left(j).wait_recv()

            @pl.when(last)
            def _():
                reduce_left(j).wait_send()
                spread_left(j).wait_send()
                spread_right(j).wait_recv()

            @pl.when(inner)
            def _():
                reduce_right(j).wait_send()
                reduce_left(j).wait_send()
                spread_left(j).wait_send()
                spread_right(j).wait_send()

    def out_work(b, k):
        @pl.when(b == 0)
        def _():
            loads[0].wait()

        @pl.when(lax.rem(b, blocks // middle) == 0)
        def _():
            at = b // (blocks // middle)
            for block in (at, middle + at):
                for d in range(1, nr):
                    piece_in(d, block).wait_recv()
                local_piece_in(block).wait()

        rows_in = take(attn, b)
        red = dot_t(rows_in, ao_ref[...]).astype(low)
        for j in range(nr):
            lanes = slice(j * width, (j + 1) * width)
            put(b, lanes, dot(rows_in, wo[j]) + dot(red, bo_ref[:, lanes]))

    gain_a = gain_ref[0:1, :]
    gain_f = gain_ref[1:2, :]

    def attn_owner(total, at):
        raw[at, :] = total
        flat = total * norm_factor(row_sum(total * total))
        return (x_half[at, :].astype(wide) + flat * gain_a).astype(low)

    load_x.wait()
    relay_stage(0, 1, out_work, attn_owner, h_all)

    def gate_slice(b, k):
        @pl.when(b == 0)
        def _():
            for s in range(4):
                @pl.when(k == s)
                def _():
                    loads_a[2 * s].wait()
                    loads_a[2 * s + 1].wait()

        rows_in = take(h_all, b)

        @pl.when(k == 0)
        def _():
            red_gu[b] = dot_t(rows_in, ag_ref[...]).astype(low)

        at = pl.multiple_of(k * a_cut, a_cut)
        lanes = pl.ds(at, a_cut)
        up_lanes = pl.ds(pl.multiple_of(hidden + at, a_cut), a_cut)
        red = red_gu[b]
        gate = dot(rows_in, wg[:, lanes]) + dot(red[:, :RANK], bg_ref[0, :, lanes])
        up = dot(rows_in, wg[:, up_lanes]) + dot(red[:, RANK:], bg_ref[1, :, lanes])
        gu[b, :, lanes] = gate.astype(low)
        gu[b, :, up_lanes] = up.astype(low)
        hid[:, lanes] = (gate * jax.nn.sigmoid(gate) * up).astype(low)

    def down_slice(b, k):
        @pl.when(jnp.logical_and(b == 0, k == 0))
        def _():
            load_d.wait()

        rows_in = hid[:, :hidden]

        @pl.when(k == 0)
        def _():
            red_down[b] = dot_t(rows_in, ad_ref[...]).astype(low)

        for s in range(nr // 2):
            j = k * (nr // 2) + s
            lanes = span(j * width, width)
            put(b, lanes, dot(rows_in, wd[j]) + dot(red_down[b], bd_ref[:, lanes]))

    def ffn_work(b, k):
        @pl.when(k < 4)
        def _():
            gate_slice(b, k)

        @pl.when(k >= 4)
        def _():
            down_slice(b, k - 4)

    def ffn_owner(total, at):
        a_raw = raw[at, :]
        h = x_half[at, :].astype(wide) + a_raw * norm_factor(row_sum(a_raw * a_raw)) * gain_a
        factor = norm_factor(row_sum(total * total))
        flat = total * factor
        out_half[at, :] = (h + flat * gain_f).astype(low)
        scaled = cot_half[at, :].astype(wide) * gain_f
        return (factor * (scaled - flat * (row_sum(scaled * flat) * (1.0 / D)))).astype(low)

    load_cot.wait()
    relay_stage(1, 6, ffn_work, ffn_owner, df_all)

    b_cut = hidden // 2

    def hidden_back(b, k):
        rows_in = take(df_all, b)

        @pl.when(k == 0)
        def _():
            back_down[...] = dot_t(rows_in, bd_ref[...]).astype(low)

        at = pl.multiple_of(k * b_cut, b_cut)
        lanes = pl.ds(at, b_cut)
        up_lanes = pl.ds(pl.multiple_of(hidden + at, b_cut), b_cut)
        back = back_down[...]
        grad = dot(back, ad_ref[:, lanes])
        for j in range(nr):
            grad = grad + dot_t(rows_in[:, j * width:(j + 1) * width], wd[j, lanes, :])
        gate = gu[b, :, lanes].astype(wide)
        up = gu[b, :, up_lanes].astype(wide)
        sigma = jax.nn.sigmoid(gate)
        silu = gate * sigma
        d_gate = (grad * up * sigma * (1.0 + gate * (1.0 - sigma))).astype(low)
        d_up = (grad * silu).astype(low)
        hid[:, lanes] = d_gate
        hid[:, up_lanes] = d_up
        cd_ref[:, lanes] += t_dot(back, (silu * up).astype(low))
        red = red_gu[b]
        cg_ref[0, :, lanes] += t_dot(red[:, :RANK], d_gate)
        cg_ref[1, :, lanes] += t_dot(red[:, RANK:], d_up)

    o_cut = width_all // 4

    def gate_back(b, k):
        @pl.when(k == 0)
        def _():
            back_gu[:, :RANK] = dot_t(hid[:, :hidden], bg_ref[0]).astype(low)
            back_gu[:, RANK:] = dot_t(hid[:, hidden:], bg_ref[1]).astype(low)

        lanes = span(k * o_cut, o_cut)
        put(b, lanes, dot_t(hid[...], wg[lanes, :]) + dot(back_gu[...], ag_ref[:, lanes]))

        @pl.when(k == 3)
        def _():
            full_ref[:2 * RANK, :] += t_dot(back_gu[...], take(h_all, b))
            full_ref[3 * RANK:, :] += t_dot(red_down[b], take(df_all, b))

    def back_work(b, k):
        @pl.when(k < 2)
        def _():
            hidden_back(b, k)

        @pl.when(k >= 2)
        def _():
            gate_back(b, k - 2)

    def back_owner(total, at):
        grad = cot_half[at, :].astype(wide) + total
        grad_half[at, :] = grad
        a_raw = raw[at, :]
        factor = norm_factor(row_sum(a_raw * a_raw))
        flat = a_raw * factor
        scaled = grad * gain_a
        return (factor * (scaled - flat * (row_sum(scaled * flat) * (1.0 / D)))).astype(low)

    relay_stage(2, 6, back_work, back_owner, da_all)

    @pl.loop(0, n)
    def _(b):
        at = span(b * own, own)
        rows_in = da_all[at, :]
        back = dot_t(rows_in, bo_ref[...]).astype(low)
        grad = dot(back, ao_ref[...])
        for j in range(nr):
            grad = grad + dot_t(rows_in[:, j * width:(j + 1) * width], wo[j])
        d_attn[at, :] = grad.astype(low)
        for d in range(1, nr):
            piece_out(d, b).start()
        local_piece_out(b).start()
        attn_rows = attn[at, :]
        co_ref[...] += t_dot(back, attn_rows)
        red = dot_t(attn_rows, ao_ref[...]).astype(low)
        full_ref[2 * RANK:3 * RANK, :] += t_dot(red, rows_in)

    @pl.loop(0, n)
    def _(b):
        for d in range(1, nr):
            piece_in(d, b).wait_send()
            piece_out(d, b).wait()
        local_piece_out(b).wait()


def middle(attn_head, x, cot_half, gains, w_out, w_gu, w_down, a_out, b_out, a_gu, b_gu, a_down, b_down, n, nr, m=16, hop=2):
    group, width_all = x.shape
    half = group // 2
    width = width_all // nr
    hidden = a_down.shape[1]
    chunks = half // m
    band = group // 4
    dma = pltpu.SemaphoreType.DMA
    any_space = pl.BlockSpec(memory_space=pl.ANY)
    shape = jax.ShapeDtypeStruct
    return pl.pallas_call(
        functools.partial(middle_kernel, n, nr, m, hop),
        out_shape=[
            shape(attn_head.shape, low),
            shape((half, width_all), low),
            shape((half, width_all), wide),
            shape((4 * RANK, width_all), wide),
            shape((RANK, a_out.shape[1]), wide),
            shape((2, RANK, hidden), wide),
            shape((RANK, hidden), wide),
        ],
        in_specs=[VM, any_space, any_space, VM, any_space, any_space, any_space] + [VM] * 6,
        out_specs=[VM] * 7,
        scratch_shapes=[
            pltpu.VMEM(w_out.shape, low),
            pltpu.VMEM(w_gu.shape, low),
            pltpu.VMEM(w_down.shape, low),
            pltpu.VMEM((half, width_all), low),
            pltpu.VMEM((half, width_all), low),
            pltpu.VMEM((half, width_all), wide),
            pltpu.VMEM((group, a_out.shape[1]), low),
            pltpu.VMEM((group, a_out.shape[1]), low),
            pltpu.VMEM((group, width_all), low),
            pltpu.VMEM((group, width_all), low),
            pltpu.VMEM((group, width_all), low),
            pltpu.VMEM((4, band, 2 * hidden), low),
            pltpu.VMEM((group, width_all), low),
            pltpu.VMEM((half, width_all), low),
            pltpu.VMEM((half, width_all), low),
            pltpu.VMEM((band, 2 * hidden), low),
            pltpu.VMEM((4, band, 2 * RANK), low),
            pltpu.VMEM((4, band, RANK), low),
            pltpu.VMEM((band, 2 * RANK), low),
            pltpu.VMEM((band, RANK), low),
            dma((3, 4, chunks)), dma((3, 4, chunks)),
            dma((nr - 1, n)), dma((nr - 1, n)), dma((nr - 1, n)), dma((nr - 1, n)), dma((n,)), dma((n,)),
            dma((4,)), dma((8,)),
        ],
        compiler_params=pltpu.CompilerParams(collective_id=0, has_side_effects=True, vmem_limit_bytes=67043328),
        name="middle",
    )(attn_head, x, cot_half, gains, w_out, w_gu, w_down, a_out, b_out, a_gu, b_gu, a_down, b_down)


def per_device(
    tokens,
    cotangent,
    seg_ids,
    positions,
    parents,
    tree_sets,
    gain_q,
    gain_k,
    gain_attn,
    gain_ffn,
    query_key_value_weight,
    output_weight,
    gate_up_weight,
    down_weight,
    query_key_value_adapter_first,
    query_key_value_adapter_second,
    output_adapter_first,
    output_adapter_second,
    gate_up_adapter_first,
    gate_up_adapter_second,
    down_adapter_first,
    down_adapter_second,
):
    dp_count = lax.axis_size("dp")
    row_count = lax.axis_size("row")
    col_count = lax.axis_size("col")
    row_at = lax.axis_index("row")
    tree_tokens = seg_ids.shape[0]
    assert tree_sets.shape[0] == 1 and col_count == 4
    set_count = output_adapter_first.shape[0]
    own = tokens.shape[0] // row_count
    group = own * col_count
    width_row = tokens.shape[1]
    width_col = gain_q.shape[0]
    hidden_col = down_weight.shape[0]
    heads_col = width_col // HEAD
    tree_set = tree_sets[0]

    def pick(table, axis):
        return lax.dynamic_index_in_dim(table, tree_set, axis, keepdims=False)

    narrow = jnp.concatenate(
        [
            pick(query_key_value_adapter_first, 1),
            pick(gate_up_adapter_first, 1),
            pick(output_adapter_second, 0)[None],
            pick(down_adapter_second, 0)[None],
        ],
        axis=0,
    ).astype(low)
    gain_pair = jnp.pad(jnp.stack([gain_attn, gain_ffn]), ((0, 6), (0, 0)))
    x, table, gains = enter(tokens, narrow.reshape(7 * RANK, width_row), gain_pair, col_count, row_count)
    a_qkv = table[: 3 * RANK]
    a_gu = table[3 * RANK : 5 * RANK]
    b_out = table[5 * RANK : 6 * RANK]
    b_down = table[6 * RANK :]
    b_qkv = pick(query_key_value_adapter_second, 1).astype(low)
    b_gu = pick(gate_up_adapter_second, 1).astype(low)
    a_out = pick(output_adapter_first, 0).astype(low)
    a_down = pick(down_adapter_first, 0).astype(low)

    def gather_rows(weight, stacked):
        share = weight.shape[0] // dp_count
        mine = lax.dynamic_slice_in_dim(weight, lax.axis_index("dp") * share, share, 0)
        return lax.all_gather(mine, ("row", "dp"), axis=0, tiled=not stacked)

    w_qkv = gather_rows(query_key_value_weight.reshape(width_row, 3 * width_col), False)
    w_gu = gather_rows(gate_up_weight.reshape(width_row, 2 * hidden_col), False)
    w_down = gather_rows(down_weight, True).reshape(row_count, hidden_col, width_row)
    w_out = gather_rows(output_weight, True).reshape(row_count, width_col, width_row)

    first = lax.axis_index("col") == 0
    final = lax.axis_index("col") == col_count - 1
    red_qkv = dot_t(x, a_qkv).astype(low)
    raw = dot(x, w_qkv)
    extra = jnp.concatenate([dot(red_qkv[:, RANK * j : RANK * (j + 1)], b_qkv[j]) for j in range(3)], axis=1)
    raw = raw + extra
    pos_own = lax.dynamic_index_in_dim(
        positions.reshape(col_count, row_count, own), row_at, 1, keepdims=False
    ).reshape(group)
    cosine, sine = angles(pos_own)
    cos2 = jnp.concatenate([cosine, cosine], axis=1)
    sin2 = jnp.concatenate([-sine, sine], axis=1)
    gq, gk = gain_q[None, :], gain_k[None, :]
    qkv_head, factors, g_half = to_heads_call(raw, gq, gk, cos2, sin2, cotangent, col_count, row_count)
    parent_at, branch_flag = tree_tables(seg_ids, parents)
    pos_down, pos_across = positions[:, None], positions[None, :]
    attn_head, lse = attend(qkv_head, parent_at, branch_flag, pos_down, pos_across)
    d_attn_head, out_half, d_h_half, full_mid, part_ao, part_bgu, part_ad = middle(
        attn_head, x, g_half, gains, w_out, w_gu, w_down, a_out, b_out, a_gu, b_gu, a_down, b_down, col_count, row_count
    )
    d_qkv_head = attend_back(
        qkv_head, d_attn_head, parent_at, branch_flag, pos_down, pos_across, lse
    )
    d_raw, layer_out = from_heads_call(
        d_qkv_head, raw, factors, gq, gk, cos2, sin2, out_half, col_count, row_count
    )
    d_q, d_k, d_v = (d_raw[:, width_col * j : width_col * (j + 1)] for j in range(3))
    back_qkv = jnp.concatenate(
        [dot_t(d, b) for d, b in zip((d_q, d_k, d_v), (b_qkv[0], b_qkv[1], b_qkv[2]))], axis=1
    ).astype(low)
    d_h_all = jnp.concatenate([jnp.where(first, d_h_half, 0.0), jnp.where(final, d_h_half, 0.0)], axis=0)
    part_in = (dot_t(d_raw, w_qkv) + dot(back_qkv, a_qkv) + d_h_all).astype(low)

    rank_own = RANK // col_count
    full = jnp.concatenate(
        [t_dot(back_qkv, x), full_mid], axis=0
    ).astype(low)
    full = full.reshape(7, col_count, rank_own, D).transpose(1, 0, 2, 3).reshape(col_count, 7 * rank_own, D)
    full = jnp.pad(full, ((0, 0), (0, rank_own), (0, 0))).reshape(col_count * 8 * rank_own, D)
    cols = jnp.concatenate(
        [t_dot(red_qkv[:, RANK * j : RANK * (j + 1)], d) for j, d in enumerate((d_q, d_k, d_v))]
        + [part_ao, part_bgu[0], part_bgu[1], part_ad],
        axis=1,
    ).astype(low)
    cols = cols.reshape(RANK * 16, width_row)
    hot = (tree_set == lax.broadcasted_iota(jnp.int32, (set_count, width_row), 0)).astype(wide)
    sets_own = set_count // dp_count
    input_grad, sets = finish(part_in, full, cols, hot, sets_own, col_count, row_count, dp_count)
    full_sets = sets[:, : 7 * rank_own].reshape(sets_own, 7, rank_own, width_row)
    col_sets = sets[:, 8 * rank_own :].reshape(sets_own, RANK // row_count, 16 * width_row)
    grad_a_qkv = full_sets[:, :3].transpose(1, 0, 2, 3)
    grad_a_gu = full_sets[:, 3:5].transpose(1, 0, 2, 3)
    grad_b_out = full_sets[:, 5]
    grad_b_down = full_sets[:, 6]
    grad_b_qkv = jnp.stack([col_sets[..., width_col * j : width_col * (j + 1)] for j in range(3)])
    grad_a_out = col_sets[..., 3 * width_col : 4 * width_col]
    gu_at = 4 * width_col
    grad_b_gu = jnp.stack([col_sets[..., gu_at + hidden_col * j : gu_at + hidden_col * (j + 1)] for j in range(2)])
    grad_a_down = col_sets[..., gu_at + 2 * hidden_col :]
    return (
        layer_out,
        input_grad,
        grad_a_qkv,
        grad_b_qkv,
        grad_a_out,
        grad_b_out,
        grad_a_gu,
        grad_b_gu,
        grad_a_down,
        grad_b_down,
    )


def solution(mesh):
    in_specs = (
        P(("dp", "col"), "row"),
        P(("dp", "col"), "row"),
        P("dp"),
        P("dp"),
        P("dp", None),
        P("dp"),
        P("col"),
        P("col"),
        P("row"),
        P("row"),
        P("row", None, "col"),
        P("col", "row"),
        P("row", None, "col"),
        P("col", "row"),
        P(None, None, None, "row"),
        P(None, None, None, "col"),
        P(None, None, "col"),
        P(None, None, "row"),
        P(None, None, None, "row"),
        P(None, None, None, "col"),
        P(None, None, "col"),
        P(None, None, "row"),
    )
    out_specs = (
        P(("dp", "col"), "row"),
        P(("dp", "col"), "row"),
        P(None, "dp", "col", "row"),
        P(None, "dp", "row", "col"),
        P("dp", "row", "col"),
        P("dp", "col", "row"),
        P(None, "dp", "col", "row"),
        P(None, "dp", "row", "col"),
        P("dp", "row", "col"),
        P("dp", "col", "row"),
    )
    return jax.shard_map(
        per_device, mesh=mesh, in_specs=in_specs, out_specs=out_specs, check_vma=False
    )
```

```python
import functools

import jax
import jax.numpy as jnp
from jax import lax
from jax.experimental import pallas as pl
from jax.experimental.pallas import tpu as pltpu
from jax.sharding import PartitionSpec as P

D = 2048
HEAD = 128
RANK = 16
SEG = 128
TRUNK = 1024
QT = 256
MESH = pl.DeviceIdType.MESH
VM = pl.BlockSpec(memory_space=pltpu.VMEM)
precise = lax.Precision.HIGHEST

epsilon = 1e-06
rope_base = 500000.0
masked_out = -1e30
low = jnp.bfloat16
wide = jnp.float32
last_last = (((1,), (1,)), ((), ()))
first_first = (((0,), (0,)), ((), ()))


def dot(left, right):
    return jnp.dot(left, right, preferred_element_type=wide)


def dot_t(left, right):
    return lax.dot_general(left, right, last_last, preferred_element_type=wide)


def t_dot(left, right):
    return lax.dot_general(left, right, first_first, preferred_element_type=wide)


def angles(positions):
    half_width = HEAD // 2
    frequency = rope_base ** (-(jnp.arange(half_width, dtype=wide) * 2.0) / HEAD)
    angle_table = positions.astype(wide)[:, None] * frequency[None, :]
    return (jnp.cos(angle_table), jnp.sin(angle_table))


def norm_factor(square_sum):
    return lax.rsqrt(square_sum * (1.0 / D) + epsilon)


def tree_tables(seg_ids, parents):
    tail_seg = seg_ids[TRUNK::SEG]
    labels = jnp.arange(parents.shape[1], dtype=jnp.int32)
    tail_parent = jnp.sum(jnp.where(tail_seg[:, None] == labels[None, :], parents[0][None, :], 0), axis=1)
    hit = (tail_seg[None, :] == tail_parent[:, None])
    at = jnp.arange(tail_seg.shape[0], dtype=jnp.int32) + TRUNK // SEG
    parent_at = jnp.sum(jnp.where(hit, at[None, :], 0), axis=1)
    bias = jnp.where(tail_parent > 0, 0.0, masked_out).astype(wide)
    return parent_at, jnp.broadcast_to(bias[:, None], (tail_seg.shape[0], SEG))


def row_sum(v): return jnp.sum(v, axis=1, keepdims=True)

def params(collective):
    return pltpu.CompilerParams(collective_id=collective, has_side_effects=True, vmem_limit_bytes=60 << 20)


def span(at, size):
    return pl.ds(pl.multiple_of(at, size), size)


def remote(src, dst, send_sem, recv_sem, to):
    return pltpu.make_async_remote_copy(
        src_ref=src, dst_ref=dst, send_sem=send_sem, recv_sem=recv_sem, device_id=to, device_id_type=MESH
    )


def greet(n, nr, extra=0):
    r, c = lax.axis_index("row"), lax.axis_index("col")
    me = r * n + c
    barrier = pltpu.get_barrier_semaphore()

    @pl.loop(1, n * nr)
    def _(d):
        peer = lax.rem(me + d, n * nr)
        pl.semaphore_signal(barrier, inc=1, device_id={"row": peer // n, "col": lax.rem(peer, n)}, device_id_type=MESH)

    pl.semaphore_wait(barrier, n * nr - 1 + extra)


def row_sums(first, second):
    ones = jnp.ones((8, first.shape[1]), wide)
    at = lax.broadcasted_iota(jnp.int32, (8, first.shape[0]), 0)
    sum_first = lax.dot_general(ones, first, last_last, preferred_element_type=wide, precision=precise)
    sum_second = lax.dot_general(ones, second, last_last, preferred_element_type=wide, precision=precise)
    return jnp.where(at < 4, sum_first, sum_second)


def down_columns(values, at):
    pick = (lax.broadcasted_iota(jnp.int32, (8, HEAD), 0) == at).astype(wide)
    return lax.dot_general(values, pick, first_first, preferred_element_type=wide, precision=precise)


def swap_stats(stats, n, send_sem, recv_sem):
    c = lax.axis_index("col")

    def copy(d):
        peer = lax.rem(c + d, n)
        return remote(stats.at[c], stats.at[c], send_sem.at[d - 1], recv_sem.at[d - 1], {"col": peer})

    for d in range(1, n):
        copy(d).start()
    for d in range(1, n):
        copy(d).wait()


def unheads_kernel(n, nr, d_ref, raw_ref, factor_ref, gq_ref, gk_ref, cos_ref, sin_ref, res_ref, out_ref, res_out,
                   stats, buf, nq, nk, pq, pk, fq, fk, send_s, recv_s, send_h, recv_h, send_o, recv_o, local_sem, local_o):
    r, c = lax.axis_index("row"), lax.axis_index("col")
    rows_all = raw_ref.shape[0]
    own = rows_all // n
    width = gq_ref.shape[1]
    heads = width // HEAD
    tree_part = own * nr
    middle = n // 2
    out_width = res_out.shape[1]

    def piece(d, b):
        peer = lax.rem(r + d, nr)
        return remote(
            d_ref.at[span(b * tree_part + peer * own, own)],
            buf.at[r, span(b * own, own)],
            send_h.at[d - 1, b], recv_h.at[d - 1, b], {"row": peer},
        )

    def local(b):
        return pltpu.make_async_copy(
            d_ref.at[span(b * tree_part + r * own, own)], buf.at[r, span(b * own, own)], local_sem.at[b]
        )

    is_owner = jnp.logical_or(c == 0, c == n - 1)
    base = jnp.where(c == 0, 0, middle)

    def result_piece(b, d):
        peer = lax.rem(r + d, nr)
        return remote(
            res_ref.at[span(b * own, own), span(peer * out_width, out_width)],
            res_out.at[span(r * own, own)],
            send_o.at[b, d], recv_o.at[d], {"row": peer, "col": base + b},
        )

    def result_local(b):
        return pltpu.make_async_copy(
            res_ref.at[span(b * own, own), span(r * out_width, out_width)], res_out.at[span(r * own, own)], local_o
        )

    for b in range(n):
        local(b).start()
    greet(n, nr)
    for b in range(n):
        for d in range(1, nr):
            piece(d, b).start()

    @pl.when(is_owner)
    def _():
        for b in range(middle):
            for d in range(nr):
                if d == 0:
                    @pl.when(base + b == c)
                    def _():
                        result_local(b).start()

                    @pl.when(base + b != c)
                    def _():
                        result_piece(b, d).start()
                else:
                    result_piece(b, d).start()

    fq[...] = down_columns(factor_ref[...], 0)
    fk[...] = down_columns(factor_ref[...], 4)
    for b in range(n):
        for d in range(1, nr):
            piece(d, b).wait_recv()
        local(b).wait()
        rows = slice(b * own, (b + 1) * own)
        cosine = cos_ref[rows, :]
        sine = sin_ref[rows, :]
        for h in range(heads):
            lanes = slice(h * HEAD, (h + 1) * HEAD)
            u = buf[h, rows, :HEAD].astype(wide)
            u = (u * cosine - pltpu.roll(u, HEAD // 2, 1) * sine) * gq_ref[:, lanes]
            nq[rows, lanes] = u
            pq[rows, lanes] = u * raw_ref[rows, lanes] * fq[rows, :]
            u = buf[h, rows, HEAD:2 * HEAD].astype(wide)
            u = (u * cosine - pltpu.roll(u, HEAD // 2, 1) * sine) * gk_ref[:, lanes]
            nk[rows, lanes] = u
            pk[rows, lanes] = u * raw_ref[rows, slice(width + h * HEAD, width + (h + 1) * HEAD)] * fk[rows, :]
            out_ref[rows, slice(2 * width + h * HEAD, 2 * width + (h + 1) * HEAD)] = buf[h, rows, 2 * HEAD:]
    stats[c] = row_sums(pq[...], pk[...])
    swap_stats(stats, n, send_s, recv_s)
    total = stats[0]
    for s in range(1, n):
        total = total + stats[s]
    mean = total * (1.0 / D) * factor_ref[...]
    pq[:, :HEAD] = down_columns(mean, 0)
    pk[:, :HEAD] = down_columns(mean, 4)
    for b in range(n):
        rows = slice(b * own, (b + 1) * own)
        for h in range(heads):
            lanes = slice(h * HEAD, (h + 1) * HEAD)
            k_lanes = slice(width + h * HEAD, width + (h + 1) * HEAD)
            out_ref[rows, lanes] = (fq[rows, :] * (nq[rows, lanes] - raw_ref[rows, lanes] * pq[rows, :HEAD])).astype(low)
            out_ref[rows, k_lanes] = (fk[rows, :] * (nk[rows, lanes] - raw_ref[rows, k_lanes] * pk[rows, :HEAD])).astype(low)
    for b in range(n):
        for d in range(1, nr):
            piece(d, b).wait_send()

    @pl.when(is_owner)
    def _():
        for b in range(middle):
            for d in range(nr):
                if d == 0:
                    @pl.when(base + b == c)
                    def _():
                        result_local(b).wait()

                    @pl.when(base + b != c)
                    def _():
                        result_piece(b, d).wait_send()
                else:
                    result_piece(b, d).wait_send()

    for d in range(nr):
        def take():
            remote(
                res_ref.at[span(0, own), span(0, out_width)], res_out.at[span(r * own, own)],
                send_o.at[0, d], recv_o.at[d], {"row": r, "col": c},
            ).wait_recv()
        if d == 0:
            pl.when(jnp.logical_not(is_owner))(take)
        else:
            take()


def from_heads_call(d_head, raw, factor, gain_q, gain_k, cos2, sin2, result, n, nr):
    rows_all, wide3 = raw.shape
    width = wide3 // 3
    dma = pltpu.SemaphoreType.DMA
    square = pltpu.VMEM((rows_all, width), wide)
    return pl.pallas_call(
        functools.partial(unheads_kernel, n, nr),
        out_shape=[
            jax.ShapeDtypeStruct((rows_all, wide3), low),
            jax.ShapeDtypeStruct((rows_all // n * nr, result.shape[1] // nr), low),
        ],
        in_specs=[VM] * 8,
        out_specs=[VM] * 2,
        scratch_shapes=[
            pltpu.VMEM((n, 8, rows_all), wide),
            pltpu.VMEM((nr, rows_all, 3 * HEAD), low),
            square, square, square, square,
            pltpu.VMEM((rows_all, HEAD), wide),
            pltpu.VMEM((rows_all, HEAD), wide),
            dma((n - 1,)), dma((n - 1,)), dma((nr - 1, n)), dma((nr - 1, n)),
            dma((n // 2, nr)), dma((nr,)), dma((n,)), dma,
        ],
        compiler_params=params(5),
        name="from_heads",
    )(d_head, raw, factor, gain_q, gain_k, cos2, sin2, result)


def finish_kernel(n, nr, ndp, m, part_ref, full_ref, col_ref, hot_ref, grad_ref, sets_ref,
                  recv_right, recv_left, send_right, send_left, own_buf, in_buf, full_recv, full_sum, full_last,
                  col_recv, owned, hot_all,
                  send_z, recv_z, send_w, recv_w, local_w, send_f, recv_f, send_c, recv_c, send_l, recv_l,
                  send_d, recv_d, send_k, recv_k):
    g, r, c = lax.axis_index("dp"), lax.axis_index("row"), lax.axis_index("col")
    own = part_ref.shape[0] // n
    width = in_buf.shape[1]
    chunks = own // m
    left = {"col": jnp.maximum(c - 1, 0)}
    right = {"col": jnp.minimum(c + 1, n - 1)}
    full_rows = full_last.shape[1]
    col_rows = col_recv.shape[1]

    def full_piece(d):
        peer = lax.rem(r + d, nr)
        return remote(full_ref.at[:, span(peer * width, width)], full_recv.at[r], send_f.at[d - 1], recv_f.at[d - 1], {"row": peer})

    def col_piece(d):
        peer = lax.rem(r + d, nr)
        return remote(col_ref.at[span(peer * col_rows, col_rows)], col_recv.at[r], send_c.at[d - 1], recv_c.at[d - 1], {"row": peer})

    def last_piece(d):
        peer = lax.rem(c + d, n)
        return remote(full_sum.at[span(peer * full_rows, full_rows)], full_last.at[c], send_l.at[d - 1], recv_l.at[d - 1], {"col": peer})

    def tree_piece(d):
        peer = lax.rem(g + d, ndp)
        return remote(owned.at[g], owned.at[g], send_d.at[d - 1], recv_d.at[d - 1], {"dp": peer})

    def hot_piece(d):
        peer = lax.rem(g + d, ndp)
        return remote(hot_all.at[g], hot_all.at[g], send_k.at[d - 1], recv_k.at[d - 1], {"dp": peer})

    def reduce(kind, b, j, src):
        rows = span(b * own + j * m, m)
        dst, to = ((recv_right, right), (recv_left, left))[kind]
        return remote(src.at[rows], dst.at[rows], send_z.at[kind, b, j], recv_z.at[kind, b, j], to)

    def width_piece(d, j):
        peer = lax.rem(r + d, nr)
        return remote(
            own_buf.at[span(j * m, m), span(peer * width, width)], in_buf.at[span(r * own + j * m, m)],
            send_w.at[d - 1, j], recv_w.at[d - 1, j], {"row": peer},
        )

    def width_local(j):
        return pltpu.make_async_copy(
            own_buf.at[span(j * m, m), span(r * width, width)], in_buf.at[span(r * own + j * m, m)], local_w.at[j]
        )

    me = r * n + c
    barrier = pltpu.get_barrier_semaphore()
    for d in range(1, ndp):
        pl.semaphore_signal(barrier, inc=1, device_id={"dp": lax.rem(g + d, ndp)}, device_id_type=MESH)

    @pl.loop(1, n * nr)
    def _(d):
        peer = lax.rem(me + d, n * nr)
        pl.semaphore_signal(barrier, inc=1, device_id={"row": peer // n, "col": lax.rem(peer, n)}, device_id_type=MESH)

    pl.semaphore_wait(barrier, n * nr - 1 + ndp - 1)
    hot_all[g] = hot_ref[...]
    for d in range(1, nr):
        full_piece(d).start()
        col_piece(d).start()

    def stage(s):
        @pl.loop(0, chunks)
        def _(j):
            for kind, b, go, edge, acc, got in (
                (0, n - 1 - s, n - 1 - s > c, c == 0, send_right, recv_right),
                (1, s, s < c, c == n - 1, send_left, recv_left),
            ):
                @pl.when(go)
                def _():
                    @pl.when(edge)
                    def _():
                        reduce(kind, b, j, part_ref).start()

                    @pl.when(jnp.logical_not(edge))
                    def _():
                        rows = span(b * own + j * m, m)
                        reduce(kind, b, j, acc).wait_recv()
                        acc[rows, :] = (part_ref[rows, :].astype(wide) + got[rows, :].astype(wide)).astype(low)
                        reduce(kind, b, j, acc).start()

    stage(0)
    for d in range(1, nr):
        full_piece(d).wait_recv()
        col_piece(d).wait_recv()
    total = full_ref[:, span(r * width, width)].astype(wide)
    col_total = col_ref[span(r * col_rows, col_rows), :].astype(wide)
    for d in range(1, nr):
        peer = lax.rem(r + d, nr)
        total = total + full_recv[peer].astype(wide)
        col_total = col_total + col_recv[peer].astype(wide)
    full_sum[...] = total.astype(low)
    owned[g, full_rows:, :] = col_total.astype(low)
    for d in range(1, n):
        last_piece(d).start()
    stage(1)
    for d in range(1, n):
        last_piece(d).wait_recv()
    last = full_sum[span(c * full_rows, full_rows), :].astype(wide)
    for d in range(1, n):
        last = last + full_last[lax.rem(c + d, n)].astype(wide)
    owned[g, :full_rows, :] = last.astype(low)
    for d in range(1, ndp):
        tree_piece(d).start()
        hot_piece(d).start()
    for s in range(2, n - 1):
        stage(s)

    rows_own = c * own

    @pl.loop(0, chunks)
    def _(j):
        rows = span(rows_own + j * m, m)
        at = span(j * m, m)

        @pl.when(c == 0)
        def _():
            reduce(1, c, j, send_left).wait_recv()
            own_buf[at, :] = (part_ref[rows, :].astype(wide) + recv_left[rows, :].astype(wide)).astype(low)

        @pl.when(c == n - 1)
        def _():
            reduce(0, c, j, send_right).wait_recv()
            own_buf[at, :] = (part_ref[rows, :].astype(wide) + recv_right[rows, :].astype(wide)).astype(low)

        @pl.when(jnp.logical_and(c > 0, c < n - 1))
        def _():
            reduce(0, c, j, send_right).wait_recv()
            reduce(1, c, j, send_left).wait_recv()
            own_buf[at, :] = (
                part_ref[rows, :].astype(wide) + recv_right[rows, :].astype(wide) + recv_left[rows, :].astype(wide)
            ).astype(low)

        for d in range(1, nr):
            width_piece(d, j).start()
        width_local(j).start()

    for d in range(1, ndp):
        tree_piece(d).wait_recv()
        hot_piece(d).wait_recv()
    sets_own = sets_ref.shape[0]
    for s in range(sets_own):
        total = owned[0].astype(wide) * hot_all[0, pl.ds(g * sets_own + s, 1), :]
        for t in range(1, ndp):
            total = total + owned[t].astype(wide) * hot_all[t, pl.ds(g * sets_own + s, 1), :]
        sets_ref[s] = total

    @pl.loop(0, chunks)
    def _(j):
        for d in range(1, nr):
            width_piece(d, j).wait()
        width_local(j).wait()

    grad_ref[...] = in_buf[...].astype(wide)
    for d in range(1, nr):
        full_piece(d).wait_send()
        col_piece(d).wait_send()
    for d in range(1, n):
        last_piece(d).wait_send()
    for d in range(1, ndp):
        tree_piece(d).wait_send()
        hot_piece(d).wait_send()
    for s in range(n - 1):
        @pl.loop(0, chunks)
        def _(j):
            @pl.when(n - 1 - s > c)
            def _():
                reduce(0, n - 1 - s, j, send_right).wait_send()

            @pl.when(s < c)
            def _():
                reduce(1, s, j, send_left).wait_send()


def finish(part, full, cols, hot, sets_own, n, nr, ndp, m=32):
    rows_all, width_all = part.shape
    own = rows_all // n
    width = width_all // nr
    chunks = own // m
    full_rows = full.shape[0] // n
    col_rows = cols.shape[0] // nr
    dma = pltpu.SemaphoreType.DMA
    big = pltpu.VMEM((rows_all, width_all), low)
    return pl.pallas_call(
        functools.partial(finish_kernel, n, nr, ndp, m),
        out_shape=[
            jax.ShapeDtypeStruct((own * nr, width), wide),
            jax.ShapeDtypeStruct((sets_own, full_rows + col_rows, width), wide),
        ],
        in_specs=[VM] * 4,
        out_specs=[VM] * 2,
        scratch_shapes=[
            big, big, big, big,
            pltpu.VMEM((own, width_all), low),
            pltpu.VMEM((own * nr, width), low),
            pltpu.VMEM((nr, full.shape[0], width), low),
            pltpu.VMEM((full.shape[0], width), low),
            pltpu.VMEM((n, full_rows, width), low),
            pltpu.VMEM((nr, col_rows, width), low),
            pltpu.VMEM((ndp, full_rows + col_rows, width), low),
            pltpu.VMEM((ndp,) + hot.shape, wide),
            dma((2, n, chunks)), dma((2, n, chunks)), dma((nr - 1, chunks)), dma((nr - 1, chunks)), dma((chunks,)),
            dma((nr - 1,)), dma((nr - 1,)), dma((nr - 1,)), dma((nr - 1,)), dma((n - 1,)), dma((n - 1,)),
            dma((ndp - 1,)), dma((ndp - 1,)), dma((ndp - 1,)), dma((ndp - 1,)),
        ],
        compiler_params=params(6),
        name="finish",
    )(part, full, cols, hot)


def flip(v):
    return v + 1 - 2 * lax.rem(v, 2)


class Share:
    def __init__(self, src, dst, cuts, sems):
        self.send, self.recv, self.local = sems
        self.src, self.cuts = src, cuts
        g, r = lax.axis_index("dp"), lax.axis_index("row")
        size = src.shape[0]
        half = size // 2
        step = half // cuts
        far = lax.rem(r + 2, 4)
        mine = lax.rem(g, 2)
        near_to, far_to, twin_to = {"row": flip(r)}, {"row": far}, {"dp": flip(g)}

        def rows(shard, part, i):
            return pl.ds(pl.multiple_of(shard * size + part * half + i * step, step), step)

        def copy(kind, i, src, dst, to):
            return remote(src, dst, self.send.at[kind, i], self.recv.at[kind, i], to)

        def hand(kind, part, to):
            return lambda i: copy(kind, i, dst.at[rows(far, part, i)], dst.at[rows(far, part, i)], to)

        whole = span(r * size, size)
        self.own = pltpu.make_async_copy(src, dst.at[whole], self.local)
        self.near = copy(0, 0, src, dst.at[whole], near_to)
        self.far = lambda i: copy(
            1, i, src.at[pl.ds(pl.multiple_of(mine * half + i * step, step), step)], dst.at[rows(r, mine, i)], far_to
        )
        self.far_near = hand(2, mine, near_to)
        self.far_twin = hand(3, mine, twin_to)
        self.twin_near = hand(4, 1 - mine, near_to)

    def start_far(self):
        for i in range(self.cuts):
            self.far(i).start()

    def start_near(self):
        self.own.start()
        self.near.start()

    def pass_far(self, i):
        self.far(i).wait_recv()
        self.far_twin(i).start()
        self.far_near(i).start()

    def pass_twin(self, i):
        self.far_twin(i).wait_recv()
        self.twin_near(i).start()

    def wait_all(self):
        self.own.wait()
        self.near.wait_recv()
        for i in range(self.cuts):
            self.far_near(i).wait_recv()
            self.twin_near(i).wait_recv()

    def drain(self):
        self.near.wait_send()
        for i in range(self.cuts):
            self.far(i).wait_send()
            self.far_near(i).wait_send()
            self.far_twin(i).wait_send()
            self.twin_near(i).wait_send()


def share_sems(cuts):
    dma = pltpu.SemaphoreType.DMA
    return [dma((5, cuts)), dma((5, cuts)), dma]


def prep_kernel(set_ref, fq_ref, sq_ref, fo_ref, so_ref, fg_ref, sg_ref, fd_ref, sd_ref,
                narrow_ref, bq_ref, ao_ref, bg_ref, ad_ref):
    for j in range(3):
        narrow_ref[j * RANK:(j + 1) * RANK, :] = fq_ref[j, 0].astype(low)
        bq_ref[j * RANK:(j + 1) * RANK, :] = sq_ref[j, 0].astype(low)
    for j in range(2):
        narrow_ref[(3 + j) * RANK:(4 + j) * RANK, :] = fg_ref[j, 0].astype(low)
        bg_ref[j] = sg_ref[j, 0].astype(low)
    narrow_ref[5 * RANK:6 * RANK, :] = so_ref[0].astype(low)
    narrow_ref[6 * RANK:, :] = sd_ref[0].astype(low)
    ao_ref[...] = fo_ref[0].astype(low)
    ad_ref[...] = fd_ref[0].astype(low)


def prep(tree_sets, tables):
    fq, sq, fo, so, fg, sg, fd, sd = tables

    def pick(table):
        if table.ndim == 4:
            return pl.BlockSpec((table.shape[0], 1) + table.shape[2:], lambda i, s: (0, s[0], 0, 0))
        return pl.BlockSpec((1,) + table.shape[1:], lambda i, s: (s[0], 0, 0))

    def out(*shape):
        return pl.BlockSpec(shape, lambda i, s: (0,) * len(shape)), jax.ShapeDtypeStruct(shape, low)

    outs = [
        out(7 * RANK, fq.shape[-1]), out(3 * RANK, sq.shape[-1]), out(RANK, fo.shape[-1]),
        out(2, RANK, sg.shape[-1]), out(RANK, fd.shape[-1]),
    ]
    return pl.pallas_call(
        prep_kernel,
        grid_spec=pltpu.PrefetchScalarGridSpec(
            num_scalar_prefetch=1, grid=(1,), in_specs=[pick(t) for t in tables], out_specs=[o[0] for o in outs]
        ),
        out_shape=[o[1] for o in outs],
        name="prep",
    )(tree_sets, *tables)


def lower_mask(size):
    return lax.broadcasted_iota(jnp.int32, (size, size), 1) <= lax.broadcasted_iota(jnp.int32, (size, size), 0)


def softmax_parts(parts):
    top = jnp.max(parts[0], axis=1, keepdims=True)
    for s in parts[1:]:
        top = jnp.maximum(top, jnp.max(s, axis=1, keepdims=True))
    raised = [jnp.exp(s - top) for s in parts]
    total = jnp.sum(raised[0], axis=1, keepdims=True)
    for e in raised[1:]:
        total = total + jnp.sum(e, axis=1, keepdims=True)
    inverse = 1.0 / total
    return [e * inverse for e in raised], top + jnp.log(total)


def tail_parts(q, qkv, at, parent, flag):
    scale = HEAD ** -0.5
    k_lanes = slice(HEAD, 2 * HEAD)
    trunk = dot_t(q, qkv[:TRUNK, k_lanes]) * scale
    branch = dot_t(q, qkv[pl.ds(parent, SEG), k_lanes]) * scale + flag
    own = jnp.where(lower_mask(SEG), dot_t(q, qkv[pl.ds(at, SEG), k_lanes]) * scale, masked_out)
    return [trunk, branch, own]


def trunk_parts(q, qkv, i):
    scale = HEAD ** -0.5
    k_lanes = slice(HEAD, 2 * HEAD)
    own = dot_t(q, qkv[i * QT:(i + 1) * QT, k_lanes]) * scale
    parts = [jnp.where(lower_mask(QT), own, masked_out)]
    if i:
        parts.append(dot_t(q, qkv[:i * QT, k_lanes]) * scale)
    return parts


def attend_body(parent_ref, flag_ref, qkv, o_ref, lse_ref):
    v_lanes = slice(2 * HEAD, 3 * HEAD)
    for i in range(TRUNK // QT):
        at = slice(i * QT, (i + 1) * QT)
        p, lse = softmax_parts(trunk_parts(qkv[at, :HEAD], qkv, i))
        o = dot(p[0].astype(low), qkv[at, v_lanes])
        if i:
            o = o + dot(p[1].astype(low), qkv[:i * QT, v_lanes])
        o_ref[at, :] = o.astype(low)
        lse_ref[at, :] = lse

    @pl.loop(0, (qkv.shape[0] - TRUNK) // SEG)
    def _(j):
        at = pl.multiple_of(TRUNK + j * SEG, SEG)
        parent = pl.multiple_of(parent_ref[j] * SEG, SEG)
        rows = pl.ds(at, SEG)
        p, lse = softmax_parts(tail_parts(qkv[rows, :HEAD], qkv, at, parent, flag_ref[pl.ds(j, 1), :]))
        o = dot(p[0].astype(low), qkv[:TRUNK, v_lanes])
        o = o + dot(p[1].astype(low), qkv[pl.ds(parent, SEG), v_lanes])
        o = o + dot(p[2].astype(low), qkv[rows, v_lanes])
        o_ref[rows, :] = o.astype(low)
        lse_ref[rows, :] = lse


def back_parts(scores, lse, d_out, keys, values):
    probs = [jnp.exp(s - lse) for s in scores]
    grads = [dot_t(d_out, v) for v in values]
    inner = sum(jnp.sum(p * g, axis=1, keepdims=True) for p, g in zip(probs, grads))
    d_scores = [(p * (g - inner)).astype(low) for p, g in zip(probs, grads)]
    dq = sum(dot(d, k) for d, k in zip(d_scores, keys))
    return d_scores, [p.astype(low) for p in probs], dq


def attend_back_kernel(parent_ref, flag_ref, qkv, do_ref, lse_ref, d_ref, dk_acc, dv_acc):
    scale = HEAD ** -0.5
    k_lanes = slice(HEAD, 2 * HEAD)
    v_lanes = slice(2 * HEAD, 3 * HEAD)
    dk_acc[...] = jnp.zeros_like(dk_acc)
    dv_acc[...] = jnp.zeros_like(dv_acc)
    for i in range(TRUNK // QT):
        at = slice(i * QT, (i + 1) * QT)
        spans = [at] + ([slice(0, i * QT)] if i else [])
        q, d_out = qkv[at, :HEAD], do_ref[at, :]
        d_scores, probs, dq = back_parts(
            trunk_parts(q, qkv, i), lse_ref[at, :], d_out, [qkv[s, k_lanes] for s in spans], [qkv[s, v_lanes] for s in spans]
        )
        d_ref[at, :HEAD] = (dq * scale).astype(low)
        for s, d, p in zip(spans, d_scores, probs):
            dk_acc[s, :] += t_dot(d, q)
            dv_acc[s, :] += t_dot(p, d_out)

    @pl.loop(0, (qkv.shape[0] - TRUNK) // SEG)
    def _(j):
        at = pl.multiple_of(TRUNK + j * SEG, SEG)
        parent = pl.multiple_of(parent_ref[j] * SEG, SEG)
        rows = pl.ds(at, SEG)
        spans = [slice(0, TRUNK), pl.ds(parent, SEG), rows]
        q, d_out = qkv[rows, :HEAD], do_ref[rows, :]
        d_scores, probs, dq = back_parts(
            tail_parts(q, qkv, at, parent, flag_ref[pl.ds(j, 1), :]), lse_ref[rows, :], d_out,
            [qkv[s, k_lanes] for s in spans], [qkv[s, v_lanes] for s in spans],
        )
        d_ref[rows, :HEAD] = (dq * scale).astype(low)
        for s, d, p in zip(spans, d_scores, probs):
            dk_acc[s, :] += t_dot(d, q)
            dv_acc[s, :] += t_dot(p, d_out)

    d_ref[:, k_lanes] = (dk_acc[...] * scale).astype(low)
    d_ref[:, v_lanes] = dv_acc[...].astype(low)


def attend(qkv, parent_at, flag):
    n = qkv.shape[0]

    def whole(*shape):
        return pl.BlockSpec(shape, lambda i, *_: (0, 0))

    return pl.pallas_call(
        attend_body,
        grid_spec=pltpu.PrefetchScalarGridSpec(
            num_scalar_prefetch=1,
            grid=(1,),
            in_specs=[whole(*flag.shape), whole(n, 3 * HEAD)],
            out_specs=[whole(n, HEAD), whole(n, 1)],
        ),
        out_shape=[jax.ShapeDtypeStruct((n, HEAD), low), jax.ShapeDtypeStruct((n, 1), wide)],
        name="attend",
    )(parent_at, flag, qkv)


def attend_back(qkv, d_o, parent_at, flag, lse):
    n = qkv.shape[0]

    def whole(*shape):
        return pl.BlockSpec(shape, lambda i, *_: (0, 0))

    return pl.pallas_call(
        attend_back_kernel,
        grid_spec=pltpu.PrefetchScalarGridSpec(
            num_scalar_prefetch=1,
            grid=(1,),
            in_specs=[whole(*flag.shape), whole(n, 3 * HEAD), whole(n, HEAD), whole(n, 1)],
            out_specs=whole(n, 3 * HEAD),
            scratch_shapes=[pltpu.VMEM((n, HEAD), wide), pltpu.VMEM((n, HEAD), wide)],
        ),
        out_shape=jax.ShapeDtypeStruct((n, 3 * HEAD), low),
        name="attend_back",
    )(parent_at, flag, qkv, d_o, lse)


def front_kernel(n, nr, m, mh, tok_ref, table_ref, gain_ref, cot_ref, wq_hbm, wo_hbm, bq_ref, gq_ref, gk_ref,
                 cos_ref, sin_ref,
                 x_ref, table_all, gain_all, half_ref, raw_ref, factor_ref, qkv_ref, wq_out, wo_out,
                 wq, wo, stats, buf, fq, fk,
                 send_a, recv_a, send_z, recv_z, send_t, recv_t, local_sem,
                 send_s, recv_s, send_h, recv_h, send_g, recv_g, local_h, local_g,
                 send_q, recv_q, local_q, send_o, recv_o, local_o, out_sems):
    g, r, c = lax.axis_index("dp"), lax.axis_index("row"), lax.axis_index("col")
    own = tok_ref.shape[0] // nr
    width = tok_ref.shape[1]
    rows_all = own * n
    heads = width // HEAD
    tree_part = own * nr
    chunks = own // m
    left = {"col": jnp.maximum(c - 1, 0)}
    right = {"col": jnp.minimum(c + 1, n - 1)}
    share_q = Share(wq_hbm, wq, 2, (send_q, recv_q, local_q))
    share_o = Share(wo_hbm, wo, 2, (send_o, recv_o, local_o))

    def piece(d, j):
        peer = lax.rem(r + d, nr)
        return remote(
            tok_ref.at[span(peer * own + j * m, m)],
            x_ref.at[span(c * own + j * m, m), span(r * width, width)],
            send_a.at[d - 1, j], recv_a.at[d - 1, j], {"row": peer},
        )

    def block(kind, s, at, j, to):
        rows = span(at * own + j * m, m)
        return remote(x_ref.at[rows], x_ref.at[rows], send_z.at[kind, s, j], recv_z.at[kind, s, j], to)

    def table_piece(d, kind):
        src, dst = ((table_ref, table_all), (gain_ref, gain_all))[kind]
        to = {"row": lax.rem(r + d, nr)}
        return remote(src, dst.at[:, span(r * width, width)], send_t.at[kind, d - 1], recv_t.at[kind, d - 1], to)

    keep = pltpu.make_async_copy(
        tok_ref.at[span(r * own, own)], x_ref.at[span(c * own, own), span(r * width, width)], local_sem.at[0]
    )
    keep_table = pltpu.make_async_copy(table_ref, table_all.at[:, span(r * width, width)], local_sem.at[1])
    keep_gain = pltpu.make_async_copy(gain_ref, gain_all.at[:, span(r * width, width)], local_sem.at[2])
    keep.start()
    keep_table.start()
    keep_gain.start()
    barrier = pltpu.get_barrier_semaphore()
    pl.semaphore_signal(barrier, inc=1, device_id={"dp": flip(g)}, device_id_type=MESH)
    greet(n, nr, 1)

    @pl.loop(0, chunks)
    def _(j):
        for d in range(1, nr):
            piece(d, j).start()

    share_q.start_far()
    share_q.start_near()
    for d in range(1, nr):
        table_piece(d, 0).start()
        table_piece(d, 1).start()
    share_o.start_far()
    share_o.start_near()
    keep.wait()

    for s in range(n):
        @pl.loop(0, chunks)
        def _(j):
            if s == 0:
                for d in range(1, nr):
                    piece(d, j).wait_recv()

            @pl.when(c - s >= 0)
            def _():
                if s > 0:
                    block(0, s - 1, jnp.maximum(c - s, 0), j, right).wait_recv()
                if s < n - 1:
                    @pl.when(c < n - 1)
                    def _():
                        block(0, s, jnp.maximum(c - s, 0), j, right).start()

            @pl.when(c + s <= n - 1)
            def _():
                if s > 0:
                    block(1, s - 1, jnp.minimum(c + s, n - 1), j, left).wait_recv()
                if s < n - 1:
                    @pl.when(c > 0)
                    def _():
                        block(1, s, jnp.minimum(c + s, n - 1), j, left).start()

        if s == 1:
            for i in range(2):
                share_q.pass_far(i)
        if s == 2:
            for i in range(2):
                share_o.pass_far(i)
                share_q.pass_twin(i)
    for i in range(2):
        share_o.pass_twin(i)

    for d in range(1, nr):
        table_piece(d, 0).wait_recv()
        table_piece(d, 1).wait_recv()
    keep_table.wait()
    keep_gain.wait()
    share_q.wait_all()
    copy_wq = pltpu.make_async_copy(wq, wq_out, out_sems.at[0])
    copy_wq.start()

    red = dot_t(x_ref[...], table_all[:3 * RANK, :]).astype(low)
    for j in range(3):
        lanes = slice(j * width, (j + 1) * width)
        raw_ref[:, lanes] = dot(x_ref[...], wq[:, lanes]) + dot(
            red[:, j * RANK:(j + 1) * RANK], bq_ref[j * RANK:(j + 1) * RANK, :]
        )
    q_all = raw_ref[:, :width]
    k_all = raw_ref[:, width:2 * width]
    stats[c] = row_sums(q_all * q_all, k_all * k_all)

    middle_at = n // 2
    owner = jnp.where(c < middle_at, 0, n - 1)
    at_owner = jnp.where(c < middle_at, c, c - middle_at)

    def cot_piece(d):
        peer = lax.rem(r + d, nr)
        return remote(
            cot_ref.at[span(peer * own, own)],
            half_ref.at[span(at_owner * own, own), span(r * width, width)],
            send_g.at[d], recv_g.at[at_owner, d], {"row": peer, "col": owner},
        )

    def cot_local():
        return pltpu.make_async_copy(
            cot_ref.at[span(r * own, own)], half_ref.at[span(at_owner * own, own), span(r * width, width)], local_g
        )

    swap_stats(stats, n, send_s, recv_s)
    total = stats[0]
    for s in range(1, n):
        total = total + stats[s]
    factor = lax.rsqrt(total * (1.0 / D) + epsilon)
    factor_ref[...] = factor
    fq[...] = down_columns(factor, 0)
    fk[...] = down_columns(factor, 4)

    def head_rows(i):
        block_at = i // (own // mh)
        inside = lax.rem(i, own // mh)
        return span(block_at * tree_part + r * own + inside * mh, mh)

    def head_piece(d, i):
        peer = lax.rem(r + d, nr)
        return remote(
            buf.at[peer, span(i * mh, mh)], qkv_ref.at[head_rows(i)], send_h.at[d - 1, i], recv_h.at[d - 1, i], {"row": peer}
        )

    def head_local(i):
        return pltpu.make_async_copy(buf.at[r, span(i * mh, mh)], qkv_ref.at[head_rows(i)], local_h.at[i])

    steps = rows_all // mh

    @pl.loop(0, steps)
    def _(i):
        rows = span(i * mh, mh)
        cosine = cos_ref[rows, :]
        sine = sin_ref[rows, :]
        for h in range(heads):
            lanes = slice(h * HEAD, (h + 1) * HEAD)
            u = raw_ref[rows, lanes] * fq[rows, :] * gq_ref[:, lanes]
            buf[h, rows, :HEAD] = (u * cosine + pltpu.roll(u, HEAD // 2, 1) * sine).astype(low)
            k_lanes = slice(width + h * HEAD, width + (h + 1) * HEAD)
            u = raw_ref[rows, k_lanes] * fk[rows, :] * gk_ref[:, lanes]
            buf[h, rows, HEAD:2 * HEAD] = (u * cosine + pltpu.roll(u, HEAD // 2, 1) * sine).astype(low)
            v_lanes = slice(2 * width + h * HEAD, 2 * width + (h + 1) * HEAD)
            buf[h, rows, 2 * HEAD:] = raw_ref[rows, v_lanes].astype(low)
        for d in range(1, nr):
            head_piece(d, i).start()
        head_local(i).start()

    for d in range(1, nr):
        cot_piece(d).start()

    @pl.when(owner == c)
    def _():
        cot_local().start()

    @pl.when(owner != c)
    def _():
        cot_piece(0).start()

    share_o.wait_all()
    copy_wo = pltpu.make_async_copy(wo, wo_out, out_sems.at[1])
    copy_wo.start()

    @pl.loop(0, steps)
    def _(i):
        for d in range(1, nr):
            head_piece(d, i).wait()
        head_local(i).wait()

    for d in range(1, nr):
        cot_piece(d).wait_send()

    @pl.when(owner != c)
    def _():
        cot_piece(0).wait_send()

    @pl.when(owner == c)
    def _():
        cot_local().wait()
        for b in range(middle_at):
            for d in range(nr):
                def take():
                    remote(
                        cot_ref.at[span(0, own)], half_ref.at[span(b * own, own), span(0, width)],
                        send_g.at[d], recv_g.at[b, d], {"row": flip(r)},
                    ).wait_recv()
                if d == 0:
                    pl.when(b != at_owner)(take)
                else:
                    take()

    @pl.loop(0, chunks)
    def _(j):
        for d in range(1, nr):
            piece(d, j).wait_send()
        for s in range(n - 1):
            @pl.when(jnp.logical_and(c - s >= 0, c < n - 1))
            def _():
                block(0, s, jnp.maximum(c - s, 0), j, right).wait_send()

            @pl.when(jnp.logical_and(c + s <= n - 1, c > 0))
            def _():
                block(1, s, jnp.minimum(c + s, n - 1), j, left).wait_send()

    for d in range(1, nr):
        table_piece(d, 0).wait_send()
        table_piece(d, 1).wait_send()
    share_q.drain()
    share_o.drain()
    copy_wq.wait()
    copy_wo.wait()


def front(tokens, table, gain, cot, w_qkv, w_out, b_qkv, gain_q, gain_k, cos2, sin2, n, nr, m=32, mh=80):
    own = tokens.shape[0] // nr
    width = tokens.shape[1]
    rows_all = own * n
    tree = own * n * nr
    chunks = own // m
    steps = rows_all // mh
    dma = pltpu.SemaphoreType.DMA
    shape = jax.ShapeDtypeStruct
    any_space = pl.BlockSpec(memory_space=pl.ANY)
    return pl.pallas_call(
        functools.partial(front_kernel, n, nr, m, mh),
        out_shape=[
            shape((rows_all, width * nr), low),
            shape((table.shape[0], width * nr), low),
            shape((gain.shape[0], width * nr), wide),
            shape((rows_all // 2, width * nr), low),
            shape((rows_all, 3 * width), wide),
            shape((8, rows_all), wide),
            shape((tree, 3 * HEAD), low),
            shape((w_qkv.shape[0] * nr, w_qkv.shape[1]), low),
            shape((w_out.shape[0] * nr, w_out.shape[1]), low),
        ],
        in_specs=[VM, VM, VM, VM, any_space, any_space] + [VM] * 5,
        out_specs=[VM] * 7 + [any_space, any_space],
        scratch_shapes=[
            pltpu.VMEM((w_qkv.shape[0] * nr, w_qkv.shape[1]), low),
            pltpu.VMEM((w_out.shape[0] * nr, w_out.shape[1]), low),
            pltpu.VMEM((n, 8, rows_all), wide),
            pltpu.VMEM((width // HEAD, rows_all, 3 * HEAD), low),
            pltpu.VMEM((rows_all, HEAD), wide),
            pltpu.VMEM((rows_all, HEAD), wide),
            dma((nr - 1, chunks)), dma((nr - 1, chunks)), dma((2, n - 1, chunks)), dma((2, n - 1, chunks)),
            dma((2, nr - 1)), dma((2, nr - 1)), dma((3,)),
            dma((n - 1,)), dma((n - 1,)), dma((nr - 1, steps)), dma((nr - 1, steps)),
            dma((nr,)), dma((n // 2, nr)), dma((steps,)), dma,
        ] + share_sems(2) + share_sems(2) + [dma((2,))],
        compiler_params=params(3),
        name="front",
    )(tokens, table, gain, cot, w_qkv, w_out, b_qkv, gain_q, gain_k, cos2, sin2)


def middle_kernel(n, nr, m, hop, cuts, head_ref, x_hbm, cot_hbm, gain_ref, wo_hbm, wg_hbm, wd_hbm,
                  table_ref, ao_ref, bg_ref, ad_ref,
                  dhead_ref, out_half, grad_half, full_ref, co_ref, cg_ref, cd_ref,
                  wo, wg, wd, x_half, cot_half, raw, attn, d_attn, h_all, df_all, da_all, gu, part,
                  recv_right, recv_left, hid, red_gu, red_down, back_gu, back_down,
                  sems_send, sems_recv, send_in, recv_in, send_out, recv_out, local_in, local_out, load,
                  send_g, recv_g, local_g, send_d, recv_d, local_d):
    g, r, c = lax.axis_index("dp"), lax.axis_index("row"), lax.axis_index("col")
    ag_ref = table_ref.at[3 * RANK:5 * RANK]
    bo_ref = table_ref.at[5 * RANK:6 * RANK]
    bd_ref = table_ref.at[6 * RANK:]
    rows_all, width_all = part.shape
    half = rows_all // 2
    own = rows_all // n
    tree_part = own * nr
    chunks = half // m
    blocks = 4
    band = half // blocks
    hidden = ad_ref.shape[1]
    width = width_all // nr
    left = {"col": jnp.maximum(c - 1, 0)}
    right = {"col": jnp.minimum(c + 1, n - 1)}
    first = c == 0
    last = c == n - 1
    inner = jnp.logical_and(c > 0, c < n - 1)

    base = jnp.where(last, half, 0)
    a_cut = hidden // 4
    share_g = Share(wg_hbm, wg, cuts, (send_g, recv_g, local_g))
    share_d = Share(wd_hbm, wd, cuts // 2, (send_d, recv_d, local_d))
    loads = [pltpu.make_async_copy(wo_hbm, wo, load.at[0])]
    load_x = pltpu.make_async_copy(x_hbm.at[span(base, half)], x_half, load.at[1])
    load_cot = pltpu.make_async_copy(cot_hbm, cot_half, load.at[2])
    loads[0].start()

    def piece_in(d, b):
        peer = lax.rem(r + d, nr)
        return remote(
            head_ref.at[span(b * tree_part + peer * own, own)],
            attn.at[span(b * own, own), span(r * HEAD, HEAD)],
            send_in.at[d - 1, b], recv_in.at[d - 1, b], {"row": peer},
        )

    def local_piece_in(b):
        return pltpu.make_async_copy(
            head_ref.at[span(b * tree_part + r * own, own)],
            attn.at[span(b * own, own), span(r * HEAD, HEAD)], local_in.at[b]
        )

    def piece_out(d, b):
        peer = lax.rem(r + d, nr)
        return remote(
            d_attn.at[span(b * own, own), span(peer * HEAD, HEAD)],
            dhead_ref.at[span(b * tree_part + r * own, own)],
            send_out.at[d - 1, b], recv_out.at[d - 1, b], {"row": peer},
        )

    def local_piece_out(b):
        return pltpu.make_async_copy(
            d_attn.at[span(b * own, own), span(r * HEAD, HEAD)],
            dhead_ref.at[span(b * tree_part + r * own, own)], local_out.at[b]
        )

    for b in range(n):
        local_piece_in(b).start()
    barrier = pltpu.get_barrier_semaphore()
    for d in range(1, nr):
        pl.semaphore_signal(barrier, inc=1, device_id={"row": lax.rem(r + d, nr)}, device_id_type=MESH)

    @pl.when(c > 0)
    def _():
        pl.semaphore_signal(barrier, inc=1, device_id=left, device_id_type=MESH)

    @pl.when(c < n - 1)
    def _():
        pl.semaphore_signal(barrier, inc=1, device_id=right, device_id_type=MESH)

    pl.semaphore_signal(barrier, inc=1, device_id={"dp": flip(g)}, device_id_type=MESH)
    full_ref[...] = jnp.zeros_like(full_ref)
    co_ref[...] = jnp.zeros_like(co_ref)
    cg_ref[...] = jnp.zeros_like(cg_ref)
    cd_ref[...] = jnp.zeros_like(cd_ref)

    @pl.when(inner)
    def _():
        pl.semaphore_wait(barrier, nr + 2)

    @pl.when(jnp.logical_not(inner))
    def _():
        pl.semaphore_wait(barrier, nr + 1)

    middle = n // 2
    for b in range(middle):
        for block in (b, middle + b):
            for d in range(1, nr):
                piece_in(d, block).start()
    load_x.start()
    load_cot.start()
    share_g.start_far()
    share_d.start_far()
    share_g.start_near()
    share_d.start_near()

    def rows(j, start=0):
        return span(start + j * m, m)

    def band_rows(b):
        return span(b * band, band), span(half + b * band, band)

    def take(ref, b):
        low_rows, high_rows = band_rows(b)
        return jnp.concatenate([ref[low_rows, :], ref[high_rows, :]], axis=0)

    def put(b, lanes, value):
        low_rows, high_rows = band_rows(b)
        part[low_rows, lanes] = value[:band].astype(low)
        part[high_rows, lanes] = value[band:].astype(low)

    def relay_stage(stage, per, work, owner_step, all_ref, pump=None):
        def send(kind, j, src, dst, to):
            return remote(src, dst, sems_send.at[stage, kind, j], sems_recv.at[stage, kind, j], to)

        def reduce_right(j):
            return send(0, j, part.at[rows(j, half)], recv_right.at[rows(j)], right)

        def reduce_left(j):
            return send(1, j, part.at[rows(j)], recv_left.at[rows(j)], left)

        def spread_left(j):
            return send(2, j, all_ref.at[rows(j, half)], all_ref.at[rows(j, half)], left)

        def spread_right(j):
            return send(3, j, all_ref.at[rows(j)], all_ref.at[rows(j)], right)

        total_slices = per * blocks
        each = chunks // blocks

        def slices_before(i):
            late = per + (jnp.maximum(i - per, 0) * per) // each
            return jnp.minimum(jnp.where(i < per, i, late), total_slices)

        @pl.loop(0, per + chunks + hop * 2 * (n - 1))
        def _(ii):
            i = ii - per

            def on(offset, who, run):
                j = i - offset

                @pl.when(jnp.logical_and(who, jnp.logical_and(j >= 0, j < chunks)))
                def _():
                    run(j)

            def mid_right(j):
                reduce_right(j).wait_recv()
                at = rows(j, half)
                part[at, :] = (part[at, :].astype(wide) + recv_right[rows(j), :].astype(wide)).astype(low)
                reduce_right(j).start()

            def mid_left(j):
                reduce_left(j).wait_recv()
                at = rows(j)
                part[at, :] = (part[at, :].astype(wide) + recv_left[at, :].astype(wide)).astype(low)
                reduce_left(j).start()

            def end_right(j):
                reduce_right(j).wait_recv()
                total = part[rows(j, half), :].astype(wide) + recv_right[rows(j), :].astype(wide)
                all_ref[rows(j, half), :] = owner_step(total, rows(j))
                spread_left(j).start()

            def end_left(j):
                reduce_left(j).wait_recv()
                total = part[rows(j), :].astype(wide) + recv_left[rows(j), :].astype(wide)
                all_ref[rows(j), :] = owner_step(total, rows(j))
                spread_right(j).start()

            def pass_left(j):
                spread_left(j).wait_recv()
                spread_left(j).start()

            def pass_right(j):
                spread_right(j).wait_recv()
                spread_right(j).start()

            on(0, first, lambda j: reduce_right(j).start())
            on(0, last, lambda j: reduce_left(j).start())
            on(hop * c, inner, mid_right)
            on(hop * (n - 1 - c), inner, mid_left)
            on(hop * (n - 1), last, end_right)
            on(hop * (n - 1), first, end_left)
            on(hop * (2 * (n - 1) - c), inner, pass_left)
            on(hop * (n - 1 + c), inner, pass_right)

            @pl.loop(slices_before(ii), slices_before(ii + 1))
            def _(t):
                work(t // per, lax.rem(t, per))

            if pump is not None:
                pump(ii)

        @pl.loop(0, chunks)
        def _(j):
            @pl.when(first)
            def _():
                reduce_right(j).wait_send()
                spread_right(j).wait_send()
                spread_left(j).wait_recv()

            @pl.when(last)
            def _():
                reduce_left(j).wait_send()
                spread_left(j).wait_send()
                spread_right(j).wait_recv()

            @pl.when(inner)
            def _():
                reduce_right(j).wait_send()
                reduce_left(j).wait_send()
                spread_left(j).wait_send()
                spread_right(j).wait_send()

    def shard(j, ref):
        return slice(j * (ref.shape[0] // nr), (j + 1) * (ref.shape[0] // nr))

    def out_work(b, k):
        @pl.when(b == 0)
        def _():
            loads[0].wait()

        @pl.when(lax.rem(b, blocks // middle) == 0)
        def _():
            at = b // (blocks // middle)
            for block in (at, middle + at):
                for d in range(1, nr):
                    piece_in(d, block).wait_recv()
                local_piece_in(block).wait()

        rows_in = take(attn, b)
        red = dot_t(rows_in, ao_ref[...]).astype(low)
        for j in range(nr):
            lanes = slice(j * width, (j + 1) * width)
            put(b, lanes, dot(rows_in, wo[shard(j, wo), :]) + dot(red, bo_ref[:, lanes]))

    gain_a = gain_ref[0:1, :]
    gain_f = gain_ref[1:2, :]

    def attn_owner(total, at):
        raw[at, :] = total
        flat = total * norm_factor(row_sum(total * total))
        return (x_half[at, :].astype(wide) + flat * gain_a).astype(low)

    first_pass = 5
    apart = 3
    late = 2
    passes = cuts + cuts // 2

    def pump(ii):
        at = ii - first_pass

        @pl.when(jnp.logical_and(at >= 0, lax.rem(at, apart) == 0))
        def _():
            t = at // apart

            @pl.when(t < cuts)
            def _():
                share_g.pass_far(t)

            @pl.when(jnp.logical_and(t >= cuts, t < passes))
            def _():
                share_d.pass_far(t - cuts)

            t = t - late

            @pl.when(jnp.logical_and(t >= 0, t < cuts))
            def _():
                share_g.pass_twin(t)

            @pl.when(jnp.logical_and(t >= cuts, t < passes))
            def _():
                share_d.pass_twin(t - cuts)

    load_x.wait()
    relay_stage(0, 1, out_work, attn_owner, h_all, pump)
    in_loop = 1 + chunks + hop * 2 * (n - 1)

    @pl.loop(in_loop, jnp.maximum(in_loop, first_pass + apart * (passes + late)))
    def _(ii):
        pump(ii)

    share_g.wait_all()

    def gate_slice(b, k):
        rows_in = take(h_all, b)

        @pl.when(k == 0)
        def _():
            red_gu[b] = dot_t(rows_in, ag_ref[...]).astype(low)

        at = pl.multiple_of(k * a_cut, a_cut)
        lanes = pl.ds(at, a_cut)
        up_lanes = pl.ds(pl.multiple_of(hidden + at, a_cut), a_cut)
        red = red_gu[b]
        gate = dot(rows_in, wg[:, lanes]) + dot(red[:, :RANK], bg_ref[0, :, lanes])
        up = dot(rows_in, wg[:, up_lanes]) + dot(red[:, RANK:], bg_ref[1, :, lanes])
        gu[b, :, lanes] = gate.astype(low)
        gu[b, :, up_lanes] = up.astype(low)
        hid[:, lanes] = (gate * jax.nn.sigmoid(gate) * up).astype(low)

    def down_slice(b, k):
        @pl.when(jnp.logical_and(b == 0, k == 0))
        def _():
            share_d.wait_all()

        rows_in = hid[:, :hidden]

        @pl.when(k == 0)
        def _():
            red_down[b] = dot_t(rows_in, ad_ref[...]).astype(low)

        for s in range(nr // 2):
            j = k * (nr // 2) + s
            lanes = span(j * width, width)
            down_rows = pl.ds(pl.multiple_of(j * hidden, hidden), hidden)
            put(b, lanes, dot(rows_in, wd[down_rows, :]) + dot(red_down[b], bd_ref[:, lanes]))

    def ffn_work(b, k):
        @pl.when(k < 4)
        def _():
            gate_slice(b, k)

        @pl.when(k >= 4)
        def _():
            down_slice(b, k - 4)

    def ffn_owner(total, at):
        a_raw = raw[at, :]
        h = x_half[at, :].astype(wide) + a_raw * norm_factor(row_sum(a_raw * a_raw)) * gain_a
        factor = norm_factor(row_sum(total * total))
        flat = total * factor
        out_half[at, :] = (h + flat * gain_f).astype(low)
        scaled = cot_half[at, :].astype(wide) * gain_f
        return (factor * (scaled - flat * (row_sum(scaled * flat) * (1.0 / D)))).astype(low)

    load_cot.wait()
    relay_stage(1, 6, ffn_work, ffn_owner, df_all)

    b_cut = hidden // 2

    def hidden_back(b, k):
        rows_in = take(df_all, b)

        @pl.when(k == 0)
        def _():
            back_down[...] = dot_t(rows_in, bd_ref[...]).astype(low)

        at = pl.multiple_of(k * b_cut, b_cut)
        lanes = pl.ds(at, b_cut)
        up_lanes = pl.ds(pl.multiple_of(hidden + at, b_cut), b_cut)
        back = back_down[...]
        grad = dot(back, ad_ref[:, lanes])
        for j in range(nr):
            down_rows = pl.ds(pl.multiple_of(j * hidden + at, b_cut), b_cut)
            grad = grad + dot_t(rows_in[:, j * width:(j + 1) * width], wd[down_rows, :])
        gate = gu[b, :, lanes].astype(wide)
        up = gu[b, :, up_lanes].astype(wide)
        sigma = jax.nn.sigmoid(gate)
        silu = gate * sigma
        d_gate = (grad * up * sigma * (1.0 + gate * (1.0 - sigma))).astype(low)
        d_up = (grad * silu).astype(low)
        hid[:, lanes] = d_gate
        hid[:, up_lanes] = d_up
        cd_ref[:, lanes] += t_dot(back, (silu * up).astype(low))
        red = red_gu[b]
        cg_ref[0, :, lanes] += t_dot(red[:, :RANK], d_gate)
        cg_ref[1, :, lanes] += t_dot(red[:, RANK:], d_up)

    o_cut = width_all // 4

    def gate_back(b, k):
        @pl.when(k == 0)
        def _():
            back_gu[:, :RANK] = dot_t(hid[:, :hidden], bg_ref[0]).astype(low)
            back_gu[:, RANK:] = dot_t(hid[:, hidden:], bg_ref[1]).astype(low)

        lanes = span(k * o_cut, o_cut)
        put(b, lanes, dot_t(hid[...], wg[lanes, :]) + dot(back_gu[...], ag_ref[:, lanes]))

        @pl.when(k == 3)
        def _():
            full_ref[:2 * RANK, :] += t_dot(back_gu[...], take(h_all, b))
            full_ref[3 * RANK:, :] += t_dot(red_down[b], take(df_all, b))

    def back_work(b, k):
        @pl.when(k < 2)
        def _():
            hidden_back(b, k)

        @pl.when(k >= 2)
        def _():
            gate_back(b, k - 2)

    def back_owner(total, at):
        grad = cot_half[at, :].astype(wide) + total
        grad_half[at, :] = grad
        a_raw = raw[at, :]
        factor = norm_factor(row_sum(a_raw * a_raw))
        flat = a_raw * factor
        scaled = grad * gain_a
        return (factor * (scaled - flat * (row_sum(scaled * flat) * (1.0 / D)))).astype(low)

    relay_stage(2, 6, back_work, back_owner, da_all)

    @pl.loop(0, n)
    def _(b):
        at = span(b * own, own)
        rows_in = da_all[at, :]
        back = dot_t(rows_in, bo_ref[...]).astype(low)
        grad = dot(back, ao_ref[...])
        for j in range(nr):
            grad = grad + dot_t(rows_in[:, j * width:(j + 1) * width], wo[shard(j, wo), :])
        d_attn[at, :] = grad.astype(low)
        for d in range(1, nr):
            piece_out(d, b).start()
        local_piece_out(b).start()
        attn_rows = attn[at, :]
        co_ref[...] += t_dot(back, attn_rows)
        red = dot_t(attn_rows, ao_ref[...]).astype(low)
        full_ref[2 * RANK:3 * RANK, :] += t_dot(red, rows_in)

    @pl.loop(0, n)
    def _(b):
        for d in range(1, nr):
            piece_in(d, b).wait_send()
            piece_out(d, b).wait()
        local_piece_out(b).wait()

    share_g.drain()
    share_d.drain()


def middle(attn_head, x, cot_half, gains, w_out, w_gu, w_down, table, a_out, b_gu, a_down, n, nr, m=16, hop=2, cuts=8):
    group, width_all = x.shape
    half = group // 2
    width = width_all // nr
    hidden = a_down.shape[1]
    chunks = half // m
    band = group // 4
    dma = pltpu.SemaphoreType.DMA
    any_space = pl.BlockSpec(memory_space=pl.ANY)
    shape = jax.ShapeDtypeStruct
    return pl.pallas_call(
        functools.partial(middle_kernel, n, nr, m, hop, cuts),
        out_shape=[
            shape(attn_head.shape, low),
            shape((half, width_all), low),
            shape((half, width_all), wide),
            shape((4 * RANK, width_all), wide),
            shape((RANK, a_out.shape[1]), wide),
            shape((2, RANK, hidden), wide),
            shape((RANK, hidden), wide),
        ],
        in_specs=[VM, any_space, any_space, VM, any_space, any_space, any_space] + [VM] * 4,
        out_specs=[VM] * 7,
        scratch_shapes=[
            pltpu.VMEM(w_out.shape, low),
            pltpu.VMEM((w_gu.shape[0] * nr, w_gu.shape[1]), low),
            pltpu.VMEM((w_down.shape[0] * nr, w_down.shape[1]), low),
            pltpu.VMEM((half, width_all), low),
            pltpu.VMEM((half, width_all), low),
            pltpu.VMEM((half, width_all), wide),
            pltpu.VMEM((group, a_out.shape[1]), low),
            pltpu.VMEM((group, a_out.shape[1]), low),
            pltpu.VMEM((group, width_all), low),
            pltpu.VMEM((group, width_all), low),
            pltpu.VMEM((group, width_all), low),
            pltpu.VMEM((4, band, 2 * hidden), low),
            pltpu.VMEM((group, width_all), low),
            pltpu.VMEM((half, width_all), low),
            pltpu.VMEM((half, width_all), low),
            pltpu.VMEM((band, 2 * hidden), low),
            pltpu.VMEM((4, band, 2 * RANK), low),
            pltpu.VMEM((4, band, RANK), low),
            pltpu.VMEM((band, 2 * RANK), low),
            pltpu.VMEM((band, RANK), low),
            dma((3, 4, chunks)), dma((3, 4, chunks)),
            dma((nr - 1, n)), dma((nr - 1, n)), dma((nr - 1, n)), dma((nr - 1, n)), dma((n,)), dma((n,)),
            dma((3,)),
        ] + share_sems(cuts) + share_sems(cuts // 2),
        compiler_params=pltpu.CompilerParams(collective_id=0, has_side_effects=True, vmem_limit_bytes=67043328),
        name="middle",
    )(attn_head, x, cot_half, gains, w_out, w_gu, w_down, table, a_out, b_gu, a_down)


def per_device(
    tokens,
    cotangent,
    seg_ids,
    positions,
    parents,
    tree_sets,
    gain_q,
    gain_k,
    gain_attn,
    gain_ffn,
    query_key_value_weight,
    output_weight,
    gate_up_weight,
    down_weight,
    query_key_value_adapter_first,
    query_key_value_adapter_second,
    output_adapter_first,
    output_adapter_second,
    gate_up_adapter_first,
    gate_up_adapter_second,
    down_adapter_first,
    down_adapter_second,
):
    dp_count = lax.axis_size("dp")
    row_count = lax.axis_size("row")
    col_count = lax.axis_size("col")
    row_at = lax.axis_index("row")
    tree_tokens = seg_ids.shape[0]
    assert tree_sets.shape[0] == 1 and col_count == 4
    set_count = output_adapter_first.shape[0]
    own = tokens.shape[0] // row_count
    group = own * col_count
    width_row = tokens.shape[1]
    width_col = gain_q.shape[0]
    hidden_col = down_weight.shape[0]
    heads_col = width_col // HEAD
    tree_set = tree_sets[0]

    tables = (
        query_key_value_adapter_first,
        query_key_value_adapter_second,
        output_adapter_first,
        output_adapter_second,
        gate_up_adapter_first,
        gate_up_adapter_second,
        down_adapter_first,
        down_adapter_second,
    )
    narrow, b_qkv, a_out, b_gu, a_down = prep(tree_sets, tables)
    gain_pair = jnp.pad(jnp.stack([gain_attn, gain_ffn]), ((0, 6), (0, 0)))
    pos_own = lax.dynamic_index_in_dim(
        positions.reshape(col_count, row_count, own), row_at, 1, keepdims=False
    ).reshape(group)
    cosine, sine = angles(pos_own)
    cos2 = jnp.concatenate([cosine, cosine], axis=1)
    sin2 = jnp.concatenate([-sine, sine], axis=1)
    gq, gk = gain_q[None, :], gain_k[None, :]
    parent_at, branch_flag = tree_tables(seg_ids, parents)
    first = lax.axis_index("col") == 0
    final = lax.axis_index("col") == col_count - 1
    x, table, gains, g_half, raw, factors, qkv_head, w_qkv, w_out = front(
        tokens,
        narrow,
        gain_pair,
        cotangent,
        query_key_value_weight.reshape(width_row, 3 * width_col),
        output_weight,
        b_qkv,
        gq,
        gk,
        cos2,
        sin2,
        col_count,
        row_count,
    )
    attn_head, lse = attend(qkv_head, parent_at, branch_flag)
    a_qkv = table[: 3 * RANK]
    d_attn_head, out_half, d_h_half, full_mid, part_ao, part_bgu, part_ad = middle(
        attn_head,
        x,
        g_half,
        gains,
        w_out,
        gate_up_weight.reshape(width_row, 2 * hidden_col),
        down_weight,
        table,
        a_out,
        b_gu,
        a_down,
        col_count,
        row_count,
    )
    d_qkv_head = attend_back(qkv_head, d_attn_head, parent_at, branch_flag, lse)
    d_raw, layer_out = from_heads_call(
        d_qkv_head, raw, factors, gq, gk, cos2, sin2, out_half, col_count, row_count
    )
    d_q, d_k, d_v = (d_raw[:, width_col * j : width_col * (j + 1)] for j in range(3))
    b_qkv = b_qkv.reshape(3, RANK, width_col)
    back_qkv = jnp.concatenate([dot_t(d, b) for d, b in zip((d_q, d_k, d_v), b_qkv)], axis=1).astype(low)
    red_qkv = dot_t(x, a_qkv).astype(low)
    d_h_all = jnp.concatenate([jnp.where(first, d_h_half, 0.0), jnp.where(final, d_h_half, 0.0)], axis=0)
    part_in = (dot_t(d_raw, w_qkv) + dot(back_qkv, a_qkv) + d_h_all).astype(low)

    rank_own = RANK // col_count
    full = jnp.concatenate(
        [t_dot(back_qkv, x), full_mid], axis=0
    ).astype(low)
    full = full.reshape(7, col_count, rank_own, D).transpose(1, 0, 2, 3).reshape(col_count, 7 * rank_own, D)
    full = jnp.pad(full, ((0, 0), (0, rank_own), (0, 0))).reshape(col_count * 8 * rank_own, D)
    cols = jnp.concatenate(
        [t_dot(red_qkv[:, RANK * j : RANK * (j + 1)], d) for j, d in enumerate((d_q, d_k, d_v))]
        + [part_ao, part_bgu[0], part_bgu[1], part_ad],
        axis=1,
    ).astype(low)
    cols = cols.reshape(RANK * 16, width_row)
    hot = (tree_set == lax.broadcasted_iota(jnp.int32, (set_count, width_row), 0)).astype(wide)
    sets_own = set_count // dp_count
    input_grad, sets = finish(part_in, full, cols, hot, sets_own, col_count, row_count, dp_count)
    full_sets = sets[:, : 7 * rank_own].reshape(sets_own, 7, rank_own, width_row)
    col_sets = sets[:, 8 * rank_own :].reshape(sets_own, RANK // row_count, 16 * width_row)
    grad_a_qkv = full_sets[:, :3].transpose(1, 0, 2, 3)
    grad_a_gu = full_sets[:, 3:5].transpose(1, 0, 2, 3)
    grad_b_out = full_sets[:, 5]
    grad_b_down = full_sets[:, 6]
    grad_b_qkv = jnp.stack([col_sets[..., width_col * j : width_col * (j + 1)] for j in range(3)])
    grad_a_out = col_sets[..., 3 * width_col : 4 * width_col]
    gu_at = 4 * width_col
    grad_b_gu = jnp.stack([col_sets[..., gu_at + hidden_col * j : gu_at + hidden_col * (j + 1)] for j in range(2)])
    grad_a_down = col_sets[..., gu_at + 2 * hidden_col :]
    return (
        layer_out,
        input_grad,
        grad_a_qkv,
        grad_b_qkv,
        grad_a_out,
        grad_b_out,
        grad_a_gu,
        grad_b_gu,
        grad_a_down,
        grad_b_down,
    )


def solution(mesh):
    in_specs = (
        P(("dp", "col"), "row"),
        P(("dp", "col"), "row"),
        P("dp"),
        P("dp"),
        P("dp", None),
        P("dp"),
        P("col"),
        P("col"),
        P("row"),
        P("row"),
        P("row", None, "col"),
        P("col", "row"),
        P("row", None, "col"),
        P("col", "row"),
        P(None, None, None, "row"),
        P(None, None, None, "col"),
        P(None, None, "col"),
        P(None, None, "row"),
        P(None, None, None, "row"),
        P(None, None, None, "col"),
        P(None, None, "col"),
        P(None, None, "row"),
    )
    out_specs = (
        P(("dp", "col"), "row"),
        P(("dp", "col"), "row"),
        P(None, "dp", "col", "row"),
        P(None, "dp", "row", "col"),
        P("dp", "row", "col"),
        P("dp", "col", "row"),
        P(None, "dp", "col", "row"),
        P(None, "dp", "row", "col"),
        P("dp", "row", "col"),
        P("dp", "col", "row"),
    )
    return jax.shard_map(
        per_device, mesh=mesh, in_specs=in_specs, out_specs=out_specs, check_vma=False
    )
```

```python
import functools

import jax
import jax.numpy as jnp
from jax import lax
from jax.experimental import pallas as pl
from jax.experimental.pallas import tpu as pltpu
from jax.sharding import PartitionSpec as P

D = 2048
HEAD = 128
RANK = 16
SEG = 128
TRUNK = 1024
QT = 256
MESH = pl.DeviceIdType.MESH
VM = pl.BlockSpec(memory_space=pltpu.VMEM)
precise = lax.Precision.HIGHEST

epsilon = 1e-06
rope_base = 500000.0
masked_out = -1e30
low = jnp.bfloat16
wide = jnp.float32
last_last = (((1,), (1,)), ((), ()))
first_first = (((0,), (0,)), ((), ()))


def dot(left, right):
    return jnp.dot(left, right, preferred_element_type=wide)


def dot_t(left, right):
    return lax.dot_general(left, right, last_last, preferred_element_type=wide)


def t_dot(left, right):
    return lax.dot_general(left, right, first_first, preferred_element_type=wide)


def angles(positions):
    half_width = HEAD // 2
    frequency = rope_base ** (-(jnp.arange(half_width, dtype=wide) * 2.0) / HEAD)
    angle_table = positions.astype(wide)[:, None] * frequency[None, :]
    return (jnp.cos(angle_table), jnp.sin(angle_table))


def norm_factor(square_sum):
    return lax.rsqrt(square_sum * (1.0 / D) + epsilon)


def tree_tables(seg_ids, parents):
    tail_seg = seg_ids[TRUNK::SEG]
    labels = jnp.arange(parents.shape[1], dtype=jnp.int32)
    tail_parent = jnp.sum(jnp.where(tail_seg[:, None] == labels[None, :], parents[0][None, :], 0), axis=1)
    hit = (tail_seg[None, :] == tail_parent[:, None])
    at = jnp.arange(tail_seg.shape[0], dtype=jnp.int32) + TRUNK // SEG
    parent_at = jnp.sum(jnp.where(hit, at[None, :], 0), axis=1)
    bias = jnp.where(tail_parent > 0, 0.0, masked_out).astype(wide)
    return parent_at, jnp.broadcast_to(bias[:, None], (tail_seg.shape[0], SEG))


def row_sum(v): return jnp.sum(v, axis=1, keepdims=True)

def params(collective):
    return pltpu.CompilerParams(collective_id=collective, has_side_effects=True, vmem_limit_bytes=60 << 20)


def span(at, size):
    return pl.ds(pl.multiple_of(at, size), size)


def remote(src, dst, send_sem, recv_sem, to):
    return pltpu.make_async_remote_copy(
        src_ref=src, dst_ref=dst, send_sem=send_sem, recv_sem=recv_sem, device_id=to, device_id_type=MESH
    )


def greet(n, nr, extra=0):
    r, c = lax.axis_index("row"), lax.axis_index("col")
    me = r * n + c
    barrier = pltpu.get_barrier_semaphore()

    @pl.loop(1, n * nr)
    def _(d):
        peer = lax.rem(me + d, n * nr)
        pl.semaphore_signal(barrier, inc=1, device_id={"row": peer // n, "col": lax.rem(peer, n)}, device_id_type=MESH)

    pl.semaphore_wait(barrier, n * nr - 1 + extra)


def row_sums(first, second):
    ones = jnp.ones((8, first.shape[1]), wide)
    at = lax.broadcasted_iota(jnp.int32, (8, first.shape[0]), 0)
    sum_first = lax.dot_general(ones, first, last_last, preferred_element_type=wide, precision=precise)
    sum_second = lax.dot_general(ones, second, last_last, preferred_element_type=wide, precision=precise)
    return jnp.where(at < 4, sum_first, sum_second)


def down_columns(values, at):
    pick = (lax.broadcasted_iota(jnp.int32, (8, HEAD), 0) == at).astype(wide)
    return lax.dot_general(values, pick, first_first, preferred_element_type=wide, precision=precise)


def flip(v):
    return v + 1 - 2 * lax.rem(v, 2)


class Share:
    def __init__(self, src, dst, cuts, sems):
        self.send, self.recv, self.local = sems
        self.src, self.cuts = src, cuts
        g, r = lax.axis_index("dp"), lax.axis_index("row")
        size = src.shape[0]
        half = size // 2
        step = half // cuts
        far = lax.rem(r + 2, 4)
        mine = lax.rem(g, 2)
        near_to, far_to, twin_to = {"row": flip(r)}, {"row": far}, {"dp": flip(g)}

        def rows(shard, part, i):
            return pl.ds(pl.multiple_of(shard * size + part * half + i * step, step), step)

        def copy(kind, i, src, dst, to):
            return remote(src, dst, self.send.at[kind, i], self.recv.at[kind, i], to)

        def hand(kind, part, to):
            return lambda i: copy(kind, i, dst.at[rows(far, part, i)], dst.at[rows(far, part, i)], to)

        whole = span(r * size, size)
        self.own = pltpu.make_async_copy(src, dst.at[whole], self.local)
        self.near = copy(0, 0, src, dst.at[whole], near_to)
        self.far = lambda i: copy(
            1, i, src.at[pl.ds(pl.multiple_of(mine * half + i * step, step), step)], dst.at[rows(r, mine, i)], far_to
        )
        self.far_near = hand(2, mine, near_to)
        self.far_twin = hand(3, mine, twin_to)
        self.twin_near = hand(4, 1 - mine, near_to)

    def start_far(self):
        for i in range(self.cuts):
            self.far(i).start()

    def start_near(self):
        self.own.start()
        self.near.start()

    def pass_far(self, i):
        self.far(i).wait_recv()
        self.far_twin(i).start()
        self.far_near(i).start()

    def pass_twin(self, i):
        self.far_twin(i).wait_recv()
        self.twin_near(i).start()

    def wait_all(self):
        self.own.wait()
        self.near.wait_recv()
        for i in range(self.cuts):
            self.far_near(i).wait_recv()
            self.twin_near(i).wait_recv()

    def drain(self):
        self.near.wait_send()
        for i in range(self.cuts):
            self.far(i).wait_send()
            self.far_near(i).wait_send()
            self.far_twin(i).wait_send()
            self.twin_near(i).wait_send()


def share_sems(cuts):
    dma = pltpu.SemaphoreType.DMA
    return [dma((5, cuts)), dma((5, cuts)), dma]


def prep_kernel(set_ref, fq_ref, sq_ref, fo_ref, so_ref, fg_ref, sg_ref, fd_ref, sd_ref,
                narrow_ref, bq_ref, ao_ref, bg_ref, ad_ref):
    for j in range(3):
        narrow_ref[j * RANK:(j + 1) * RANK, :] = fq_ref[j, 0].astype(low)
        bq_ref[j * RANK:(j + 1) * RANK, :] = sq_ref[j, 0].astype(low)
    for j in range(2):
        narrow_ref[(3 + j) * RANK:(4 + j) * RANK, :] = fg_ref[j, 0].astype(low)
        bg_ref[j] = sg_ref[j, 0].astype(low)
    narrow_ref[5 * RANK:6 * RANK, :] = so_ref[0].astype(low)
    narrow_ref[6 * RANK:, :] = sd_ref[0].astype(low)
    ao_ref[...] = fo_ref[0].astype(low)
    ad_ref[...] = fd_ref[0].astype(low)


def prep(tree_sets, tables):
    fq, sq, fo, so, fg, sg, fd, sd = tables

    def pick(table):
        if table.ndim == 4:
            return pl.BlockSpec((table.shape[0], 1) + table.shape[2:], lambda i, s: (0, s[0], 0, 0))
        return pl.BlockSpec((1,) + table.shape[1:], lambda i, s: (s[0], 0, 0))

    def out(*shape):
        return pl.BlockSpec(shape, lambda i, s: (0,) * len(shape)), jax.ShapeDtypeStruct(shape, low)

    outs = [
        out(7 * RANK, fq.shape[-1]), out(3 * RANK, sq.shape[-1]), out(RANK, fo.shape[-1]),
        out(2, RANK, sg.shape[-1]), out(RANK, fd.shape[-1]),
    ]
    return pl.pallas_call(
        prep_kernel,
        grid_spec=pltpu.PrefetchScalarGridSpec(
            num_scalar_prefetch=1, grid=(1,), in_specs=[pick(t) for t in tables], out_specs=[o[0] for o in outs]
        ),
        out_shape=[o[1] for o in outs],
        name="prep",
    )(tree_sets, *tables)


def lower_mask(size):
    return lax.broadcasted_iota(jnp.int32, (size, size), 1) <= lax.broadcasted_iota(jnp.int32, (size, size), 0)


def softmax_parts(parts):
    top = jnp.max(parts[0], axis=1, keepdims=True)
    for s in parts[1:]:
        top = jnp.maximum(top, jnp.max(s, axis=1, keepdims=True))
    raised = [jnp.exp(s - top) for s in parts]
    total = jnp.sum(raised[0], axis=1, keepdims=True)
    for e in raised[1:]:
        total = total + jnp.sum(e, axis=1, keepdims=True)
    inverse = 1.0 / total
    return [e * inverse for e in raised], top + jnp.log(total)


def tail_parts(q, qkv, at, parent, flag):
    scale = HEAD ** -0.5
    k_lanes = slice(HEAD, 2 * HEAD)
    trunk = dot_t(q, qkv[:TRUNK, k_lanes]) * scale
    branch = dot_t(q, qkv[pl.ds(parent, SEG), k_lanes]) * scale + flag
    own = jnp.where(lower_mask(SEG), dot_t(q, qkv[pl.ds(at, SEG), k_lanes]) * scale, masked_out)
    return [trunk, branch, own]


def trunk_parts(q, qkv, i):
    scale = HEAD ** -0.5
    k_lanes = slice(HEAD, 2 * HEAD)
    own = dot_t(q, qkv[i * QT:(i + 1) * QT, k_lanes]) * scale
    parts = [jnp.where(lower_mask(QT), own, masked_out)]
    if i:
        parts.append(dot_t(q, qkv[:i * QT, k_lanes]) * scale)
    return parts


def attend_body(parent_ref, flag_ref, qkv, o_ref, lse_ref):
    v_lanes = slice(2 * HEAD, 3 * HEAD)
    for i in range(TRUNK // QT):
        at = slice(i * QT, (i + 1) * QT)
        p, lse = softmax_parts(trunk_parts(qkv[at, :HEAD], qkv, i))
        o = dot(p[0].astype(low), qkv[at, v_lanes])
        if i:
            o = o + dot(p[1].astype(low), qkv[:i * QT, v_lanes])
        o_ref[at, :] = o.astype(low)
        lse_ref[at, :] = lse

    @pl.loop(0, (qkv.shape[0] - TRUNK) // SEG)
    def _(j):
        at = pl.multiple_of(TRUNK + j * SEG, SEG)
        parent = pl.multiple_of(parent_ref[j] * SEG, SEG)
        rows = pl.ds(at, SEG)
        p, lse = softmax_parts(tail_parts(qkv[rows, :HEAD], qkv, at, parent, flag_ref[pl.ds(j, 1), :]))
        o = dot(p[0].astype(low), qkv[:TRUNK, v_lanes])
        o = o + dot(p[1].astype(low), qkv[pl.ds(parent, SEG), v_lanes])
        o = o + dot(p[2].astype(low), qkv[rows, v_lanes])
        o_ref[rows, :] = o.astype(low)
        lse_ref[rows, :] = lse


def back_parts(scores, lse, d_out, keys, values):
    probs = [jnp.exp(s - lse) for s in scores]
    grads = [dot_t(d_out, v) for v in values]
    inner = sum(jnp.sum(p * g, axis=1, keepdims=True) for p, g in zip(probs, grads))
    d_scores = [(p * (g - inner)).astype(low) for p, g in zip(probs, grads)]
    dq = sum(dot(d, k) for d, k in zip(d_scores, keys))
    return d_scores, [p.astype(low) for p in probs], dq


def attend_back_kernel(parent_ref, flag_ref, qkv, do_ref, lse_ref, d_ref, dk_acc, dv_acc):
    scale = HEAD ** -0.5
    k_lanes = slice(HEAD, 2 * HEAD)
    v_lanes = slice(2 * HEAD, 3 * HEAD)
    dk_acc[...] = jnp.zeros_like(dk_acc)
    dv_acc[...] = jnp.zeros_like(dv_acc)
    for i in range(TRUNK // QT):
        at = slice(i * QT, (i + 1) * QT)
        spans = [at] + ([slice(0, i * QT)] if i else [])
        q, d_out = qkv[at, :HEAD], do_ref[at, :]
        d_scores, probs, dq = back_parts(
            trunk_parts(q, qkv, i), lse_ref[at, :], d_out, [qkv[s, k_lanes] for s in spans], [qkv[s, v_lanes] for s in spans]
        )
        d_ref[at, :HEAD] = (dq * scale).astype(low)
        for s, d, p in zip(spans, d_scores, probs):
            dk_acc[s, :] += t_dot(d, q)
            dv_acc[s, :] += t_dot(p, d_out)

    @pl.loop(0, (qkv.shape[0] - TRUNK) // SEG)
    def _(j):
        at = pl.multiple_of(TRUNK + j * SEG, SEG)
        parent = pl.multiple_of(parent_ref[j] * SEG, SEG)
        rows = pl.ds(at, SEG)
        spans = [slice(0, TRUNK), pl.ds(parent, SEG), rows]
        q, d_out = qkv[rows, :HEAD], do_ref[rows, :]
        d_scores, probs, dq = back_parts(
            tail_parts(q, qkv, at, parent, flag_ref[pl.ds(j, 1), :]), lse_ref[rows, :], d_out,
            [qkv[s, k_lanes] for s in spans], [qkv[s, v_lanes] for s in spans],
        )
        d_ref[rows, :HEAD] = (dq * scale).astype(low)
        for s, d, p in zip(spans, d_scores, probs):
            dk_acc[s, :] += t_dot(d, q)
            dv_acc[s, :] += t_dot(p, d_out)

    d_ref[:, k_lanes] = (dk_acc[...] * scale).astype(low)
    d_ref[:, v_lanes] = dv_acc[...].astype(low)


def attend(qkv, parent_at, flag):
    n = qkv.shape[0]

    def whole(*shape):
        return pl.BlockSpec(shape, lambda i, *_: (0, 0))

    return pl.pallas_call(
        attend_body,
        grid_spec=pltpu.PrefetchScalarGridSpec(
            num_scalar_prefetch=1,
            grid=(1,),
            in_specs=[whole(*flag.shape), whole(n, 3 * HEAD)],
            out_specs=[whole(n, HEAD), whole(n, 1)],
        ),
        out_shape=[jax.ShapeDtypeStruct((n, HEAD), low), jax.ShapeDtypeStruct((n, 1), wide)],
        name="attend",
    )(parent_at, flag, qkv)


def attend_back(qkv, d_o, parent_at, flag, lse):
    n = qkv.shape[0]

    def whole(*shape):
        return pl.BlockSpec(shape, lambda i, *_: (0, 0))

    return pl.pallas_call(
        attend_back_kernel,
        grid_spec=pltpu.PrefetchScalarGridSpec(
            num_scalar_prefetch=1,
            grid=(1,),
            in_specs=[whole(*flag.shape), whole(n, 3 * HEAD), whole(n, HEAD), whole(n, 1)],
            out_specs=whole(n, 3 * HEAD),
            scratch_shapes=[pltpu.VMEM((n, HEAD), wide), pltpu.VMEM((n, HEAD), wide)],
        ),
        out_shape=jax.ShapeDtypeStruct((n, 3 * HEAD), low),
        name="attend_back",
    )(parent_at, flag, qkv, d_o, lse)


def front_kernel(n, nr, m, mh, tok_ref, table_ref, gain_ref, cot_ref, wq_hbm, wo_hbm, bq_ref, gq_ref, gk_ref,
                 cos_ref, sin_ref,
                 x_ref, table_all, gain_all, half_ref, raw_ref, factor_ref, qkv_ref, wq_out, wo_out,
                 wq, wo, stats, buf, fq, fk, red, cot_own,
                 send_a, recv_a, send_z, recv_z, send_t, recv_t, local_sem,
                 send_s, recv_s, send_h, recv_h, send_g, recv_g, local_h, local_g, send_e, recv_e,
                 send_q, recv_q, local_q, send_o, recv_o, local_o, out_sems):
    g, r, c = lax.axis_index("dp"), lax.axis_index("row"), lax.axis_index("col")
    own = tok_ref.shape[0] // nr
    width = tok_ref.shape[1]
    rows_all = own * n
    heads = width // HEAD
    tree_part = own * nr
    chunks = own // m
    left = {"col": jnp.maximum(c - 1, 0)}
    right = {"col": jnp.minimum(c + 1, n - 1)}
    share_q = Share(wq_hbm, wq, 2, (send_q, recv_q, local_q))
    share_o = Share(wo_hbm, wo, 2, (send_o, recv_o, local_o))

    def piece(d, j):
        peer = lax.rem(r + d, nr)
        return remote(
            tok_ref.at[span(peer * own + j * m, m)],
            x_ref.at[span(c * own + j * m, m), span(r * width, width)],
            send_a.at[d - 1, j], recv_a.at[d - 1, j], {"row": peer},
        )

    def block(kind, s, at, j, to):
        rows = span(at * own + j * m, m)
        return remote(x_ref.at[rows], x_ref.at[rows], send_z.at[kind, s, j], recv_z.at[kind, s, j], to)

    def table_piece(d, kind):
        src, dst = ((table_ref, table_all), (gain_ref, gain_all))[kind]
        to = {"row": lax.rem(r + d, nr)}
        return remote(src, dst.at[:, span(r * width, width)], send_t.at[kind, d - 1], recv_t.at[kind, d - 1], to)

    keep = pltpu.make_async_copy(
        tok_ref.at[span(r * own, own)], x_ref.at[span(c * own, own), span(r * width, width)], local_sem.at[0]
    )
    keep_table = pltpu.make_async_copy(table_ref, table_all.at[:, span(r * width, width)], local_sem.at[1])
    keep_gain = pltpu.make_async_copy(gain_ref, gain_all.at[:, span(r * width, width)], local_sem.at[2])
    keep.start()
    keep_table.start()
    keep_gain.start()
    barrier = pltpu.get_barrier_semaphore()
    pl.semaphore_signal(barrier, inc=1, device_id={"dp": flip(g)}, device_id_type=MESH)
    greet(n, nr, 1)

    @pl.loop(0, chunks)
    def _(j):
        for d in range(1, nr):
            piece(d, j).start()

    middle_at = n // 2
    owner = jnp.where(c < middle_at, 0, n - 1)
    at_owner = jnp.where(c < middle_at, c, c - middle_at)
    is_owner = owner == c

    def cot_piece(d):
        peer = lax.rem(r + d, nr)
        return remote(
            cot_ref.at[span(peer * own, own)], cot_own.at[:, span(r * width, width)], send_g.at[d - 1], recv_g.at[d - 1], {"row": peer}
        )

    cot_local = pltpu.make_async_copy(cot_ref.at[span(r * own, own)], cot_own.at[:, span(r * width, width)], local_g.at[0])
    cot_keep = pltpu.make_async_copy(cot_own, half_ref.at[span(at_owner * own, own)], local_g.at[1])

    def cot_move(b):
        return remote(cot_own, half_ref.at[span(b * own, own)], send_e, recv_e.at[b], {"col": owner})

    share_q.start_far()
    share_q.start_near()
    for d in range(1, nr):
        table_piece(d, 0).start()
        table_piece(d, 1).start()
    share_o.start_far()
    share_o.start_near()
    cot_local.start()
    for d in range(1, nr):
        cot_piece(d).start()
    keep.wait()

    def head_rows(i):
        block_at = i // (own // mh)
        inside = lax.rem(i, own // mh)
        return span(block_at * tree_part + r * own + inside * mh, mh)

    def head_piece(d, i):
        peer = lax.rem(r + d, nr)
        return remote(
            buf.at[peer, span(i * mh, mh)], qkv_ref.at[head_rows(i)], send_h.at[d - 1, i], recv_h.at[d - 1, i], {"row": peer}
        )

    def head_local(i):
        return pltpu.make_async_copy(buf.at[r, span(i * mh, mh)], qkv_ref.at[head_rows(i)], local_h.at[i])

    def stat_copy(b, d):
        peer = lax.rem(c + d, n)
        return remote(stats.at[c, b], stats.at[c, b], send_s.at[b, d - 1], recv_s.at[b, d - 1], {"col": peer})

    def product_block(b):
        rows = span(b * own, own)
        x_rows = x_ref[rows, :]
        red[...] = dot_t(x_rows, table_all[:3 * RANK, :]).astype(low)
        for j in range(3):
            lanes = slice(j * width, (j + 1) * width)
            raw_ref[rows, lanes] = dot(x_rows, wq[:, lanes]) + dot(
                red[:, j * RANK:(j + 1) * RANK], bq_ref[j * RANK:(j + 1) * RANK, :]
            )
        q_rows = raw_ref[rows, :width]
        k_rows = raw_ref[rows, width:2 * width]
        stats[c, b] = row_sums(q_rows * q_rows, k_rows * k_rows)
        for d in range(1, n):
            stat_copy(b, d).start()

    per = own // mh

    def head_block(b):
        for d in range(1, n):
            stat_copy(b, d).wait()
        total = stats[0, b]
        for s in range(1, n):
            total = total + stats[s, b]
        factor = lax.rsqrt(total * (1.0 / D) + epsilon)
        factor_ref[b] = factor
        fq[...] = down_columns(factor, 0)
        fk[...] = down_columns(factor, 4)

        @pl.loop(0, per)
        def _(i):
            rows = span(b * own + i * mh, mh)
            inside = span(i * mh, mh)
            cosine = cos_ref[rows, :]
            sine = sin_ref[rows, :]
            for h in range(heads):
                lanes = slice(h * HEAD, (h + 1) * HEAD)
                u = raw_ref[rows, lanes] * fq[inside, :] * gq_ref[:, lanes]
                buf[h, rows, :HEAD] = (u * cosine + pltpu.roll(u, HEAD // 2, 1) * sine).astype(low)
                k_lanes = slice(width + h * HEAD, width + (h + 1) * HEAD)
                u = raw_ref[rows, k_lanes] * fk[inside, :] * gk_ref[:, lanes]
                buf[h, rows, HEAD:2 * HEAD] = (u * cosine + pltpu.roll(u, HEAD // 2, 1) * sine).astype(low)
                v_lanes = slice(2 * width + h * HEAD, 2 * width + (h + 1) * HEAD)
                buf[h, rows, 2 * HEAD:] = raw_ref[rows, v_lanes].astype(low)
            for d in range(1, nr):
                head_piece(d, b * per + i).start()
            head_local(b * per + i).start()

    def early():
        for d in range(1, nr):
            table_piece(d, 0).wait_recv()
            table_piece(d, 1).wait_recv()
        keep_table.wait()
        keep_gain.wait()
        share_q.wait_all()
        copy_wq.start()

        @pl.loop(1, n - 1)
        def _(b):
            product_block(b)

        @pl.when(jnp.logical_not(is_owner))
        def _():
            cot_move(at_owner).start()

        @pl.when(is_owner)
        def _():
            cot_keep.start()

        @pl.loop(1, n - 1)
        def _(b):
            head_block(b)

    def late():
        @pl.loop(0, 2)
        def _(i):
            product_block(i * (n - 1))

        for i in range(2):
            share_o.pass_twin(i)

        @pl.loop(0, 2)
        def _(i):
            head_block(i * (n - 1))

    copy_wq = pltpu.make_async_copy(wq, wq_out, out_sems.at[0])

    for s in range(n):
        @pl.loop(0, chunks)
        def _(j):
            if s == 0:
                for d in range(1, nr):
                    piece(d, j).wait_recv()

            @pl.when(c - s >= 0)
            def _():
                if s > 0:
                    block(0, s - 1, jnp.maximum(c - s, 0), j, right).wait_recv()
                if s < n - 1:
                    @pl.when(c < n - 1)
                    def _():
                        block(0, s, jnp.maximum(c - s, 0), j, right).start()

            @pl.when(c + s <= n - 1)
            def _():
                if s > 0:
                    block(1, s - 1, jnp.minimum(c + s, n - 1), j, left).wait_recv()
                if s < n - 1:
                    @pl.when(c > 0)
                    def _():
                        block(1, s, jnp.minimum(c + s, n - 1), j, left).start()

        if s == 1:
            for i in range(2):
                share_q.pass_far(i)
        if s == n - 2:
            for i in range(2):
                share_o.pass_far(i)
                share_q.pass_twin(i)
            cot_local.wait()
            for d in range(1, nr):
                cot_piece(d).wait_recv()
            early()
        if s == n - 1:
            late()
    steps = rows_all // mh

    share_o.wait_all()
    copy_wo = pltpu.make_async_copy(wo, wo_out, out_sems.at[1])
    copy_wo.start()

    @pl.loop(0, steps)
    def _(i):
        for d in range(1, nr):
            head_piece(d, i).wait()
        head_local(i).wait()

    for d in range(1, nr):
        cot_piece(d).wait_send()

    @pl.when(jnp.logical_not(is_owner))
    def _():
        cot_move(at_owner).wait_send()

    @pl.when(is_owner)
    def _():
        cot_keep.wait()
        for b in range(middle_at):
            @pl.when(b != at_owner)
            def _():
                remote(cot_own, half_ref.at[span(b * own, own)], send_e, recv_e.at[b], {"row": flip(r)}).wait_recv()

    @pl.loop(0, chunks)
    def _(j):
        for d in range(1, nr):
            piece(d, j).wait_send()
        for s in range(n - 1):
            @pl.when(jnp.logical_and(c - s >= 0, c < n - 1))
            def _():
                block(0, s, jnp.maximum(c - s, 0), j, right).wait_send()

            @pl.when(jnp.logical_and(c + s <= n - 1, c > 0))
            def _():
                block(1, s, jnp.minimum(c + s, n - 1), j, left).wait_send()

    for d in range(1, nr):
        table_piece(d, 0).wait_send()
        table_piece(d, 1).wait_send()
    share_q.drain()
    share_o.drain()
    copy_wq.wait()
    copy_wo.wait()


def front(tokens, table, gain, cot, w_qkv, w_out, b_qkv, gain_q, gain_k, cos2, sin2, n, nr, m=32, mh=80):
    own = tokens.shape[0] // nr
    width = tokens.shape[1]
    rows_all = own * n
    tree = own * n * nr
    chunks = own // m
    steps = rows_all // mh
    dma = pltpu.SemaphoreType.DMA
    shape = jax.ShapeDtypeStruct
    any_space = pl.BlockSpec(memory_space=pl.ANY)
    return pl.pallas_call(
        functools.partial(front_kernel, n, nr, m, mh),
        out_shape=[
            shape((rows_all, width * nr), low),
            shape((table.shape[0], width * nr), low),
            shape((gain.shape[0], width * nr), wide),
            shape((rows_all // 2, width * nr), low),
            shape((rows_all, 3 * width), wide),
            shape((n, 8, own), wide),
            shape((tree, 3 * HEAD), low),
            shape((w_qkv.shape[0] * nr, w_qkv.shape[1]), low),
            shape((w_out.shape[0] * nr, w_out.shape[1]), low),
        ],
        in_specs=[VM, VM, VM, VM, any_space, any_space] + [VM] * 5,
        out_specs=[VM] * 7 + [any_space, any_space],
        scratch_shapes=[
            pltpu.VMEM((w_qkv.shape[0] * nr, w_qkv.shape[1]), low),
            pltpu.VMEM((w_out.shape[0] * nr, w_out.shape[1]), low),
            pltpu.VMEM((n, n, 8, own), wide),
            pltpu.VMEM((width // HEAD, rows_all, 3 * HEAD), low),
            pltpu.VMEM((own, HEAD), wide),
            pltpu.VMEM((own, HEAD), wide),
            pltpu.VMEM((own, 3 * RANK), low),
            pltpu.VMEM((own, width * nr), low),
            dma((nr - 1, chunks)), dma((nr - 1, chunks)), dma((2, n - 1, chunks)), dma((2, n - 1, chunks)),
            dma((2, nr - 1)), dma((2, nr - 1)), dma((3,)),
            dma((n, n - 1)), dma((n, n - 1)), dma((nr - 1, steps)), dma((nr - 1, steps)),
            dma((nr - 1,)), dma((nr - 1,)), dma((steps,)), dma((2,)), dma, dma((n // 2,)),
        ] + share_sems(2) + share_sems(2) + [dma((2,))],
        compiler_params=params(3),
        name="front",
    )(tokens, table, gain, cot, w_qkv, w_out, b_qkv, gain_q, gain_k, cos2, sin2)


def one_hot_rows(out_rows, in_rows, source):
    at = lax.broadcasted_iota(jnp.int32, (out_rows, in_rows), 0)
    return (lax.broadcasted_iota(jnp.int32, (out_rows, in_rows), 1) == source(at)).astype(low)


def rear_kernel(n, nr, ndp, m, d_ref, raw_ref, factor_ref, gq_ref, gk_ref, cos_ref, sin_ref, res_ref, x_ref, wq_hbm,
                table_ref, bq_ref, dh_ref, full_ref, co_ref, cg_ref, cd_ref, hot_ref,
                grad_ref, layer_ref, sets_ref,
                wq, stats, buf, nq, nk, pq, pk, fq, fk, d_raw, part, recv_right, recv_left, own_buf, layer_own,
                back, red, full, cols, full_recv, full_sum, full_last, col_recv, owned, hot_all,
                send_s, recv_s, send_h, recv_h, local_h, send_o, recv_o, local_o, load,
                send_z, recv_z, send_w, recv_w, local_w, send_v, recv_v, local_v,
                send_f, recv_f, send_c, recv_c, send_l, recv_l, send_d, recv_d, send_k, recv_k):
    g, r, c = lax.axis_index("dp"), lax.axis_index("row"), lax.axis_index("col")
    rows_all, width_all = part.shape
    own = rows_all // n
    width = gq_ref.shape[1]
    heads = width // HEAD
    tree_part = own * nr
    middle_at = n // 2
    chunks = own // m
    left = {"col": jnp.maximum(c - 1, 0)}
    right = {"col": jnp.minimum(c + 1, n - 1)}
    load_w = pltpu.make_async_copy(wq_hbm, wq, load)
    load_w.start()

    def piece(d, b):
        peer = lax.rem(r + d, nr)
        return remote(
            d_ref.at[span(b * tree_part + peer * own, own)], buf.at[r, span(b * own, own)],
            send_h.at[d - 1, b], recv_h.at[d - 1, b], {"row": peer},
        )

    def local(b):
        return pltpu.make_async_copy(
            d_ref.at[span(b * tree_part + r * own, own)], buf.at[r, span(b * own, own)], local_h.at[b]
        )

    is_owner = jnp.logical_or(c == 0, c == n - 1)
    base = jnp.where(c == 0, 0, middle_at)

    def result_piece(b):
        return remote(res_ref.at[span(b * own, own)], layer_own, send_o.at[b], recv_o, {"col": base + b})

    def result_local(b):
        return pltpu.make_async_copy(res_ref.at[span(b * own, own)], layer_own, local_o)

    def width_piece(src, dst, send_sem, recv_sem, d, j, size):
        peer = lax.rem(r + d, nr)
        return remote(
            src.at[span(j * size, size), span(peer * width, width)], dst.at[span(r * own + j * size, size)],
            send_sem.at[d - 1, j], recv_sem.at[d - 1, j], {"row": peer},
        )

    def width_local(src, dst, sem, j, size):
        return pltpu.make_async_copy(
            src.at[span(j * size, size), span(r * width, width)], dst.at[span(r * own + j * size, size)], sem.at[j]
        )

    for b in range(n):
        local(b).start()
    me = r * n + c
    barrier = pltpu.get_barrier_semaphore()
    for d in range(1, ndp):
        pl.semaphore_signal(barrier, inc=1, device_id={"dp": lax.rem(g + d, ndp)}, device_id_type=MESH)
    greet(n, nr, ndp - 1)
    for b in (0, n - 1) + tuple(range(1, n - 1)):
        for d in range(1, nr):
            piece(d, b).start()

    @pl.when(is_owner)
    def _():
        for b in range(middle_at):
            @pl.when(base + b == c)
            def _():
                result_local(b).start()

            @pl.when(base + b != c)
            def _():
                result_piece(b).start()

    hot_all[g] = hot_ref[...]
    red[...] = dot_t(x_ref[...], table_ref[:3 * RANK, :]).astype(low)

    def stat_copy(b, d):
        peer = lax.rem(c + d, n)
        return remote(stats.at[c, b], stats.at[c, b], send_s.at[b, d - 1], recv_s.at[b, d - 1], {"col": peer})

    def norm_block(b):
        for d in range(1, nr):
            piece(d, b).wait_recv()
        local(b).wait()
        rows = span(b * own, own)
        fq[rows, :] = down_columns(factor_ref[b], 0)
        fk[rows, :] = down_columns(factor_ref[b], 4)
        cosine = cos_ref[rows, :]
        sine = sin_ref[rows, :]
        for h in range(heads):
            lanes = slice(h * HEAD, (h + 1) * HEAD)
            k_lanes = slice(width + h * HEAD, width + (h + 1) * HEAD)
            v_lanes = slice(2 * width + h * HEAD, 2 * width + (h + 1) * HEAD)
            u = buf[h, rows, :HEAD].astype(wide)
            u = (u * cosine - pltpu.roll(u, HEAD // 2, 1) * sine) * gq_ref[:, lanes]
            nq[rows, lanes] = u
            pq[rows, lanes] = u * raw_ref[rows, lanes] * fq[rows, :]
            u = buf[h, rows, HEAD:2 * HEAD].astype(wide)
            u = (u * cosine - pltpu.roll(u, HEAD // 2, 1) * sine) * gk_ref[:, lanes]
            nk[rows, lanes] = u
            pk[rows, lanes] = u * raw_ref[rows, k_lanes] * fk[rows, :]
            d_raw[rows, v_lanes] = buf[h, rows, 2 * HEAD:]
        stats[c, b] = row_sums(pq[rows, :], pk[rows, :])
        for d in range(1, n):
            stat_copy(b, d).start()

    def mean_block(b):
        for d in range(1, n):
            stat_copy(b, d).wait()
        total = stats[0, b]
        for s in range(1, n):
            total = total + stats[s, b]
        mean = total * (1.0 / D) * factor_ref[b]
        rows = span(b * own, own)
        pq[rows, :HEAD] = down_columns(mean, 0)
        pk[rows, :HEAD] = down_columns(mean, 4)

    def back_block(b):
        rows = span(b * own, own)
        for h in range(heads):
            lanes = slice(h * HEAD, (h + 1) * HEAD)
            k_lanes = slice(width + h * HEAD, width + (h + 1) * HEAD)
            d_raw[rows, lanes] = (fq[rows, :] * (nq[rows, lanes] - raw_ref[rows, lanes] * pq[rows, :HEAD])).astype(low)
            d_raw[rows, k_lanes] = (fk[rows, :] * (nk[rows, lanes] - raw_ref[rows, k_lanes] * pk[rows, :HEAD])).astype(low)
        for j in range(3):
            back[rows, j * RANK:(j + 1) * RANK] = dot_t(
                d_raw[rows, j * width:(j + 1) * width], bq_ref[j * RANK:(j + 1) * RANK, :]
            ).astype(low)
        mine = jnp.where(b < middle_at, c == 0, c == n - 1)
        held = span(lax.rem(b, middle_at) * own, own)
        for k in range(width_all // width):
            lanes = slice(k * width, (k + 1) * width)
            value = dot_t(d_raw[rows, :], wq[lanes, :]) + dot(back[rows, :], table_ref[:3 * RANK, lanes])
            part[rows, lanes] = (value + jnp.where(mine, dh_ref[held, lanes], 0.0)).astype(low)

    def reduce(kind, b, j):
        rows = span(b * own + j * m, m)
        dst, to = ((recv_right, right), (recv_left, left))[kind]
        return remote(part.at[rows], dst.at[rows], send_z.at[kind, b, j], recv_z.at[kind, b, j], to)

    def stage(s, at_edge=True, inside=True):
        @pl.loop(0, chunks)
        def _(j):
            for kind, b, go, edge, got in (
                (0, n - 1 - s, n - 1 - s > c, c == 0, recv_right),
                (1, s, s < c, c == n - 1, recv_left),
            ):
                if at_edge:
                    @pl.when(jnp.logical_and(go, edge))
                    def _():
                        reduce(kind, b, j).start()

                if inside:
                    @pl.when(jnp.logical_and(go, jnp.logical_not(edge)))
                    def _():
                        rows = span(b * own + j * m, m)
                        reduce(kind, b, j).wait_recv()
                        part[rows, :] = (part[rows, :].astype(wide) + got[rows, :].astype(wide)).astype(low)
                        reduce(kind, b, j).start()

    def full_piece(d):
        peer = lax.rem(r + d, nr)
        return remote(full.at[:, span(peer * width, width)], full_recv.at[r], send_f.at[d - 1], recv_f.at[d - 1], {"row": peer})

    col_rows = col_recv.shape[1]
    full_rows = full_last.shape[1]

    def col_piece(d):
        peer = lax.rem(r + d, nr)
        return remote(cols.at[span(peer * col_rows, col_rows)], col_recv.at[r], send_c.at[d - 1], recv_c.at[d - 1], {"row": peer})

    def last_piece(d):
        peer = lax.rem(c + d, n)
        return remote(full_sum.at[span(peer * full_rows, full_rows)], full_last.at[c], send_l.at[d - 1], recv_l.at[d - 1], {"col": peer})

    def tree_piece(d):
        return remote(owned.at[g], owned.at[g], send_d.at[d - 1], recv_d.at[d - 1], {"dp": lax.rem(g + d, ndp)})

    def hot_piece(d):
        return remote(hot_all.at[g], hot_all.at[g], send_k.at[d - 1], recv_k.at[d - 1], {"dp": lax.rem(g + d, ndp)})

    @pl.loop(0, 2)
    def _(i):
        norm_block(i * (n - 1))

    load_w.wait()

    @pl.loop(0, 2)
    def _(i):
        mean_block(i * (n - 1))
        back_block(i * (n - 1))

    stage(0, inside=False)

    @pl.loop(1, n - 1)
    def _(b):
        norm_block(b)

    stage(0, at_edge=False)

    @pl.loop(1, n - 1)
    def _(b):
        mean_block(b)
        back_block(b)

    rank_own = RANK // n
    groups = full.shape[0] // (n * rank_own) - 1
    stacked = jnp.concatenate([t_dot(back[...], x_ref[...]), full_ref[...]], axis=0).astype(low)
    order = one_hot_rows(
        full.shape[0], stacked.shape[0],
        lambda o: jnp.where(
            lax.rem(o, full_rows) < groups * rank_own,
            lax.rem(o, full_rows) // rank_own * RANK + o // full_rows * rank_own + lax.rem(o, rank_own), -1
        ),
    )
    full[...] = dot(order, stacked).astype(low)
    pieces = [t_dot(red[:, j * RANK:(j + 1) * RANK], d_raw[:, j * width:(j + 1) * width]) for j in range(3)]
    pieces.append(co_ref[...])
    for j in range(2):
        pieces += [cg_ref[j, :, k * width:(k + 1) * width] for k in range(cg_ref.shape[2] // width)]
    pieces += [cd_ref[:, k * width:(k + 1) * width] for k in range(cd_ref.shape[1] // width)]
    stacked = jnp.concatenate(pieces, axis=0).astype(low)
    rank_row = RANK // nr
    order = one_hot_rows(
        cols.shape[0], stacked.shape[0],
        lambda o: lax.rem(o, col_rows) // rank_row * RANK + o // col_rows * rank_row + lax.rem(o, rank_row),
    )
    cols[...] = dot(order, stacked).astype(low)
    for d in range(1, nr):
        full_piece(d).start()
        col_piece(d).start()
    stage(1)

    @pl.when(is_owner)
    def _():
        for b in range(middle_at):
            @pl.when(base + b == c)
            def _():
                result_local(b).wait()

            @pl.when(base + b != c)
            def _():
                result_piece(b).wait_send()

    @pl.when(jnp.logical_not(is_owner))
    def _():
        remote(res_ref.at[span(0, own)], layer_own, send_o.at[0], recv_o, right).wait_recv()

    for d in range(1, nr):
        width_piece(layer_own, layer_ref, send_v, recv_v, d, 0, own).start()
    width_local(layer_own, layer_ref, local_v, 0, own).start()
    for d in range(1, nr):
        full_piece(d).wait_recv()
        col_piece(d).wait_recv()
    total = full[:, span(r * width, width)].astype(wide)
    col_total = cols[span(r * col_rows, col_rows), :].astype(wide)
    for d in range(1, nr):
        peer = lax.rem(r + d, nr)
        total = total + full_recv[peer].astype(wide)
        col_total = col_total + col_recv[peer].astype(wide)
    full_sum[...] = total.astype(low)
    owned[g, full_rows:, :] = col_total.astype(low)
    for d in range(1, n):
        last_piece(d).start()
    for s in range(2, n - 1):
        stage(s)
    for d in range(1, n):
        last_piece(d).wait_recv()
    last = full_sum[span(c * full_rows, full_rows), :].astype(wide)
    for d in range(1, n):
        last = last + full_last[lax.rem(c + d, n)].astype(wide)
    owned[g, :full_rows, :] = last.astype(low)
    for d in range(1, ndp):
        tree_piece(d).start()
        hot_piece(d).start()

    @pl.loop(0, chunks)
    def _(j):
        rows = span(c * own + j * m, m)
        at = span(j * m, m)
        own_buf[at, :] = part[rows, :]

        @pl.when(c > 0)
        def _():
            reduce(0, c, j).wait_recv()
            own_buf[at, :] = (own_buf[at, :].astype(wide) + recv_right[rows, :].astype(wide)).astype(low)

        @pl.when(c < n - 1)
        def _():
            reduce(1, c, j).wait_recv()
            own_buf[at, :] = (own_buf[at, :].astype(wide) + recv_left[rows, :].astype(wide)).astype(low)

        for d in range(1, nr):
            width_piece(own_buf, grad_ref, send_w, recv_w, d, j, m).start()
        width_local(own_buf, grad_ref, local_w, j, m).start()

    for d in range(1, ndp):
        tree_piece(d).wait_recv()
        hot_piece(d).wait_recv()
    sets_own = sets_ref.shape[0]
    for s in range(sets_own):
        total = owned[0].astype(wide) * hot_all[0, pl.ds(g * sets_own + s, 1), :]
        for t in range(1, ndp):
            total = total + owned[t].astype(wide) * hot_all[t, pl.ds(g * sets_own + s, 1), :]
        sets_ref[s] = total

    @pl.loop(0, chunks)
    def _(j):
        for d in range(1, nr):
            width_piece(own_buf, grad_ref, send_w, recv_w, d, j, m).wait()
        width_local(own_buf, grad_ref, local_w, j, m).wait()

    for d in range(1, nr):
        width_piece(layer_own, layer_ref, send_v, recv_v, d, 0, own).wait()
        full_piece(d).wait_send()
        col_piece(d).wait_send()
        for b in range(n):
            piece(d, b).wait_send()
    width_local(layer_own, layer_ref, local_v, 0, own).wait()
    for d in range(1, n):
        last_piece(d).wait_send()
    for d in range(1, ndp):
        tree_piece(d).wait_send()
        hot_piece(d).wait_send()
    for s in range(n - 1):
        @pl.loop(0, chunks)
        def _(j):
            @pl.when(n - 1 - s > c)
            def _():
                reduce(0, n - 1 - s, j).wait_send()

            @pl.when(s < c)
            def _():
                reduce(1, s, j).wait_send()


def rear(d_head, raw, factor, gain_q, gain_k, cos2, sin2, result, x, w_qkv, table, b_qkv, d_h, full_mid, part_ao,
         part_bgu, part_ad, hot, sets_own, n, nr, ndp, m=32):
    rows_all, wide3 = raw.shape
    width = wide3 // 3
    width_all = x.shape[1]
    own = rows_all // n
    chunks = own // m
    full_rows = 8 * RANK // n
    col_blocks = 4 + 3 * part_ad.shape[1] // width
    col_rows = col_blocks * RANK // nr
    dma = pltpu.SemaphoreType.DMA
    shape = jax.ShapeDtypeStruct
    any_space = pl.BlockSpec(memory_space=pl.ANY)
    square = pltpu.VMEM((rows_all, width), wide)
    lane = pltpu.VMEM((rows_all, HEAD), wide)
    big = pltpu.VMEM((rows_all, width_all), low)
    return pl.pallas_call(
        functools.partial(rear_kernel, n, nr, ndp, m),
        out_shape=[
            shape((own * nr, width), low),
            shape((own * nr, width), low),
            shape((sets_own, full_rows + col_rows, width), wide),
        ],
        in_specs=[VM] * 9 + [any_space] + [VM] * 8,
        out_specs=[VM] * 3,
        scratch_shapes=[
            pltpu.VMEM(w_qkv.shape, low),
            pltpu.VMEM((n, n, 8, own), wide),
            pltpu.VMEM((nr, rows_all, 3 * HEAD), low),
            square, square, square, square, lane, lane,
            pltpu.VMEM((rows_all, wide3), low),
            big, big, big,
            pltpu.VMEM((own, width_all), low),
            pltpu.VMEM((own, width_all), low),
            pltpu.VMEM((rows_all, 3 * RANK), low),
            pltpu.VMEM((rows_all, 3 * RANK), low),
            pltpu.VMEM((n * full_rows, width_all), low),
            pltpu.VMEM((nr * col_rows, width), low),
            pltpu.VMEM((nr, n * full_rows, width), low),
            pltpu.VMEM((n * full_rows, width), low),
            pltpu.VMEM((n, full_rows, width), low),
            pltpu.VMEM((nr, col_rows, width), low),
            pltpu.VMEM((ndp, full_rows + col_rows, width), low),
            pltpu.VMEM((ndp,) + hot.shape, wide),
            dma((n, n - 1)), dma((n, n - 1)), dma((nr - 1, n)), dma((nr - 1, n)), dma((n,)),
            dma((n // 2,)), dma, dma, dma,
            dma((2, n, chunks)), dma((2, n, chunks)), dma((nr - 1, chunks)), dma((nr - 1, chunks)), dma((chunks,)),
            dma((nr - 1, 1)), dma((nr - 1, 1)), dma((1,)),
            dma((nr - 1,)), dma((nr - 1,)), dma((nr - 1,)), dma((nr - 1,)), dma((n - 1,)), dma((n - 1,)),
            dma((ndp - 1,)), dma((ndp - 1,)), dma((ndp - 1,)), dma((ndp - 1,)),
        ],
        compiler_params=params(5),
        name="rear",
    )(d_head, raw, factor, gain_q, gain_k, cos2, sin2, result, x, w_qkv, table, b_qkv, d_h, full_mid, part_ao, part_bgu, part_ad, hot)


def unpack_kernel(rank_own, rank_row, grad_ref, layer_ref, sets_ref, layer_out, input_grad, a_qkv, b_qkv, a_out, b_out, a_gu, b_gu, a_down, b_down):
    layer_out[...] = layer_ref[...]
    input_grad[...] = grad_ref[...].astype(wide)
    width = grad_ref.shape[1]
    first = 8 * rank_own

    def column(s, at):
        return sets_ref[s, first + at * rank_row:first + (at + 1) * rank_row, :]

    for s in range(sets_ref.shape[0]):
        for j in range(3):
            a_qkv[j, s] = sets_ref[s, j * rank_own:(j + 1) * rank_own, :]
            b_qkv[j, s] = column(s, j)
        for j in range(2):
            a_gu[j, s] = sets_ref[s, (3 + j) * rank_own:(4 + j) * rank_own, :]
        b_out[s] = sets_ref[s, 5 * rank_own:6 * rank_own, :]
        b_down[s] = sets_ref[s, 6 * rank_own:7 * rank_own, :]
        a_out[s] = column(s, 3)
        per = a_down.shape[2] // width
        for k in range(per):
            lanes = slice(k * width, (k + 1) * width)
            b_gu[0, s, :, lanes] = column(s, 4 + k)
            b_gu[1, s, :, lanes] = column(s, 4 + per + k)
            a_down[s, :, lanes] = column(s, 4 + 2 * per + k)


def unpack(grad, layer, sets, rank_own, rank_row, hidden):
    sets_own = sets.shape[0]
    width = grad.shape[1]
    shape = jax.ShapeDtypeStruct
    return pl.pallas_call(
        functools.partial(unpack_kernel, rank_own, rank_row),
        out_shape=[
            shape(layer.shape, low),
            shape(grad.shape, wide),
            shape((3, sets_own, rank_own, width), wide),
            shape((3, sets_own, rank_row, width), wide),
            shape((sets_own, rank_row, width), wide),
            shape((sets_own, rank_own, width), wide),
            shape((2, sets_own, rank_own, width), wide),
            shape((2, sets_own, rank_row, hidden), wide),
            shape((sets_own, rank_row, hidden), wide),
            shape((sets_own, rank_own, width), wide),
        ],
        in_specs=[VM] * 3,
        out_specs=[VM] * 10,
        name="unpack",
    )(grad, layer, sets)


def middle_kernel(n, nr, m, hop, cuts, head_ref, x_hbm, cot_hbm, gain_ref, wo_hbm, wg_hbm, wd_hbm,
                  table_ref, ao_ref, bg_ref, ad_ref,
                  dhead_ref, out_half, grad_half, full_ref, co_ref, cg_ref, cd_ref,
                  wo, wg, wd, x_half, cot_half, raw, attn, d_attn, h_all, df_all, da_all, gu, part,
                  recv_right, recv_left, hid, red_gu, red_down, back_gu, back_down,
                  sems_send, sems_recv, send_in, recv_in, send_out, recv_out, local_in, local_out, load,
                  send_g, recv_g, local_g, send_d, recv_d, local_d):
    g, r, c = lax.axis_index("dp"), lax.axis_index("row"), lax.axis_index("col")
    ag_ref = table_ref.at[3 * RANK:5 * RANK]
    bo_ref = table_ref.at[5 * RANK:6 * RANK]
    bd_ref = table_ref.at[6 * RANK:]
    rows_all, width_all = part.shape
    half = rows_all // 2
    own = rows_all // n
    tree_part = own * nr
    chunks = half // m
    blocks = 4
    band = half // blocks
    hidden = ad_ref.shape[1]
    width = width_all // nr
    left = {"col": jnp.maximum(c - 1, 0)}
    right = {"col": jnp.minimum(c + 1, n - 1)}
    first = c == 0
    last = c == n - 1
    inner = jnp.logical_and(c > 0, c < n - 1)

    base = jnp.where(last, half, 0)
    a_cut = hidden // 4
    share_g = Share(wg_hbm, wg, cuts, (send_g, recv_g, local_g))
    share_d = Share(wd_hbm, wd, cuts // 2, (send_d, recv_d, local_d))
    loads = [pltpu.make_async_copy(wo_hbm, wo, load.at[0])]
    load_x = pltpu.make_async_copy(x_hbm.at[span(base, half)], x_half, load.at[1])
    load_cot = pltpu.make_async_copy(cot_hbm, cot_half, load.at[2])
    loads[0].start()

    def piece_in(d, b):
        peer = lax.rem(r + d, nr)
        return remote(
            head_ref.at[span(b * tree_part + peer * own, own)],
            attn.at[span(b * own, own), span(r * HEAD, HEAD)],
            send_in.at[d - 1, b], recv_in.at[d - 1, b], {"row": peer},
        )

    def local_piece_in(b):
        return pltpu.make_async_copy(
            head_ref.at[span(b * tree_part + r * own, own)],
            attn.at[span(b * own, own), span(r * HEAD, HEAD)], local_in.at[b]
        )

    def piece_out(d, b):
        peer = lax.rem(r + d, nr)
        return remote(
            d_attn.at[span(b * own, own), span(peer * HEAD, HEAD)],
            dhead_ref.at[span(b * tree_part + r * own, own)],
            send_out.at[d - 1, b], recv_out.at[d - 1, b], {"row": peer},
        )

    def local_piece_out(b):
        return pltpu.make_async_copy(
            d_attn.at[span(b * own, own), span(r * HEAD, HEAD)],
            dhead_ref.at[span(b * tree_part + r * own, own)], local_out.at[b]
        )

    for b in range(n):
        local_piece_in(b).start()
    barrier = pltpu.get_barrier_semaphore()
    for d in range(1, nr):
        pl.semaphore_signal(barrier, inc=1, device_id={"row": lax.rem(r + d, nr)}, device_id_type=MESH)

    @pl.when(c > 0)
    def _():
        pl.semaphore_signal(barrier, inc=1, device_id=left, device_id_type=MESH)

    @pl.when(c < n - 1)
    def _():
        pl.semaphore_signal(barrier, inc=1, device_id=right, device_id_type=MESH)

    pl.semaphore_signal(barrier, inc=1, device_id={"dp": flip(g)}, device_id_type=MESH)
    full_ref[...] = jnp.zeros_like(full_ref)
    co_ref[...] = jnp.zeros_like(co_ref)
    cg_ref[...] = jnp.zeros_like(cg_ref)
    cd_ref[...] = jnp.zeros_like(cd_ref)

    @pl.when(inner)
    def _():
        pl.semaphore_wait(barrier, nr + 2)

    @pl.when(jnp.logical_not(inner))
    def _():
        pl.semaphore_wait(barrier, nr + 1)

    middle = n // 2
    for b in range(middle):
        for block in (b, middle + b):
            for d in range(1, nr):
                piece_in(d, block).start()
    load_x.start()
    load_cot.start()
    share_g.start_far()
    share_d.start_far()
    share_g.start_near()
    share_d.start_near()

    def rows(j, start=0):
        return span(start + j * m, m)

    def band_rows(b):
        return span(b * band, band), span(half + b * band, band)

    def take(ref, b):
        low_rows, high_rows = band_rows(b)
        return jnp.concatenate([ref[low_rows, :], ref[high_rows, :]], axis=0)

    def put(b, lanes, value):
        low_rows, high_rows = band_rows(b)
        part[low_rows, lanes] = value[:band].astype(low)
        part[high_rows, lanes] = value[band:].astype(low)

    def relay_stage(stage, per, work, owner_step, all_ref, pump=None):
        def send(kind, j, src, dst, to):
            return remote(src, dst, sems_send.at[stage, kind, j], sems_recv.at[stage, kind, j], to)

        def reduce_right(j):
            return send(0, j, part.at[rows(j, half)], recv_right.at[rows(j)], right)

        def reduce_left(j):
            return send(1, j, part.at[rows(j)], recv_left.at[rows(j)], left)

        def spread_left(j):
            return send(2, j, all_ref.at[rows(j, half)], all_ref.at[rows(j, half)], left)

        def spread_right(j):
            return send(3, j, all_ref.at[rows(j)], all_ref.at[rows(j)], right)

        total_slices = per * blocks
        each = chunks // blocks

        def slices_before(i):
            late = per + (jnp.maximum(i - per, 0) * per) // each
            return jnp.minimum(jnp.where(i < per, i, late), total_slices)

        @pl.loop(0, per + chunks + hop * 2 * (n - 1))
        def _(ii):
            i = ii - per

            def on(offset, who, run):
                j = i - offset

                @pl.when(jnp.logical_and(who, jnp.logical_and(j >= 0, j < chunks)))
                def _():
                    run(j)

            def mid_right(j):
                reduce_right(j).wait_recv()
                at = rows(j, half)
                part[at, :] = (part[at, :].astype(wide) + recv_right[rows(j), :].astype(wide)).astype(low)
                reduce_right(j).start()

            def mid_left(j):
                reduce_left(j).wait_recv()
                at = rows(j)
                part[at, :] = (part[at, :].astype(wide) + recv_left[at, :].astype(wide)).astype(low)
                reduce_left(j).start()

            def end_right(j):
                reduce_right(j).wait_recv()
                total = part[rows(j, half), :].astype(wide) + recv_right[rows(j), :].astype(wide)
                all_ref[rows(j, half), :] = owner_step(total, rows(j))
                spread_left(j).start()

            def end_left(j):
                reduce_left(j).wait_recv()
                total = part[rows(j), :].astype(wide) + recv_left[rows(j), :].astype(wide)
                all_ref[rows(j), :] = owner_step(total, rows(j))
                spread_right(j).start()

            def pass_left(j):
                spread_left(j).wait_recv()
                spread_left(j).start()

            def pass_right(j):
                spread_right(j).wait_recv()
                spread_right(j).start()

            on(0, first, lambda j: reduce_right(j).start())
            on(0, last, lambda j: reduce_left(j).start())
            on(hop * c, inner, mid_right)
            on(hop * (n - 1 - c), inner, mid_left)
            on(hop * (n - 1), last, end_right)
            on(hop * (n - 1), first, end_left)
            on(hop * (2 * (n - 1) - c), inner, pass_left)
            on(hop * (n - 1 + c), inner, pass_right)

            @pl.loop(slices_before(ii), slices_before(ii + 1))
            def _(t):
                work(t // per, lax.rem(t, per))

            if pump is not None:
                pump(ii)

        @pl.loop(0, chunks)
        def _(j):
            @pl.when(first)
            def _():
                reduce_right(j).wait_send()
                spread_right(j).wait_send()
                spread_left(j).wait_recv()

            @pl.when(last)
            def _():
                reduce_left(j).wait_send()
                spread_left(j).wait_send()
                spread_right(j).wait_recv()

            @pl.when(inner)
            def _():
                reduce_right(j).wait_send()
                reduce_left(j).wait_send()
                spread_left(j).wait_send()
                spread_right(j).wait_send()

    def shard(j, ref):
        return slice(j * (ref.shape[0] // nr), (j + 1) * (ref.shape[0] // nr))

    def out_work(b, k):
        @pl.when(b == 0)
        def _():
            loads[0].wait()

        @pl.when(lax.rem(b, blocks // middle) == 0)
        def _():
            at = b // (blocks // middle)
            for block in (at, middle + at):
                for d in range(1, nr):
                    piece_in(d, block).wait_recv()
                local_piece_in(block).wait()

        rows_in = take(attn, b)
        red = dot_t(rows_in, ao_ref[...]).astype(low)
        for j in range(nr):
            lanes = slice(j * width, (j + 1) * width)
            put(b, lanes, dot(rows_in, wo[shard(j, wo), :]) + dot(red, bo_ref[:, lanes]))

    gain_a = gain_ref[0:1, :]
    gain_f = gain_ref[1:2, :]

    def attn_owner(total, at):
        raw[at, :] = total
        flat = total * norm_factor(row_sum(total * total))
        return (x_half[at, :].astype(wide) + flat * gain_a).astype(low)

    first_pass = 5
    apart = 3
    late = 2
    passes = cuts + cuts // 2

    def pump(ii):
        at = ii - first_pass

        @pl.when(jnp.logical_and(at >= 0, lax.rem(at, apart) == 0))
        def _():
            t = at // apart

            @pl.when(t < cuts)
            def _():
                share_g.pass_far(t)

            @pl.when(jnp.logical_and(t >= cuts, t < passes))
            def _():
                share_d.pass_far(t - cuts)

            t = t - late

            @pl.when(jnp.logical_and(t >= 0, t < cuts))
            def _():
                share_g.pass_twin(t)

            @pl.when(jnp.logical_and(t >= cuts, t < passes))
            def _():
                share_d.pass_twin(t - cuts)

    load_x.wait()
    relay_stage(0, 1, out_work, attn_owner, h_all, pump)
    in_loop = 1 + chunks + hop * 2 * (n - 1)

    @pl.loop(in_loop, jnp.maximum(in_loop, first_pass + apart * (passes + late)))
    def _(ii):
        pump(ii)

    share_g.wait_all()

    def gate_slice(b, k):
        rows_in = take(h_all, b)

        @pl.when(k == 0)
        def _():
            red_gu[b] = dot_t(rows_in, ag_ref[...]).astype(low)

        at = pl.multiple_of(k * a_cut, a_cut)
        lanes = pl.ds(at, a_cut)
        up_lanes = pl.ds(pl.multiple_of(hidden + at, a_cut), a_cut)
        red = red_gu[b]
        gate = dot(rows_in, wg[:, lanes]) + dot(red[:, :RANK], bg_ref[0, :, lanes])
        up = dot(rows_in, wg[:, up_lanes]) + dot(red[:, RANK:], bg_ref[1, :, lanes])
        gu[b, :, lanes] = gate.astype(low)
        gu[b, :, up_lanes] = up.astype(low)
        hid[:, lanes] = (gate * jax.nn.sigmoid(gate) * up).astype(low)

    def down_slice(b, k):
        @pl.when(jnp.logical_and(b == 0, k == 0))
        def _():
            share_d.wait_all()

        rows_in = hid[:, :hidden]

        @pl.when(k == 0)
        def _():
            red_down[b] = dot_t(rows_in, ad_ref[...]).astype(low)

        for s in range(nr // 2):
            j = k * (nr // 2) + s
            lanes = span(j * width, width)
            down_rows = pl.ds(pl.multiple_of(j * hidden, hidden), hidden)
            put(b, lanes, dot(rows_in, wd[down_rows, :]) + dot(red_down[b], bd_ref[:, lanes]))

    def ffn_work(b, k):
        @pl.when(k < 4)
        def _():
            gate_slice(b, k)

        @pl.when(k >= 4)
        def _():
            down_slice(b, k - 4)

    def ffn_owner(total, at):
        a_raw = raw[at, :]
        h = x_half[at, :].astype(wide) + a_raw * norm_factor(row_sum(a_raw * a_raw)) * gain_a
        factor = norm_factor(row_sum(total * total))
        flat = total * factor
        out_half[at, :] = (h + flat * gain_f).astype(low)
        scaled = cot_half[at, :].astype(wide) * gain_f
        return (factor * (scaled - flat * (row_sum(scaled * flat) * (1.0 / D)))).astype(low)

    load_cot.wait()
    relay_stage(1, 6, ffn_work, ffn_owner, df_all)

    b_cut = hidden // 2

    def hidden_back(b, k):
        rows_in = take(df_all, b)

        @pl.when(k == 0)
        def _():
            back_down[...] = dot_t(rows_in, bd_ref[...]).astype(low)

        at = pl.multiple_of(k * b_cut, b_cut)
        lanes = pl.ds(at, b_cut)
        up_lanes = pl.ds(pl.multiple_of(hidden + at, b_cut), b_cut)
        back = back_down[...]
        grad = dot(back, ad_ref[:, lanes])
        for j in range(nr):
            down_rows = pl.ds(pl.multiple_of(j * hidden + at, b_cut), b_cut)
            grad = grad + dot_t(rows_in[:, j * width:(j + 1) * width], wd[down_rows, :])
        gate = gu[b, :, lanes].astype(wide)
        up = gu[b, :, up_lanes].astype(wide)
        sigma = jax.nn.sigmoid(gate)
        silu = gate * sigma
        d_gate = (grad * up * sigma * (1.0 + gate * (1.0 - sigma))).astype(low)
        d_up = (grad * silu).astype(low)
        hid[:, lanes] = d_gate
        hid[:, up_lanes] = d_up
        cd_ref[:, lanes] += t_dot(back, (silu * up).astype(low))
        red = red_gu[b]
        cg_ref[0, :, lanes] += t_dot(red[:, :RANK], d_gate)
        cg_ref[1, :, lanes] += t_dot(red[:, RANK:], d_up)

    o_cut = width_all // 4

    def gate_back(b, k):
        @pl.when(k == 0)
        def _():
            back_gu[:, :RANK] = dot_t(hid[:, :hidden], bg_ref[0]).astype(low)
            back_gu[:, RANK:] = dot_t(hid[:, hidden:], bg_ref[1]).astype(low)

        lanes = span(k * o_cut, o_cut)
        put(b, lanes, dot_t(hid[...], wg[lanes, :]) + dot(back_gu[...], ag_ref[:, lanes]))

        @pl.when(k == 3)
        def _():
            full_ref[:2 * RANK, :] += t_dot(back_gu[...], take(h_all, b))
            full_ref[3 * RANK:, :] += t_dot(red_down[b], take(df_all, b))

    def back_work(b, k):
        @pl.when(k < 2)
        def _():
            hidden_back(b, k)

        @pl.when(k >= 2)
        def _():
            gate_back(b, k - 2)

    def back_owner(total, at):
        grad = cot_half[at, :].astype(wide) + total
        grad_half[at, :] = grad
        a_raw = raw[at, :]
        factor = norm_factor(row_sum(a_raw * a_raw))
        flat = a_raw * factor
        scaled = grad * gain_a
        return (factor * (scaled - flat * (row_sum(scaled * flat) * (1.0 / D)))).astype(low)

    relay_stage(2, 6, back_work, back_owner, da_all)

    @pl.loop(0, n)
    def _(b):
        at = span(b * own, own)
        rows_in = da_all[at, :]
        back = dot_t(rows_in, bo_ref[...]).astype(low)
        grad = dot(back, ao_ref[...])
        for j in range(nr):
            grad = grad + dot_t(rows_in[:, j * width:(j + 1) * width], wo[shard(j, wo), :])
        d_attn[at, :] = grad.astype(low)
        for d in range(1, nr):
            piece_out(d, b).start()
        local_piece_out(b).start()
        attn_rows = attn[at, :]
        co_ref[...] += t_dot(back, attn_rows)
        red = dot_t(attn_rows, ao_ref[...]).astype(low)
        full_ref[2 * RANK:3 * RANK, :] += t_dot(red, rows_in)

    @pl.loop(0, n)
    def _(b):
        for d in range(1, nr):
            piece_in(d, b).wait_send()
            piece_out(d, b).wait()
        local_piece_out(b).wait()

    share_g.drain()
    share_d.drain()


def middle(attn_head, x, cot_half, gains, w_out, w_gu, w_down, table, a_out, b_gu, a_down, n, nr, m=16, hop=2, cuts=8):
    group, width_all = x.shape
    half = group // 2
    width = width_all // nr
    hidden = a_down.shape[1]
    chunks = half // m
    band = group // 4
    dma = pltpu.SemaphoreType.DMA
    any_space = pl.BlockSpec(memory_space=pl.ANY)
    shape = jax.ShapeDtypeStruct
    return pl.pallas_call(
        functools.partial(middle_kernel, n, nr, m, hop, cuts),
        out_shape=[
            shape(attn_head.shape, low),
            shape((half, width_all), low),
            shape((half, width_all), wide),
            shape((4 * RANK, width_all), wide),
            shape((RANK, a_out.shape[1]), wide),
            shape((2, RANK, hidden), wide),
            shape((RANK, hidden), wide),
        ],
        in_specs=[VM, any_space, any_space, VM, any_space, any_space, any_space] + [VM] * 4,
        out_specs=[VM] * 7,
        scratch_shapes=[
            pltpu.VMEM(w_out.shape, low),
            pltpu.VMEM((w_gu.shape[0] * nr, w_gu.shape[1]), low),
            pltpu.VMEM((w_down.shape[0] * nr, w_down.shape[1]), low),
            pltpu.VMEM((half, width_all), low),
            pltpu.VMEM((half, width_all), low),
            pltpu.VMEM((half, width_all), wide),
            pltpu.VMEM((group, a_out.shape[1]), low),
            pltpu.VMEM((group, a_out.shape[1]), low),
            pltpu.VMEM((group, width_all), low),
            pltpu.VMEM((group, width_all), low),
            pltpu.VMEM((group, width_all), low),
            pltpu.VMEM((4, band, 2 * hidden), low),
            pltpu.VMEM((group, width_all), low),
            pltpu.VMEM((half, width_all), low),
            pltpu.VMEM((half, width_all), low),
            pltpu.VMEM((band, 2 * hidden), low),
            pltpu.VMEM((4, band, 2 * RANK), low),
            pltpu.VMEM((4, band, RANK), low),
            pltpu.VMEM((band, 2 * RANK), low),
            pltpu.VMEM((band, RANK), low),
            dma((3, 4, chunks)), dma((3, 4, chunks)),
            dma((nr - 1, n)), dma((nr - 1, n)), dma((nr - 1, n)), dma((nr - 1, n)), dma((n,)), dma((n,)),
            dma((3,)),
        ] + share_sems(cuts) + share_sems(cuts // 2),
        compiler_params=pltpu.CompilerParams(collective_id=0, has_side_effects=True, vmem_limit_bytes=67043328),
        name="middle",
    )(attn_head, x, cot_half, gains, w_out, w_gu, w_down, table, a_out, b_gu, a_down)


def per_device(
    tokens,
    cotangent,
    seg_ids,
    positions,
    parents,
    tree_sets,
    gain_q,
    gain_k,
    gain_attn,
    gain_ffn,
    query_key_value_weight,
    output_weight,
    gate_up_weight,
    down_weight,
    query_key_value_adapter_first,
    query_key_value_adapter_second,
    output_adapter_first,
    output_adapter_second,
    gate_up_adapter_first,
    gate_up_adapter_second,
    down_adapter_first,
    down_adapter_second,
):
    dp_count = lax.axis_size("dp")
    row_count = lax.axis_size("row")
    col_count = lax.axis_size("col")
    row_at = lax.axis_index("row")
    tree_tokens = seg_ids.shape[0]
    assert tree_sets.shape[0] == 1 and col_count == 4
    set_count = output_adapter_first.shape[0]
    own = tokens.shape[0] // row_count
    group = own * col_count
    width_row = tokens.shape[1]
    width_col = gain_q.shape[0]
    hidden_col = down_weight.shape[0]
    tree_set = tree_sets[0]

    tables = (
        query_key_value_adapter_first,
        query_key_value_adapter_second,
        output_adapter_first,
        output_adapter_second,
        gate_up_adapter_first,
        gate_up_adapter_second,
        down_adapter_first,
        down_adapter_second,
    )
    narrow, b_qkv, a_out, b_gu, a_down = prep(tree_sets, tables)
    gain_pair = jnp.pad(jnp.stack([gain_attn, gain_ffn]), ((0, 6), (0, 0)))
    pos_own = lax.dynamic_index_in_dim(
        positions.reshape(col_count, row_count, own), row_at, 1, keepdims=False
    ).reshape(group)
    cosine, sine = angles(pos_own)
    cos2 = jnp.concatenate([cosine, cosine], axis=1)
    sin2 = jnp.concatenate([-sine, sine], axis=1)
    gq, gk = gain_q[None, :], gain_k[None, :]
    parent_at, branch_flag = tree_tables(seg_ids, parents)
    x, table, gains, g_half, raw, factors, qkv_head, w_qkv, w_out = front(
        tokens,
        narrow,
        gain_pair,
        cotangent,
        query_key_value_weight.reshape(width_row, 3 * width_col),
        output_weight,
        b_qkv,
        gq,
        gk,
        cos2,
        sin2,
        col_count,
        row_count,
    )
    attn_head, lse = attend(qkv_head, parent_at, branch_flag)
    d_attn_head, out_half, d_h_half, full_mid, part_ao, part_bgu, part_ad = middle(
        attn_head,
        x,
        g_half,
        gains,
        w_out,
        gate_up_weight.reshape(width_row, 2 * hidden_col),
        down_weight,
        table,
        a_out,
        b_gu,
        a_down,
        col_count,
        row_count,
    )
    d_qkv_head = attend_back(qkv_head, d_attn_head, parent_at, branch_flag, lse)
    hot = (tree_set == lax.broadcasted_iota(jnp.int32, (set_count, width_row), 0)).astype(wide)
    in_grad, layer, sets = rear(
        d_qkv_head,
        raw,
        factors,
        gq,
        gk,
        cos2,
        sin2,
        out_half,
        x,
        w_qkv,
        table,
        b_qkv,
        d_h_half,
        full_mid,
        part_ao,
        part_bgu,
        part_ad,
        hot,
        set_count // dp_count,
        col_count,
        row_count,
        dp_count,
    )
    return tuple(unpack(in_grad, layer, sets, RANK // col_count, RANK // row_count, hidden_col))


def solution(mesh):
    in_specs = (
        P(("dp", "col"), "row"),
        P(("dp", "col"), "row"),
        P("dp"),
        P("dp"),
        P("dp", None),
        P("dp"),
        P("col"),
        P("col"),
        P("row"),
        P("row"),
        P("row", None, "col"),
        P("col", "row"),
        P("row", None, "col"),
        P("col", "row"),
        P(None, None, None, "row"),
        P(None, None, None, "col"),
        P(None, None, "col"),
        P(None, None, "row"),
        P(None, None, None, "row"),
        P(None, None, None, "col"),
        P(None, None, "col"),
        P(None, None, "row"),
    )
    out_specs = (
        P(("dp", "col"), "row"),
        P(("dp", "col"), "row"),
        P(None, "dp", "col", "row"),
        P(None, "dp", "row", "col"),
        P("dp", "row", "col"),
        P("dp", "col", "row"),
        P(None, "dp", "col", "row"),
        P(None, "dp", "row", "col"),
        P("dp", "row", "col"),
        P("dp", "col", "row"),
    )
    return jax.shard_map(
        per_device, mesh=mesh, in_specs=in_specs, out_specs=out_specs, check_vma=False
    )
```

```python
import functools

import jax
import jax.numpy as jnp
from jax import lax
from jax.experimental import pallas as pl
from jax.experimental.pallas import tpu as pltpu
from jax.sharding import PartitionSpec as P

D = 2048
HEAD = 128
RANK = 16
SEG = 128
TRUNK = 1024
QT = 256
MESH = pl.DeviceIdType.MESH
VM = pl.BlockSpec(memory_space=pltpu.VMEM)
precise = lax.Precision.HIGHEST

epsilon = 1e-06
rope_base = 500000.0
masked_out = -1e30
low = jnp.bfloat16
wide = jnp.float32
last_last = (((1,), (1,)), ((), ()))
first_first = (((0,), (0,)), ((), ()))


def dot(left, right):
    return jnp.dot(left, right, preferred_element_type=wide)


def dot_t(left, right):
    return lax.dot_general(left, right, last_last, preferred_element_type=wide)


def t_dot(left, right):
    return lax.dot_general(left, right, first_first, preferred_element_type=wide)


def angles(positions):
    half_width = HEAD // 2
    frequency = rope_base ** (-(jnp.arange(half_width, dtype=wide) * 2.0) / HEAD)
    angle_table = positions.astype(wide)[:, None] * frequency[None, :]
    return (jnp.cos(angle_table), jnp.sin(angle_table))


def norm_factor(square_sum):
    return lax.rsqrt(square_sum * (1.0 / D) + epsilon)


def tree_tables(seg_ids, parents):
    tail_seg = seg_ids[TRUNK::SEG]
    labels = jnp.arange(parents.shape[1], dtype=jnp.int32)
    tail_parent = jnp.sum(jnp.where(tail_seg[:, None] == labels[None, :], parents[0][None, :], 0), axis=1)
    hit = (tail_seg[None, :] == tail_parent[:, None])
    at = jnp.arange(tail_seg.shape[0], dtype=jnp.int32) + TRUNK // SEG
    parent_at = jnp.sum(jnp.where(hit, at[None, :], 0), axis=1)
    bias = jnp.where(tail_parent > 0, 0.0, masked_out).astype(wide)
    return parent_at, jnp.broadcast_to(bias[:, None], (tail_seg.shape[0], SEG))


def row_sum(v): return jnp.sum(v, axis=1, keepdims=True)

def params(collective):
    return pltpu.CompilerParams(collective_id=collective, has_side_effects=True, vmem_limit_bytes=60 << 20)


def span(at, size):
    return pl.ds(pl.multiple_of(at, size), size)


def remote(src, dst, send_sem, recv_sem, to):
    return pltpu.make_async_remote_copy(
        src_ref=src, dst_ref=dst, send_sem=send_sem, recv_sem=recv_sem, device_id=to, device_id_type=MESH
    )


def greet(n, nr, extra=0):
    r, c = lax.axis_index("row"), lax.axis_index("col")
    me = r * n + c
    barrier = pltpu.get_barrier_semaphore()

    @pl.loop(1, n * nr)
    def _(d):
        peer = lax.rem(me + d, n * nr)
        pl.semaphore_signal(barrier, inc=1, device_id={"row": peer // n, "col": lax.rem(peer, n)}, device_id_type=MESH)

    pl.semaphore_wait(barrier, n * nr - 1 + extra)


def row_sums(first, second):
    ones = jnp.ones((8, first.shape[1]), wide)
    at = lax.broadcasted_iota(jnp.int32, (8, first.shape[0]), 0)
    sum_first = lax.dot_general(ones, first, last_last, preferred_element_type=wide, precision=precise)
    sum_second = lax.dot_general(ones, second, last_last, preferred_element_type=wide, precision=precise)
    return jnp.where(at < 4, sum_first, sum_second)


def down_columns(values, at):
    pick = (lax.broadcasted_iota(jnp.int32, (8, HEAD), 0) == at).astype(wide)
    return lax.dot_general(values, pick, first_first, preferred_element_type=wide, precision=precise)


def flip(v):
    return v + 1 - 2 * lax.rem(v, 2)


class Share:
    def __init__(self, src, dst, cuts, sems):
        self.send, self.recv, self.local = sems
        self.src, self.cuts = src, cuts
        g, r = lax.axis_index("dp"), lax.axis_index("row")
        size = src.shape[0]
        half = size // 2
        step = half // cuts
        far = lax.rem(r + 2, 4)
        mine = lax.rem(g, 2)
        near_to, far_to, twin_to = {"row": flip(r)}, {"row": far}, {"dp": flip(g)}

        def rows(shard, part, i):
            return pl.ds(pl.multiple_of(shard * size + part * half + i * step, step), step)

        def copy(kind, i, src, dst, to):
            return remote(src, dst, self.send.at[kind, i], self.recv.at[kind, i], to)

        def hand(kind, part, to):
            return lambda i: copy(kind, i, dst.at[rows(far, part, i)], dst.at[rows(far, part, i)], to)

        whole = span(r * size, size)
        self.own = pltpu.make_async_copy(src, dst.at[whole], self.local)
        self.near = copy(0, 0, src, dst.at[whole], near_to)
        self.far = lambda i: copy(
            1, i, src.at[pl.ds(pl.multiple_of(mine * half + i * step, step), step)], dst.at[rows(r, mine, i)], far_to
        )
        self.far_near = hand(2, mine, near_to)
        self.far_twin = hand(3, mine, twin_to)
        self.twin_near = hand(4, 1 - mine, near_to)

    def start_far(self):
        for i in range(self.cuts):
            self.far(i).start()

    def start_near(self):
        self.own.start()
        self.near.start()

    def pass_far(self, i):
        self.far(i).wait_recv()
        self.far_twin(i).start()
        self.far_near(i).start()

    def pass_twin(self, i):
        self.far_twin(i).wait_recv()
        self.twin_near(i).start()

    def wait_all(self):
        self.own.wait()
        self.near.wait_recv()
        for i in range(self.cuts):
            self.far_near(i).wait_recv()
            self.twin_near(i).wait_recv()

    def drain(self):
        self.near.wait_send()
        for i in range(self.cuts):
            self.far(i).wait_send()
            self.far_near(i).wait_send()
            self.far_twin(i).wait_send()
            self.twin_near(i).wait_send()


def share_sems(cuts):
    dma = pltpu.SemaphoreType.DMA
    return [dma((5, cuts)), dma((5, cuts)), dma]


def prep_kernel(set_ref, fq_ref, sq_ref, fo_ref, so_ref, fg_ref, sg_ref, fd_ref, sd_ref,
                narrow_ref, bq_ref, ao_ref, bg_ref, ad_ref):
    for j in range(3):
        narrow_ref[j * RANK:(j + 1) * RANK, :] = fq_ref[j, 0].astype(low)
        bq_ref[j * RANK:(j + 1) * RANK, :] = sq_ref[j, 0].astype(low)
    for j in range(2):
        narrow_ref[(3 + j) * RANK:(4 + j) * RANK, :] = fg_ref[j, 0].astype(low)
        bg_ref[j] = sg_ref[j, 0].astype(low)
    narrow_ref[5 * RANK:6 * RANK, :] = so_ref[0].astype(low)
    narrow_ref[6 * RANK:, :] = sd_ref[0].astype(low)
    ao_ref[...] = fo_ref[0].astype(low)
    ad_ref[...] = fd_ref[0].astype(low)


def prep(tree_sets, tables):
    fq, sq, fo, so, fg, sg, fd, sd = tables

    def pick(table):
        if table.ndim == 4:
            return pl.BlockSpec((table.shape[0], 1) + table.shape[2:], lambda i, s: (0, s[0], 0, 0))
        return pl.BlockSpec((1,) + table.shape[1:], lambda i, s: (s[0], 0, 0))

    def out(*shape):
        return pl.BlockSpec(shape, lambda i, s: (0,) * len(shape)), jax.ShapeDtypeStruct(shape, low)

    outs = [
        out(7 * RANK, fq.shape[-1]), out(3 * RANK, sq.shape[-1]), out(RANK, fo.shape[-1]),
        out(2, RANK, sg.shape[-1]), out(RANK, fd.shape[-1]),
    ]
    return pl.pallas_call(
        prep_kernel,
        grid_spec=pltpu.PrefetchScalarGridSpec(
            num_scalar_prefetch=1, grid=(1,), in_specs=[pick(t) for t in tables], out_specs=[o[0] for o in outs]
        ),
        out_shape=[o[1] for o in outs],
        name="prep",
    )(tree_sets, *tables)


def lower_mask(size):
    return lax.broadcasted_iota(jnp.int32, (size, size), 1) <= lax.broadcasted_iota(jnp.int32, (size, size), 0)


def softmax_parts(parts):
    top = jnp.max(parts[0], axis=1, keepdims=True)
    for s in parts[1:]:
        top = jnp.maximum(top, jnp.max(s, axis=1, keepdims=True))
    raised = [jnp.exp(s - top) for s in parts]
    total = jnp.sum(raised[0], axis=1, keepdims=True)
    for e in raised[1:]:
        total = total + jnp.sum(e, axis=1, keepdims=True)
    inverse = 1.0 / total
    return [e * inverse for e in raised], top + jnp.log(total)


def tail_parts(q, qkv, at, parent, flag):
    scale = HEAD ** -0.5
    k_lanes = slice(HEAD, 2 * HEAD)
    trunk = dot_t(q, qkv[:TRUNK, k_lanes]) * scale
    branch = dot_t(q, qkv[pl.ds(parent, SEG), k_lanes]) * scale + flag
    own = jnp.where(lower_mask(SEG), dot_t(q, qkv[pl.ds(at, SEG), k_lanes]) * scale, masked_out)
    return [trunk, branch, own]


def trunk_parts(q, qkv, i):
    scale = HEAD ** -0.5
    k_lanes = slice(HEAD, 2 * HEAD)
    own = dot_t(q, qkv[i * QT:(i + 1) * QT, k_lanes]) * scale
    parts = [jnp.where(lower_mask(QT), own, masked_out)]
    if i:
        parts.append(dot_t(q, qkv[:i * QT, k_lanes]) * scale)
    return parts


def attend_body(parent_ref, flag_ref, qkv, o_ref, lse_ref):
    v_lanes = slice(2 * HEAD, 3 * HEAD)
    for i in range(TRUNK // QT):
        at = slice(i * QT, (i + 1) * QT)
        p, lse = softmax_parts(trunk_parts(qkv[at, :HEAD], qkv, i))
        o = dot(p[0].astype(low), qkv[at, v_lanes])
        if i:
            o = o + dot(p[1].astype(low), qkv[:i * QT, v_lanes])
        o_ref[at, :] = o.astype(low)
        lse_ref[at, :] = lse

    @pl.loop(0, (qkv.shape[0] - TRUNK) // SEG)
    def _(j):
        at = pl.multiple_of(TRUNK + j * SEG, SEG)
        parent = pl.multiple_of(parent_ref[j] * SEG, SEG)
        rows = pl.ds(at, SEG)
        p, lse = softmax_parts(tail_parts(qkv[rows, :HEAD], qkv, at, parent, flag_ref[pl.ds(j, 1), :]))
        o = dot(p[0].astype(low), qkv[:TRUNK, v_lanes])
        o = o + dot(p[1].astype(low), qkv[pl.ds(parent, SEG), v_lanes])
        o = o + dot(p[2].astype(low), qkv[rows, v_lanes])
        o_ref[rows, :] = o.astype(low)
        lse_ref[rows, :] = lse


def back_parts(scores, lse, d_out, keys, values):
    probs = [jnp.exp(s - lse) for s in scores]
    grads = [dot_t(d_out, v) for v in values]
    inner = sum(jnp.sum(p * g, axis=1, keepdims=True) for p, g in zip(probs, grads))
    d_scores = [(p * (g - inner)).astype(low) for p, g in zip(probs, grads)]
    dq = sum(dot(d, k) for d, k in zip(d_scores, keys))
    return d_scores, [p.astype(low) for p in probs], dq


def attend_back_kernel(parent_ref, flag_ref, qkv, do_ref, lse_ref, d_ref, dk_acc, dv_acc):
    scale = HEAD ** -0.5
    k_lanes = slice(HEAD, 2 * HEAD)
    v_lanes = slice(2 * HEAD, 3 * HEAD)
    dk_acc[...] = jnp.zeros_like(dk_acc)
    dv_acc[...] = jnp.zeros_like(dv_acc)
    for i in range(TRUNK // QT):
        at = slice(i * QT, (i + 1) * QT)
        spans = [at] + ([slice(0, i * QT)] if i else [])
        q, d_out = qkv[at, :HEAD], do_ref[at, :]
        d_scores, probs, dq = back_parts(
            trunk_parts(q, qkv, i), lse_ref[at, :], d_out, [qkv[s, k_lanes] for s in spans], [qkv[s, v_lanes] for s in spans]
        )
        d_ref[at, :HEAD] = (dq * scale).astype(low)
        for s, d, p in zip(spans, d_scores, probs):
            dk_acc[s, :] += t_dot(d, q)
            dv_acc[s, :] += t_dot(p, d_out)

    @pl.loop(0, (qkv.shape[0] - TRUNK) // SEG)
    def _(j):
        at = pl.multiple_of(TRUNK + j * SEG, SEG)
        parent = pl.multiple_of(parent_ref[j] * SEG, SEG)
        rows = pl.ds(at, SEG)
        spans = [slice(0, TRUNK), pl.ds(parent, SEG), rows]
        q, d_out = qkv[rows, :HEAD], do_ref[rows, :]
        d_scores, probs, dq = back_parts(
            tail_parts(q, qkv, at, parent, flag_ref[pl.ds(j, 1), :]), lse_ref[rows, :], d_out,
            [qkv[s, k_lanes] for s in spans], [qkv[s, v_lanes] for s in spans],
        )
        d_ref[rows, :HEAD] = (dq * scale).astype(low)
        for s, d, p in zip(spans, d_scores, probs):
            dk_acc[s, :] += t_dot(d, q)
            dv_acc[s, :] += t_dot(p, d_out)

    d_ref[:, k_lanes] = (dk_acc[...] * scale).astype(low)
    d_ref[:, v_lanes] = dv_acc[...].astype(low)


def attend(qkv, parent_at, flag):
    n = qkv.shape[0]

    def whole(*shape):
        return pl.BlockSpec(shape, lambda i, *_: (0, 0))

    return pl.pallas_call(
        attend_body,
        grid_spec=pltpu.PrefetchScalarGridSpec(
            num_scalar_prefetch=1,
            grid=(1,),
            in_specs=[whole(*flag.shape), whole(n, 3 * HEAD)],
            out_specs=[whole(n, HEAD), whole(n, 1)],
        ),
        out_shape=[jax.ShapeDtypeStruct((n, HEAD), low), jax.ShapeDtypeStruct((n, 1), wide)],
        name="attend",
    )(parent_at, flag, qkv)


def attend_back(qkv, d_o, parent_at, flag, lse):
    n = qkv.shape[0]

    def whole(*shape):
        return pl.BlockSpec(shape, lambda i, *_: (0, 0))

    return pl.pallas_call(
        attend_back_kernel,
        grid_spec=pltpu.PrefetchScalarGridSpec(
            num_scalar_prefetch=1,
            grid=(1,),
            in_specs=[whole(*flag.shape), whole(n, 3 * HEAD), whole(n, HEAD), whole(n, 1)],
            out_specs=whole(n, 3 * HEAD),
            scratch_shapes=[pltpu.VMEM((n, HEAD), wide), pltpu.VMEM((n, HEAD), wide)],
        ),
        out_shape=jax.ShapeDtypeStruct((n, 3 * HEAD), low),
        name="attend_back",
    )(parent_at, flag, qkv, d_o, lse)


def front_kernel(n, nr, m, mh, tok_ref, table_ref, gain_ref, cot_ref, wq_hbm, wo_hbm, bq_ref, gq_ref, gk_ref,
                 cos_ref, sin_ref,
                 x_ref, table_all, gain_all, half_ref, raw_ref, factor_ref, qkv_ref, wq_out, wo_out,
                 wq, wo, stats, buf, fq, fk, red, cot_own,
                 send_a, recv_a, send_z, recv_z, send_t, recv_t, local_sem,
                 send_s, recv_s, send_h, recv_h, send_g, recv_g, local_h, local_g, send_e, recv_e,
                 send_q, recv_q, local_q, send_o, recv_o, local_o, out_sems):
    g, r, c = lax.axis_index("dp"), lax.axis_index("row"), lax.axis_index("col")
    own = tok_ref.shape[0] // nr
    width = tok_ref.shape[1]
    rows_all = own * n
    heads = width // HEAD
    tree_part = own * nr
    chunks = own // m
    left = {"col": jnp.maximum(c - 1, 0)}
    right = {"col": jnp.minimum(c + 1, n - 1)}
    share_q = Share(wq_hbm, wq, 2, (send_q, recv_q, local_q))
    share_o = Share(wo_hbm, wo, 2, (send_o, recv_o, local_o))

    def piece(d, j):
        peer = lax.rem(r + d, nr)
        return remote(
            tok_ref.at[span(peer * own + j * m, m)],
            x_ref.at[span(c * own + j * m, m), span(r * width, width)],
            send_a.at[d - 1, j], recv_a.at[d - 1, j], {"row": peer},
        )

    def block(kind, s, at, j, to):
        rows = span(at * own + j * m, m)
        return remote(x_ref.at[rows], x_ref.at[rows], send_z.at[kind, s, j], recv_z.at[kind, s, j], to)

    def table_piece(d, kind):
        src, dst = ((table_ref, table_all), (gain_ref, gain_all))[kind]
        to = {"row": lax.rem(r + d, nr)}
        return remote(src, dst.at[:, span(r * width, width)], send_t.at[kind, d - 1], recv_t.at[kind, d - 1], to)

    keep = pltpu.make_async_copy(
        tok_ref.at[span(r * own, own)], x_ref.at[span(c * own, own), span(r * width, width)], local_sem.at[0]
    )
    keep_table = pltpu.make_async_copy(table_ref, table_all.at[:, span(r * width, width)], local_sem.at[1])
    keep_gain = pltpu.make_async_copy(gain_ref, gain_all.at[:, span(r * width, width)], local_sem.at[2])
    keep.start()
    keep_table.start()
    keep_gain.start()
    barrier = pltpu.get_barrier_semaphore()
    pl.semaphore_signal(barrier, inc=1, device_id={"dp": flip(g)}, device_id_type=MESH)
    greet(n, nr, 1)

    @pl.loop(0, chunks)
    def _(j):
        for d in range(1, nr):
            piece(d, j).start()

    middle_at = n // 2
    owner = jnp.where(c < middle_at, 0, n - 1)
    at_owner = jnp.where(c < middle_at, c, c - middle_at)
    is_owner = owner == c

    def cot_piece(d):
        peer = lax.rem(r + d, nr)
        return remote(
            cot_ref.at[span(peer * own, own)], cot_own.at[:, span(r * width, width)], send_g.at[d - 1], recv_g.at[d - 1], {"row": peer}
        )

    cot_local = pltpu.make_async_copy(cot_ref.at[span(r * own, own)], cot_own.at[:, span(r * width, width)], local_g.at[0])
    cot_keep = pltpu.make_async_copy(cot_own, half_ref.at[span(at_owner * own, own)], local_g.at[1])

    def cot_move(b):
        return remote(cot_own, half_ref.at[span(b * own, own)], send_e, recv_e.at[b], {"col": owner})

    share_q.start_far()
    share_q.start_near()
    for d in range(1, nr):
        table_piece(d, 0).start()
        table_piece(d, 1).start()
    share_o.start_far()
    share_o.start_near()
    cot_local.start()
    for d in range(1, nr):
        cot_piece(d).start()
    keep.wait()

    def head_rows(i):
        block_at = i // (own // mh)
        inside = lax.rem(i, own // mh)
        return span(block_at * tree_part + r * own + inside * mh, mh)

    def head_piece(d, i):
        peer = lax.rem(r + d, nr)
        return remote(
            buf.at[peer, span(i * mh, mh)], qkv_ref.at[head_rows(i)], send_h.at[d - 1, i], recv_h.at[d - 1, i], {"row": peer}
        )

    def head_local(i):
        return pltpu.make_async_copy(buf.at[r, span(i * mh, mh)], qkv_ref.at[head_rows(i)], local_h.at[i])

    def stat_copy(b, d):
        peer = lax.rem(c + d, n)
        return remote(stats.at[c, b], stats.at[c, b], send_s.at[b, d - 1], recv_s.at[b, d - 1], {"col": peer})

    def product_block(b):
        rows = span(b * own, own)
        x_rows = x_ref[rows, :]
        red[...] = dot_t(x_rows, table_all[:3 * RANK, :]).astype(low)
        for j in range(3):
            lanes = slice(j * width, (j + 1) * width)
            raw_ref[rows, lanes] = dot(x_rows, wq[:, lanes]) + dot(
                red[:, j * RANK:(j + 1) * RANK], bq_ref[j * RANK:(j + 1) * RANK, :]
            )
        q_rows = raw_ref[rows, :width]
        k_rows = raw_ref[rows, width:2 * width]
        stats[c, b] = row_sums(q_rows * q_rows, k_rows * k_rows)
        for d in range(1, n):
            stat_copy(b, d).start()

    per = own // mh

    def head_block(b):
        for d in range(1, n):
            stat_copy(b, d).wait()
        total = stats[0, b]
        for s in range(1, n):
            total = total + stats[s, b]
        factor = lax.rsqrt(total * (1.0 / D) + epsilon)
        factor_ref[b] = factor
        fq[...] = down_columns(factor, 0)
        fk[...] = down_columns(factor, 4)

        @pl.loop(0, per)
        def _(i):
            rows = span(b * own + i * mh, mh)
            inside = span(i * mh, mh)
            cosine = cos_ref[rows, :]
            sine = sin_ref[rows, :]
            for h in range(heads):
                lanes = slice(h * HEAD, (h + 1) * HEAD)
                u = raw_ref[rows, lanes] * fq[inside, :] * gq_ref[:, lanes]
                buf[h, rows, :HEAD] = (u * cosine + pltpu.roll(u, HEAD // 2, 1) * sine).astype(low)
                k_lanes = slice(width + h * HEAD, width + (h + 1) * HEAD)
                u = raw_ref[rows, k_lanes] * fk[inside, :] * gk_ref[:, lanes]
                buf[h, rows, HEAD:2 * HEAD] = (u * cosine + pltpu.roll(u, HEAD // 2, 1) * sine).astype(low)
                v_lanes = slice(2 * width + h * HEAD, 2 * width + (h + 1) * HEAD)
                buf[h, rows, 2 * HEAD:] = raw_ref[rows, v_lanes].astype(low)
            for d in range(1, nr):
                head_piece(d, b * per + i).start()
            head_local(b * per + i).start()

    def early():
        for d in range(1, nr):
            table_piece(d, 0).wait_recv()
            table_piece(d, 1).wait_recv()
        keep_table.wait()
        keep_gain.wait()
        share_q.wait_all()
        copy_wq.start()

        @pl.loop(1, n - 1)
        def _(b):
            product_block(b)

        @pl.when(jnp.logical_not(is_owner))
        def _():
            cot_move(at_owner).start()

        @pl.when(is_owner)
        def _():
            cot_keep.start()

        @pl.loop(1, n - 1)
        def _(b):
            head_block(b)

    def late():
        @pl.loop(0, 2)
        def _(i):
            product_block(i * (n - 1))

        for i in range(2):
            share_o.pass_twin(i)

        @pl.loop(0, 2)
        def _(i):
            head_block(i * (n - 1))

    copy_wq = pltpu.make_async_copy(wq, wq_out, out_sems.at[0])

    for s in range(n):
        @pl.loop(0, chunks)
        def _(j):
            if s == 0:
                for d in range(1, nr):
                    piece(d, j).wait_recv()

            @pl.when(c - s >= 0)
            def _():
                if s > 0:
                    block(0, s - 1, jnp.maximum(c - s, 0), j, right).wait_recv()
                if s < n - 1:
                    @pl.when(c < n - 1)
                    def _():
                        block(0, s, jnp.maximum(c - s, 0), j, right).start()

            @pl.when(c + s <= n - 1)
            def _():
                if s > 0:
                    block(1, s - 1, jnp.minimum(c + s, n - 1), j, left).wait_recv()
                if s < n - 1:
                    @pl.when(c > 0)
                    def _():
                        block(1, s, jnp.minimum(c + s, n - 1), j, left).start()

        if s == 1:
            for i in range(2):
                share_q.pass_far(i)
        if s == n - 2:
            for i in range(2):
                share_o.pass_far(i)
                share_q.pass_twin(i)
            cot_local.wait()
            for d in range(1, nr):
                cot_piece(d).wait_recv()
            early()
        if s == n - 1:
            late()
    steps = rows_all // mh

    share_o.wait_all()
    copy_wo = pltpu.make_async_copy(wo, wo_out, out_sems.at[1])
    copy_wo.start()

    @pl.loop(0, steps)
    def _(i):
        for d in range(1, nr):
            head_piece(d, i).wait()
        head_local(i).wait()

    for d in range(1, nr):
        cot_piece(d).wait_send()

    @pl.when(jnp.logical_not(is_owner))
    def _():
        cot_move(at_owner).wait_send()

    @pl.when(is_owner)
    def _():
        cot_keep.wait()
        for b in range(middle_at):
            @pl.when(b != at_owner)
            def _():
                remote(cot_own, half_ref.at[span(b * own, own)], send_e, recv_e.at[b], {"row": flip(r)}).wait_recv()

    @pl.loop(0, chunks)
    def _(j):
        for d in range(1, nr):
            piece(d, j).wait_send()
        for s in range(n - 1):
            @pl.when(jnp.logical_and(c - s >= 0, c < n - 1))
            def _():
                block(0, s, jnp.maximum(c - s, 0), j, right).wait_send()

            @pl.when(jnp.logical_and(c + s <= n - 1, c > 0))
            def _():
                block(1, s, jnp.minimum(c + s, n - 1), j, left).wait_send()

    for d in range(1, nr):
        table_piece(d, 0).wait_send()
        table_piece(d, 1).wait_send()
    share_q.drain()
    share_o.drain()
    copy_wq.wait()
    copy_wo.wait()


def front(tokens, table, gain, cot, w_qkv, w_out, b_qkv, gain_q, gain_k, cos2, sin2, n, nr, m=32, mh=80):
    own = tokens.shape[0] // nr
    width = tokens.shape[1]
    rows_all = own * n
    tree = own * n * nr
    chunks = own // m
    steps = rows_all // mh
    dma = pltpu.SemaphoreType.DMA
    shape = jax.ShapeDtypeStruct
    any_space = pl.BlockSpec(memory_space=pl.ANY)
    return pl.pallas_call(
        functools.partial(front_kernel, n, nr, m, mh),
        out_shape=[
            shape((rows_all, width * nr), low),
            shape((table.shape[0], width * nr), low),
            shape((gain.shape[0], width * nr), wide),
            shape((rows_all // 2, width * nr), low),
            shape((rows_all, 3 * width), wide),
            shape((n, 8, own), wide),
            shape((tree, 3 * HEAD), low),
            shape((w_qkv.shape[0] * nr, w_qkv.shape[1]), low),
            shape((w_out.shape[0] * nr, w_out.shape[1]), low),
        ],
        in_specs=[VM, VM, VM, VM, any_space, any_space] + [VM] * 5,
        out_specs=[VM] * 7 + [any_space, any_space],
        scratch_shapes=[
            pltpu.VMEM((w_qkv.shape[0] * nr, w_qkv.shape[1]), low),
            pltpu.VMEM((w_out.shape[0] * nr, w_out.shape[1]), low),
            pltpu.VMEM((n, n, 8, own), wide),
            pltpu.VMEM((width // HEAD, rows_all, 3 * HEAD), low),
            pltpu.VMEM((own, HEAD), wide),
            pltpu.VMEM((own, HEAD), wide),
            pltpu.VMEM((own, 3 * RANK), low),
            pltpu.VMEM((own, width * nr), low),
            dma((nr - 1, chunks)), dma((nr - 1, chunks)), dma((2, n - 1, chunks)), dma((2, n - 1, chunks)),
            dma((2, nr - 1)), dma((2, nr - 1)), dma((3,)),
            dma((n, n - 1)), dma((n, n - 1)), dma((nr - 1, steps)), dma((nr - 1, steps)),
            dma((nr - 1,)), dma((nr - 1,)), dma((steps,)), dma((2,)), dma, dma((n // 2,)),
        ] + share_sems(2) + share_sems(2) + [dma((2,))],
        compiler_params=params(3),
        name="front",
    )(tokens, table, gain, cot, w_qkv, w_out, b_qkv, gain_q, gain_k, cos2, sin2)


def one_hot_rows(out_rows, in_rows, source):
    at = lax.broadcasted_iota(jnp.int32, (out_rows, in_rows), 0)
    return (lax.broadcasted_iota(jnp.int32, (out_rows, in_rows), 1) == source(at)).astype(low)


def rear_kernel(n, nr, ndp, m, d_ref, raw_hbm, factor_ref, gq_ref, gk_ref, cos_ref, sin_ref, res_ref, x_hbm, wq_hbm,
                table_ref, bq_ref, dh_hbm, full_hbm, co_hbm, cg_hbm, cd_hbm, hot_ref,
                grad_ref, layer_ref, sets_ref,
                raw_ref, x_ref, dh_ref, full_ref, co_ref, cg_ref, cd_ref, wq, stats, buf, nq, nk, pq, pk, fq, fk, d_raw, part, recv_right, recv_left, own_buf, layer_own,
                back, red, full, cols, col_stack, full_recv, full_sum, full_last, col_recv, owned, hot_all,
                send_s, recv_s, send_h, recv_h, local_h, send_o, recv_o, local_o, load,
                send_z, recv_z, send_w, recv_w, local_w, send_v, recv_v, local_v,
                send_f, recv_f, send_c, recv_c, send_l, recv_l, send_d, recv_d, send_k, recv_k):
    g, r, c = lax.axis_index("dp"), lax.axis_index("row"), lax.axis_index("col")
    rows_all, width_all = part.shape
    own = rows_all // n
    width = gq_ref.shape[1]
    heads = width // HEAD
    tree_part = own * nr
    middle_at = n // 2
    chunks = own // m
    hop = 2
    ahead = 2
    left = {"col": jnp.maximum(c - 1, 0)}
    right = {"col": jnp.minimum(c + 1, n - 1)}
    load_raw = pltpu.make_async_copy(raw_hbm, raw_ref, load.at[0])
    load_x = pltpu.make_async_copy(x_hbm, x_ref, load.at[1])
    load_w = pltpu.make_async_copy(wq_hbm, wq, load.at[2])
    loads = [
        pltpu.make_async_copy(src, dst, load.at[3 + i])
        for i, (src, dst) in enumerate(
            ((dh_hbm, dh_ref), (full_hbm, full_ref), (co_hbm, co_ref), (cg_hbm, cg_ref), (cd_hbm, cd_ref))
        )
    ]

    def piece(d, b):
        peer = lax.rem(r + d, nr)
        return remote(
            d_ref.at[span(b * tree_part + peer * own, own)], buf.at[r, span(b * own, own)],
            send_h.at[d - 1, b], recv_h.at[d - 1, b], {"row": peer},
        )

    def local(b):
        return pltpu.make_async_copy(
            d_ref.at[span(b * tree_part + r * own, own)], buf.at[r, span(b * own, own)], local_h.at[b]
        )

    is_owner = jnp.logical_or(c == 0, c == n - 1)
    base = jnp.where(c == 0, 0, middle_at)

    def result_piece(b):
        return remote(res_ref.at[span(b * own, own)], layer_own, send_o.at[b], recv_o, {"col": base + b})

    def result_local(b):
        return pltpu.make_async_copy(res_ref.at[span(b * own, own)], layer_own, local_o)

    def width_piece(src, dst, send_sem, recv_sem, d, j, size):
        peer = lax.rem(r + d, nr)
        return remote(
            src.at[span(j * size, size), span(peer * width, width)], dst.at[span(r * own + j * size, size)],
            send_sem.at[d - 1, j], recv_sem.at[d - 1, j], {"row": peer},
        )

    def width_local(src, dst, sem, j, size):
        return pltpu.make_async_copy(
            src.at[span(j * size, size), span(r * width, width)], dst.at[span(r * own + j * size, size)], sem.at[j]
        )

    for b in range(n):
        local(b).start()
    load_raw.start()
    load_x.start()
    load_w.start()
    for copy in loads:
        copy.start()
    me = r * n + c
    barrier = pltpu.get_barrier_semaphore()
    for d in range(1, ndp):
        pl.semaphore_signal(barrier, inc=1, device_id={"dp": lax.rem(g + d, ndp)}, device_id_type=MESH)
    greet(n, nr, ndp - 1)
    for b in (0, n - 1) + tuple(range(1, n - 1)):
        for d in range(1, nr):
            piece(d, b).start()

    @pl.when(is_owner)
    def _():
        for b in range(middle_at):
            @pl.when(base + b == c)
            def _():
                result_local(b).start()

            @pl.when(base + b != c)
            def _():
                result_piece(b).start()

    hot_all[g] = hot_ref[...]
    load_x.wait()
    red[...] = dot_t(x_ref[...], table_ref[:3 * RANK, :]).astype(low)
    load_raw.wait()

    def stat_copy(b, d):
        peer = lax.rem(c + d, n)
        return remote(stats.at[c, b], stats.at[c, b], send_s.at[b, d - 1], recv_s.at[b, d - 1], {"col": peer})

    def norm_block(b):
        for d in range(1, nr):
            piece(d, b).wait_recv()
        local(b).wait()
        rows = span(b * own, own)
        fq[rows, :] = down_columns(factor_ref[b], 0)
        fk[rows, :] = down_columns(factor_ref[b], 4)
        cosine = cos_ref[rows, :]
        sine = sin_ref[rows, :]
        for h in range(heads):
            lanes = slice(h * HEAD, (h + 1) * HEAD)
            k_lanes = slice(width + h * HEAD, width + (h + 1) * HEAD)
            v_lanes = slice(2 * width + h * HEAD, 2 * width + (h + 1) * HEAD)
            u = buf[h, rows, :HEAD].astype(wide)
            u = (u * cosine - pltpu.roll(u, HEAD // 2, 1) * sine) * gq_ref[:, lanes]
            nq[rows, lanes] = u
            pq[rows, lanes] = u * raw_ref[rows, lanes] * fq[rows, :]
            u = buf[h, rows, HEAD:2 * HEAD].astype(wide)
            u = (u * cosine - pltpu.roll(u, HEAD // 2, 1) * sine) * gk_ref[:, lanes]
            nk[rows, lanes] = u
            pk[rows, lanes] = u * raw_ref[rows, k_lanes] * fk[rows, :]
            d_raw[rows, v_lanes] = buf[h, rows, 2 * HEAD:]
        stats[c, b] = row_sums(pq[rows, :], pk[rows, :])
        for d in range(1, n):
            stat_copy(b, d).start()

    def mean_block(b):
        for d in range(1, n):
            stat_copy(b, d).wait()
        total = stats[0, b]
        for s in range(1, n):
            total = total + stats[s, b]
        mean = total * (1.0 / D) * factor_ref[b]
        rows = span(b * own, own)
        pq[rows, :HEAD] = down_columns(mean, 0)
        pk[rows, :HEAD] = down_columns(mean, 4)

    def back_block(b):
        rows = span(b * own, own)
        for h in range(heads):
            lanes = slice(h * HEAD, (h + 1) * HEAD)
            k_lanes = slice(width + h * HEAD, width + (h + 1) * HEAD)
            d_raw[rows, lanes] = (fq[rows, :] * (nq[rows, lanes] - raw_ref[rows, lanes] * pq[rows, :HEAD])).astype(low)
            d_raw[rows, k_lanes] = (fk[rows, :] * (nk[rows, lanes] - raw_ref[rows, k_lanes] * pk[rows, :HEAD])).astype(low)
        for j in range(3):
            back[rows, j * RANK:(j + 1) * RANK] = dot_t(
                d_raw[rows, j * width:(j + 1) * width], bq_ref[j * RANK:(j + 1) * RANK, :]
            ).astype(low)
        mine = jnp.where(b < middle_at, c == 0, c == n - 1)
        held = span(lax.rem(b, middle_at) * own, own)
        for k in range(width_all // width):
            lanes = slice(k * width, (k + 1) * width)
            value = dot_t(d_raw[rows, :], wq[lanes, :]) + dot(back[rows, :], table_ref[:3 * RANK, lanes])
            part[rows, lanes] = (value + jnp.where(mine, dh_ref[held, lanes], 0.0)).astype(low)

    def reduce(kind, b, j):
        rows = span(b * own + j * m, m)
        dst, to = ((recv_right, right), (recv_left, left))[kind]
        return remote(part.at[rows], dst.at[rows], send_z.at[kind, b, j], recv_z.at[kind, b, j], to)

    def stage(s, at_edge=True, inside=True, jobs=()):
        @pl.loop(0, chunks + hop * (n - 2))
        def _(i):
            for at, job in enumerate(jobs):
                pl.when(i == at)(job)

            for kind, b, go, edge, got, j in (
                (0, n - 1 - s, n - 1 - s > c, c == 0, recv_right, i - hop * c),
                (1, s, s < c, c == n - 1, recv_left, i - hop * (n - 1 - c)),
            ):
                go = jnp.logical_and(go, jnp.logical_and(j >= 0, j < chunks))
                if at_edge:
                    @pl.when(jnp.logical_and(go, edge))
                    def _():
                        @pl.when(j >= ahead)
                        def _():
                            reduce(kind, b, j - ahead).wait_send()

                        reduce(kind, b, j).start()

                if inside:
                    @pl.when(jnp.logical_and(go, jnp.logical_not(edge)))
                    def _():
                        rows = span(b * own + j * m, m)
                        reduce(kind, b, j).wait_recv()
                        part[rows, :] = (part[rows, :].astype(wide) + got[rows, :].astype(wide)).astype(low)
                        reduce(kind, b, j).start()

    def full_piece(d):
        peer = lax.rem(r + d, nr)
        return remote(full.at[:, span(peer * width, width)], full_recv.at[r], send_f.at[d - 1], recv_f.at[d - 1], {"row": peer})

    col_rows = col_recv.shape[1]
    full_rows = full_last.shape[1]

    def col_piece(d):
        peer = lax.rem(r + d, nr)
        return remote(cols.at[span(peer * col_rows, col_rows)], col_recv.at[r], send_c.at[d - 1], recv_c.at[d - 1], {"row": peer})

    def last_piece(d):
        peer = lax.rem(c + d, n)
        return remote(full_sum.at[span(peer * full_rows, full_rows)], full_last.at[c], send_l.at[d - 1], recv_l.at[d - 1], {"col": peer})

    def tree_piece(d):
        return remote(owned.at[g], owned.at[g], send_d.at[d - 1], recv_d.at[d - 1], {"dp": lax.rem(g + d, ndp)})

    def hot_piece(d):
        return remote(hot_all.at[g], hot_all.at[g], send_k.at[d - 1], recv_k.at[d - 1], {"dp": lax.rem(g + d, ndp)})

    @pl.loop(0, 2)
    def _(i):
        norm_block(i * (n - 1))

    load_w.wait()
    loads[0].wait()

    @pl.loop(0, 2)
    def _(i):
        mean_block(i * (n - 1))
        back_block(i * (n - 1))

    @pl.loop(1, n - 1)
    def _(b):
        norm_block(b)

    stage(0)

    @pl.loop(1, n - 1)
    def _(b):
        mean_block(b)
        back_block(b)

    for copy in loads[1:]:
        copy.wait()

    rank_own = RANK // n
    groups = full.shape[0] // (n * rank_own) - 1
    rank_row = RANK // nr
    per_wide = cd_ref.shape[1] // width

    def full_job():
        stacked = jnp.concatenate([t_dot(back[...], x_ref[...]), full_ref[...]], axis=0).astype(low)
        order = one_hot_rows(
            full.shape[0], stacked.shape[0],
            lambda o: jnp.where(
                lax.rem(o, full_rows) < groups * rank_own,
                lax.rem(o, full_rows) // rank_own * RANK + o // full_rows * rank_own + lax.rem(o, rank_own), -1
            ),
        )
        full[...] = dot(order, stacked).astype(low)

    def raw_job():
        for j in range(3):
            col_stack[j * RANK:(j + 1) * RANK, :] = t_dot(
                red[:, j * RANK:(j + 1) * RANK], d_raw[:, j * width:(j + 1) * width]
            ).astype(low)
        col_stack[3 * RANK:4 * RANK, :] = co_ref[...].astype(low)

    def wide_job():
        for k in range(per_wide):
            lanes = slice(k * width, (k + 1) * width)
            for j, value in enumerate((cg_ref[0, :, lanes], cg_ref[1, :, lanes], cd_ref[:, lanes])):
                at = (4 + j * per_wide + k) * RANK
                col_stack[at:at + RANK, :] = value.astype(low)

    def col_job():
        order = one_hot_rows(
            cols.shape[0], cols.shape[0],
            lambda o: lax.rem(o, col_rows) // rank_row * RANK + o // col_rows * rank_row + lax.rem(o, rank_row),
        )
        cols[...] = dot(order, col_stack[...]).astype(low)

    stage(1, jobs=(wide_job, raw_job, col_job, full_job))
    for d in range(1, nr):
        full_piece(d).start()
        col_piece(d).start()

    @pl.when(is_owner)
    def _():
        for b in range(middle_at):
            @pl.when(base + b == c)
            def _():
                result_local(b).wait()

            @pl.when(base + b != c)
            def _():
                result_piece(b).wait_send()

    @pl.when(jnp.logical_not(is_owner))
    def _():
        remote(res_ref.at[span(0, own)], layer_own, send_o.at[0], recv_o, right).wait_recv()

    for d in range(1, nr):
        width_piece(layer_own, layer_ref, send_v, recv_v, d, 0, own).start()
    width_local(layer_own, layer_ref, local_v, 0, own).start()
    def row_job():
        for d in range(1, nr):
            full_piece(d).wait_recv()
            col_piece(d).wait_recv()
        total = full[:, span(r * width, width)].astype(wide)
        col_total = cols[span(r * col_rows, col_rows), :].astype(wide)
        for d in range(1, nr):
            peer = lax.rem(r + d, nr)
            total = total + full_recv[peer].astype(wide)
            col_total = col_total + col_recv[peer].astype(wide)
        full_sum[...] = total.astype(low)
        owned[g, full_rows:, :] = col_total.astype(low)
        for d in range(1, n):
            last_piece(d).start()

    stage(2, jobs=(lambda: None, row_job))
    for d in range(1, n):
        last_piece(d).wait_recv()
    last = full_sum[span(c * full_rows, full_rows), :].astype(wide)
    for d in range(1, n):
        last = last + full_last[lax.rem(c + d, n)].astype(wide)
    owned[g, :full_rows, :] = last.astype(low)
    for d in range(1, ndp):
        tree_piece(d).start()
        hot_piece(d).start()

    @pl.loop(0, chunks)
    def _(j):
        rows = span(c * own + j * m, m)
        at = span(j * m, m)
        own_buf[at, :] = part[rows, :]

        @pl.when(c > 0)
        def _():
            reduce(0, c, j).wait_recv()
            own_buf[at, :] = (own_buf[at, :].astype(wide) + recv_right[rows, :].astype(wide)).astype(low)

        @pl.when(c < n - 1)
        def _():
            reduce(1, c, j).wait_recv()
            own_buf[at, :] = (own_buf[at, :].astype(wide) + recv_left[rows, :].astype(wide)).astype(low)

        for d in range(1, nr):
            width_piece(own_buf, grad_ref, send_w, recv_w, d, j, m).start()
        width_local(own_buf, grad_ref, local_w, j, m).start()

    for d in range(1, ndp):
        tree_piece(d).wait_recv()
        hot_piece(d).wait_recv()
    sets_own = sets_ref.shape[0]
    for s in range(sets_own):
        total = owned[0].astype(wide) * hot_all[0, pl.ds(g * sets_own + s, 1), :]
        for t in range(1, ndp):
            total = total + owned[t].astype(wide) * hot_all[t, pl.ds(g * sets_own + s, 1), :]
        sets_ref[s] = total

    @pl.loop(0, chunks)
    def _(j):
        for d in range(1, nr):
            width_piece(own_buf, grad_ref, send_w, recv_w, d, j, m).wait()
        width_local(own_buf, grad_ref, local_w, j, m).wait()

    for d in range(1, nr):
        width_piece(layer_own, layer_ref, send_v, recv_v, d, 0, own).wait()
        full_piece(d).wait_send()
        col_piece(d).wait_send()
        for b in range(n):
            piece(d, b).wait_send()
    width_local(layer_own, layer_ref, local_v, 0, own).wait()
    for d in range(1, n):
        last_piece(d).wait_send()
    for d in range(1, ndp):
        tree_piece(d).wait_send()
        hot_piece(d).wait_send()
    for s in range(n - 1):
        @pl.loop(0, chunks)
        def _(j):
            late = j >= chunks - ahead

            @pl.when(jnp.logical_and(n - 1 - s > c, jnp.logical_or(c > 0, late)))
            def _():
                reduce(0, n - 1 - s, j).wait_send()

            @pl.when(jnp.logical_and(s < c, jnp.logical_or(c < n - 1, late)))
            def _():
                reduce(1, s, j).wait_send()


def rear(d_head, raw, factor, gain_q, gain_k, cos2, sin2, result, x, w_qkv, table, b_qkv, d_h, full_mid, part_ao,
         part_bgu, part_ad, hot, sets_own, n, nr, ndp, m=32):
    rows_all, wide3 = raw.shape
    width = wide3 // 3
    width_all = x.shape[1]
    own = rows_all // n
    chunks = own // m
    full_rows = 8 * RANK // n
    col_blocks = 4 + 3 * part_ad.shape[1] // width
    col_rows = col_blocks * RANK // nr
    dma = pltpu.SemaphoreType.DMA
    shape = jax.ShapeDtypeStruct
    any_space = pl.BlockSpec(memory_space=pl.ANY)
    square = pltpu.VMEM((rows_all, width), wide)
    lane = pltpu.VMEM((rows_all, HEAD), wide)
    big = pltpu.VMEM((rows_all, width_all), low)
    return pl.pallas_call(
        functools.partial(rear_kernel, n, nr, ndp, m),
        out_shape=[
            shape((own * nr, width), low),
            shape((own * nr, width), low),
            shape((sets_own, full_rows + col_rows, width), wide),
        ],
        in_specs=[any_space] * 2 + [VM] * 5 + [any_space] * 3 + [VM] * 2 + [any_space] * 5 + [VM],
        out_specs=[VM] * 3,
        scratch_shapes=[
            pltpu.VMEM(raw.shape, wide),
            pltpu.VMEM(x.shape, low),
            pltpu.VMEM(d_h.shape, wide),
            pltpu.VMEM(full_mid.shape, wide),
            pltpu.VMEM(part_ao.shape, wide),
            pltpu.VMEM(part_bgu.shape, wide),
            pltpu.VMEM(part_ad.shape, wide),
            pltpu.VMEM(w_qkv.shape, low),
            pltpu.VMEM((n, n, 8, own), wide),
            pltpu.VMEM((nr, rows_all, 3 * HEAD), low),
            square, square, square, square, lane, lane,
            pltpu.VMEM((rows_all, wide3), low),
            big, big, big,
            pltpu.VMEM((own, width_all), low),
            pltpu.VMEM((own, width_all), low),
            pltpu.VMEM((rows_all, 3 * RANK), low),
            pltpu.VMEM((rows_all, 3 * RANK), low),
            pltpu.VMEM((n * full_rows, width_all), low),
            pltpu.VMEM((nr * col_rows, width), low),
            pltpu.VMEM((nr * col_rows, width), low),
            pltpu.VMEM((nr, n * full_rows, width), low),
            pltpu.VMEM((n * full_rows, width), low),
            pltpu.VMEM((n, full_rows, width), low),
            pltpu.VMEM((nr, col_rows, width), low),
            pltpu.VMEM((ndp, full_rows + col_rows, width), low),
            pltpu.VMEM((ndp,) + hot.shape, wide),
            dma((n, n - 1)), dma((n, n - 1)), dma((nr - 1, n)), dma((nr - 1, n)), dma((n,)),
            dma((n // 2,)), dma, dma, dma((8,)),
            dma((2, n, chunks)), dma((2, n, chunks)), dma((nr - 1, chunks)), dma((nr - 1, chunks)), dma((chunks,)),
            dma((nr - 1, 1)), dma((nr - 1, 1)), dma((1,)),
            dma((nr - 1,)), dma((nr - 1,)), dma((nr - 1,)), dma((nr - 1,)), dma((n - 1,)), dma((n - 1,)),
            dma((ndp - 1,)), dma((ndp - 1,)), dma((ndp - 1,)), dma((ndp - 1,)),
        ],
        compiler_params=params(5),
        name="rear",
    )(d_head, raw, factor, gain_q, gain_k, cos2, sin2, result, x, w_qkv, table, b_qkv, d_h, full_mid, part_ao, part_bgu, part_ad, hot)


def unpack_kernel(rank_own, rank_row, grad_ref, layer_ref, sets_ref, layer_out, input_grad, a_qkv, b_qkv, a_out, b_out, a_gu, b_gu, a_down, b_down):
    layer_out[...] = layer_ref[...]
    input_grad[...] = grad_ref[...].astype(wide)
    width = grad_ref.shape[1]
    first = 8 * rank_own

    def column(s, at):
        return sets_ref[s, first + at * rank_row:first + (at + 1) * rank_row, :]

    for s in range(sets_ref.shape[0]):
        for j in range(3):
            a_qkv[j, s] = sets_ref[s, j * rank_own:(j + 1) * rank_own, :]
            b_qkv[j, s] = column(s, j)
        for j in range(2):
            a_gu[j, s] = sets_ref[s, (3 + j) * rank_own:(4 + j) * rank_own, :]
        b_out[s] = sets_ref[s, 5 * rank_own:6 * rank_own, :]
        b_down[s] = sets_ref[s, 6 * rank_own:7 * rank_own, :]
        a_out[s] = column(s, 3)
        per = a_down.shape[2] // width
        for k in range(per):
            lanes = slice(k * width, (k + 1) * width)
            b_gu[0, s, :, lanes] = column(s, 4 + k)
            b_gu[1, s, :, lanes] = column(s, 4 + per + k)
            a_down[s, :, lanes] = column(s, 4 + 2 * per + k)


def unpack(grad, layer, sets, rank_own, rank_row, hidden):
    sets_own = sets.shape[0]
    width = grad.shape[1]
    shape = jax.ShapeDtypeStruct
    return pl.pallas_call(
        functools.partial(unpack_kernel, rank_own, rank_row),
        out_shape=[
            shape(layer.shape, low),
            shape(grad.shape, wide),
            shape((3, sets_own, rank_own, width), wide),
            shape((3, sets_own, rank_row, width), wide),
            shape((sets_own, rank_row, width), wide),
            shape((sets_own, rank_own, width), wide),
            shape((2, sets_own, rank_own, width), wide),
            shape((2, sets_own, rank_row, hidden), wide),
            shape((sets_own, rank_row, hidden), wide),
            shape((sets_own, rank_own, width), wide),
        ],
        in_specs=[VM] * 3,
        out_specs=[VM] * 10,
        name="unpack",
    )(grad, layer, sets)


def middle_kernel(n, nr, m, hop, cuts, head_ref, x_hbm, cot_hbm, gain_ref, wo_hbm, wg_hbm, wd_hbm,
                  table_ref, ao_ref, bg_ref, ad_ref,
                  dhead_ref, out_half, grad_half, full_ref, co_ref, cg_ref, cd_ref,
                  wo, wg, wd, x_half, cot_half, raw, attn, d_attn, h_all, df_all, da_all, gu, part,
                  recv_right, recv_left, hid, red_gu, red_down, back_gu, back_down,
                  sems_send, sems_recv, send_in, recv_in, send_out, recv_out, local_in, local_out, load,
                  send_g, recv_g, local_g, send_d, recv_d, local_d):
    g, r, c = lax.axis_index("dp"), lax.axis_index("row"), lax.axis_index("col")
    ag_ref = table_ref.at[3 * RANK:5 * RANK]
    bo_ref = table_ref.at[5 * RANK:6 * RANK]
    bd_ref = table_ref.at[6 * RANK:]
    rows_all, width_all = part.shape
    half = rows_all // 2
    own = rows_all // n
    tree_part = own * nr
    chunks = half // m
    blocks = 4
    band = half // blocks
    hidden = ad_ref.shape[1]
    width = width_all // nr
    left = {"col": jnp.maximum(c - 1, 0)}
    right = {"col": jnp.minimum(c + 1, n - 1)}
    first = c == 0
    last = c == n - 1
    inner = jnp.logical_and(c > 0, c < n - 1)

    base = jnp.where(last, half, 0)
    a_cut = hidden // 4
    share_g = Share(wg_hbm, wg, cuts, (send_g, recv_g, local_g))
    share_d = Share(wd_hbm, wd, cuts // 2, (send_d, recv_d, local_d))
    loads = [pltpu.make_async_copy(wo_hbm, wo, load.at[0])]
    load_x = pltpu.make_async_copy(x_hbm.at[span(base, half)], x_half, load.at[1])
    load_cot = pltpu.make_async_copy(cot_hbm, cot_half, load.at[2])
    loads[0].start()

    def piece_in(d, b):
        peer = lax.rem(r + d, nr)
        return remote(
            head_ref.at[span(b * tree_part + peer * own, own)],
            attn.at[span(b * own, own), span(r * HEAD, HEAD)],
            send_in.at[d - 1, b], recv_in.at[d - 1, b], {"row": peer},
        )

    def local_piece_in(b):
        return pltpu.make_async_copy(
            head_ref.at[span(b * tree_part + r * own, own)],
            attn.at[span(b * own, own), span(r * HEAD, HEAD)], local_in.at[b]
        )

    per_block = blocks // (n // 2)

    def out_rows(b, side):
        at = side * (n // 2) + b // per_block
        inside = lax.rem(b, per_block) * band
        return span(at * own + inside, band), span(at * tree_part + r * own + inside, band)

    def piece_out(d, b, side):
        peer = lax.rem(r + d, nr)
        here, there = out_rows(b, side)
        return remote(
            d_attn.at[here, span(peer * HEAD, HEAD)], dhead_ref.at[there],
            send_out.at[side * (nr - 1) + d - 1, b], recv_out.at[side * (nr - 1) + d - 1, b], {"row": peer},
        )

    def local_piece_out(b, side):
        here, there = out_rows(b, side)
        return pltpu.make_async_copy(d_attn.at[here, span(r * HEAD, HEAD)], dhead_ref.at[there], local_out.at[side, b])

    for b in range(n):
        local_piece_in(b).start()
    barrier = pltpu.get_barrier_semaphore()
    for d in range(1, nr):
        pl.semaphore_signal(barrier, inc=1, device_id={"row": lax.rem(r + d, nr)}, device_id_type=MESH)

    @pl.when(c > 0)
    def _():
        pl.semaphore_signal(barrier, inc=1, device_id=left, device_id_type=MESH)

    @pl.when(c < n - 1)
    def _():
        pl.semaphore_signal(barrier, inc=1, device_id=right, device_id_type=MESH)

    pl.semaphore_signal(barrier, inc=1, device_id={"dp": flip(g)}, device_id_type=MESH)
    full_ref[...] = jnp.zeros_like(full_ref)
    co_ref[...] = jnp.zeros_like(co_ref)
    cg_ref[...] = jnp.zeros_like(cg_ref)
    cd_ref[...] = jnp.zeros_like(cd_ref)

    @pl.when(inner)
    def _():
        pl.semaphore_wait(barrier, nr + 2)

    @pl.when(jnp.logical_not(inner))
    def _():
        pl.semaphore_wait(barrier, nr + 1)

    middle = n // 2
    for b in range(middle):
        for block in (b, middle + b):
            for d in range(1, nr):
                piece_in(d, block).start()
    load_x.start()
    load_cot.start()
    share_g.start_far()
    share_d.start_far()
    share_g.start_near()
    share_d.start_near()

    def rows(j, start=0):
        return span(start + j * m, m)

    def band_rows(b):
        return span(b * band, band), span(half + b * band, band)

    def take(ref, b):
        low_rows, high_rows = band_rows(b)
        return jnp.concatenate([ref[low_rows, :], ref[high_rows, :]], axis=0)

    def put(b, lanes, value):
        low_rows, high_rows = band_rows(b)
        part[low_rows, lanes] = value[:band].astype(low)
        part[high_rows, lanes] = value[band:].astype(low)

    around = hop * 2 * (n - 1)
    each = chunks // blocks

    def relay_stage(stage, per, done, work, owner_step, all_ref, pump=None, coming=None):
        def send(kind, j, src, dst, to):
            return remote(src, dst, sems_send.at[stage, kind, j], sems_recv.at[stage, kind, j], to)

        def reduce_right(j):
            return send(0, j, part.at[rows(j, half)], recv_right.at[rows(j)], right)

        def reduce_left(j):
            return send(1, j, part.at[rows(j)], recv_left.at[rows(j)], left)

        def spread_left(j):
            return send(2, j, all_ref.at[rows(j, half)], all_ref.at[rows(j, half)], left)

        def spread_right(j):
            return send(3, j, all_ref.at[rows(j)], all_ref.at[rows(j)], right)

        total_slices = per * blocks
        lead = 0 if done else per

        def slices_before(i):
            if done:
                return jnp.minimum(done + i, total_slices)
            late = per + (jnp.maximum(i - per, 0) * per) // each
            return jnp.minimum(jnp.where(i < per, i, late), total_slices)

        @pl.loop(0, lead + chunks + around)
        def _(ii):
            i = ii - lead

            def on(offset, who, run):
                j = i - offset

                @pl.when(jnp.logical_and(who, jnp.logical_and(j >= 0, j < chunks)))
                def _():
                    run(j)

            def mid_right(j):
                reduce_right(j).wait_recv()
                at = rows(j, half)
                part[at, :] = (part[at, :].astype(wide) + recv_right[rows(j), :].astype(wide)).astype(low)
                reduce_right(j).start()

            def mid_left(j):
                reduce_left(j).wait_recv()
                at = rows(j)
                part[at, :] = (part[at, :].astype(wide) + recv_left[at, :].astype(wide)).astype(low)
                reduce_left(j).start()

            def end_right(j):
                reduce_right(j).wait_recv()
                total = part[rows(j, half), :].astype(wide) + recv_right[rows(j), :].astype(wide)
                all_ref[rows(j, half), :] = owner_step(total, rows(j))
                spread_left(j).start()

            def end_left(j):
                reduce_left(j).wait_recv()
                total = part[rows(j), :].astype(wide) + recv_left[rows(j), :].astype(wide)
                all_ref[rows(j), :] = owner_step(total, rows(j))
                spread_right(j).start()

            def pass_left(j):
                spread_left(j).wait_recv()
                spread_left(j).start()

            def pass_right(j):
                spread_right(j).wait_recv()
                spread_right(j).start()

            def arrived(j):
                @pl.when(first)
                def _():
                    reduce_right(j).wait_send()
                    spread_left(j).wait_recv()

                @pl.when(last)
                def _():
                    reduce_left(j).wait_send()
                    spread_right(j).wait_recv()

                @pl.when(inner)
                def _():
                    reduce_right(j).wait_send()
                    reduce_left(j).wait_send()

            on(0, first, lambda j: reduce_right(j).start())
            on(0, last, lambda j: reduce_left(j).start())
            on(hop * c, inner, mid_right)
            on(hop * (n - 1 - c), inner, mid_left)
            on(hop * (n - 1), last, end_right)
            on(hop * (n - 1), first, end_left)
            on(hop * (2 * (n - 1) - c), inner, pass_left)
            on(hop * (n - 1 + c), inner, pass_right)
            on(around, True, arrived)

            @pl.loop(slices_before(ii), slices_before(ii + 1))
            def _(t):
                work(t // per, lax.rem(t, per))

            if coming is not None:
                next_work, next_per, next_before = coming

                @pl.loop(next_before(i), next_before(i + 1))
                def _(t):
                    next_work(t // next_per, lax.rem(t, next_per))

            if pump is not None:
                pump(ii)

        @pl.loop(0, chunks)
        def _(j):
            @pl.when(first)
            def _():
                spread_right(j).wait_send()

            @pl.when(last)
            def _():
                spread_left(j).wait_send()

            @pl.when(inner)
            def _():
                spread_left(j).wait_send()
                spread_right(j).wait_send()

    def shard(j, ref):
        return slice(j * (ref.shape[0] // nr), (j + 1) * (ref.shape[0] // nr))

    def out_work(b, k):
        @pl.when(b == 0)
        def _():
            loads[0].wait()

        @pl.when(lax.rem(b, blocks // middle) == 0)
        def _():
            at = b // (blocks // middle)
            for block in (at, middle + at):
                for d in range(1, nr):
                    piece_in(d, block).wait_recv()
                local_piece_in(block).wait()

        rows_in = take(attn, b)
        red = dot_t(rows_in, ao_ref[...]).astype(low)
        for j in range(nr):
            lanes = slice(j * width, (j + 1) * width)
            put(b, lanes, dot(rows_in, wo[shard(j, wo), :]) + dot(red, bo_ref[:, lanes]))

    gain_a = gain_ref[0:1, :]
    gain_f = gain_ref[1:2, :]

    def attn_owner(total, at):
        raw[at, :] = total
        flat = total * norm_factor(row_sum(total * total))
        return (x_half[at, :].astype(wide) + flat * gain_a).astype(low)

    first_pass = 5
    apart = 3
    late = 2
    passes = cuts + cuts // 2

    def pump(ii):
        at = ii - first_pass

        @pl.when(jnp.logical_and(at >= 0, lax.rem(at, apart) == 0))
        def _():
            t = at // apart

            @pl.when(t < cuts)
            def _():
                share_g.pass_far(t)

            @pl.when(jnp.logical_and(t >= cuts, t < passes))
            def _():
                share_d.pass_far(t - cuts)

            t = t - late

            @pl.when(jnp.logical_and(t >= 0, t < cuts))
            def _():
                share_g.pass_twin(t)

            @pl.when(jnp.logical_and(t >= cuts, t < passes))
            def _():
                share_d.pass_twin(t - cuts)

    load_x.wait()
    relay_stage(0, 1, 0, out_work, attn_owner, h_all, pump)
    in_loop = 1 + chunks + hop * 2 * (n - 1)

    @pl.loop(in_loop, jnp.maximum(in_loop, first_pass + apart * (passes + late)))
    def _(ii):
        pump(ii)

    share_g.wait_all()

    def gate_slice(b, k):
        rows_in = take(h_all, b)

        @pl.when(k == 0)
        def _():
            red_gu[b] = dot_t(rows_in, ag_ref[...]).astype(low)

        at = pl.multiple_of(k * a_cut, a_cut)
        lanes = pl.ds(at, a_cut)
        up_lanes = pl.ds(pl.multiple_of(hidden + at, a_cut), a_cut)
        red = red_gu[b]
        gate = dot(rows_in, wg[:, lanes]) + dot(red[:, :RANK], bg_ref[0, :, lanes])
        up = dot(rows_in, wg[:, up_lanes]) + dot(red[:, RANK:], bg_ref[1, :, lanes])
        gu[b, :, lanes] = gate.astype(low)
        gu[b, :, up_lanes] = up.astype(low)
        hid[:, lanes] = (gate * jax.nn.sigmoid(gate) * up).astype(low)

    def down_slice(b, k):
        @pl.when(jnp.logical_and(b == 0, k == 0))
        def _():
            share_d.wait_all()

        rows_in = hid[:, :hidden]

        @pl.when(k == 0)
        def _():
            red_down[b] = dot_t(rows_in, ad_ref[...]).astype(low)

        for s in range(nr // 2):
            j = k * (nr // 2) + s
            lanes = span(j * width, width)
            down_rows = pl.ds(pl.multiple_of(j * hidden, hidden), hidden)
            put(b, lanes, dot(rows_in, wd[down_rows, :]) + dot(red_down[b], bd_ref[:, lanes]))

    def ffn_work(b, k):
        @pl.when(k < 4)
        def _():
            gate_slice(b, k)

        @pl.when(k >= 4)
        def _():
            down_slice(b, k - 4)

    def ffn_owner(total, at):
        a_raw = raw[at, :]
        h = x_half[at, :].astype(wide) + a_raw * norm_factor(row_sum(a_raw * a_raw)) * gain_a
        factor = norm_factor(row_sum(total * total))
        flat = total * factor
        out_half[at, :] = (h + flat * gain_f).astype(low)
        scaled = cot_half[at, :].astype(wide) * gain_f
        return (factor * (scaled - flat * (row_sum(scaled * flat) * (1.0 / D)))).astype(low)

    b_cut = hidden // 2

    def hidden_back(b, k):
        rows_in = take(df_all, b)

        @pl.when(k == 0)
        def _():
            back_down[...] = dot_t(rows_in, bd_ref[...]).astype(low)

        at = pl.multiple_of(k * b_cut, b_cut)
        lanes = pl.ds(at, b_cut)
        up_lanes = pl.ds(pl.multiple_of(hidden + at, b_cut), b_cut)
        back = back_down[...]
        grad = dot(back, ad_ref[:, lanes])
        for j in range(nr):
            down_rows = pl.ds(pl.multiple_of(j * hidden + at, b_cut), b_cut)
            grad = grad + dot_t(rows_in[:, j * width:(j + 1) * width], wd[down_rows, :])
        gate = gu[b, :, lanes].astype(wide)
        up = gu[b, :, up_lanes].astype(wide)
        sigma = jax.nn.sigmoid(gate)
        silu = gate * sigma
        d_gate = (grad * up * sigma * (1.0 + gate * (1.0 - sigma))).astype(low)
        d_up = (grad * silu).astype(low)
        hid[:, lanes] = d_gate
        hid[:, up_lanes] = d_up
        cd_ref[:, lanes] += t_dot(back, (silu * up).astype(low))
        red = red_gu[b]
        cg_ref[0, :, lanes] += t_dot(red[:, :RANK], d_gate)
        cg_ref[1, :, lanes] += t_dot(red[:, RANK:], d_up)

    o_cut = width_all // 4

    def gate_back(b, k):
        @pl.when(k == 0)
        def _():
            back_gu[:, :RANK] = dot_t(hid[:, :hidden], bg_ref[0]).astype(low)
            back_gu[:, RANK:] = dot_t(hid[:, hidden:], bg_ref[1]).astype(low)

        lanes = span(k * o_cut, o_cut)
        put(b, lanes, dot_t(hid[...], wg[lanes, :]) + dot(back_gu[...], ag_ref[:, lanes]))

        @pl.when(k == 3)
        def _():
            full_ref[:2 * RANK, :] += t_dot(back_gu[...], take(h_all, b))
            full_ref[3 * RANK:, :] += t_dot(red_down[b], take(df_all, b))

    def back_work(b, k):
        @pl.when(k < 2)
        def _():
            hidden_back(b, k)

        @pl.when(k >= 2)
        def _():
            gate_back(b, k - 2)

    def back_owner(total, at):
        grad = cot_half[at, :].astype(wide) + total
        grad_half[at, :] = grad
        a_raw = raw[at, :]
        factor = norm_factor(row_sum(a_raw * a_raw))
        flat = a_raw * factor
        scaled = grad * gain_a
        return (factor * (scaled - flat * (row_sum(scaled * flat) * (1.0 / D)))).astype(low)

    def out_back(b, k):
        rows_in = take(da_all, b)
        back = dot_t(rows_in, bo_ref[...]).astype(low)
        grad = dot(back, ao_ref[...])
        for j in range(nr):
            grad = grad + dot_t(rows_in[:, j * width:(j + 1) * width], wo[shard(j, wo), :])
        for side in range(2):
            d_attn[out_rows(b, side)[0], :] = grad[side * band:(side + 1) * band].astype(low)
            for d in range(1, nr):
                piece_out(d, b, side).start()
            local_piece_out(b, side).start()
        attn_rows = take(attn, b)
        co_ref[...] += t_dot(back, attn_rows)
        red = dot_t(attn_rows, ao_ref[...]).astype(low)
        full_ref[2 * RANK:3 * RANK, :] += t_dot(red, rows_in)

    begin = around + each

    def back_before(i):
        return jnp.clip(i - begin, 0, chunks - each)

    def out_before(i):
        return jnp.clip((i - around - 1) // each, 0, blocks - 1)

    load_cot.wait()
    relay_stage(1, 6, 0, ffn_work, ffn_owner, df_all, None, (back_work, 6, back_before))
    relay_stage(2, 6, chunks - each, back_work, back_owner, da_all, None, (out_back, 1, out_before))
    out_back(blocks - 1, 0)

    @pl.loop(0, n)
    def _(b):
        for d in range(1, nr):
            piece_in(d, b).wait_send()

    @pl.loop(0, blocks)
    def _(b):
        for side in range(2):
            for d in range(1, nr):
                piece_out(d, b, side).wait()
            local_piece_out(b, side).wait()

    share_g.drain()
    share_d.drain()


def middle(attn_head, x, cot_half, gains, w_out, w_gu, w_down, table, a_out, b_gu, a_down, n, nr, m=16, hop=2, cuts=8):
    group, width_all = x.shape
    half = group // 2
    width = width_all // nr
    hidden = a_down.shape[1]
    chunks = half // m
    band = group // 4
    dma = pltpu.SemaphoreType.DMA
    any_space = pl.BlockSpec(memory_space=pl.ANY)
    shape = jax.ShapeDtypeStruct
    return pl.pallas_call(
        functools.partial(middle_kernel, n, nr, m, hop, cuts),
        out_shape=[
            shape(attn_head.shape, low),
            shape((half, width_all), low),
            shape((half, width_all), wide),
            shape((4 * RANK, width_all), wide),
            shape((RANK, a_out.shape[1]), wide),
            shape((2, RANK, hidden), wide),
            shape((RANK, hidden), wide),
        ],
        in_specs=[VM, any_space, any_space, VM, any_space, any_space, any_space] + [VM] * 4,
        out_specs=[VM] * 7,
        scratch_shapes=[
            pltpu.VMEM(w_out.shape, low),
            pltpu.VMEM((w_gu.shape[0] * nr, w_gu.shape[1]), low),
            pltpu.VMEM((w_down.shape[0] * nr, w_down.shape[1]), low),
            pltpu.VMEM((half, width_all), low),
            pltpu.VMEM((half, width_all), low),
            pltpu.VMEM((half, width_all), wide),
            pltpu.VMEM((group, a_out.shape[1]), low),
            pltpu.VMEM((group, a_out.shape[1]), low),
            pltpu.VMEM((group, width_all), low),
            pltpu.VMEM((group, width_all), low),
            pltpu.VMEM((group, width_all), low),
            pltpu.VMEM((4, band, 2 * hidden), low),
            pltpu.VMEM((group, width_all), low),
            pltpu.VMEM((half, width_all), low),
            pltpu.VMEM((half, width_all), low),
            pltpu.VMEM((band, 2 * hidden), low),
            pltpu.VMEM((4, band, 2 * RANK), low),
            pltpu.VMEM((4, band, RANK), low),
            pltpu.VMEM((band, 2 * RANK), low),
            pltpu.VMEM((band, RANK), low),
            dma((3, 4, chunks)), dma((3, 4, chunks)),
            dma((nr - 1, n)), dma((nr - 1, n)), dma((2 * (nr - 1), 4)), dma((2 * (nr - 1), 4)), dma((n,)), dma((2, 4)),
            dma((3,)),
        ] + share_sems(cuts) + share_sems(cuts // 2),
        compiler_params=pltpu.CompilerParams(collective_id=0, has_side_effects=True, vmem_limit_bytes=67043328),
        name="middle",
    )(attn_head, x, cot_half, gains, w_out, w_gu, w_down, table, a_out, b_gu, a_down)


def per_device(
    tokens,
    cotangent,
    seg_ids,
    positions,
    parents,
    tree_sets,
    gain_q,
    gain_k,
    gain_attn,
    gain_ffn,
    query_key_value_weight,
    output_weight,
    gate_up_weight,
    down_weight,
    query_key_value_adapter_first,
    query_key_value_adapter_second,
    output_adapter_first,
    output_adapter_second,
    gate_up_adapter_first,
    gate_up_adapter_second,
    down_adapter_first,
    down_adapter_second,
):
    dp_count = lax.axis_size("dp")
    row_count = lax.axis_size("row")
    col_count = lax.axis_size("col")
    row_at = lax.axis_index("row")
    tree_tokens = seg_ids.shape[0]
    assert tree_sets.shape[0] == 1 and col_count == 4
    set_count = output_adapter_first.shape[0]
    own = tokens.shape[0] // row_count
    group = own * col_count
    width_row = tokens.shape[1]
    width_col = gain_q.shape[0]
    hidden_col = down_weight.shape[0]
    tree_set = tree_sets[0]

    tables = (
        query_key_value_adapter_first,
        query_key_value_adapter_second,
        output_adapter_first,
        output_adapter_second,
        gate_up_adapter_first,
        gate_up_adapter_second,
        down_adapter_first,
        down_adapter_second,
    )
    narrow, b_qkv, a_out, b_gu, a_down = prep(tree_sets, tables)
    gain_pair = jnp.pad(jnp.stack([gain_attn, gain_ffn]), ((0, 6), (0, 0)))
    pos_own = lax.dynamic_index_in_dim(
        positions.reshape(col_count, row_count, own), row_at, 1, keepdims=False
    ).reshape(group)
    cosine, sine = angles(pos_own)
    cos2 = jnp.concatenate([cosine, cosine], axis=1)
    sin2 = jnp.concatenate([-sine, sine], axis=1)
    gq, gk = gain_q[None, :], gain_k[None, :]
    parent_at, branch_flag = tree_tables(seg_ids, parents)
    x, table, gains, g_half, raw, factors, qkv_head, w_qkv, w_out = front(
        tokens,
        narrow,
        gain_pair,
        cotangent,
        query_key_value_weight.reshape(width_row, 3 * width_col),
        output_weight,
        b_qkv,
        gq,
        gk,
        cos2,
        sin2,
        col_count,
        row_count,
    )
    attn_head, lse = attend(qkv_head, parent_at, branch_flag)
    d_attn_head, out_half, d_h_half, full_mid, part_ao, part_bgu, part_ad = middle(
        attn_head,
        x,
        g_half,
        gains,
        w_out,
        gate_up_weight.reshape(width_row, 2 * hidden_col),
        down_weight,
        table,
        a_out,
        b_gu,
        a_down,
        col_count,
        row_count,
    )
    d_qkv_head = attend_back(qkv_head, d_attn_head, parent_at, branch_flag, lse)
    hot = (tree_set == lax.broadcasted_iota(jnp.int32, (set_count, width_row), 0)).astype(wide)
    in_grad, layer, sets = rear(
        d_qkv_head,
        raw,
        factors,
        gq,
        gk,
        cos2,
        sin2,
        out_half,
        x,
        w_qkv,
        table,
        b_qkv,
        d_h_half,
        full_mid,
        part_ao,
        part_bgu,
        part_ad,
        hot,
        set_count // dp_count,
        col_count,
        row_count,
        dp_count,
    )
    return tuple(unpack(in_grad, layer, sets, RANK // col_count, RANK // row_count, hidden_col))


def solution(mesh):
    in_specs = (
        P(("dp", "col"), "row"),
        P(("dp", "col"), "row"),
        P("dp"),
        P("dp"),
        P("dp", None),
        P("dp"),
        P("col"),
        P("col"),
        P("row"),
        P("row"),
        P("row", None, "col"),
        P("col", "row"),
        P("row", None, "col"),
        P("col", "row"),
        P(None, None, None, "row"),
        P(None, None, None, "col"),
        P(None, None, "col"),
        P(None, None, "row"),
        P(None, None, None, "row"),
        P(None, None, None, "col"),
        P(None, None, "col"),
        P(None, None, "row"),
    )
    out_specs = (
        P(("dp", "col"), "row"),
        P(("dp", "col"), "row"),
        P(None, "dp", "col", "row"),
        P(None, "dp", "row", "col"),
        P("dp", "row", "col"),
        P("dp", "col", "row"),
        P(None, "dp", "col", "row"),
        P(None, "dp", "row", "col"),
        P("dp", "row", "col"),
        P("dp", "col", "row"),
    )
    return jax.shard_map(
        per_device, mesh=mesh, in_specs=in_specs, out_specs=out_specs, check_vma=False
    )
```

```python
import functools

import jax
import jax.numpy as jnp
from jax import lax
from jax.experimental import pallas as pl
from jax.experimental.pallas import tpu as pltpu
from jax.sharding import PartitionSpec as P

D = 2048
HEAD = 128
RANK = 16
SEG = 128
TRUNK = 1024
QT = 256
MESH = pl.DeviceIdType.MESH
VM = pl.BlockSpec(memory_space=pltpu.VMEM)
precise = lax.Precision.HIGHEST

epsilon = 1e-06
rope_base = 500000.0
masked_out = -1e30
low = jnp.bfloat16
wide = jnp.float32
last_last = (((1,), (1,)), ((), ()))
first_first = (((0,), (0,)), ((), ()))


def dot(left, right):
    return jnp.dot(left, right, preferred_element_type=wide)


def dot_t(left, right):
    return lax.dot_general(left, right, last_last, preferred_element_type=wide)


def t_dot(left, right):
    return lax.dot_general(left, right, first_first, preferred_element_type=wide)


def angles(positions):
    lane = jnp.arange(HEAD, dtype=jnp.int32)
    frequency = rope_base ** (-((lane % (HEAD // 2)).astype(wide) * 2.0) / HEAD)
    angle_table = positions.astype(wide)[:, None] * frequency[None, :]
    return (jnp.cos(angle_table), jnp.where(lane < HEAD // 2, -1.0, 1.0) * jnp.sin(angle_table))


def norm_factor(square_sum):
    return lax.rsqrt(square_sum * (1.0 / D) + epsilon)


def tree_tables(seg_ids, parents):
    tail_seg = seg_ids[TRUNK::SEG]
    labels = jnp.arange(parents.shape[1], dtype=jnp.int32)
    tail_parent = jnp.sum(jnp.where(tail_seg[:, None] == labels[None, :], parents[0][None, :], 0), axis=1)
    hit = (tail_seg[None, :] == tail_parent[:, None])
    at = jnp.arange(tail_seg.shape[0], dtype=jnp.int32) + TRUNK // SEG
    parent_at = jnp.sum(jnp.where(hit, at[None, :], 0), axis=1)
    bias = jnp.where(tail_parent > 0, 0.0, masked_out).astype(wide)
    return parent_at, jnp.broadcast_to(bias[:, None], (tail_seg.shape[0], SEG))


def row_sum(v): return jnp.sum(v, axis=1, keepdims=True)

def params(collective):
    return pltpu.CompilerParams(collective_id=collective, has_side_effects=True, vmem_limit_bytes=60 << 20)


def span(at, size):
    return pl.ds(pl.multiple_of(at, size), size)


def remote(src, dst, send_sem, recv_sem, to):
    return pltpu.make_async_remote_copy(
        src_ref=src, dst_ref=dst, send_sem=send_sem, recv_sem=recv_sem, device_id=to, device_id_type=MESH
    )


def greet(n, nr, extra=0):
    r, c = lax.axis_index("row"), lax.axis_index("col")
    me = r * n + c
    barrier = pltpu.get_barrier_semaphore()

    @pl.loop(1, n * nr)
    def _(d):
        peer = lax.rem(me + d, n * nr)
        pl.semaphore_signal(barrier, inc=1, device_id={"row": peer // n, "col": lax.rem(peer, n)}, device_id_type=MESH)

    pl.semaphore_wait(barrier, n * nr - 1 + extra)


def row_sums(first, second):
    ones = jnp.ones((8, first.shape[1]), wide)
    at = lax.broadcasted_iota(jnp.int32, (8, first.shape[0]), 0)
    sum_first = lax.dot_general(ones, first, last_last, preferred_element_type=wide, precision=precise)
    sum_second = lax.dot_general(ones, second, last_last, preferred_element_type=wide, precision=precise)
    return jnp.where(at < 4, sum_first, sum_second)


def down_columns(values, at):
    pick = (lax.broadcasted_iota(jnp.int32, (8, HEAD), 0) == at).astype(wide)
    return lax.dot_general(values, pick, first_first, preferred_element_type=wide, precision=precise)


def flip(v):
    return v + 1 - 2 * lax.rem(v, 2)


class Share:
    def __init__(self, src, dst, cuts, sems):
        self.send, self.recv, self.local = sems
        self.src, self.cuts = src, cuts
        g, r = lax.axis_index("dp"), lax.axis_index("row")
        size = src.shape[0]
        half = size // 2
        step = half // cuts
        far = lax.rem(r + 2, 4)
        mine = lax.rem(g, 2)
        near_to, far_to, twin_to = {"row": flip(r)}, {"row": far}, {"dp": flip(g)}

        def rows(shard, part, i):
            return pl.ds(pl.multiple_of(shard * size + part * half + i * step, step), step)

        def copy(kind, i, src, dst, to):
            return remote(src, dst, self.send.at[kind, i], self.recv.at[kind, i], to)

        def hand(kind, part, to):
            return lambda i: copy(kind, i, dst.at[rows(far, part, i)], dst.at[rows(far, part, i)], to)

        whole = span(r * size, size)
        self.own = pltpu.make_async_copy(src, dst.at[whole], self.local)
        self.near = copy(0, 0, src, dst.at[whole], near_to)
        self.far = lambda i: copy(
            1, i, src.at[pl.ds(pl.multiple_of(mine * half + i * step, step), step)], dst.at[rows(r, mine, i)], far_to
        )
        self.far_near = hand(2, mine, near_to)
        self.far_twin = hand(3, mine, twin_to)
        self.twin_near = hand(4, 1 - mine, near_to)

    def start_far(self):
        for i in range(self.cuts):
            self.far(i).start()

    def start_near(self):
        self.own.start()
        self.near.start()

    def pass_far(self, i):
        self.far(i).wait_recv()
        self.far_twin(i).start()
        self.far_near(i).start()

    def pass_twin(self, i):
        self.far_twin(i).wait_recv()
        self.twin_near(i).start()

    def wait_all(self):
        self.own.wait()
        self.near.wait_recv()
        for i in range(self.cuts):
            self.far_near(i).wait_recv()
            self.twin_near(i).wait_recv()

    def drain(self):
        self.near.wait_send()
        for i in range(self.cuts):
            self.far(i).wait_send()
            self.far_near(i).wait_send()
            self.far_twin(i).wait_send()
            self.twin_near(i).wait_send()


def share_sems(cuts):
    dma = pltpu.SemaphoreType.DMA
    return [dma((5, cuts)), dma((5, cuts)), dma]


def prep_kernel(set_ref, fq_ref, sq_ref, fo_ref, so_ref, fg_ref, sg_ref, fd_ref, sd_ref,
                narrow_ref, bq_ref, ao_ref, bg_ref, ad_ref):
    for j in range(3):
        narrow_ref[j * RANK:(j + 1) * RANK, :] = fq_ref[j, 0].astype(low)
        bq_ref[j * RANK:(j + 1) * RANK, :] = sq_ref[j, 0].astype(low)
    for j in range(2):
        narrow_ref[(3 + j) * RANK:(4 + j) * RANK, :] = fg_ref[j, 0].astype(low)
        bg_ref[j] = sg_ref[j, 0].astype(low)
    narrow_ref[5 * RANK:6 * RANK, :] = so_ref[0].astype(low)
    narrow_ref[6 * RANK:, :] = sd_ref[0].astype(low)
    ao_ref[...] = fo_ref[0].astype(low)
    ad_ref[...] = fd_ref[0].astype(low)


def prep(tree_sets, tables):
    fq, sq, fo, so, fg, sg, fd, sd = tables

    def pick(table):
        if table.ndim == 4:
            return pl.BlockSpec((table.shape[0], 1) + table.shape[2:], lambda i, s: (0, s[0], 0, 0))
        return pl.BlockSpec((1,) + table.shape[1:], lambda i, s: (s[0], 0, 0))

    def out(*shape):
        return pl.BlockSpec(shape, lambda i, s: (0,) * len(shape)), jax.ShapeDtypeStruct(shape, low)

    outs = [
        out(7 * RANK, fq.shape[-1]), out(3 * RANK, sq.shape[-1]), out(RANK, fo.shape[-1]),
        out(2, RANK, sg.shape[-1]), out(RANK, fd.shape[-1]),
    ]
    return pl.pallas_call(
        prep_kernel,
        grid_spec=pltpu.PrefetchScalarGridSpec(
            num_scalar_prefetch=1, grid=(1,), in_specs=[pick(t) for t in tables], out_specs=[o[0] for o in outs]
        ),
        out_shape=[o[1] for o in outs],
        name="prep",
    )(tree_sets, *tables)


def lower_mask(size):
    return lax.broadcasted_iota(jnp.int32, (size, size), 1) <= lax.broadcasted_iota(jnp.int32, (size, size), 0)


def softmax_parts(parts):
    top = jnp.max(parts[0], axis=1, keepdims=True)
    for s in parts[1:]:
        top = jnp.maximum(top, jnp.max(s, axis=1, keepdims=True))
    raised = [jnp.exp(s - top) for s in parts]
    total = jnp.sum(raised[0], axis=1, keepdims=True)
    for e in raised[1:]:
        total = total + jnp.sum(e, axis=1, keepdims=True)
    inverse = 1.0 / total
    return raised, inverse, top + jnp.log(total)


def tail_parts(q, qkv, at, parent, flag):
    scale = HEAD ** -0.5
    k_lanes = slice(HEAD, 2 * HEAD)
    trunk = dot_t(q, qkv[:TRUNK, k_lanes]) * scale
    branch = dot_t(q, qkv[pl.ds(parent, SEG), k_lanes]) * scale + flag
    own = jnp.where(lower_mask(SEG), dot_t(q, qkv[pl.ds(at, SEG), k_lanes]) * scale, masked_out)
    return [trunk, branch, own]


def trunk_parts(q, qkv, i):
    scale = HEAD ** -0.5
    k_lanes = slice(HEAD, 2 * HEAD)
    own = dot_t(q, qkv[i * QT:(i + 1) * QT, k_lanes]) * scale
    parts = [jnp.where(lower_mask(QT), own, masked_out)]
    if i:
        parts.append(dot_t(q, qkv[:i * QT, k_lanes]) * scale)
    return parts


def attend_body(parent_ref, flag_ref, qkv, o_ref, lse_ref):
    v_lanes = slice(2 * HEAD, 3 * HEAD)
    for i in range(TRUNK // QT):
        at = slice(i * QT, (i + 1) * QT)
        p, inverse, lse = softmax_parts(trunk_parts(qkv[at, :HEAD], qkv, i))
        o = dot(p[0].astype(low), qkv[at, v_lanes])
        if i:
            o = o + dot(p[1].astype(low), qkv[:i * QT, v_lanes])
        o_ref[at, :] = (o * inverse).astype(low)
        lse_ref[at, :] = lse

    @pl.loop(0, (qkv.shape[0] - TRUNK) // SEG, unroll=2)
    def _(j):
        at = pl.multiple_of(TRUNK + j * SEG, SEG)
        parent = pl.multiple_of(parent_ref[j] * SEG, SEG)
        rows = pl.ds(at, SEG)
        p, inverse, lse = softmax_parts(tail_parts(qkv[rows, :HEAD], qkv, at, parent, flag_ref[pl.ds(j, 1), :]))
        o = dot(p[0].astype(low), qkv[:TRUNK, v_lanes])
        o = o + dot(p[1].astype(low), qkv[pl.ds(parent, SEG), v_lanes])
        o = o + dot(p[2].astype(low), qkv[rows, v_lanes])
        o_ref[rows, :] = (o * inverse).astype(low)
        lse_ref[rows, :] = lse


def back_parts(scores, lse, d_out, keys, values):
    probs = [jnp.exp(s - lse) for s in scores]
    grads = [dot_t(d_out, v) for v in values]
    inner = sum(jnp.sum(p * g, axis=1, keepdims=True) for p, g in zip(probs, grads))
    d_scores = [(p * (g - inner)).astype(low) for p, g in zip(probs, grads)]
    dq = sum(dot(d, k) for d, k in zip(d_scores, keys))
    return d_scores, [p.astype(low) for p in probs], dq


def attend_back_kernel(parent_ref, flag_ref, qkv, do_ref, lse_ref, d_ref, dk_acc, dv_acc):
    scale = HEAD ** -0.5
    k_lanes = slice(HEAD, 2 * HEAD)
    v_lanes = slice(2 * HEAD, 3 * HEAD)
    dk_acc[...] = jnp.zeros_like(dk_acc)
    dv_acc[...] = jnp.zeros_like(dv_acc)
    for i in range(TRUNK // QT):
        at = slice(i * QT, (i + 1) * QT)
        spans = [at] + ([slice(0, i * QT)] if i else [])
        q, d_out = qkv[at, :HEAD], do_ref[at, :]
        d_scores, probs, dq = back_parts(
            trunk_parts(q, qkv, i), lse_ref[at, :], d_out, [qkv[s, k_lanes] for s in spans], [qkv[s, v_lanes] for s in spans]
        )
        d_ref[at, :HEAD] = (dq * scale).astype(low)
        for s, d, p in zip(spans, d_scores, probs):
            dk_acc[s, :] += t_dot(d, q)
            dv_acc[s, :] += t_dot(p, d_out)

    @pl.loop(0, (qkv.shape[0] - TRUNK) // SEG, unroll=2)
    def _(j):
        at = pl.multiple_of(TRUNK + j * SEG, SEG)
        parent = pl.multiple_of(parent_ref[j] * SEG, SEG)
        rows = pl.ds(at, SEG)
        spans = [slice(0, TRUNK), pl.ds(parent, SEG), rows]
        q, d_out = qkv[rows, :HEAD], do_ref[rows, :]
        d_scores, probs, dq = back_parts(
            tail_parts(q, qkv, at, parent, flag_ref[pl.ds(j, 1), :]), lse_ref[rows, :], d_out,
            [qkv[s, k_lanes] for s in spans], [qkv[s, v_lanes] for s in spans],
        )
        d_ref[rows, :HEAD] = (dq * scale).astype(low)
        for s, d, p in zip(spans, d_scores, probs):
            dk_acc[s, :] += t_dot(d, q)
            dv_acc[s, :] += t_dot(p, d_out)

    d_ref[:, k_lanes] = (dk_acc[...] * scale).astype(low)
    d_ref[:, v_lanes] = dv_acc[...].astype(low)


def attend(qkv, parent_at, flag):
    n = qkv.shape[0]

    def whole(*shape):
        return pl.BlockSpec(shape, lambda i, *_: (0, 0))

    return pl.pallas_call(
        attend_body,
        grid_spec=pltpu.PrefetchScalarGridSpec(
            num_scalar_prefetch=1,
            grid=(1,),
            in_specs=[whole(*flag.shape), whole(n, 3 * HEAD)],
            out_specs=[whole(n, HEAD), whole(n, 1)],
        ),
        out_shape=[jax.ShapeDtypeStruct((n, HEAD), low), jax.ShapeDtypeStruct((n, 1), wide)],
        name="attend",
    )(parent_at, flag, qkv)


def attend_back(qkv, d_o, parent_at, flag, lse):
    n = qkv.shape[0]

    def whole(*shape):
        return pl.BlockSpec(shape, lambda i, *_: (0, 0))

    return pl.pallas_call(
        attend_back_kernel,
        grid_spec=pltpu.PrefetchScalarGridSpec(
            num_scalar_prefetch=1,
            grid=(1,),
            in_specs=[whole(*flag.shape), whole(n, 3 * HEAD), whole(n, HEAD), whole(n, 1)],
            out_specs=whole(n, 3 * HEAD),
            scratch_shapes=[pltpu.VMEM((n, HEAD), wide), pltpu.VMEM((n, HEAD), wide)],
        ),
        out_shape=jax.ShapeDtypeStruct((n, 3 * HEAD), low),
        name="attend_back",
    )(parent_at, flag, qkv, d_o, lse)


def front_kernel(n, nr, m, mh, tok_ref, table_ref, gain_ref, cot_ref, wq_hbm, wo_hbm, gu_hbm, bq_ref, gq_ref, gk_ref,
                 cos_ref, sin_ref,
                 x_out, table_all, gain_all, half_ref, raw_out, factor_ref, qkv_ref, wq_out, wo_out, gu_out,
                 x_ref, raw_ref, gu_pair, gu_flat, wq, wo, stats, buf, fq, fk, red, cot_own,
                 send_a, recv_a, send_z, recv_z, send_t, recv_t, local_sem,
                 send_s, recv_s, send_h, recv_h, send_g, recv_g, local_h, local_g, send_e, recv_e,
                 send_q, recv_q, local_q, send_o, recv_o, local_o, out_sems):
    g, r, c = lax.axis_index("dp"), lax.axis_index("row"), lax.axis_index("col")
    own = tok_ref.shape[0] // nr
    width = tok_ref.shape[1]
    rows_all = own * n
    heads = width // HEAD
    tree_part = own * nr
    chunks = own // m
    left = {"col": jnp.maximum(c - 1, 0)}
    right = {"col": jnp.minimum(c + 1, n - 1)}
    share_q = Share(wq_hbm, wq, 2, (send_q, recv_q, local_q))
    share_o = Share(wo_hbm, wo, 2, (send_o, recv_o, local_o))

    def piece(d, j):
        peer = lax.rem(r + d, nr)
        return remote(
            tok_ref.at[span(peer * own + j * m, m)],
            x_ref.at[span(c * own + j * m, m), span(r * width, width)],
            send_a.at[d - 1, j], recv_a.at[d - 1, j], {"row": peer},
        )

    def block(kind, s, at, j, to):
        rows = span(at * own + j * m, m)
        return remote(x_ref.at[rows], x_ref.at[rows], send_z.at[kind, s, j], recv_z.at[kind, s, j], to)

    def table_piece(d, kind):
        src, dst = ((table_ref, table_all), (gain_ref, gain_all))[kind]
        to = {"row": lax.rem(r + d, nr)}
        return remote(src, dst.at[:, span(r * width, width)], send_t.at[kind, d - 1], recv_t.at[kind, d - 1], to)

    keep = pltpu.make_async_copy(
        tok_ref.at[span(r * own, own)], x_ref.at[span(c * own, own), span(r * width, width)], local_sem.at[0]
    )
    keep_table = pltpu.make_async_copy(table_ref, table_all.at[:, span(r * width, width)], local_sem.at[1])
    keep_gain = pltpu.make_async_copy(gain_ref, gain_all.at[:, span(r * width, width)], local_sem.at[2])
    keep.start()
    keep_table.start()
    keep_gain.start()
    barrier = pltpu.get_barrier_semaphore()
    pl.semaphore_signal(barrier, inc=1, device_id={"dp": flip(g)}, device_id_type=MESH)
    greet(n, nr, 1)

    @pl.loop(0, chunks)
    def _(j):
        for d in range(1, nr):
            piece(d, j).start()


    load_gu = pltpu.make_async_copy(gu_hbm, gu_pair, out_sems.at[4])
    copy_gu = pltpu.make_async_copy(gu_flat, gu_out, out_sems.at[5])
    gu_step = gu_flat.shape[0] // 8

    def flatten(i):
        @pl.when(i == 0)
        def _():
            load_gu.wait()

        rows = span(i * gu_step, gu_step)
        gu_flat[rows, :] = gu_pair[rows].reshape(gu_step, gu_flat.shape[1])

    middle_at = n // 2
    owner = jnp.where(c < middle_at, 0, n - 1)
    at_owner = jnp.where(c < middle_at, c, c - middle_at)
    is_owner = owner == c

    def cot_piece(d):
        peer = lax.rem(r + d, nr)
        return remote(
            cot_ref.at[span(peer * own, own)], cot_own.at[:, span(r * width, width)], send_g.at[d - 1], recv_g.at[d - 1], {"row": peer}
        )

    cot_local = pltpu.make_async_copy(cot_ref.at[span(r * own, own)], cot_own.at[:, span(r * width, width)], local_g.at[0])
    cot_keep = pltpu.make_async_copy(cot_own, half_ref.at[span(at_owner * own, own)], local_g.at[1])

    def cot_move(b):
        return remote(cot_own, half_ref.at[span(b * own, own)], send_e, recv_e.at[b], {"col": owner})

    share_q.start_far()
    share_q.start_near()
    for d in range(1, nr):
        table_piece(d, 0).start()
        table_piece(d, 1).start()
    share_o.start_far()
    share_o.start_near()
    cot_local.start()
    for d in range(1, nr):
        cot_piece(d).start()
    load_gu.start()
    keep.wait()

    def head_rows(i):
        block_at = i // (own // mh)
        inside = lax.rem(i, own // mh)
        return span(block_at * tree_part + r * own + inside * mh, mh)

    def head_piece(d, i):
        peer = lax.rem(r + d, nr)
        return remote(
            buf.at[peer, span(i * mh, mh)], qkv_ref.at[head_rows(i)], send_h.at[d - 1, i], recv_h.at[d - 1, i], {"row": peer}
        )

    def head_local(i):
        return pltpu.make_async_copy(buf.at[r, span(i * mh, mh)], qkv_ref.at[head_rows(i)], local_h.at[i])

    def stat_copy(b, d):
        peer = lax.rem(c + d, n)
        return remote(stats.at[c, b], stats.at[c, b], send_s.at[b, d - 1], recv_s.at[b, d - 1], {"col": peer})

    def product_block(b):
        rows = span(b * own, own)
        x_rows = x_ref[rows, :]
        red[...] = dot_t(x_rows, table_all[:3 * RANK, :]).astype(low)
        for j in range(3):
            lanes = slice(j * width, (j + 1) * width)
            raw_ref[rows, lanes] = dot(x_rows, wq[:, lanes]) + dot(
                red[:, j * RANK:(j + 1) * RANK], bq_ref[j * RANK:(j + 1) * RANK, :]
            )
        q_rows = raw_ref[rows, :width]
        k_rows = raw_ref[rows, width:2 * width]
        stats[c, b] = row_sums(q_rows * q_rows, k_rows * k_rows)
        for d in range(1, n):
            stat_copy(b, d).start()

    per = own // mh

    def head_block(b):
        for d in range(1, n):
            stat_copy(b, d).wait()
        total = stats[0, b]
        for s in range(1, n):
            total = total + stats[s, b]
        factor = lax.rsqrt(total * (1.0 / D) + epsilon)
        factor_ref[b] = factor
        fq[...] = down_columns(factor, 0)
        fk[...] = down_columns(factor, 4)

        @pl.loop(0, per)
        def _(i):
            rows = span(b * own + i * mh, mh)
            inside = span(i * mh, mh)
            cosine = cos_ref[rows, :]
            sine = sin_ref[rows, :]
            for h in range(heads):
                lanes = slice(h * HEAD, (h + 1) * HEAD)
                u = raw_ref[rows, lanes] * fq[inside, :] * gq_ref[:, lanes]
                buf[h, rows, :HEAD] = (u * cosine + pltpu.roll(u, HEAD // 2, 1) * sine).astype(low)
                k_lanes = slice(width + h * HEAD, width + (h + 1) * HEAD)
                u = raw_ref[rows, k_lanes] * fk[inside, :] * gk_ref[:, lanes]
                buf[h, rows, HEAD:2 * HEAD] = (u * cosine + pltpu.roll(u, HEAD // 2, 1) * sine).astype(low)
                v_lanes = slice(2 * width + h * HEAD, 2 * width + (h + 1) * HEAD)
                buf[h, rows, 2 * HEAD:] = raw_ref[rows, v_lanes].astype(low)
            for d in range(1, nr):
                head_piece(d, b * per + i).start()
            head_local(b * per + i).start()

    def both_phases(last_step):
        for d in range(1, nr):
            table_piece(d, 0).wait_recv()
            table_piece(d, 1).wait_recv()
        keep_table.wait()
        keep_gain.wait()
        share_q.wait_all()
        copy_wq.start()

        @pl.loop(0, 2)
        def _(phase):
            def at(i):
                return jnp.where(phase == 0, 1 + i, i * (n - 1))

            pl.when(phase == 1)(last_step)

            @pl.loop(0, 2)
            def _(i):
                product_block(at(i))

            @pl.when(phase == 0)
            def _():
                @pl.when(jnp.logical_not(is_owner))
                def _():
                    cot_move(at_owner).start()

                @pl.when(is_owner)
                def _():
                    cot_keep.start()

            @pl.when(phase == 1)
            def _():
                copy_x.start()
                copy_raw.start()
                for i in range(2):
                    share_o.pass_twin(i)

            @pl.loop(0, 2)
            def _(i):
                head_block(at(i))

    copy_wq = pltpu.make_async_copy(wq, wq_out, out_sems.at[0])
    copy_x = pltpu.make_async_copy(x_ref, x_out, out_sems.at[2])
    copy_raw = pltpu.make_async_copy(raw_ref, raw_out, out_sems.at[3])

    def ring_step(s):
        @pl.loop(0, chunks)
        def _(j):
            if s == 0:
                for d in range(1, nr):
                    piece(d, j).wait_recv()

            @pl.when(c - s >= 0)
            def _():
                if s > 0:
                    block(0, s - 1, jnp.maximum(c - s, 0), j, right).wait_recv()
                if s < n - 1:
                    @pl.when(c < n - 1)
                    def _():
                        block(0, s, jnp.maximum(c - s, 0), j, right).start()

            @pl.when(c + s <= n - 1)
            def _():
                if s > 0:
                    block(1, s - 1, jnp.minimum(c + s, n - 1), j, left).wait_recv()
                if s < n - 1:
                    @pl.when(c > 0)
                    def _():
                        block(1, s, jnp.minimum(c + s, n - 1), j, left).start()

            if 0 < s < n - 1:
                @pl.when(j < 8 // (n - 2))
                def _():
                    flatten((s - 1) * (8 // (n - 2)) + j)

        if s == 1:
            for i in range(2):
                share_q.pass_far(i)
        if s == n - 2:
            copy_gu.start()
        if s == n - 2:
            for i in range(2):
                share_o.pass_far(i)
                share_q.pass_twin(i)
            cot_local.wait()
            for d in range(1, nr):
                cot_piece(d).wait_recv()
    steps = rows_all // mh

    for s in range(n - 1):
        ring_step(s)
    both_phases(lambda: ring_step(n - 1))

    share_o.wait_all()
    copy_wo = pltpu.make_async_copy(wo, wo_out, out_sems.at[1])
    copy_wo.start()

    @pl.loop(0, steps)
    def _(i):
        for d in range(1, nr):
            head_piece(d, i).wait()
        head_local(i).wait()

    for d in range(1, nr):
        cot_piece(d).wait_send()

    @pl.when(jnp.logical_not(is_owner))
    def _():
        cot_move(at_owner).wait_send()

    @pl.when(is_owner)
    def _():
        cot_keep.wait()
        for b in range(middle_at):
            @pl.when(b != at_owner)
            def _():
                remote(cot_own, half_ref.at[span(b * own, own)], send_e, recv_e.at[b], {"row": flip(r)}).wait_recv()

    @pl.loop(0, chunks)
    def _(j):
        for d in range(1, nr):
            piece(d, j).wait_send()
        for s in range(n - 1):
            @pl.when(jnp.logical_and(c - s >= 0, c < n - 1))
            def _():
                block(0, s, jnp.maximum(c - s, 0), j, right).wait_send()

            @pl.when(jnp.logical_and(c + s <= n - 1, c > 0))
            def _():
                block(1, s, jnp.minimum(c + s, n - 1), j, left).wait_send()

    for d in range(1, nr):
        table_piece(d, 0).wait_send()
        table_piece(d, 1).wait_send()
    share_q.drain()
    share_o.drain()
    copy_wq.wait()
    copy_wo.wait()
    copy_x.wait()
    copy_raw.wait()
    copy_gu.wait()


def front(tokens, table, gain, cot, w_qkv, w_out, w_gu, b_qkv, gain_q, gain_k, cos2, sin2, n, nr, m=32, mh=80):
    own = tokens.shape[0] // nr
    width = tokens.shape[1]
    rows_all = own * n
    tree = own * n * nr
    chunks = own // m
    steps = rows_all // mh
    dma = pltpu.SemaphoreType.DMA
    shape = jax.ShapeDtypeStruct
    any_space = pl.BlockSpec(memory_space=pl.ANY)
    return pl.pallas_call(
        functools.partial(front_kernel, n, nr, m, mh),
        out_shape=[
            shape((rows_all, width * nr), low),
            shape((table.shape[0], width * nr), low),
            shape((gain.shape[0], width * nr), wide),
            shape((rows_all // 2, width * nr), low),
            shape((rows_all, 3 * width), wide),
            shape((n, 8, own), wide),
            shape((tree, 3 * HEAD), low),
            shape((w_qkv.shape[0] * nr, w_qkv.shape[1]), low),
            shape((w_out.shape[0] * nr, w_out.shape[1]), low),
            shape((w_gu.shape[0], 2 * w_gu.shape[2]), low),
        ],
        in_specs=[any_space, VM, VM] + [any_space] * 4 + [VM] * 5,
        out_specs=[any_space, VM, VM, any_space, any_space, VM, any_space, any_space, any_space, any_space],
        scratch_shapes=[
            pltpu.VMEM((rows_all, width * nr), low),
            pltpu.VMEM((rows_all, 3 * width), wide),
            pltpu.VMEM(w_gu.shape, low),
            pltpu.VMEM((w_gu.shape[0], 2 * w_gu.shape[2]), low),
            pltpu.VMEM((w_qkv.shape[0] * nr, w_qkv.shape[1]), low),
            pltpu.VMEM((w_out.shape[0] * nr, w_out.shape[1]), low),
            pltpu.VMEM((n, n, 8, own), wide),
            pltpu.VMEM((width // HEAD, rows_all, 3 * HEAD), low),
            pltpu.VMEM((own, HEAD), wide),
            pltpu.VMEM((own, HEAD), wide),
            pltpu.VMEM((own, 3 * RANK), low),
            pltpu.VMEM((own, width * nr), low),
            dma((nr - 1, chunks)), dma((nr - 1, chunks)), dma((2, n - 1, chunks)), dma((2, n - 1, chunks)),
            dma((2, nr - 1)), dma((2, nr - 1)), dma((3,)),
            dma((n, n - 1)), dma((n, n - 1)), dma((nr - 1, steps)), dma((nr - 1, steps)),
            dma((nr - 1,)), dma((nr - 1,)), dma((steps,)), dma((2,)), dma, dma((n // 2,)),
        ] + share_sems(2) + share_sems(2) + [dma((6,))],
        compiler_params=params(3),
        name="front",
    )(tokens, table, gain, cot, w_qkv, w_out, w_gu, b_qkv, gain_q, gain_k, cos2, sin2)


def one_hot_rows(out_rows, in_rows, source):
    at = lax.broadcasted_iota(jnp.int32, (out_rows, in_rows), 0)
    return (lax.broadcasted_iota(jnp.int32, (out_rows, in_rows), 1) == source(at)).astype(low)


def rear_kernel(n, nr, ndp, m, d_ref, raw_hbm, factor_ref, gq_ref, gk_ref, cos_ref, sin_ref, res_ref, x_hbm, wq_hbm,
                table_ref, bq_ref, dh_hbm, full_hbm, co_hbm, cg_hbm, cd_hbm, hot_ref,
                grad_ref, layer_ref, sets_ref,
                raw_ref, x_ref, dh_ref, full_ref, co_ref, cg_ref, cd_ref, wq, stats, buf, nq, nk, pq, pk, fq, fk, d_raw, part, recv_right, recv_left, own_buf, layer_own,
                back, red, full, cols, col_stack, full_recv, full_sum, full_last, col_recv, owned, hot_all,
                send_s, recv_s, send_h, recv_h, local_h, send_o, recv_o, local_o, load,
                send_z, recv_z, send_w, recv_w, local_w, send_v, recv_v, local_v,
                send_f, recv_f, send_c, recv_c, send_l, recv_l, send_d, recv_d, send_k, recv_k):
    g, r, c = lax.axis_index("dp"), lax.axis_index("row"), lax.axis_index("col")
    rows_all, width_all = part.shape
    own = rows_all // n
    width = gq_ref.shape[1]
    heads = width // HEAD
    tree_part = own * nr
    middle_at = n // 2
    chunks = own // m
    hop = 2
    ahead = 2
    left = {"col": jnp.maximum(c - 1, 0)}
    right = {"col": jnp.minimum(c + 1, n - 1)}
    load_raw = pltpu.make_async_copy(raw_hbm, raw_ref, load.at[0])
    load_x = pltpu.make_async_copy(x_hbm, x_ref, load.at[1])
    load_w = pltpu.make_async_copy(wq_hbm, wq, load.at[2])
    loads = [
        pltpu.make_async_copy(src, dst, load.at[3 + i])
        for i, (src, dst) in enumerate(
            ((dh_hbm, dh_ref), (full_hbm, full_ref), (co_hbm, co_ref), (cg_hbm, cg_ref), (cd_hbm, cd_ref))
        )
    ]

    def piece(d, b):
        peer = lax.rem(r + d, nr)
        return remote(
            d_ref.at[span(b * tree_part + peer * own, own)], buf.at[r, span(b * own, own)],
            send_h.at[d - 1, b], recv_h.at[d - 1, b], {"row": peer},
        )

    def local(b):
        return pltpu.make_async_copy(
            d_ref.at[span(b * tree_part + r * own, own)], buf.at[r, span(b * own, own)], local_h.at[b]
        )

    is_owner = jnp.logical_or(c == 0, c == n - 1)
    base = jnp.where(c == 0, 0, middle_at)

    def result_piece(b):
        return remote(res_ref.at[span(b * own, own)], layer_own, send_o.at[b], recv_o, {"col": base + b})

    def result_local(b):
        return pltpu.make_async_copy(res_ref.at[span(b * own, own)], layer_own, local_o)

    def width_piece(src, dst, send_sem, recv_sem, d, j, size):
        peer = lax.rem(r + d, nr)
        return remote(
            src.at[span(j * size, size), span(peer * width, width)], dst.at[span(r * own + j * size, size)],
            send_sem.at[d - 1, j], recv_sem.at[d - 1, j], {"row": peer},
        )

    def width_local(src, dst, sem, j, size):
        return pltpu.make_async_copy(
            src.at[span(j * size, size), span(r * width, width)], dst.at[span(r * own + j * size, size)], sem.at[j]
        )

    for b in range(n):
        local(b).start()
    load_raw.start()
    load_x.start()
    load_w.start()
    for copy in loads:
        copy.start()
    me = r * n + c
    barrier = pltpu.get_barrier_semaphore()
    for d in range(1, ndp):
        pl.semaphore_signal(barrier, inc=1, device_id={"dp": lax.rem(g + d, ndp)}, device_id_type=MESH)
    greet(n, nr, ndp - 1)
    for b in (0, n - 1) + tuple(range(1, n - 1)):
        for d in range(1, nr):
            piece(d, b).start()

    @pl.when(is_owner)
    def _():
        for b in range(middle_at):
            @pl.when(base + b == c)
            def _():
                result_local(b).start()

            @pl.when(base + b != c)
            def _():
                result_piece(b).start()

    hot_all[g] = hot_ref[...]
    load_x.wait()
    red[...] = dot_t(x_ref[...], table_ref[:3 * RANK, :]).astype(low)
    load_raw.wait()

    def stat_copy(b, d):
        peer = lax.rem(c + d, n)
        return remote(stats.at[c, b], stats.at[c, b], send_s.at[b, d - 1], recv_s.at[b, d - 1], {"col": peer})

    def norm_block(b):
        for d in range(1, nr):
            piece(d, b).wait_recv()
        local(b).wait()
        rows = span(b * own, own)
        fq[rows, :] = down_columns(factor_ref[b], 0)
        fk[rows, :] = down_columns(factor_ref[b], 4)
        cosine = cos_ref[rows, :]
        sine = sin_ref[rows, :]
        for h in range(heads):
            lanes = slice(h * HEAD, (h + 1) * HEAD)
            k_lanes = slice(width + h * HEAD, width + (h + 1) * HEAD)
            v_lanes = slice(2 * width + h * HEAD, 2 * width + (h + 1) * HEAD)
            u = buf[h, rows, :HEAD].astype(wide)
            u = (u * cosine - pltpu.roll(u, HEAD // 2, 1) * sine) * gq_ref[:, lanes]
            nq[rows, lanes] = u
            pq[rows, lanes] = u * raw_ref[rows, lanes] * fq[rows, :]
            u = buf[h, rows, HEAD:2 * HEAD].astype(wide)
            u = (u * cosine - pltpu.roll(u, HEAD // 2, 1) * sine) * gk_ref[:, lanes]
            nk[rows, lanes] = u
            pk[rows, lanes] = u * raw_ref[rows, k_lanes] * fk[rows, :]
            d_raw[rows, v_lanes] = buf[h, rows, 2 * HEAD:]
        stats[c, b] = row_sums(pq[rows, :], pk[rows, :])
        for d in range(1, n):
            stat_copy(b, d).start()

    def mean_block(b):
        for d in range(1, n):
            stat_copy(b, d).wait()
        total = stats[0, b]
        for s in range(1, n):
            total = total + stats[s, b]
        mean = total * (1.0 / D) * factor_ref[b]
        rows = span(b * own, own)
        pq[rows, :HEAD] = down_columns(mean, 0)
        pk[rows, :HEAD] = down_columns(mean, 4)

    def back_block(b):
        rows = span(b * own, own)
        for h in range(heads):
            lanes = slice(h * HEAD, (h + 1) * HEAD)
            k_lanes = slice(width + h * HEAD, width + (h + 1) * HEAD)
            d_raw[rows, lanes] = (fq[rows, :] * (nq[rows, lanes] - raw_ref[rows, lanes] * pq[rows, :HEAD])).astype(low)
            d_raw[rows, k_lanes] = (fk[rows, :] * (nk[rows, lanes] - raw_ref[rows, k_lanes] * pk[rows, :HEAD])).astype(low)
        for j in range(3):
            back[rows, j * RANK:(j + 1) * RANK] = dot_t(
                d_raw[rows, j * width:(j + 1) * width], bq_ref[j * RANK:(j + 1) * RANK, :]
            ).astype(low)
        mine = jnp.where(b < middle_at, c == 0, c == n - 1)
        held = span(lax.rem(b, middle_at) * own, own)
        for k in range(width_all // width):
            lanes = slice(k * width, (k + 1) * width)
            value = dot_t(d_raw[rows, :], wq[lanes, :]) + dot(back[rows, :], table_ref[:3 * RANK, lanes])
            part[rows, lanes] = (value + jnp.where(mine, dh_ref[held, lanes], 0.0)).astype(low)

    def full_piece(d):
        peer = lax.rem(r + d, nr)
        return remote(full.at[:, span(peer * width, width)], full_recv.at[r], send_f.at[d - 1], recv_f.at[d - 1], {"row": peer})

    col_rows = col_recv.shape[1]
    full_rows = full_last.shape[1]

    def col_piece(d):
        peer = lax.rem(r + d, nr)
        return remote(cols.at[span(peer * col_rows, col_rows)], col_recv.at[r], send_c.at[d - 1], recv_c.at[d - 1], {"row": peer})

    def last_piece(d):
        peer = lax.rem(c + d, n)
        return remote(full_sum.at[span(peer * full_rows, full_rows)], full_last.at[c], send_l.at[d - 1], recv_l.at[d - 1], {"col": peer})

    def tree_piece(d):
        return remote(owned.at[g], owned.at[g], send_d.at[d - 1], recv_d.at[d - 1], {"dp": lax.rem(g + d, ndp)})

    def hot_piece(d):
        return remote(hot_all.at[g], hot_all.at[g], send_k.at[d - 1], recv_k.at[d - 1], {"dp": lax.rem(g + d, ndp)})

    def reduce(kind, b, j):
        rows = span(b * own + j * m, m)
        dst, to = ((recv_right, right), (recv_left, left))[kind]
        return remote(part.at[rows], dst.at[rows], send_z.at[kind, b, j], recv_z.at[kind, b, j], to)

    def stage(s, at_edge=True, inside=True, jobs=()):
        @pl.loop(0, chunks + hop * (n - 2))
        def _(i):
            for at, job in enumerate(jobs):
                pl.when(i == at)(job)

            for kind, b, go, edge, got, j in (
                (0, n - 1 - s, n - 1 - s > c, c == 0, recv_right, i - hop * c),
                (1, s, s < c, c == n - 1, recv_left, i - hop * (n - 1 - c)),
            ):
                go = jnp.logical_and(go, jnp.logical_and(j >= 0, j < chunks))
                if at_edge:
                    @pl.when(jnp.logical_and(go, edge))
                    def _():
                        @pl.when(j >= ahead)
                        def _():
                            reduce(kind, b, j - ahead).wait_send()

                        reduce(kind, b, j).start()

                if inside:
                    @pl.when(jnp.logical_and(go, jnp.logical_not(edge)))
                    def _():
                        rows = span(b * own + j * m, m)
                        reduce(kind, b, j).wait_recv()
                        part[rows, :] = (part[rows, :].astype(wide) + got[rows, :].astype(wide)).astype(low)
                        reduce(kind, b, j).start()

    @pl.loop(0, 2)
    def _(phase):
        def at(i):
            return jnp.where(phase == 0, i * (n - 1), 1 + i)

        @pl.loop(0, 2)
        def _(i):
            norm_block(at(i))

        @pl.when(phase == 0)
        def _():
            load_w.wait()
            loads[0].wait()

        @pl.when(phase == 1)
        def _():
            stage(0)

        @pl.loop(0, 2)
        def _(i):
            mean_block(at(i))
            back_block(at(i))

    for copy in loads[1:]:
        copy.wait()

    rank_own = RANK // n
    groups = full.shape[0] // (n * rank_own) - 1
    rank_row = RANK // nr
    per_wide = cd_ref.shape[1] // width

    def full_job():
        stacked = jnp.concatenate([t_dot(back[...], x_ref[...]), full_ref[...]], axis=0).astype(low)
        order = one_hot_rows(
            full.shape[0], stacked.shape[0],
            lambda o: jnp.where(
                lax.rem(o, full_rows) < groups * rank_own,
                lax.rem(o, full_rows) // rank_own * RANK + o // full_rows * rank_own + lax.rem(o, rank_own), -1
            ),
        )
        full[...] = dot(order, stacked).astype(low)

    def raw_job():
        for j in range(3):
            col_stack[j * RANK:(j + 1) * RANK, :] = t_dot(
                red[:, j * RANK:(j + 1) * RANK], d_raw[:, j * width:(j + 1) * width]
            ).astype(low)
        col_stack[3 * RANK:4 * RANK, :] = co_ref[...].astype(low)

    def wide_job():
        for k in range(per_wide):
            lanes = slice(k * width, (k + 1) * width)
            for j, value in enumerate((cg_ref[0, :, lanes], cg_ref[1, :, lanes], cd_ref[:, lanes])):
                at = (4 + j * per_wide + k) * RANK
                col_stack[at:at + RANK, :] = value.astype(low)

    def col_job():
        order = one_hot_rows(
            cols.shape[0], cols.shape[0],
            lambda o: lax.rem(o, col_rows) // rank_row * RANK + o // col_rows * rank_row + lax.rem(o, rank_row),
        )
        cols[...] = dot(order, col_stack[...]).astype(low)

    stage(1, jobs=(wide_job, raw_job, col_job, full_job))
    for d in range(1, nr):
        full_piece(d).start()
        col_piece(d).start()

    @pl.when(is_owner)
    def _():
        for b in range(middle_at):
            @pl.when(base + b == c)
            def _():
                result_local(b).wait()

            @pl.when(base + b != c)
            def _():
                result_piece(b).wait_send()

    @pl.when(jnp.logical_not(is_owner))
    def _():
        remote(res_ref.at[span(0, own)], layer_own, send_o.at[0], recv_o, right).wait_recv()

    for d in range(1, nr):
        width_piece(layer_own, layer_ref, send_v, recv_v, d, 0, own).start()
    width_local(layer_own, layer_ref, local_v, 0, own).start()
    def row_job():
        for d in range(1, nr):
            full_piece(d).wait_recv()
            col_piece(d).wait_recv()
        total = full[:, span(r * width, width)].astype(wide)
        col_total = cols[span(r * col_rows, col_rows), :].astype(wide)
        for d in range(1, nr):
            peer = lax.rem(r + d, nr)
            total = total + full_recv[peer].astype(wide)
            col_total = col_total + col_recv[peer].astype(wide)
        full_sum[...] = total.astype(low)
        owned[g, full_rows:, :] = col_total.astype(low)
        for d in range(1, n):
            last_piece(d).start()

    stage(2, jobs=(lambda: None, row_job))
    for d in range(1, n):
        last_piece(d).wait_recv()
    last = full_sum[span(c * full_rows, full_rows), :].astype(wide)
    for d in range(1, n):
        last = last + full_last[lax.rem(c + d, n)].astype(wide)
    owned[g, :full_rows, :] = last.astype(low)
    for d in range(1, ndp):
        tree_piece(d).start()
        hot_piece(d).start()

    @pl.loop(0, chunks)
    def _(j):
        rows = span(c * own + j * m, m)
        at = span(j * m, m)
        own_buf[at, :] = part[rows, :]

        @pl.when(c > 0)
        def _():
            reduce(0, c, j).wait_recv()
            own_buf[at, :] = (own_buf[at, :].astype(wide) + recv_right[rows, :].astype(wide)).astype(low)

        @pl.when(c < n - 1)
        def _():
            reduce(1, c, j).wait_recv()
            own_buf[at, :] = (own_buf[at, :].astype(wide) + recv_left[rows, :].astype(wide)).astype(low)

        for d in range(1, nr):
            width_piece(own_buf, grad_ref, send_w, recv_w, d, j, m).start()
        width_local(own_buf, grad_ref, local_w, j, m).start()

    for d in range(1, ndp):
        tree_piece(d).wait_recv()
        hot_piece(d).wait_recv()
    sets_own = sets_ref.shape[0]
    for s in range(sets_own):
        total = owned[0].astype(wide) * hot_all[0, pl.ds(g * sets_own + s, 1), :]
        for t in range(1, ndp):
            total = total + owned[t].astype(wide) * hot_all[t, pl.ds(g * sets_own + s, 1), :]
        sets_ref[s] = total

    @pl.loop(0, chunks)
    def _(j):
        for d in range(1, nr):
            width_piece(own_buf, grad_ref, send_w, recv_w, d, j, m).wait()
        width_local(own_buf, grad_ref, local_w, j, m).wait()

    for d in range(1, nr):
        width_piece(layer_own, layer_ref, send_v, recv_v, d, 0, own).wait()
        full_piece(d).wait_send()
        col_piece(d).wait_send()
        for b in range(n):
            piece(d, b).wait_send()
    width_local(layer_own, layer_ref, local_v, 0, own).wait()
    for d in range(1, n):
        last_piece(d).wait_send()
    for d in range(1, ndp):
        tree_piece(d).wait_send()
        hot_piece(d).wait_send()
    for s in range(n - 1):
        @pl.loop(0, chunks)
        def _(j):
            late = j >= chunks - ahead

            @pl.when(jnp.logical_and(n - 1 - s > c, jnp.logical_or(c > 0, late)))
            def _():
                reduce(0, n - 1 - s, j).wait_send()

            @pl.when(jnp.logical_and(s < c, jnp.logical_or(c < n - 1, late)))
            def _():
                reduce(1, s, j).wait_send()


def rear(d_head, raw, factor, gain_q, gain_k, cos2, sin2, result, x, w_qkv, table, b_qkv, d_h, full_mid, part_ao,
         part_bgu, part_ad, hot, sets_own, n, nr, ndp, m=32):
    rows_all, wide3 = raw.shape
    width = wide3 // 3
    width_all = x.shape[1]
    own = rows_all // n
    chunks = own // m
    full_rows = 8 * RANK // n
    col_blocks = 4 + 3 * part_ad.shape[1] // width
    col_rows = col_blocks * RANK // nr
    dma = pltpu.SemaphoreType.DMA
    shape = jax.ShapeDtypeStruct
    any_space = pl.BlockSpec(memory_space=pl.ANY)
    square = pltpu.VMEM((rows_all, width), wide)
    lane = pltpu.VMEM((rows_all, HEAD), wide)
    big = pltpu.VMEM((rows_all, width_all), low)
    return pl.pallas_call(
        functools.partial(rear_kernel, n, nr, ndp, m),
        out_shape=[
            shape((own * nr, width), low),
            shape((own * nr, width), low),
            shape((sets_own, full_rows + col_rows, width), wide),
        ],
        in_specs=[any_space] * 2 + [VM] * 5 + [any_space] * 3 + [VM] * 2 + [any_space] * 5 + [VM],
        out_specs=[VM] * 3,
        scratch_shapes=[
            pltpu.VMEM(raw.shape, wide),
            pltpu.VMEM(x.shape, low),
            pltpu.VMEM(d_h.shape, wide),
            pltpu.VMEM(full_mid.shape, wide),
            pltpu.VMEM(part_ao.shape, wide),
            pltpu.VMEM(part_bgu.shape, wide),
            pltpu.VMEM(part_ad.shape, wide),
            pltpu.VMEM(w_qkv.shape, low),
            pltpu.VMEM((n, n, 8, own), wide),
            pltpu.VMEM((nr, rows_all, 3 * HEAD), low),
            square, square, square, square, lane, lane,
            pltpu.VMEM((rows_all, wide3), low),
            big, big, big,
            pltpu.VMEM((own, width_all), low),
            pltpu.VMEM((own, width_all), low),
            pltpu.VMEM((rows_all, 3 * RANK), low),
            pltpu.VMEM((rows_all, 3 * RANK), low),
            pltpu.VMEM((n * full_rows, width_all), low),
            pltpu.VMEM((nr * col_rows, width), low),
            pltpu.VMEM((nr * col_rows, width), low),
            pltpu.VMEM((nr, n * full_rows, width), low),
            pltpu.VMEM((n * full_rows, width), low),
            pltpu.VMEM((n, full_rows, width), low),
            pltpu.VMEM((nr, col_rows, width), low),
            pltpu.VMEM((ndp, full_rows + col_rows, width), low),
            pltpu.VMEM((ndp,) + hot.shape, wide),
            dma((n, n - 1)), dma((n, n - 1)), dma((nr - 1, n)), dma((nr - 1, n)), dma((n,)),
            dma((n // 2,)), dma, dma, dma((8,)),
            dma((2, n, chunks)), dma((2, n, chunks)), dma((nr - 1, chunks)), dma((nr - 1, chunks)), dma((chunks,)),
            dma((nr - 1, 1)), dma((nr - 1, 1)), dma((1,)),
            dma((nr - 1,)), dma((nr - 1,)), dma((nr - 1,)), dma((nr - 1,)), dma((n - 1,)), dma((n - 1,)),
            dma((ndp - 1,)), dma((ndp - 1,)), dma((ndp - 1,)), dma((ndp - 1,)),
        ],
        compiler_params=params(5),
        name="rear",
    )(d_head, raw, factor, gain_q, gain_k, cos2, sin2, result, x, w_qkv, table, b_qkv, d_h, full_mid, part_ao, part_bgu, part_ad, hot)


def unpack_kernel(rank_own, rank_row, grad_ref, layer_ref, sets_ref, layer_out, input_grad, a_qkv, b_qkv, a_out, b_out, a_gu, b_gu, a_down, b_down):
    layer_out[...] = layer_ref[...]
    input_grad[...] = grad_ref[...].astype(wide)
    width = grad_ref.shape[1]
    first = 8 * rank_own

    def column(s, at):
        return sets_ref[s, first + at * rank_row:first + (at + 1) * rank_row, :]

    for s in range(sets_ref.shape[0]):
        for j in range(3):
            a_qkv[j, s] = sets_ref[s, j * rank_own:(j + 1) * rank_own, :]
            b_qkv[j, s] = column(s, j)
        for j in range(2):
            a_gu[j, s] = sets_ref[s, (3 + j) * rank_own:(4 + j) * rank_own, :]
        b_out[s] = sets_ref[s, 5 * rank_own:6 * rank_own, :]
        b_down[s] = sets_ref[s, 6 * rank_own:7 * rank_own, :]
        a_out[s] = column(s, 3)
        per = a_down.shape[2] // width
        for k in range(per):
            lanes = slice(k * width, (k + 1) * width)
            b_gu[0, s, :, lanes] = column(s, 4 + k)
            b_gu[1, s, :, lanes] = column(s, 4 + per + k)
            a_down[s, :, lanes] = column(s, 4 + 2 * per + k)


def unpack(grad, layer, sets, rank_own, rank_row, hidden):
    sets_own = sets.shape[0]
    width = grad.shape[1]
    shape = jax.ShapeDtypeStruct
    return pl.pallas_call(
        functools.partial(unpack_kernel, rank_own, rank_row),
        out_shape=[
            shape(layer.shape, low),
            shape(grad.shape, wide),
            shape((3, sets_own, rank_own, width), wide),
            shape((3, sets_own, rank_row, width), wide),
            shape((sets_own, rank_row, width), wide),
            shape((sets_own, rank_own, width), wide),
            shape((2, sets_own, rank_own, width), wide),
            shape((2, sets_own, rank_row, hidden), wide),
            shape((sets_own, rank_row, hidden), wide),
            shape((sets_own, rank_own, width), wide),
        ],
        in_specs=[VM] * 3,
        out_specs=[VM] * 10,
        name="unpack",
    )(grad, layer, sets)


def middle_kernel(n, nr, m, hop, cuts, head_ref, x_hbm, cot_hbm, gain_ref, wo_hbm, wg_hbm, wd_hbm,
                  table_ref, ao_ref, bg_ref, ad_ref,
                  dhead_ref, out_hbm, grad_hbm, full_ref, co_ref, cg_ref, cd_ref,
                  out_half, grad_half, wo, wg, wd, x_half, cot_half, raw, attn, d_attn, h_all, df_all, da_all, gu, part,
                  recv_right, recv_left, hid, red_gu, red_down, back_gu, back_down,
                  sems_send, sems_recv, send_in, recv_in, send_out, recv_out, local_in, local_out, load,
                  send_g, recv_g, local_g, send_d, recv_d, local_d):
    g, r, c = lax.axis_index("dp"), lax.axis_index("row"), lax.axis_index("col")
    ag_ref = table_ref.at[3 * RANK:5 * RANK]
    bo_ref = table_ref.at[5 * RANK:6 * RANK]
    bd_ref = table_ref.at[6 * RANK:]
    rows_all, width_all = part.shape
    half = rows_all // 2
    own = rows_all // n
    tree_part = own * nr
    chunks = half // m
    blocks = 4
    band = half // blocks
    hidden = ad_ref.shape[1]
    width = width_all // nr
    left = {"col": jnp.maximum(c - 1, 0)}
    right = {"col": jnp.minimum(c + 1, n - 1)}
    first = c == 0
    last = c == n - 1
    inner = jnp.logical_and(c > 0, c < n - 1)

    base = jnp.where(last, half, 0)
    a_cut = hidden // 4
    share_g = Share(wg_hbm, wg, cuts, (send_g, recv_g, local_g))
    share_d = Share(wd_hbm, wd, cuts // 2, (send_d, recv_d, local_d))
    loads = [pltpu.make_async_copy(wo_hbm, wo, load.at[0])]
    load_x = pltpu.make_async_copy(x_hbm.at[span(base, half)], x_half, load.at[1])
    load_cot = pltpu.make_async_copy(cot_hbm, cot_half, load.at[2])
    store_out = pltpu.make_async_copy(out_half, out_hbm, load.at[3])
    store_grad = pltpu.make_async_copy(grad_half, grad_hbm, load.at[4])
    is_owner = jnp.logical_or(first, last)
    loads[0].start()

    def piece_in(d, b):
        peer = lax.rem(r + d, nr)
        return remote(
            head_ref.at[span(b * tree_part + peer * own, own)],
            attn.at[span(b * own, own), span(r * HEAD, HEAD)],
            send_in.at[d - 1, b], recv_in.at[d - 1, b], {"row": peer},
        )

    def local_piece_in(b):
        return pltpu.make_async_copy(
            head_ref.at[span(b * tree_part + r * own, own)],
            attn.at[span(b * own, own), span(r * HEAD, HEAD)], local_in.at[b]
        )

    per_block = blocks // (n // 2)

    def out_rows(b, side):
        at = side * (n // 2) + b // per_block
        inside = lax.rem(b, per_block) * band
        return span(at * own + inside, band), span(at * tree_part + r * own + inside, band)

    def piece_out(d, b, side):
        peer = lax.rem(r + d, nr)
        here, there = out_rows(b, side)
        return remote(
            d_attn.at[here, span(peer * HEAD, HEAD)], dhead_ref.at[there],
            send_out.at[side * (nr - 1) + d - 1, b], recv_out.at[side * (nr - 1) + d - 1, b], {"row": peer},
        )

    def local_piece_out(b, side):
        here, there = out_rows(b, side)
        return pltpu.make_async_copy(d_attn.at[here, span(r * HEAD, HEAD)], dhead_ref.at[there], local_out.at[side, b])

    for b in range(n):
        local_piece_in(b).start()
    barrier = pltpu.get_barrier_semaphore()
    for d in range(1, nr):
        pl.semaphore_signal(barrier, inc=1, device_id={"row": lax.rem(r + d, nr)}, device_id_type=MESH)

    @pl.when(c > 0)
    def _():
        pl.semaphore_signal(barrier, inc=1, device_id=left, device_id_type=MESH)

    @pl.when(c < n - 1)
    def _():
        pl.semaphore_signal(barrier, inc=1, device_id=right, device_id_type=MESH)

    pl.semaphore_signal(barrier, inc=1, device_id={"dp": flip(g)}, device_id_type=MESH)
    full_ref[...] = jnp.zeros_like(full_ref)
    co_ref[...] = jnp.zeros_like(co_ref)
    cg_ref[...] = jnp.zeros_like(cg_ref)
    cd_ref[...] = jnp.zeros_like(cd_ref)

    @pl.when(inner)
    def _():
        pl.semaphore_wait(barrier, nr + 2)

    @pl.when(jnp.logical_not(inner))
    def _():
        pl.semaphore_wait(barrier, nr + 1)

    middle = n // 2
    for b in range(middle):
        for block in (b, middle + b):
            for d in range(1, nr):
                piece_in(d, block).start()
    load_x.start()
    load_cot.start()
    share_g.start_far()
    share_d.start_far()
    share_g.start_near()
    share_d.start_near()

    def rows(j, start=0):
        return span(start + j * m, m)

    def band_rows(b):
        return span(b * band, band), span(half + b * band, band)

    def take(ref, b):
        low_rows, high_rows = band_rows(b)
        return jnp.concatenate([ref[low_rows, :], ref[high_rows, :]], axis=0)

    def put(b, lanes, value):
        low_rows, high_rows = band_rows(b)
        part[low_rows, lanes] = value[:band].astype(low)
        part[high_rows, lanes] = value[band:].astype(low)

    around = hop * 2 * (n - 1)
    each = chunks // blocks

    def relay_stage(stage, per, done, work, owner_step, all_ref, pump=None, coming=None):
        def send(kind, j, src, dst, to):
            return remote(src, dst, sems_send.at[stage, kind, j], sems_recv.at[stage, kind, j], to)

        def reduce_right(j):
            return send(0, j, part.at[rows(j, half)], recv_right.at[rows(j)], right)

        def reduce_left(j):
            return send(1, j, part.at[rows(j)], recv_left.at[rows(j)], left)

        def spread_left(j):
            return send(2, j, all_ref.at[rows(j, half)], all_ref.at[rows(j, half)], left)

        def spread_right(j):
            return send(3, j, all_ref.at[rows(j)], all_ref.at[rows(j)], right)

        total_slices = per * blocks
        lead = 0 if done else per

        def slices_before(i):
            if done:
                return jnp.minimum(done + i, total_slices)
            late = per + (jnp.maximum(i - per, 0) * per) // each
            return jnp.minimum(jnp.where(i < per, i, late), total_slices)

        @pl.loop(0, lead + chunks + around + (1 if coming is not None else 0))
        def _(ii):
            i = ii - lead

            def on(offset, who, run):
                j = i - offset

                @pl.when(jnp.logical_and(who, jnp.logical_and(j >= 0, j < chunks)))
                def _():
                    run(j)

            def mid_right(j):
                reduce_right(j).wait_recv()
                at = rows(j, half)
                part[at, :] = (part[at, :].astype(wide) + recv_right[rows(j), :].astype(wide)).astype(low)
                reduce_right(j).start()

            def mid_left(j):
                reduce_left(j).wait_recv()
                at = rows(j)
                part[at, :] = (part[at, :].astype(wide) + recv_left[at, :].astype(wide)).astype(low)
                reduce_left(j).start()

            def end_right(j):
                reduce_right(j).wait_recv()
                total = part[rows(j, half), :].astype(wide) + recv_right[rows(j), :].astype(wide)
                all_ref[rows(j, half), :] = owner_step(total, rows(j))
                spread_left(j).start()

            def end_left(j):
                reduce_left(j).wait_recv()
                total = part[rows(j), :].astype(wide) + recv_left[rows(j), :].astype(wide)
                all_ref[rows(j), :] = owner_step(total, rows(j))
                spread_right(j).start()

            def pass_left(j):
                spread_left(j).wait_recv()
                spread_left(j).start()

            def pass_right(j):
                spread_right(j).wait_recv()
                spread_right(j).start()

            def arrived(j):
                @pl.when(first)
                def _():
                    reduce_right(j).wait_send()
                    spread_left(j).wait_recv()

                @pl.when(last)
                def _():
                    reduce_left(j).wait_send()
                    spread_right(j).wait_recv()

                @pl.when(inner)
                def _():
                    reduce_right(j).wait_send()
                    reduce_left(j).wait_send()

            on(0, first, lambda j: reduce_right(j).start())
            on(0, last, lambda j: reduce_left(j).start())
            on(hop * c, inner, mid_right)
            on(hop * (n - 1 - c), inner, mid_left)
            on(hop * (n - 1), last, end_right)
            on(hop * (n - 1), first, end_left)
            on(hop * (2 * (n - 1) - c), inner, pass_left)
            on(hop * (n - 1 + c), inner, pass_right)
            on(around, True, arrived)

            @pl.loop(slices_before(ii), slices_before(ii + 1))
            def _(t):
                work(t // per, lax.rem(t, per))

            if coming is not None:
                next_work, next_per, next_before = coming

                @pl.loop(next_before(i), next_before(i + 1))
                def _(t):
                    next_work(t // next_per, lax.rem(t, next_per))

            if pump is not None:
                pump(ii)

        @pl.loop(0, chunks)
        def _(j):
            @pl.when(first)
            def _():
                spread_right(j).wait_send()

            @pl.when(last)
            def _():
                spread_left(j).wait_send()

            @pl.when(inner)
            def _():
                spread_left(j).wait_send()
                spread_right(j).wait_send()

    def shard(j, ref):
        return slice(j * (ref.shape[0] // nr), (j + 1) * (ref.shape[0] // nr))

    def out_work(b, k):
        @pl.when(b == 0)
        def _():
            loads[0].wait()

        @pl.when(lax.rem(b, blocks // middle) == 0)
        def _():
            at = b // (blocks // middle)
            for block in (at, middle + at):
                for d in range(1, nr):
                    piece_in(d, block).wait_recv()
                local_piece_in(block).wait()

        rows_in = take(attn, b)
        red = dot_t(rows_in, ao_ref[...]).astype(low)
        for j in range(nr):
            lanes = slice(j * width, (j + 1) * width)
            put(b, lanes, dot(rows_in, wo[shard(j, wo), :]) + dot(red, bo_ref[:, lanes]))

    gain_a = gain_ref[0:1, :]
    gain_f = gain_ref[1:2, :]

    def attn_owner(total, at):
        raw[at, :] = total
        flat = total * norm_factor(row_sum(total * total))
        return (x_half[at, :].astype(wide) + flat * gain_a).astype(low)

    first_pass = 5
    apart = 3
    late = 2
    passes = cuts + cuts // 2

    def pump(ii):
        at = ii - first_pass

        @pl.when(jnp.logical_and(at >= 0, lax.rem(at, apart) == 0))
        def _():
            t = at // apart

            @pl.when(t < cuts)
            def _():
                share_g.pass_far(t)

            @pl.when(jnp.logical_and(t >= cuts, t < passes))
            def _():
                share_d.pass_far(t - cuts)

            t = t - late

            @pl.when(jnp.logical_and(t >= 0, t < cuts))
            def _():
                share_g.pass_twin(t)

            @pl.when(jnp.logical_and(t >= cuts, t < passes))
            def _():
                share_d.pass_twin(t - cuts)

    load_x.wait()
    relay_stage(0, 1, 0, out_work, attn_owner, h_all, pump)
    in_loop = 1 + chunks + around

    share_g.wait_all()

    def gate_slice(b, k):
        rows_in = take(h_all, b)

        @pl.when(k == 0)
        def _():
            red_gu[b] = dot_t(rows_in, ag_ref[...]).astype(low)

        at = pl.multiple_of(k * a_cut, a_cut)
        lanes = pl.ds(at, a_cut)
        up_lanes = pl.ds(pl.multiple_of(hidden + at, a_cut), a_cut)
        red = red_gu[b]
        gate = dot(rows_in, wg[:, lanes]) + dot(red[:, :RANK], bg_ref[0, :, lanes])
        up = dot(rows_in, wg[:, up_lanes]) + dot(red[:, RANK:], bg_ref[1, :, lanes])
        gu[b, :, lanes] = gate.astype(low)
        gu[b, :, up_lanes] = up.astype(low)
        hid[:, lanes] = (gate * jax.nn.sigmoid(gate) * up).astype(low)

    def down_slice(b, k):
        @pl.when(jnp.logical_and(b == 0, k == 0))
        def _():
            @pl.loop(in_loop, jnp.maximum(in_loop, first_pass + apart * (passes + late)))
            def _(ii):
                pump(ii)

            share_d.wait_all()

        rows_in = hid[:, :hidden]

        @pl.when(k == 0)
        def _():
            red_down[b] = dot_t(rows_in, ad_ref[...]).astype(low)

        for s in range(nr // 2):
            j = k * (nr // 2) + s
            lanes = span(j * width, width)
            down_rows = pl.ds(pl.multiple_of(j * hidden, hidden), hidden)
            put(b, lanes, dot(rows_in, wd[down_rows, :]) + dot(red_down[b], bd_ref[:, lanes]))

    def ffn_work(b, k):
        @pl.when(k < 4)
        def _():
            gate_slice(b, k)

        @pl.when(k >= 4)
        def _():
            down_slice(b, k - 4)

    def ffn_owner(total, at):
        a_raw = raw[at, :]
        h = x_half[at, :].astype(wide) + a_raw * norm_factor(row_sum(a_raw * a_raw)) * gain_a
        factor = norm_factor(row_sum(total * total))
        flat = total * factor
        out_half[at, :] = (h + flat * gain_f).astype(low)
        scaled = cot_half[at, :].astype(wide) * gain_f
        return (factor * (scaled - flat * (row_sum(scaled * flat) * (1.0 / D)))).astype(low)

    b_cut = hidden // 2

    def hidden_back(b, k):
        rows_in = take(df_all, b)

        @pl.when(k == 0)
        def _():
            back_down[...] = dot_t(rows_in, bd_ref[...]).astype(low)

        at = pl.multiple_of(k * b_cut, b_cut)
        lanes = pl.ds(at, b_cut)
        up_lanes = pl.ds(pl.multiple_of(hidden + at, b_cut), b_cut)
        back = back_down[...]
        grad = dot(back, ad_ref[:, lanes])
        for j in range(nr):
            down_rows = pl.ds(pl.multiple_of(j * hidden + at, b_cut), b_cut)
            grad = grad + dot_t(rows_in[:, j * width:(j + 1) * width], wd[down_rows, :])
        gate = gu[b, :, lanes].astype(wide)
        up = gu[b, :, up_lanes].astype(wide)
        sigma = jax.nn.sigmoid(gate)
        silu = gate * sigma
        d_gate = (grad * up * sigma * (1.0 + gate * (1.0 - sigma))).astype(low)
        d_up = (grad * silu).astype(low)
        hid[:, lanes] = d_gate
        hid[:, up_lanes] = d_up
        cd_ref[:, lanes] += t_dot(back, (silu * up).astype(low))
        red = red_gu[b]
        cg_ref[0, :, lanes] += t_dot(red[:, :RANK], d_gate)
        cg_ref[1, :, lanes] += t_dot(red[:, RANK:], d_up)

    o_cut = width_all // 4

    def gate_back(b, k):
        @pl.when(k == 0)
        def _():
            back_gu[:, :RANK] = dot_t(hid[:, :hidden], bg_ref[0]).astype(low)
            back_gu[:, RANK:] = dot_t(hid[:, hidden:], bg_ref[1]).astype(low)

        lanes = span(k * o_cut, o_cut)
        put(b, lanes, dot_t(hid[...], wg[lanes, :]) + dot(back_gu[...], ag_ref[:, lanes]))

        @pl.when(k == 3)
        def _():
            full_ref[:2 * RANK, :] += t_dot(back_gu[...], take(h_all, b))
            full_ref[3 * RANK:, :] += t_dot(red_down[b], take(df_all, b))

    def back_work(b, k):
        @pl.when(k < 2)
        def _():
            hidden_back(b, k)

        @pl.when(k >= 2)
        def _():
            gate_back(b, k - 2)

    def back_owner(total, at):
        grad = cot_half[at, :].astype(wide) + total
        grad_half[at, :] = grad
        a_raw = raw[at, :]
        factor = norm_factor(row_sum(a_raw * a_raw))
        flat = a_raw * factor
        scaled = grad * gain_a
        return (factor * (scaled - flat * (row_sum(scaled * flat) * (1.0 / D)))).astype(low)

    def out_back(b, k):
        rows_in = take(da_all, b)
        back = dot_t(rows_in, bo_ref[...]).astype(low)
        grad = dot(back, ao_ref[...])
        for j in range(nr):
            grad = grad + dot_t(rows_in[:, j * width:(j + 1) * width], wo[shard(j, wo), :])
        for side in range(2):
            d_attn[out_rows(b, side)[0], :] = grad[side * band:(side + 1) * band].astype(low)
            for d in range(1, nr):
                piece_out(d, b, side).start()
            local_piece_out(b, side).start()
        attn_rows = take(attn, b)
        co_ref[...] += t_dot(back, attn_rows)
        red = dot_t(attn_rows, ao_ref[...]).astype(low)
        full_ref[2 * RANK:3 * RANK, :] += t_dot(red, rows_in)

    begin = around + each

    def back_before(i):
        return jnp.clip(i - begin, 0, chunks - each)

    def out_before(i):
        return jnp.clip((i - around - 1) // each, 0, blocks)

    load_cot.wait()
    relay_stage(1, 6, 0, ffn_work, ffn_owner, df_all, None, (back_work, 6, back_before))
    pl.when(is_owner)(store_out.start)
    relay_stage(2, 6, chunks - each, back_work, back_owner, da_all, None, (out_back, 1, out_before))
    pl.when(is_owner)(store_grad.start)

    @pl.loop(0, n)
    def _(b):
        for d in range(1, nr):
            piece_in(d, b).wait_send()

    @pl.loop(0, blocks)
    def _(b):
        for side in range(2):
            for d in range(1, nr):
                piece_out(d, b, side).wait()
            local_piece_out(b, side).wait()

    share_g.drain()
    share_d.drain()

    @pl.when(is_owner)
    def _():
        store_out.wait()
        store_grad.wait()


def middle(attn_head, x, cot_half, gains, w_out, w_gu, w_down, table, a_out, b_gu, a_down, n, nr, m=16, hop=2, cuts=8):
    group, width_all = x.shape
    half = group // 2
    width = width_all // nr
    hidden = a_down.shape[1]
    chunks = half // m
    band = group // 4
    dma = pltpu.SemaphoreType.DMA
    any_space = pl.BlockSpec(memory_space=pl.ANY)
    shape = jax.ShapeDtypeStruct
    return pl.pallas_call(
        functools.partial(middle_kernel, n, nr, m, hop, cuts),
        out_shape=[
            shape(attn_head.shape, low),
            shape((half, width_all), low),
            shape((half, width_all), wide),
            shape((4 * RANK, width_all), wide),
            shape((RANK, a_out.shape[1]), wide),
            shape((2, RANK, hidden), wide),
            shape((RANK, hidden), wide),
        ],
        in_specs=[any_space, any_space, any_space, VM, any_space, any_space, any_space] + [VM] * 4,
        out_specs=[any_space] * 3 + [VM] * 4,
        scratch_shapes=[
            pltpu.VMEM((half, width_all), low),
            pltpu.VMEM((half, width_all), wide),
            pltpu.VMEM(w_out.shape, low),
            pltpu.VMEM((w_gu.shape[0] * nr, w_gu.shape[1]), low),
            pltpu.VMEM((w_down.shape[0] * nr, w_down.shape[1]), low),
            pltpu.VMEM((half, width_all), low),
            pltpu.VMEM((half, width_all), low),
            pltpu.VMEM((half, width_all), wide),
            pltpu.VMEM((group, a_out.shape[1]), low),
            pltpu.VMEM((group, a_out.shape[1]), low),
            pltpu.VMEM((group, width_all), low),
            pltpu.VMEM((group, width_all), low),
            pltpu.VMEM((group, width_all), low),
            pltpu.VMEM((4, band, 2 * hidden), low),
            pltpu.VMEM((group, width_all), low),
            pltpu.VMEM((half, width_all), low),
            pltpu.VMEM((half, width_all), low),
            pltpu.VMEM((band, 2 * hidden), low),
            pltpu.VMEM((4, band, 2 * RANK), low),
            pltpu.VMEM((4, band, RANK), low),
            pltpu.VMEM((band, 2 * RANK), low),
            pltpu.VMEM((band, RANK), low),
            dma((3, 4, chunks)), dma((3, 4, chunks)),
            dma((nr - 1, n)), dma((nr - 1, n)), dma((2 * (nr - 1), 4)), dma((2 * (nr - 1), 4)), dma((n,)), dma((2, 4)),
            dma((5,)),
        ] + share_sems(cuts) + share_sems(cuts // 2),
        compiler_params=pltpu.CompilerParams(collective_id=0, has_side_effects=True, vmem_limit_bytes=67043328),
        name="middle",
    )(attn_head, x, cot_half, gains, w_out, w_gu, w_down, table, a_out, b_gu, a_down)


def per_device(
    tokens,
    cotangent,
    seg_ids,
    positions,
    parents,
    tree_sets,
    gain_q,
    gain_k,
    gain_attn,
    gain_ffn,
    query_key_value_weight,
    output_weight,
    gate_up_weight,
    down_weight,
    query_key_value_adapter_first,
    query_key_value_adapter_second,
    output_adapter_first,
    output_adapter_second,
    gate_up_adapter_first,
    gate_up_adapter_second,
    down_adapter_first,
    down_adapter_second,
):
    dp_count = lax.axis_size("dp")
    row_count = lax.axis_size("row")
    col_count = lax.axis_size("col")
    row_at = lax.axis_index("row")
    tree_tokens = seg_ids.shape[0]
    assert tree_sets.shape[0] == 1 and col_count == 4
    set_count = output_adapter_first.shape[0]
    own = tokens.shape[0] // row_count
    group = own * col_count
    width_row = tokens.shape[1]
    width_col = gain_q.shape[0]
    hidden_col = down_weight.shape[0]
    tree_set = tree_sets[0]

    tables = (
        query_key_value_adapter_first,
        query_key_value_adapter_second,
        output_adapter_first,
        output_adapter_second,
        gate_up_adapter_first,
        gate_up_adapter_second,
        down_adapter_first,
        down_adapter_second,
    )
    narrow, b_qkv, a_out, b_gu, a_down = prep(tree_sets, tables)
    gain_pair = jnp.pad(jnp.stack([gain_attn, gain_ffn]), ((0, 6), (0, 0)))
    pos_own = lax.dynamic_index_in_dim(
        positions.reshape(col_count, row_count, own), row_at, 1, keepdims=False
    ).reshape(group)
    cos2, sin2 = angles(pos_own)
    gq, gk = gain_q[None, :], gain_k[None, :]
    parent_at, branch_flag = tree_tables(seg_ids, parents)
    x, table, gains, g_half, raw, factors, qkv_head, w_qkv, w_out, w_gu = front(
        tokens,
        narrow,
        gain_pair,
        cotangent,
        query_key_value_weight.reshape(width_row, 3 * width_col),
        output_weight,
        gate_up_weight,
        b_qkv,
        gq,
        gk,
        cos2,
        sin2,
        col_count,
        row_count,
    )
    attn_head, lse = attend(qkv_head, parent_at, branch_flag)
    d_attn_head, out_half, d_h_half, full_mid, part_ao, part_bgu, part_ad = middle(
        attn_head,
        x,
        g_half,
        gains,
        w_out,
        w_gu,
        down_weight,
        table,
        a_out,
        b_gu,
        a_down,
        col_count,
        row_count,
    )
    d_qkv_head = attend_back(qkv_head, d_attn_head, parent_at, branch_flag, lse)
    hot = (tree_set == lax.broadcasted_iota(jnp.int32, (set_count, width_row), 0)).astype(wide)
    in_grad, layer, sets = rear(
        d_qkv_head,
        raw,
        factors,
        gq,
        gk,
        cos2,
        sin2,
        out_half,
        x,
        w_qkv,
        table,
        b_qkv,
        d_h_half,
        full_mid,
        part_ao,
        part_bgu,
        part_ad,
        hot,
        set_count // dp_count,
        col_count,
        row_count,
        dp_count,
    )
    return tuple(unpack(in_grad, layer, sets, RANK // col_count, RANK // row_count, hidden_col))


def solution(mesh):
    in_specs = (
        P(("dp", "col"), "row"),
        P(("dp", "col"), "row"),
        P("dp"),
        P("dp"),
        P("dp", None),
        P("dp"),
        P("col"),
        P("col"),
        P("row"),
        P("row"),
        P("row", None, "col"),
        P("col", "row"),
        P("row", None, "col"),
        P("col", "row"),
        P(None, None, None, "row"),
        P(None, None, None, "col"),
        P(None, None, "col"),
        P(None, None, "row"),
        P(None, None, None, "row"),
        P(None, None, None, "col"),
        P(None, None, "col"),
        P(None, None, "row"),
    )
    out_specs = (
        P(("dp", "col"), "row"),
        P(("dp", "col"), "row"),
        P(None, "dp", "col", "row"),
        P(None, "dp", "row", "col"),
        P("dp", "row", "col"),
        P("dp", "col", "row"),
        P(None, "dp", "col", "row"),
        P(None, "dp", "row", "col"),
        P("dp", "row", "col"),
        P("dp", "col", "row"),
    )
    return jax.shard_map(
        per_device, mesh=mesh, in_specs=in_specs, out_specs=out_specs, check_vma=False
    )
```

```python
import functools

import jax
import jax.numpy as jnp
from jax import lax
from jax.experimental import pallas as pl
from jax.experimental.pallas import tpu as pltpu
from jax.sharding import PartitionSpec as P

D = 2048
HEAD = 128
RANK = 16
SEG = 128
TRUNK = 1024
QT = 256
MESH = pl.DeviceIdType.MESH
VM = pl.BlockSpec(memory_space=pltpu.VMEM)
precise = lax.Precision.HIGHEST

epsilon = 1e-06
rope_base = 500000.0
masked_out = -1e30
low = jnp.bfloat16
wide = jnp.float32
last_last = (((1,), (1,)), ((), ()))
first_first = (((0,), (0,)), ((), ()))


def dot(left, right):
    return jnp.dot(left, right, preferred_element_type=wide)


def dot_t(left, right):
    return lax.dot_general(left, right, last_last, preferred_element_type=wide)


def t_dot(left, right):
    return lax.dot_general(left, right, first_first, preferred_element_type=wide)


def angles(positions):
    lane = jnp.arange(HEAD, dtype=jnp.int32)
    frequency = rope_base ** (-((lane % (HEAD // 2)).astype(wide) * 2.0) / HEAD)
    angle_table = positions.astype(wide)[:, None] * frequency[None, :]
    return (jnp.cos(angle_table), jnp.where(lane < HEAD // 2, -1.0, 1.0) * jnp.sin(angle_table))


def norm_factor(square_sum):
    return lax.rsqrt(square_sum * (1.0 / D) + epsilon)


def tree_tables(seg_ids, parents):
    tail_seg = seg_ids[TRUNK::SEG]
    labels = jnp.arange(parents.shape[1], dtype=jnp.int32)
    tail_parent = jnp.sum(jnp.where(tail_seg[:, None] == labels[None, :], parents[0][None, :], 0), axis=1)
    hit = (tail_seg[None, :] == tail_parent[:, None])
    at = jnp.arange(tail_seg.shape[0], dtype=jnp.int32) + TRUNK // SEG
    parent_at = jnp.sum(jnp.where(hit, at[None, :], 0), axis=1)
    bias = jnp.where(tail_parent > 0, 0.0, masked_out).astype(wide)
    return parent_at, jnp.broadcast_to(bias[:, None], (tail_seg.shape[0], SEG))


def row_sum(v): return jnp.sum(v, axis=1, keepdims=True)

def params(collective):
    return pltpu.CompilerParams(collective_id=collective, has_side_effects=True, vmem_limit_bytes=60 << 20)


def span(at, size):
    return pl.ds(pl.multiple_of(at, size), size)


def remote(src, dst, send_sem, recv_sem, to):
    return pltpu.make_async_remote_copy(
        src_ref=src, dst_ref=dst, send_sem=send_sem, recv_sem=recv_sem, device_id=to, device_id_type=MESH
    )


def greet(n, nr, extra=0):
    r, c = lax.axis_index("row"), lax.axis_index("col")
    me = r * n + c
    barrier = pltpu.get_barrier_semaphore()

    @pl.loop(1, n * nr)
    def _(d):
        peer = lax.rem(me + d, n * nr)
        pl.semaphore_signal(barrier, inc=1, device_id={"row": peer // n, "col": lax.rem(peer, n)}, device_id_type=MESH)

    pl.semaphore_wait(barrier, n * nr - 1 + extra)


def row_sums(first, second):
    ones = jnp.ones((8, first.shape[1]), wide)
    at = lax.broadcasted_iota(jnp.int32, (8, first.shape[0]), 0)
    sum_first = lax.dot_general(ones, first, last_last, preferred_element_type=wide, precision=precise)
    sum_second = lax.dot_general(ones, second, last_last, preferred_element_type=wide, precision=precise)
    return jnp.where(at < 4, sum_first, sum_second)


def down_columns(values, at):
    pick = (lax.broadcasted_iota(jnp.int32, (8, HEAD), 0) == at).astype(wide)
    return lax.dot_general(values, pick, first_first, preferred_element_type=wide, precision=precise)


def flip(v):
    return v + 1 - 2 * lax.rem(v, 2)


class Share:
    def __init__(self, src, dst, cuts, sems):
        self.send, self.recv, self.local = sems
        self.src, self.cuts = src, cuts
        g, r = lax.axis_index("dp"), lax.axis_index("row")
        size = src.shape[0]
        half = size // 2
        step = half // cuts
        far = lax.rem(r + 2, 4)
        mine = lax.rem(g, 2)
        near_to, far_to, twin_to = {"row": flip(r)}, {"row": far}, {"dp": flip(g)}

        def rows(shard, part, i):
            return pl.ds(pl.multiple_of(shard * size + part * half + i * step, step), step)

        def copy(kind, i, src, dst, to):
            return remote(src, dst, self.send.at[kind, i], self.recv.at[kind, i], to)

        def hand(kind, part, to):
            return lambda i: copy(kind, i, dst.at[rows(far, part, i)], dst.at[rows(far, part, i)], to)

        whole = span(r * size, size)
        self.own = pltpu.make_async_copy(src, dst.at[whole], self.local)
        self.near = copy(0, 0, src, dst.at[whole], near_to)
        self.far = lambda i: copy(
            1, i, src.at[pl.ds(pl.multiple_of(mine * half + i * step, step), step)], dst.at[rows(r, mine, i)], far_to
        )
        self.far_near = hand(2, mine, near_to)
        self.far_twin = hand(3, mine, twin_to)
        self.twin_near = hand(4, 1 - mine, near_to)

    def start_far(self):
        for i in range(self.cuts):
            self.far(i).start()

    def start_near(self):
        self.own.start()
        self.near.start()

    def pass_far(self, i):
        self.far(i).wait_recv()
        self.far_twin(i).start()
        self.far_near(i).start()

    def pass_twin(self, i):
        self.far_twin(i).wait_recv()
        self.twin_near(i).start()

    def wait_all(self):
        self.own.wait()
        self.near.wait_recv()
        for i in range(self.cuts):
            self.far_near(i).wait_recv()
            self.twin_near(i).wait_recv()

    def drain(self):
        self.near.wait_send()
        for i in range(self.cuts):
            self.far(i).wait_send()
            self.far_near(i).wait_send()
            self.far_twin(i).wait_send()
            self.twin_near(i).wait_send()


def share_sems(cuts):
    dma = pltpu.SemaphoreType.DMA
    return [dma((5, cuts)), dma((5, cuts)), dma]


def prep_kernel(set_ref, fq_ref, sq_ref, fo_ref, so_ref, fg_ref, sg_ref, fd_ref, sd_ref,
                narrow_ref, bq_ref, ao_ref, bg_ref, ad_ref):
    for j in range(3):
        narrow_ref[j * RANK:(j + 1) * RANK, :] = fq_ref[j, 0].astype(low)
        bq_ref[j * RANK:(j + 1) * RANK, :] = sq_ref[j, 0].astype(low)
    for j in range(2):
        narrow_ref[(3 + j) * RANK:(4 + j) * RANK, :] = fg_ref[j, 0].astype(low)
        bg_ref[j] = sg_ref[j, 0].astype(low)
    narrow_ref[5 * RANK:6 * RANK, :] = so_ref[0].astype(low)
    narrow_ref[6 * RANK:, :] = sd_ref[0].astype(low)
    ao_ref[...] = fo_ref[0].astype(low)
    ad_ref[...] = fd_ref[0].astype(low)


def prep(tree_sets, tables):
    fq, sq, fo, so, fg, sg, fd, sd = tables

    def pick(table):
        if table.ndim == 4:
            return pl.BlockSpec((table.shape[0], 1) + table.shape[2:], lambda i, s: (0, s[0], 0, 0))
        return pl.BlockSpec((1,) + table.shape[1:], lambda i, s: (s[0], 0, 0))

    def out(*shape):
        return pl.BlockSpec(shape, lambda i, s: (0,) * len(shape)), jax.ShapeDtypeStruct(shape, low)

    outs = [
        out(7 * RANK, fq.shape[-1]), out(3 * RANK, sq.shape[-1]), out(RANK, fo.shape[-1]),
        out(2, RANK, sg.shape[-1]), out(RANK, fd.shape[-1]),
    ]
    return pl.pallas_call(
        prep_kernel,
        grid_spec=pltpu.PrefetchScalarGridSpec(
            num_scalar_prefetch=1, grid=(1,), in_specs=[pick(t) for t in tables], out_specs=[o[0] for o in outs]
        ),
        out_shape=[o[1] for o in outs],
        name="prep",
    )(tree_sets, *tables)


def lower_mask(size):
    return lax.broadcasted_iota(jnp.int32, (size, size), 1) <= lax.broadcasted_iota(jnp.int32, (size, size), 0)


def softmax_parts(parts):
    top = jnp.max(parts[0], axis=1, keepdims=True)
    for s in parts[1:]:
        top = jnp.maximum(top, jnp.max(s, axis=1, keepdims=True))
    raised = [jnp.exp(s - top) for s in parts]
    total = jnp.sum(raised[0], axis=1, keepdims=True)
    for e in raised[1:]:
        total = total + jnp.sum(e, axis=1, keepdims=True)
    inverse = 1.0 / total
    return raised, inverse, top + jnp.log(total)


def tail_parts(q, qkv, at, parent, flag):
    scale = HEAD ** -0.5
    k_lanes = slice(HEAD, 2 * HEAD)
    trunk = dot_t(q, qkv[:TRUNK, k_lanes]) * scale
    branch = dot_t(q, qkv[pl.ds(parent, SEG), k_lanes]) * scale + flag
    own = jnp.where(lower_mask(SEG), dot_t(q, qkv[pl.ds(at, SEG), k_lanes]) * scale, masked_out)
    return [trunk, branch, own]


def trunk_parts(q, qkv, i):
    scale = HEAD ** -0.5
    k_lanes = slice(HEAD, 2 * HEAD)
    own = dot_t(q, qkv[i * QT:(i + 1) * QT, k_lanes]) * scale
    parts = [jnp.where(lower_mask(QT), own, masked_out)]
    if i:
        parts.append(dot_t(q, qkv[:i * QT, k_lanes]) * scale)
    return parts


def attend_body(parent_ref, flag_ref, qkv, o_ref, lse_ref):
    v_lanes = slice(2 * HEAD, 3 * HEAD)
    for i in range(TRUNK // QT):
        at = slice(i * QT, (i + 1) * QT)
        p, inverse, lse = softmax_parts(trunk_parts(qkv[at, :HEAD], qkv, i))
        o = dot(p[0].astype(low), qkv[at, v_lanes])
        if i:
            o = o + dot(p[1].astype(low), qkv[:i * QT, v_lanes])
        o_ref[at, :] = (o * inverse).astype(low)
        lse_ref[at, :] = lse

    @pl.loop(0, (qkv.shape[0] - TRUNK) // SEG, unroll=4)
    def _(j):
        at = pl.multiple_of(TRUNK + j * SEG, SEG)
        parent = pl.multiple_of(parent_ref[j] * SEG, SEG)
        rows = pl.ds(at, SEG)
        p, inverse, lse = softmax_parts(tail_parts(qkv[rows, :HEAD], qkv, at, parent, flag_ref[pl.ds(j, 1), :]))
        o = dot(p[0].astype(low), qkv[:TRUNK, v_lanes])
        o = o + dot(p[1].astype(low), qkv[pl.ds(parent, SEG), v_lanes])
        o = o + dot(p[2].astype(low), qkv[rows, v_lanes])
        o_ref[rows, :] = (o * inverse).astype(low)
        lse_ref[rows, :] = lse


def back_parts(scores, lse, d_out, keys, values):
    probs = [jnp.exp(s - lse) for s in scores]
    grads = [dot_t(d_out, v) for v in values]
    inner = sum(jnp.sum(p * g, axis=1, keepdims=True) for p, g in zip(probs, grads))
    d_scores = [(p * (g - inner)).astype(low) for p, g in zip(probs, grads)]
    dq = sum(dot(d, k) for d, k in zip(d_scores, keys))
    return d_scores, [p.astype(low) for p in probs], dq


def attend_back_kernel(parent_ref, flag_ref, qkv, do_ref, lse_ref, d_ref, dk_acc, dv_acc):
    scale = HEAD ** -0.5
    k_lanes = slice(HEAD, 2 * HEAD)
    v_lanes = slice(2 * HEAD, 3 * HEAD)
    dk_acc[...] = jnp.zeros_like(dk_acc)
    dv_acc[...] = jnp.zeros_like(dv_acc)
    for i in range(TRUNK // QT):
        at = slice(i * QT, (i + 1) * QT)
        spans = [at] + ([slice(0, i * QT)] if i else [])
        q, d_out = qkv[at, :HEAD], do_ref[at, :]
        d_scores, probs, dq = back_parts(
            trunk_parts(q, qkv, i), lse_ref[at, :], d_out, [qkv[s, k_lanes] for s in spans], [qkv[s, v_lanes] for s in spans]
        )
        d_ref[at, :HEAD] = (dq * scale).astype(low)
        for s, d, p in zip(spans, d_scores, probs):
            dk_acc[s, :] += t_dot(d, q)
            dv_acc[s, :] += t_dot(p, d_out)

    @pl.loop(0, (qkv.shape[0] - TRUNK) // SEG, unroll=3)
    def _(j):
        at = pl.multiple_of(TRUNK + j * SEG, SEG)
        parent = pl.multiple_of(parent_ref[j] * SEG, SEG)
        rows = pl.ds(at, SEG)
        spans = [slice(0, TRUNK), pl.ds(parent, SEG), rows]
        q, d_out = qkv[rows, :HEAD], do_ref[rows, :]
        d_scores, probs, dq = back_parts(
            tail_parts(q, qkv, at, parent, flag_ref[pl.ds(j, 1), :]), lse_ref[rows, :], d_out,
            [qkv[s, k_lanes] for s in spans], [qkv[s, v_lanes] for s in spans],
        )
        d_ref[rows, :HEAD] = (dq * scale).astype(low)
        for s, d, p in zip(spans, d_scores, probs):
            dk_acc[s, :] += t_dot(d, q)
            dv_acc[s, :] += t_dot(p, d_out)

    d_ref[:, k_lanes] = (dk_acc[...] * scale).astype(low)
    d_ref[:, v_lanes] = dv_acc[...].astype(low)


def attend(qkv, parent_at, flag):
    n = qkv.shape[0]

    def whole(*shape):
        return pl.BlockSpec(shape, lambda i, *_: (0, 0))

    return pl.pallas_call(
        attend_body,
        grid_spec=pltpu.PrefetchScalarGridSpec(
            num_scalar_prefetch=1,
            grid=(1,),
            in_specs=[whole(*flag.shape), whole(n, 3 * HEAD)],
            out_specs=[whole(n, HEAD), whole(n, 1)],
        ),
        out_shape=[jax.ShapeDtypeStruct((n, HEAD), low), jax.ShapeDtypeStruct((n, 1), wide)],
        name="attend",
    )(parent_at, flag, qkv)


def attend_back(qkv, d_o, parent_at, flag, lse):
    n = qkv.shape[0]

    def whole(*shape):
        return pl.BlockSpec(shape, lambda i, *_: (0, 0))

    return pl.pallas_call(
        attend_back_kernel,
        grid_spec=pltpu.PrefetchScalarGridSpec(
            num_scalar_prefetch=1,
            grid=(1,),
            in_specs=[whole(*flag.shape), whole(n, 3 * HEAD), whole(n, HEAD), whole(n, 1)],
            out_specs=whole(n, 3 * HEAD),
            scratch_shapes=[pltpu.VMEM((n, HEAD), wide), pltpu.VMEM((n, HEAD), wide)],
        ),
        out_shape=jax.ShapeDtypeStruct((n, 3 * HEAD), low),
        name="attend_back",
    )(parent_at, flag, qkv, d_o, lse)


def front_kernel(n, nr, m, mh, tok_ref, table_ref, gain_ref, cot_ref, wq_hbm, wo_hbm, gu_hbm, bq_ref, gq_ref, gk_ref,
                 cos_ref, sin_ref,
                 x_out, table_all, gain_all, half_ref, raw_out, factor_ref, qkv_ref, wq_out, wo_out, gu_out,
                 x_ref, raw_ref, gu_pair, gu_flat, wq, wo, stats, buf, fq, fk, red, cot_own,
                 send_a, recv_a, send_z, recv_z, send_t, recv_t, local_sem,
                 send_s, recv_s, send_h, recv_h, send_g, recv_g, local_h, local_g, send_e, recv_e,
                 send_q, recv_q, local_q, send_o, recv_o, local_o, out_sems):
    g, r, c = lax.axis_index("dp"), lax.axis_index("row"), lax.axis_index("col")
    own = tok_ref.shape[0] // nr
    width = tok_ref.shape[1]
    rows_all = own * n
    heads = width // HEAD
    tree_part = own * nr
    chunks = own // m
    left = {"col": jnp.maximum(c - 1, 0)}
    right = {"col": jnp.minimum(c + 1, n - 1)}
    share_q = Share(wq_hbm, wq, 2, (send_q, recv_q, local_q))
    share_o = Share(wo_hbm, wo, 2, (send_o, recv_o, local_o))

    def piece(d, j):
        peer = lax.rem(r + d, nr)
        return remote(
            tok_ref.at[span(peer * own + j * m, m)],
            x_ref.at[span(c * own + j * m, m), span(r * width, width)],
            send_a.at[d - 1, j], recv_a.at[d - 1, j], {"row": peer},
        )

    def block(kind, s, at, j, to):
        rows = span(at * own + j * m, m)
        return remote(x_ref.at[rows], x_ref.at[rows], send_z.at[kind, s, j], recv_z.at[kind, s, j], to)

    def table_piece(d, kind):
        src, dst = ((table_ref, table_all), (gain_ref, gain_all))[kind]
        to = {"row": lax.rem(r + d, nr)}
        return remote(src, dst.at[:, span(r * width, width)], send_t.at[kind, d - 1], recv_t.at[kind, d - 1], to)

    keep = pltpu.make_async_copy(
        tok_ref.at[span(r * own, own)], x_ref.at[span(c * own, own), span(r * width, width)], local_sem.at[0]
    )
    keep_table = pltpu.make_async_copy(table_ref, table_all.at[:, span(r * width, width)], local_sem.at[1])
    keep_gain = pltpu.make_async_copy(gain_ref, gain_all.at[:, span(r * width, width)], local_sem.at[2])
    keep.start()
    keep_table.start()
    keep_gain.start()
    barrier = pltpu.get_barrier_semaphore()
    pl.semaphore_signal(barrier, inc=1, device_id={"dp": flip(g)}, device_id_type=MESH)
    greet(n, nr, 1)

    @pl.loop(0, chunks)
    def _(j):
        for d in range(1, nr):
            piece(d, j).start()


    load_gu = pltpu.make_async_copy(gu_hbm, gu_pair, out_sems.at[4])
    copy_gu = pltpu.make_async_copy(gu_flat, gu_out, out_sems.at[5])
    gu_step = gu_flat.shape[0] // 8

    def flatten(i):
        @pl.when(i == 0)
        def _():
            load_gu.wait()

        rows = span(i * gu_step, gu_step)
        gu_flat[rows, :] = gu_pair[rows].reshape(gu_step, gu_flat.shape[1])

    middle_at = n // 2
    owner = jnp.where(c < middle_at, 0, n - 1)
    at_owner = jnp.where(c < middle_at, c, c - middle_at)
    is_owner = owner == c

    def cot_piece(d):
        peer = lax.rem(r + d, nr)
        return remote(
            cot_ref.at[span(peer * own, own)], cot_own.at[:, span(r * width, width)], send_g.at[d - 1], recv_g.at[d - 1], {"row": peer}
        )

    cot_local = pltpu.make_async_copy(cot_ref.at[span(r * own, own)], cot_own.at[:, span(r * width, width)], local_g.at[0])
    cot_keep = pltpu.make_async_copy(cot_own, half_ref.at[span(at_owner * own, own)], local_g.at[1])

    def cot_move(b):
        return remote(cot_own, half_ref.at[span(b * own, own)], send_e, recv_e.at[b], {"col": owner})

    share_q.start_far()
    share_q.start_near()
    for d in range(1, nr):
        table_piece(d, 0).start()
        table_piece(d, 1).start()
    share_o.start_far()
    share_o.start_near()
    cot_local.start()
    for d in range(1, nr):
        cot_piece(d).start()
    load_gu.start()
    keep.wait()

    def head_rows(i):
        block_at = i // (own // mh)
        inside = lax.rem(i, own // mh)
        return span(block_at * tree_part + r * own + inside * mh, mh)

    def head_piece(d, i):
        peer = lax.rem(r + d, nr)
        return remote(
            buf.at[peer, span(i * mh, mh)], qkv_ref.at[head_rows(i)], send_h.at[d - 1, i], recv_h.at[d - 1, i], {"row": peer}
        )

    def head_local(i):
        return pltpu.make_async_copy(buf.at[r, span(i * mh, mh)], qkv_ref.at[head_rows(i)], local_h.at[i])

    def stat_copy(b, d):
        peer = lax.rem(c + d, n)
        return remote(stats.at[c, b], stats.at[c, b], send_s.at[b, d - 1], recv_s.at[b, d - 1], {"col": peer})

    def product_block(b):
        rows = span(b * own, own)
        x_rows = x_ref[rows, :]
        red[...] = dot_t(x_rows, table_all[:3 * RANK, :]).astype(low)
        for j in range(3):
            lanes = slice(j * width, (j + 1) * width)
            raw_ref[rows, lanes] = dot(x_rows, wq[:, lanes]) + dot(
                red[:, j * RANK:(j + 1) * RANK], bq_ref[j * RANK:(j + 1) * RANK, :]
            )
        q_rows = raw_ref[rows, :width]
        k_rows = raw_ref[rows, width:2 * width]
        stats[c, b] = row_sums(q_rows * q_rows, k_rows * k_rows)
        for d in range(1, n):
            stat_copy(b, d).start()

    per = own // mh

    def head_block(b):
        for d in range(1, n):
            stat_copy(b, d).wait()
        total = stats[0, b]
        for s in range(1, n):
            total = total + stats[s, b]
        factor = lax.rsqrt(total * (1.0 / D) + epsilon)
        factor_ref[b] = factor
        fq[...] = down_columns(factor, 0)
        fk[...] = down_columns(factor, 4)

        @pl.loop(0, per)
        def _(i):
            rows = span(b * own + i * mh, mh)
            inside = span(i * mh, mh)
            cosine = cos_ref[rows, :]
            sine = sin_ref[rows, :]
            for h in range(heads):
                lanes = slice(h * HEAD, (h + 1) * HEAD)
                u = raw_ref[rows, lanes] * fq[inside, :] * gq_ref[:, lanes]
                buf[h, rows, :HEAD] = (u * cosine + pltpu.roll(u, HEAD // 2, 1) * sine).astype(low)
                k_lanes = slice(width + h * HEAD, width + (h + 1) * HEAD)
                u = raw_ref[rows, k_lanes] * fk[inside, :] * gk_ref[:, lanes]
                buf[h, rows, HEAD:2 * HEAD] = (u * cosine + pltpu.roll(u, HEAD // 2, 1) * sine).astype(low)
                v_lanes = slice(2 * width + h * HEAD, 2 * width + (h + 1) * HEAD)
                buf[h, rows, 2 * HEAD:] = raw_ref[rows, v_lanes].astype(low)
            for d in range(1, nr):
                head_piece(d, b * per + i).start()
            head_local(b * per + i).start()

    def both_phases(last_step):
        for d in range(1, nr):
            table_piece(d, 0).wait_recv()
            table_piece(d, 1).wait_recv()
        keep_table.wait()
        keep_gain.wait()
        share_q.wait_all()
        copy_wq.start()

        @pl.loop(0, 2)
        def _(phase):
            def at(i):
                return jnp.where(phase == 0, 1 + i, i * (n - 1))

            pl.when(phase == 1)(last_step)

            @pl.loop(0, 2)
            def _(i):
                product_block(at(i))

            @pl.when(phase == 0)
            def _():
                @pl.when(jnp.logical_not(is_owner))
                def _():
                    cot_move(at_owner).start()

                @pl.when(is_owner)
                def _():
                    cot_keep.start()

            @pl.when(phase == 1)
            def _():
                copy_x.start()
                copy_raw.start()
                for i in range(2):
                    share_o.pass_twin(i)

            @pl.loop(0, 2)
            def _(i):
                head_block(at(i))

    copy_wq = pltpu.make_async_copy(wq, wq_out, out_sems.at[0])
    copy_x = pltpu.make_async_copy(x_ref, x_out, out_sems.at[2])
    copy_raw = pltpu.make_async_copy(raw_ref, raw_out, out_sems.at[3])

    def ring_step(s):
        @pl.loop(0, chunks)
        def _(j):
            if s == 0:
                for d in range(1, nr):
                    piece(d, j).wait_recv()

            @pl.when(c - s >= 0)
            def _():
                if s > 0:
                    block(0, s - 1, jnp.maximum(c - s, 0), j, right).wait_recv()
                if s < n - 1:
                    @pl.when(c < n - 1)
                    def _():
                        block(0, s, jnp.maximum(c - s, 0), j, right).start()

            @pl.when(c + s <= n - 1)
            def _():
                if s > 0:
                    block(1, s - 1, jnp.minimum(c + s, n - 1), j, left).wait_recv()
                if s < n - 1:
                    @pl.when(c > 0)
                    def _():
                        block(1, s, jnp.minimum(c + s, n - 1), j, left).start()

            if 0 < s < n - 1:
                @pl.when(j < 8 // (n - 2))
                def _():
                    flatten((s - 1) * (8 // (n - 2)) + j)

        if s == 1:
            for i in range(2):
                share_q.pass_far(i)
        if s == n - 2:
            copy_gu.start()
        if s == n - 2:
            for i in range(2):
                share_o.pass_far(i)
                share_q.pass_twin(i)
            cot_local.wait()
            for d in range(1, nr):
                cot_piece(d).wait_recv()
    steps = rows_all // mh

    for s in range(n - 1):
        ring_step(s)
    both_phases(lambda: ring_step(n - 1))

    share_o.wait_all()
    copy_wo = pltpu.make_async_copy(wo, wo_out, out_sems.at[1])
    copy_wo.start()

    @pl.loop(0, steps)
    def _(i):
        for d in range(1, nr):
            head_piece(d, i).wait()
        head_local(i).wait()

    for d in range(1, nr):
        cot_piece(d).wait_send()

    @pl.when(jnp.logical_not(is_owner))
    def _():
        cot_move(at_owner).wait_send()

    @pl.when(is_owner)
    def _():
        cot_keep.wait()
        for b in range(middle_at):
            @pl.when(b != at_owner)
            def _():
                remote(cot_own, half_ref.at[span(b * own, own)], send_e, recv_e.at[b], {"row": flip(r)}).wait_recv()

    @pl.loop(0, chunks)
    def _(j):
        for d in range(1, nr):
            piece(d, j).wait_send()
        for s in range(n - 1):
            @pl.when(jnp.logical_and(c - s >= 0, c < n - 1))
            def _():
                block(0, s, jnp.maximum(c - s, 0), j, right).wait_send()

            @pl.when(jnp.logical_and(c + s <= n - 1, c > 0))
            def _():
                block(1, s, jnp.minimum(c + s, n - 1), j, left).wait_send()

    for d in range(1, nr):
        table_piece(d, 0).wait_send()
        table_piece(d, 1).wait_send()
    share_q.drain()
    share_o.drain()
    copy_wq.wait()
    copy_wo.wait()
    copy_x.wait()
    copy_raw.wait()
    copy_gu.wait()


def front(tokens, table, gain, cot, w_qkv, w_out, w_gu, b_qkv, gain_q, gain_k, cos2, sin2, n, nr, m=32, mh=80):
    own = tokens.shape[0] // nr
    width = tokens.shape[1]
    rows_all = own * n
    tree = own * n * nr
    chunks = own // m
    steps = rows_all // mh
    dma = pltpu.SemaphoreType.DMA
    shape = jax.ShapeDtypeStruct
    any_space = pl.BlockSpec(memory_space=pl.ANY)
    return pl.pallas_call(
        functools.partial(front_kernel, n, nr, m, mh),
        out_shape=[
            shape((rows_all, width * nr), low),
            shape((table.shape[0], width * nr), low),
            shape((gain.shape[0], width * nr), wide),
            shape((rows_all // 2, width * nr), low),
            shape((rows_all, 3 * width), wide),
            shape((n, 8, own), wide),
            shape((tree, 3 * HEAD), low),
            shape((w_qkv.shape[0] * nr, w_qkv.shape[1]), low),
            shape((w_out.shape[0] * nr, w_out.shape[1]), low),
            shape((w_gu.shape[0], 2 * w_gu.shape[2]), low),
        ],
        in_specs=[any_space, VM, VM] + [any_space] * 4 + [VM] * 5,
        out_specs=[any_space, VM, VM, any_space, any_space, VM, any_space, any_space, any_space, any_space],
        scratch_shapes=[
            pltpu.VMEM((rows_all, width * nr), low),
            pltpu.VMEM((rows_all, 3 * width), wide),
            pltpu.VMEM(w_gu.shape, low),
            pltpu.VMEM((w_gu.shape[0], 2 * w_gu.shape[2]), low),
            pltpu.VMEM((w_qkv.shape[0] * nr, w_qkv.shape[1]), low),
            pltpu.VMEM((w_out.shape[0] * nr, w_out.shape[1]), low),
            pltpu.VMEM((n, n, 8, own), wide),
            pltpu.VMEM((width // HEAD, rows_all, 3 * HEAD), low),
            pltpu.VMEM((own, HEAD), wide),
            pltpu.VMEM((own, HEAD), wide),
            pltpu.VMEM((own, 3 * RANK), low),
            pltpu.VMEM((own, width * nr), low),
            dma((nr - 1, chunks)), dma((nr - 1, chunks)), dma((2, n - 1, chunks)), dma((2, n - 1, chunks)),
            dma((2, nr - 1)), dma((2, nr - 1)), dma((3,)),
            dma((n, n - 1)), dma((n, n - 1)), dma((nr - 1, steps)), dma((nr - 1, steps)),
            dma((nr - 1,)), dma((nr - 1,)), dma((steps,)), dma((2,)), dma, dma((n // 2,)),
        ] + share_sems(2) + share_sems(2) + [dma((6,))],
        compiler_params=params(3),
        name="front",
    )(tokens, table, gain, cot, w_qkv, w_out, w_gu, b_qkv, gain_q, gain_k, cos2, sin2)


def one_hot_rows(out_rows, in_rows, source):
    at = lax.broadcasted_iota(jnp.int32, (out_rows, in_rows), 0)
    return (lax.broadcasted_iota(jnp.int32, (out_rows, in_rows), 1) == source(at)).astype(low)


def rear_kernel(n, nr, ndp, m, d_ref, raw_hbm, factor_ref, gq_ref, gk_ref, cos_ref, sin_ref, res_ref, x_hbm, wq_hbm,
                table_ref, bq_ref, dh_hbm, full_hbm, co_hbm, cg_hbm, cd_hbm, hot_ref,
                grad_ref, layer_ref, sets_ref,
                raw_ref, x_ref, dh_ref, full_ref, co_ref, cg_ref, cd_ref, wq, stats, buf, nq, nk, pq, pk, fq, fk, d_raw, part, recv_right, recv_left, own_buf, layer_own,
                back, red, full, cols, col_stack, full_recv, full_sum, full_last, col_recv, owned, hot_all,
                send_s, recv_s, send_h, recv_h, local_h, send_o, recv_o, local_o, load,
                send_z, recv_z, send_w, recv_w, local_w, send_v, recv_v, local_v,
                send_f, recv_f, send_c, recv_c, send_l, recv_l, send_d, recv_d, send_k, recv_k):
    g, r, c = lax.axis_index("dp"), lax.axis_index("row"), lax.axis_index("col")
    rows_all, width_all = part.shape
    own = rows_all // n
    width = gq_ref.shape[1]
    heads = width // HEAD
    tree_part = own * nr
    middle_at = n // 2
    chunks = own // m
    hop = 2
    ahead = 2
    left = {"col": jnp.maximum(c - 1, 0)}
    right = {"col": jnp.minimum(c + 1, n - 1)}
    load_raw = pltpu.make_async_copy(raw_hbm, raw_ref, load.at[0])
    load_x = pltpu.make_async_copy(x_hbm, x_ref, load.at[1])
    load_w = pltpu.make_async_copy(wq_hbm, wq, load.at[2])
    loads = [
        pltpu.make_async_copy(src, dst, load.at[3 + i])
        for i, (src, dst) in enumerate(
            ((dh_hbm, dh_ref), (full_hbm, full_ref), (co_hbm, co_ref), (cg_hbm, cg_ref), (cd_hbm, cd_ref))
        )
    ]

    def piece(d, b):
        peer = lax.rem(r + d, nr)
        return remote(
            d_ref.at[span(b * tree_part + peer * own, own)], buf.at[r, span(b * own, own)],
            send_h.at[d - 1, b], recv_h.at[d - 1, b], {"row": peer},
        )

    def local(b):
        return pltpu.make_async_copy(
            d_ref.at[span(b * tree_part + r * own, own)], buf.at[r, span(b * own, own)], local_h.at[b]
        )

    is_owner = jnp.logical_or(c == 0, c == n - 1)
    base = jnp.where(c == 0, 0, middle_at)

    def result_piece(b):
        return remote(res_ref.at[span(b * own, own)], layer_own, send_o.at[b], recv_o, {"col": base + b})

    def result_local(b):
        return pltpu.make_async_copy(res_ref.at[span(b * own, own)], layer_own, local_o)

    def width_piece(src, dst, send_sem, recv_sem, d, j, size):
        peer = lax.rem(r + d, nr)
        return remote(
            src.at[span(j * size, size), span(peer * width, width)], dst.at[span(r * own + j * size, size)],
            send_sem.at[d - 1, j], recv_sem.at[d - 1, j], {"row": peer},
        )

    def width_local(src, dst, sem, j, size):
        return pltpu.make_async_copy(
            src.at[span(j * size, size), span(r * width, width)], dst.at[span(r * own + j * size, size)], sem.at[j]
        )

    for b in range(n):
        local(b).start()
    load_raw.start()
    load_x.start()
    load_w.start()
    for copy in loads:
        copy.start()
    me = r * n + c
    barrier = pltpu.get_barrier_semaphore()
    for d in range(1, ndp):
        pl.semaphore_signal(barrier, inc=1, device_id={"dp": lax.rem(g + d, ndp)}, device_id_type=MESH)
    greet(n, nr, ndp - 1)
    for b in (0, n - 1) + tuple(range(1, n - 1)):
        for d in range(1, nr):
            piece(d, b).start()

    @pl.when(is_owner)
    def _():
        for b in range(middle_at):
            @pl.when(base + b == c)
            def _():
                result_local(b).start()

            @pl.when(base + b != c)
            def _():
                result_piece(b).start()

    hot_all[g] = hot_ref[...]
    load_x.wait()
    red[...] = dot_t(x_ref[...], table_ref[:3 * RANK, :]).astype(low)
    load_raw.wait()

    def stat_copy(b, d):
        peer = lax.rem(c + d, n)
        return remote(stats.at[c, b], stats.at[c, b], send_s.at[b, d - 1], recv_s.at[b, d - 1], {"col": peer})

    def norm_block(b):
        for d in range(1, nr):
            piece(d, b).wait_recv()
        local(b).wait()
        rows = span(b * own, own)
        fq[rows, :] = down_columns(factor_ref[b], 0)
        fk[rows, :] = down_columns(factor_ref[b], 4)
        cosine = cos_ref[rows, :]
        sine = sin_ref[rows, :]
        for h in range(heads):
            lanes = slice(h * HEAD, (h + 1) * HEAD)
            k_lanes = slice(width + h * HEAD, width + (h + 1) * HEAD)
            v_lanes = slice(2 * width + h * HEAD, 2 * width + (h + 1) * HEAD)
            u = buf[h, rows, :HEAD].astype(wide)
            u = (u * cosine - pltpu.roll(u, HEAD // 2, 1) * sine) * gq_ref[:, lanes]
            nq[rows, lanes] = u
            pq[rows, lanes] = u * raw_ref[rows, lanes] * fq[rows, :]
            u = buf[h, rows, HEAD:2 * HEAD].astype(wide)
            u = (u * cosine - pltpu.roll(u, HEAD // 2, 1) * sine) * gk_ref[:, lanes]
            nk[rows, lanes] = u
            pk[rows, lanes] = u * raw_ref[rows, k_lanes] * fk[rows, :]
            d_raw[rows, v_lanes] = buf[h, rows, 2 * HEAD:]
        stats[c, b] = row_sums(pq[rows, :], pk[rows, :])
        for d in range(1, n):
            stat_copy(b, d).start()

    def mean_block(b):
        for d in range(1, n):
            stat_copy(b, d).wait()
        total = stats[0, b]
        for s in range(1, n):
            total = total + stats[s, b]
        mean = total * (1.0 / D) * factor_ref[b]
        rows = span(b * own, own)
        pq[rows, :HEAD] = down_columns(mean, 0)
        pk[rows, :HEAD] = down_columns(mean, 4)

    def back_block(b):
        rows = span(b * own, own)
        for h in range(heads):
            lanes = slice(h * HEAD, (h + 1) * HEAD)
            k_lanes = slice(width + h * HEAD, width + (h + 1) * HEAD)
            d_raw[rows, lanes] = (fq[rows, :] * (nq[rows, lanes] - raw_ref[rows, lanes] * pq[rows, :HEAD])).astype(low)
            d_raw[rows, k_lanes] = (fk[rows, :] * (nk[rows, lanes] - raw_ref[rows, k_lanes] * pk[rows, :HEAD])).astype(low)
        for j in range(3):
            back[rows, j * RANK:(j + 1) * RANK] = dot_t(
                d_raw[rows, j * width:(j + 1) * width], bq_ref[j * RANK:(j + 1) * RANK, :]
            ).astype(low)
        mine = jnp.where(b < middle_at, c == 0, c == n - 1)
        held = span(lax.rem(b, middle_at) * own, own)
        for k in range(width_all // width):
            lanes = slice(k * width, (k + 1) * width)
            value = dot_t(d_raw[rows, :], wq[lanes, :]) + dot(back[rows, :], table_ref[:3 * RANK, lanes])
            part[rows, lanes] = (value + jnp.where(mine, dh_ref[held, lanes], 0.0)).astype(low)

    def full_piece(d):
        peer = lax.rem(r + d, nr)
        return remote(full.at[:, span(peer * width, width)], full_recv.at[r], send_f.at[d - 1], recv_f.at[d - 1], {"row": peer})

    col_rows = col_recv.shape[1]
    full_rows = full_last.shape[1]

    def col_piece(d):
        peer = lax.rem(r + d, nr)
        return remote(cols.at[span(peer * col_rows, col_rows)], col_recv.at[r], send_c.at[d - 1], recv_c.at[d - 1], {"row": peer})

    def last_piece(d):
        peer = lax.rem(c + d, n)
        return remote(full_sum.at[span(peer * full_rows, full_rows)], full_last.at[c], send_l.at[d - 1], recv_l.at[d - 1], {"col": peer})

    def tree_piece(d):
        return remote(owned.at[g], owned.at[g], send_d.at[d - 1], recv_d.at[d - 1], {"dp": lax.rem(g + d, ndp)})

    def hot_piece(d):
        return remote(hot_all.at[g], hot_all.at[g], send_k.at[d - 1], recv_k.at[d - 1], {"dp": lax.rem(g + d, ndp)})

    def reduce(kind, b, j):
        rows = span(b * own + j * m, m)
        dst, to = ((recv_right, right), (recv_left, left))[kind]
        return remote(part.at[rows], dst.at[rows], send_z.at[kind, b, j], recv_z.at[kind, b, j], to)

    def stage(s, at_edge=True, inside=True, jobs=()):
        @pl.loop(0, chunks + hop * (n - 2))
        def _(i):
            for at, job in enumerate(jobs):
                pl.when(i == at)(job)

            for kind, b, go, edge, got, j in (
                (0, n - 1 - s, n - 1 - s > c, c == 0, recv_right, i - hop * c),
                (1, s, s < c, c == n - 1, recv_left, i - hop * (n - 1 - c)),
            ):
                go = jnp.logical_and(go, jnp.logical_and(j >= 0, j < chunks))
                if at_edge:
                    @pl.when(jnp.logical_and(go, edge))
                    def _():
                        @pl.when(j >= ahead)
                        def _():
                            reduce(kind, b, j - ahead).wait_send()

                        reduce(kind, b, j).start()

                if inside:
                    @pl.when(jnp.logical_and(go, jnp.logical_not(edge)))
                    def _():
                        rows = span(b * own + j * m, m)
                        reduce(kind, b, j).wait_recv()
                        part[rows, :] = (part[rows, :].astype(wide) + got[rows, :].astype(wide)).astype(low)
                        reduce(kind, b, j).start()

    @pl.loop(0, 2)
    def _(phase):
        def at(i):
            return jnp.where(phase == 0, i * (n - 1), 1 + i)

        @pl.loop(0, 2)
        def _(i):
            norm_block(at(i))

        @pl.when(phase == 0)
        def _():
            load_w.wait()
            loads[0].wait()

        @pl.when(phase == 1)
        def _():
            stage(0)

        @pl.loop(0, 2)
        def _(i):
            mean_block(at(i))
            back_block(at(i))

    for copy in loads[1:]:
        copy.wait()

    rank_own = RANK // n
    groups = full.shape[0] // (n * rank_own) - 1
    rank_row = RANK // nr
    per_wide = cd_ref.shape[1] // width

    def full_job():
        stacked = jnp.concatenate([t_dot(back[...], x_ref[...]), full_ref[...]], axis=0).astype(low)
        order = one_hot_rows(
            full.shape[0], stacked.shape[0],
            lambda o: jnp.where(
                lax.rem(o, full_rows) < groups * rank_own,
                lax.rem(o, full_rows) // rank_own * RANK + o // full_rows * rank_own + lax.rem(o, rank_own), -1
            ),
        )
        full[...] = dot(order, stacked).astype(low)

    def raw_job():
        for j in range(3):
            col_stack[j * RANK:(j + 1) * RANK, :] = t_dot(
                red[:, j * RANK:(j + 1) * RANK], d_raw[:, j * width:(j + 1) * width]
            ).astype(low)
        col_stack[3 * RANK:4 * RANK, :] = co_ref[...].astype(low)

    def wide_job():
        for k in range(per_wide):
            lanes = slice(k * width, (k + 1) * width)
            for j, value in enumerate((cg_ref[0, :, lanes], cg_ref[1, :, lanes], cd_ref[:, lanes])):
                at = (4 + j * per_wide + k) * RANK
                col_stack[at:at + RANK, :] = value.astype(low)

    def col_job():
        order = one_hot_rows(
            cols.shape[0], cols.shape[0],
            lambda o: lax.rem(o, col_rows) // rank_row * RANK + o // col_rows * rank_row + lax.rem(o, rank_row),
        )
        cols[...] = dot(order, col_stack[...]).astype(low)

    stage(1, jobs=(wide_job, raw_job, col_job, full_job))
    for d in range(1, nr):
        full_piece(d).start()
        col_piece(d).start()

    @pl.when(is_owner)
    def _():
        for b in range(middle_at):
            @pl.when(base + b == c)
            def _():
                result_local(b).wait()

            @pl.when(base + b != c)
            def _():
                result_piece(b).wait_send()

    @pl.when(jnp.logical_not(is_owner))
    def _():
        remote(res_ref.at[span(0, own)], layer_own, send_o.at[0], recv_o, right).wait_recv()

    for d in range(1, nr):
        width_piece(layer_own, layer_ref, send_v, recv_v, d, 0, own).start()
    width_local(layer_own, layer_ref, local_v, 0, own).start()
    def row_job():
        for d in range(1, nr):
            full_piece(d).wait_recv()
            col_piece(d).wait_recv()
        total = full[:, span(r * width, width)].astype(wide)
        col_total = cols[span(r * col_rows, col_rows), :].astype(wide)
        for d in range(1, nr):
            peer = lax.rem(r + d, nr)
            total = total + full_recv[peer].astype(wide)
            col_total = col_total + col_recv[peer].astype(wide)
        full_sum[...] = total.astype(low)
        owned[g, full_rows:, :] = col_total.astype(low)
        for d in range(1, n):
            last_piece(d).start()

    stage(2, jobs=(lambda: None, row_job))
    for d in range(1, n):
        last_piece(d).wait_recv()
    last = full_sum[span(c * full_rows, full_rows), :].astype(wide)
    for d in range(1, n):
        last = last + full_last[lax.rem(c + d, n)].astype(wide)
    owned[g, :full_rows, :] = last.astype(low)
    for d in range(1, ndp):
        tree_piece(d).start()
        hot_piece(d).start()

    @pl.loop(0, chunks)
    def _(j):
        rows = span(c * own + j * m, m)
        at = span(j * m, m)
        own_buf[at, :] = part[rows, :]

        @pl.when(c > 0)
        def _():
            reduce(0, c, j).wait_recv()
            own_buf[at, :] = (own_buf[at, :].astype(wide) + recv_right[rows, :].astype(wide)).astype(low)

        @pl.when(c < n - 1)
        def _():
            reduce(1, c, j).wait_recv()
            own_buf[at, :] = (own_buf[at, :].astype(wide) + recv_left[rows, :].astype(wide)).astype(low)

        for d in range(1, nr):
            width_piece(own_buf, grad_ref, send_w, recv_w, d, j, m).start()
        width_local(own_buf, grad_ref, local_w, j, m).start()

    for d in range(1, ndp):
        tree_piece(d).wait_recv()
        hot_piece(d).wait_recv()
    sets_own = sets_ref.shape[0]
    for s in range(sets_own):
        total = owned[0].astype(wide) * hot_all[0, pl.ds(g * sets_own + s, 1), :]
        for t in range(1, ndp):
            total = total + owned[t].astype(wide) * hot_all[t, pl.ds(g * sets_own + s, 1), :]
        sets_ref[s] = total

    @pl.loop(0, chunks)
    def _(j):
        for d in range(1, nr):
            width_piece(own_buf, grad_ref, send_w, recv_w, d, j, m).wait()
        width_local(own_buf, grad_ref, local_w, j, m).wait()

    for d in range(1, nr):
        width_piece(layer_own, layer_ref, send_v, recv_v, d, 0, own).wait()
        full_piece(d).wait_send()
        col_piece(d).wait_send()
        for b in range(n):
            piece(d, b).wait_send()
    width_local(layer_own, layer_ref, local_v, 0, own).wait()
    for d in range(1, n):
        last_piece(d).wait_send()
    for d in range(1, ndp):
        tree_piece(d).wait_send()
        hot_piece(d).wait_send()
    for s in range(n - 1):
        @pl.loop(0, chunks)
        def _(j):
            late = j >= chunks - ahead

            @pl.when(jnp.logical_and(n - 1 - s > c, jnp.logical_or(c > 0, late)))
            def _():
                reduce(0, n - 1 - s, j).wait_send()

            @pl.when(jnp.logical_and(s < c, jnp.logical_or(c < n - 1, late)))
            def _():
                reduce(1, s, j).wait_send()


def rear(d_head, raw, factor, gain_q, gain_k, cos2, sin2, result, x, w_qkv, table, b_qkv, d_h, full_mid, part_ao,
         part_bgu, part_ad, hot, sets_own, n, nr, ndp, m=32):
    rows_all, wide3 = raw.shape
    width = wide3 // 3
    width_all = x.shape[1]
    own = rows_all // n
    chunks = own // m
    full_rows = 8 * RANK // n
    col_blocks = 4 + 3 * part_ad.shape[1] // width
    col_rows = col_blocks * RANK // nr
    dma = pltpu.SemaphoreType.DMA
    shape = jax.ShapeDtypeStruct
    any_space = pl.BlockSpec(memory_space=pl.ANY)
    square = pltpu.VMEM((rows_all, width), wide)
    lane = pltpu.VMEM((rows_all, HEAD), wide)
    big = pltpu.VMEM((rows_all, width_all), low)
    return pl.pallas_call(
        functools.partial(rear_kernel, n, nr, ndp, m),
        out_shape=[
            shape((own * nr, width), low),
            shape((own * nr, width), low),
            shape((sets_own, full_rows + col_rows, width), wide),
        ],
        in_specs=[any_space] * 2 + [VM] * 5 + [any_space] * 3 + [VM] * 2 + [any_space] * 5 + [VM],
        out_specs=[VM] * 3,
        scratch_shapes=[
            pltpu.VMEM(raw.shape, wide),
            pltpu.VMEM(x.shape, low),
            pltpu.VMEM(d_h.shape, wide),
            pltpu.VMEM(full_mid.shape, wide),
            pltpu.VMEM(part_ao.shape, wide),
            pltpu.VMEM(part_bgu.shape, wide),
            pltpu.VMEM(part_ad.shape, wide),
            pltpu.VMEM(w_qkv.shape, low),
            pltpu.VMEM((n, n, 8, own), wide),
            pltpu.VMEM((nr, rows_all, 3 * HEAD), low),
            square, square, square, square, lane, lane,
            pltpu.VMEM((rows_all, wide3), low),
            big, big, big,
            pltpu.VMEM((own, width_all), low),
            pltpu.VMEM((own, width_all), low),
            pltpu.VMEM((rows_all, 3 * RANK), low),
            pltpu.VMEM((rows_all, 3 * RANK), low),
            pltpu.VMEM((n * full_rows, width_all), low),
            pltpu.VMEM((nr * col_rows, width), low),
            pltpu.VMEM((nr * col_rows, width), low),
            pltpu.VMEM((nr, n * full_rows, width), low),
            pltpu.VMEM((n * full_rows, width), low),
            pltpu.VMEM((n, full_rows, width), low),
            pltpu.VMEM((nr, col_rows, width), low),
            pltpu.VMEM((ndp, full_rows + col_rows, width), low),
            pltpu.VMEM((ndp,) + hot.shape, wide),
            dma((n, n - 1)), dma((n, n - 1)), dma((nr - 1, n)), dma((nr - 1, n)), dma((n,)),
            dma((n // 2,)), dma, dma, dma((8,)),
            dma((2, n, chunks)), dma((2, n, chunks)), dma((nr - 1, chunks)), dma((nr - 1, chunks)), dma((chunks,)),
            dma((nr - 1, 1)), dma((nr - 1, 1)), dma((1,)),
            dma((nr - 1,)), dma((nr - 1,)), dma((nr - 1,)), dma((nr - 1,)), dma((n - 1,)), dma((n - 1,)),
            dma((ndp - 1,)), dma((ndp - 1,)), dma((ndp - 1,)), dma((ndp - 1,)),
        ],
        compiler_params=params(5),
        name="rear",
    )(d_head, raw, factor, gain_q, gain_k, cos2, sin2, result, x, w_qkv, table, b_qkv, d_h, full_mid, part_ao, part_bgu, part_ad, hot)


def unpack_kernel(rank_own, rank_row, grad_ref, layer_ref, sets_ref, layer_out, input_grad, a_qkv, b_qkv, a_out, b_out, a_gu, b_gu, a_down, b_down):
    layer_out[...] = layer_ref[...]
    input_grad[...] = grad_ref[...].astype(wide)
    width = grad_ref.shape[1]
    first = 8 * rank_own

    def column(s, at):
        return sets_ref[s, first + at * rank_row:first + (at + 1) * rank_row, :]

    for s in range(sets_ref.shape[0]):
        for j in range(3):
            a_qkv[j, s] = sets_ref[s, j * rank_own:(j + 1) * rank_own, :]
            b_qkv[j, s] = column(s, j)
        for j in range(2):
            a_gu[j, s] = sets_ref[s, (3 + j) * rank_own:(4 + j) * rank_own, :]
        b_out[s] = sets_ref[s, 5 * rank_own:6 * rank_own, :]
        b_down[s] = sets_ref[s, 6 * rank_own:7 * rank_own, :]
        a_out[s] = column(s, 3)
        per = a_down.shape[2] // width
        for k in range(per):
            lanes = slice(k * width, (k + 1) * width)
            b_gu[0, s, :, lanes] = column(s, 4 + k)
            b_gu[1, s, :, lanes] = column(s, 4 + per + k)
            a_down[s, :, lanes] = column(s, 4 + 2 * per + k)


def unpack(grad, layer, sets, rank_own, rank_row, hidden):
    sets_own = sets.shape[0]
    width = grad.shape[1]
    shape = jax.ShapeDtypeStruct
    return pl.pallas_call(
        functools.partial(unpack_kernel, rank_own, rank_row),
        out_shape=[
            shape(layer.shape, low),
            shape(grad.shape, wide),
            shape((3, sets_own, rank_own, width), wide),
            shape((3, sets_own, rank_row, width), wide),
            shape((sets_own, rank_row, width), wide),
            shape((sets_own, rank_own, width), wide),
            shape((2, sets_own, rank_own, width), wide),
            shape((2, sets_own, rank_row, hidden), wide),
            shape((sets_own, rank_row, hidden), wide),
            shape((sets_own, rank_own, width), wide),
        ],
        in_specs=[VM] * 3,
        out_specs=[VM] * 10,
        name="unpack",
    )(grad, layer, sets)


def middle_kernel(n, nr, m, hop, cuts, head_ref, x_hbm, cot_hbm, gain_ref, wo_hbm, wg_hbm, wd_hbm,
                  table_ref, ao_ref, bg_ref, ad_ref,
                  dhead_ref, out_hbm, grad_hbm, full_ref, co_ref, cg_ref, cd_ref,
                  out_half, grad_half, wo, wg, wd, x_half, cot_half, raw, attn, d_attn, h_all, df_all, da_all, gu, part,
                  recv_right, recv_left, hid, red_gu, red_down, back_gu, back_down,
                  sems_send, sems_recv, send_in, recv_in, send_out, recv_out, local_in, local_out, load,
                  send_g, recv_g, local_g, send_d, recv_d, local_d):
    g, r, c = lax.axis_index("dp"), lax.axis_index("row"), lax.axis_index("col")
    ag_ref = table_ref.at[3 * RANK:5 * RANK]
    bo_ref = table_ref.at[5 * RANK:6 * RANK]
    bd_ref = table_ref.at[6 * RANK:]
    rows_all, width_all = part.shape
    half = rows_all // 2
    own = rows_all // n
    tree_part = own * nr
    chunks = half // m
    blocks = 4
    band = half // blocks
    hidden = ad_ref.shape[1]
    width = width_all // nr
    left = {"col": jnp.maximum(c - 1, 0)}
    right = {"col": jnp.minimum(c + 1, n - 1)}
    first = c == 0
    last = c == n - 1
    inner = jnp.logical_and(c > 0, c < n - 1)

    base = jnp.where(last, half, 0)
    a_cut = hidden // 4
    share_g = Share(wg_hbm, wg, cuts, (send_g, recv_g, local_g))
    share_d = Share(wd_hbm, wd, cuts // 2, (send_d, recv_d, local_d))
    loads = [pltpu.make_async_copy(wo_hbm, wo, load.at[0])]
    load_x = pltpu.make_async_copy(x_hbm.at[span(base, half)], x_half, load.at[1])
    load_cot = pltpu.make_async_copy(cot_hbm, cot_half, load.at[2])
    store_out = pltpu.make_async_copy(out_half, out_hbm, load.at[3])
    store_grad = pltpu.make_async_copy(grad_half, grad_hbm, load.at[4])
    is_owner = jnp.logical_or(first, last)
    loads[0].start()

    def piece_in(d, b):
        peer = lax.rem(r + d, nr)
        return remote(
            head_ref.at[span(b * tree_part + peer * own, own)],
            attn.at[span(b * own, own), span(r * HEAD, HEAD)],
            send_in.at[d - 1, b], recv_in.at[d - 1, b], {"row": peer},
        )

    def local_piece_in(b):
        return pltpu.make_async_copy(
            head_ref.at[span(b * tree_part + r * own, own)],
            attn.at[span(b * own, own), span(r * HEAD, HEAD)], local_in.at[b]
        )

    per_block = blocks // (n // 2)

    def out_rows(b, side):
        at = side * (n // 2) + b // per_block
        inside = lax.rem(b, per_block) * band
        return span(at * own + inside, band), span(at * tree_part + r * own + inside, band)

    def piece_out(d, b, side):
        peer = lax.rem(r + d, nr)
        here, there = out_rows(b, side)
        return remote(
            d_attn.at[here, span(peer * HEAD, HEAD)], dhead_ref.at[there],
            send_out.at[side * (nr - 1) + d - 1, b], recv_out.at[side * (nr - 1) + d - 1, b], {"row": peer},
        )

    def local_piece_out(b, side):
        here, there = out_rows(b, side)
        return pltpu.make_async_copy(d_attn.at[here, span(r * HEAD, HEAD)], dhead_ref.at[there], local_out.at[side, b])

    for b in range(n):
        local_piece_in(b).start()
    barrier = pltpu.get_barrier_semaphore()
    for d in range(1, nr):
        pl.semaphore_signal(barrier, inc=1, device_id={"row": lax.rem(r + d, nr)}, device_id_type=MESH)

    @pl.when(c > 0)
    def _():
        pl.semaphore_signal(barrier, inc=1, device_id=left, device_id_type=MESH)

    @pl.when(c < n - 1)
    def _():
        pl.semaphore_signal(barrier, inc=1, device_id=right, device_id_type=MESH)

    pl.semaphore_signal(barrier, inc=1, device_id={"dp": flip(g)}, device_id_type=MESH)
    full_ref[...] = jnp.zeros_like(full_ref)
    co_ref[...] = jnp.zeros_like(co_ref)
    cg_ref[...] = jnp.zeros_like(cg_ref)
    cd_ref[...] = jnp.zeros_like(cd_ref)

    @pl.when(inner)
    def _():
        pl.semaphore_wait(barrier, nr + 2)

    @pl.when(jnp.logical_not(inner))
    def _():
        pl.semaphore_wait(barrier, nr + 1)

    middle = n // 2
    for b in range(middle):
        for block in (b, middle + b):
            for d in range(1, nr):
                piece_in(d, block).start()
    load_x.start()
    load_cot.start()
    share_g.start_far()
    share_d.start_far()
    share_g.start_near()
    share_d.start_near()

    def rows(j, start=0):
        return span(start + j * m, m)

    def band_rows(b):
        return span(b * band, band), span(half + b * band, band)

    def take(ref, b):
        low_rows, high_rows = band_rows(b)
        return jnp.concatenate([ref[low_rows, :], ref[high_rows, :]], axis=0)

    def put(b, lanes, value):
        low_rows, high_rows = band_rows(b)
        part[low_rows, lanes] = value[:band].astype(low)
        part[high_rows, lanes] = value[band:].astype(low)

    around = hop * 2 * (n - 1)
    each = chunks // blocks

    def relay_stage(stage, owner_step, all_ref):
        def send(kind, j, src, dst, to):
            return remote(src, dst, sems_send.at[stage, kind, j], sems_recv.at[stage, kind, j], to)

        def reduce_right(j):
            return send(0, j, part.at[rows(j, half)], recv_right.at[rows(j)], right)

        def reduce_left(j):
            return send(1, j, part.at[rows(j)], recv_left.at[rows(j)], left)

        def spread_left(j):
            return send(2, j, all_ref.at[rows(j, half)], all_ref.at[rows(j, half)], left)

        def spread_right(j):
            return send(3, j, all_ref.at[rows(j)], all_ref.at[rows(j)], right)

        def step(i):
            def on(offset, who, run):
                j = i - offset

                @pl.when(jnp.logical_and(who, jnp.logical_and(j >= 0, j < chunks)))
                def _():
                    run(j)

            def mid_right(j):
                reduce_right(j).wait_recv()
                at = rows(j, half)
                part[at, :] = (part[at, :].astype(wide) + recv_right[rows(j), :].astype(wide)).astype(low)
                reduce_right(j).start()

            def mid_left(j):
                reduce_left(j).wait_recv()
                at = rows(j)
                part[at, :] = (part[at, :].astype(wide) + recv_left[at, :].astype(wide)).astype(low)
                reduce_left(j).start()

            def end_right(j):
                reduce_right(j).wait_recv()
                total = part[rows(j, half), :].astype(wide) + recv_right[rows(j), :].astype(wide)
                all_ref[rows(j, half), :] = owner_step(total, rows(j))
                spread_left(j).start()

            def end_left(j):
                reduce_left(j).wait_recv()
                total = part[rows(j), :].astype(wide) + recv_left[rows(j), :].astype(wide)
                all_ref[rows(j), :] = owner_step(total, rows(j))
                spread_right(j).start()

            def pass_left(j):
                spread_left(j).wait_recv()
                spread_left(j).start()

            def pass_right(j):
                spread_right(j).wait_recv()
                spread_right(j).start()

            def arrived(j):
                @pl.when(first)
                def _():
                    reduce_right(j).wait_send()
                    spread_left(j).wait_recv()

                @pl.when(last)
                def _():
                    reduce_left(j).wait_send()
                    spread_right(j).wait_recv()

                @pl.when(inner)
                def _():
                    reduce_right(j).wait_send()
                    reduce_left(j).wait_send()

            on(0, first, lambda j: reduce_right(j).start())
            on(0, last, lambda j: reduce_left(j).start())
            on(hop * c, inner, mid_right)
            on(hop * (n - 1 - c), inner, mid_left)
            on(hop * (n - 1), last, end_right)
            on(hop * (n - 1), first, end_left)
            on(hop * (2 * (n - 1) - c), inner, pass_left)
            on(hop * (n - 1 + c), inner, pass_right)
            on(around, True, arrived)

        def rest():
            @pl.loop(0, chunks)
            def _(j):
                @pl.when(first)
                def _():
                    spread_right(j).wait_send()

                @pl.when(last)
                def _():
                    spread_left(j).wait_send()

                @pl.when(inner)
                def _():
                    spread_left(j).wait_send()
                    spread_right(j).wait_send()

        return step, rest

    def slices(before, i, per, work):
        @pl.loop(before(i), before(i + 1))
        def _(t):
            work(t // per, lax.rem(t, per))

    def paced(per):
        def before(i):
            late = per + (jnp.maximum(i - per, 0) * per) // each
            return jnp.minimum(jnp.where(i < per, i, late), per * blocks)

        return before

    def shard(j, ref):
        return slice(j * (ref.shape[0] // nr), (j + 1) * (ref.shape[0] // nr))

    def out_work(b, k):
        @pl.when(b == 0)
        def _():
            loads[0].wait()

        @pl.when(lax.rem(b, blocks // middle) == 0)
        def _():
            at = b // (blocks // middle)
            for block in (at, middle + at):
                for d in range(1, nr):
                    piece_in(d, block).wait_recv()
                local_piece_in(block).wait()

        rows_in = take(attn, b)
        red = dot_t(rows_in, ao_ref[...]).astype(low)
        for j in range(nr):
            lanes = slice(j * width, (j + 1) * width)
            put(b, lanes, dot(rows_in, wo[shard(j, wo), :]) + dot(red, bo_ref[:, lanes]))

    gain_a = gain_ref[0:1, :]
    gain_f = gain_ref[1:2, :]

    def attn_owner(total, at):
        raw[at, :] = total
        flat = total * norm_factor(row_sum(total * total))
        return (x_half[at, :].astype(wide) + flat * gain_a).astype(low)

    first_pass = 4
    apart = 2
    late = 3
    passes = cuts + cuts // 2

    def pump(ii):
        at = ii - first_pass

        @pl.when(jnp.logical_and(at >= 0, lax.rem(at, apart) == 0))
        def _():
            t = at // apart

            @pl.when(t < cuts)
            def _():
                share_g.pass_far(t)

            @pl.when(jnp.logical_and(t >= cuts, t < passes))
            def _():
                share_d.pass_far(t - cuts)

            t = t - late

            @pl.when(jnp.logical_and(t >= 0, t < cuts))
            def _():
                share_g.pass_twin(t)

            @pl.when(jnp.logical_and(t >= cuts, t < passes))
            def _():
                share_d.pass_twin(t - cuts)

    load_x.wait()
    in_loop = 1 + chunks + around
    step, rest = relay_stage(0, attn_owner, h_all)
    out_pace = paced(1)

    @pl.loop(0, in_loop)
    def _(ii):
        step(ii - 1)
        slices(out_pace, ii, 1, out_work)
        pump(ii)

    rest()

    share_g.wait_all()

    def gate_slice(b, k):
        rows_in = take(h_all, b)

        @pl.when(k == 0)
        def _():
            red_gu[b] = dot_t(rows_in, ag_ref[...]).astype(low)

        at = pl.multiple_of(k * a_cut, a_cut)
        lanes = pl.ds(at, a_cut)
        up_lanes = pl.ds(pl.multiple_of(hidden + at, a_cut), a_cut)
        red = red_gu[b]
        gate = dot(rows_in, wg[:, lanes]) + dot(red[:, :RANK], bg_ref[0, :, lanes])
        up = dot(rows_in, wg[:, up_lanes]) + dot(red[:, RANK:], bg_ref[1, :, lanes])
        gu[b, :, lanes] = gate.astype(low)
        gu[b, :, up_lanes] = up.astype(low)
        hid[:, lanes] = (gate * jax.nn.sigmoid(gate) * up).astype(low)

    def down_slice(b, k):
        @pl.when(jnp.logical_and(b == 0, k == 0))
        def _():
            @pl.loop(in_loop, jnp.maximum(in_loop, first_pass + apart * (passes + late)))
            def _(ii):
                pump(ii)

            share_d.wait_all()

        rows_in = hid[:, :hidden]

        @pl.when(k == 0)
        def _():
            red_down[b] = dot_t(rows_in, ad_ref[...]).astype(low)

        for s in range(nr // 2):
            j = k * (nr // 2) + s
            lanes = span(j * width, width)
            down_rows = pl.ds(pl.multiple_of(j * hidden, hidden), hidden)
            put(b, lanes, dot(rows_in, wd[down_rows, :]) + dot(red_down[b], bd_ref[:, lanes]))

    def ffn_work(b, k):
        @pl.when(k < 4)
        def _():
            gate_slice(b, k)

        @pl.when(k >= 4)
        def _():
            down_slice(b, k - 4)

    def ffn_owner(total, at):
        a_raw = raw[at, :]
        h = x_half[at, :].astype(wide) + a_raw * norm_factor(row_sum(a_raw * a_raw)) * gain_a
        factor = norm_factor(row_sum(total * total))
        flat = total * factor
        out_half[at, :] = (h + flat * gain_f).astype(low)
        scaled = cot_half[at, :].astype(wide) * gain_f
        return (factor * (scaled - flat * (row_sum(scaled * flat) * (1.0 / D)))).astype(low)

    b_cut = hidden // 2

    def hidden_back(b, k):
        rows_in = take(df_all, b)

        @pl.when(k == 0)
        def _():
            back_down[...] = dot_t(rows_in, bd_ref[...]).astype(low)

        at = pl.multiple_of(k * b_cut, b_cut)
        lanes = pl.ds(at, b_cut)
        up_lanes = pl.ds(pl.multiple_of(hidden + at, b_cut), b_cut)
        back = back_down[...]
        grad = dot(back, ad_ref[:, lanes])
        for j in range(nr):
            down_rows = pl.ds(pl.multiple_of(j * hidden + at, b_cut), b_cut)
            grad = grad + dot_t(rows_in[:, j * width:(j + 1) * width], wd[down_rows, :])
        gate = gu[b, :, lanes].astype(wide)
        up = gu[b, :, up_lanes].astype(wide)
        sigma = jax.nn.sigmoid(gate)
        silu = gate * sigma
        d_gate = (grad * up * sigma * (1.0 + gate * (1.0 - sigma))).astype(low)
        d_up = (grad * silu).astype(low)
        hid[:, lanes] = d_gate
        hid[:, up_lanes] = d_up
        cd_ref[:, lanes] += t_dot(back, (silu * up).astype(low))
        red = red_gu[b]
        cg_ref[0, :, lanes] += t_dot(red[:, :RANK], d_gate)
        cg_ref[1, :, lanes] += t_dot(red[:, RANK:], d_up)

    o_cut = width_all // 4

    def gate_back(b, k):
        @pl.when(k == 0)
        def _():
            back_gu[:, :RANK] = dot_t(hid[:, :hidden], bg_ref[0]).astype(low)
            back_gu[:, RANK:] = dot_t(hid[:, hidden:], bg_ref[1]).astype(low)

        lanes = span(k * o_cut, o_cut)
        put(b, lanes, dot_t(hid[...], wg[lanes, :]) + dot(back_gu[...], ag_ref[:, lanes]))

        @pl.when(k == 3)
        def _():
            full_ref[:2 * RANK, :] += t_dot(back_gu[...], take(h_all, b))
            full_ref[3 * RANK:, :] += t_dot(red_down[b], take(df_all, b))

    def back_work(b, k):
        @pl.when(k < 2)
        def _():
            hidden_back(b, k)

        @pl.when(k >= 2)
        def _():
            gate_back(b, k - 2)

    def back_owner(total, at):
        grad = cot_half[at, :].astype(wide) + total
        grad_half[at, :] = grad
        a_raw = raw[at, :]
        factor = norm_factor(row_sum(a_raw * a_raw))
        flat = a_raw * factor
        scaled = grad * gain_a
        return (factor * (scaled - flat * (row_sum(scaled * flat) * (1.0 / D)))).astype(low)

    def out_back(b, k):
        rows_in = take(da_all, b)
        back = dot_t(rows_in, bo_ref[...]).astype(low)
        grad = dot(back, ao_ref[...])
        for j in range(nr):
            grad = grad + dot_t(rows_in[:, j * width:(j + 1) * width], wo[shard(j, wo), :])
        for side in range(2):
            d_attn[out_rows(b, side)[0], :] = grad[side * band:(side + 1) * band].astype(low)
            for d in range(1, nr):
                piece_out(d, b, side).start()
            local_piece_out(b, side).start()
        attn_rows = take(attn, b)
        co_ref[...] += t_dot(back, attn_rows)
        red = dot_t(attn_rows, ao_ref[...]).astype(low)
        full_ref[2 * RANK:3 * RANK, :] += t_dot(red, rows_in)

    begin = around + each

    def back_before(i):
        return jnp.clip(i - begin, 0, 6 * blocks)

    def out_before(i):
        return jnp.clip((i - around - 1) // each, 0, blocks)

    load_cot.wait()
    step_f, rest_f = relay_stage(1, ffn_owner, df_all)
    step_b, rest_b = relay_stage(2, back_owner, da_all)
    ffn_pace = paced(6)
    period = 26

    @pl.loop(0, 6 + period + chunks + around + 1)
    def _(ii):
        i = ii - 6
        step_f(i)
        step_b(i - period)
        slices(ffn_pace, ii, 6, ffn_work)
        slices(back_before, i, 6, back_work)
        slices(out_before, i - period, 1, out_back)

    pl.when(is_owner)(store_out.start)
    rest_f()
    rest_b()
    pl.when(is_owner)(store_grad.start)

    @pl.loop(0, n)
    def _(b):
        for d in range(1, nr):
            piece_in(d, b).wait_send()

    @pl.loop(0, blocks)
    def _(b):
        for side in range(2):
            for d in range(1, nr):
                piece_out(d, b, side).wait()
            local_piece_out(b, side).wait()

    share_g.drain()
    share_d.drain()

    @pl.when(is_owner)
    def _():
        store_out.wait()
        store_grad.wait()


def middle(attn_head, x, cot_half, gains, w_out, w_gu, w_down, table, a_out, b_gu, a_down, n, nr, m=16, hop=2, cuts=8):
    group, width_all = x.shape
    half = group // 2
    width = width_all // nr
    hidden = a_down.shape[1]
    chunks = half // m
    band = group // 4
    dma = pltpu.SemaphoreType.DMA
    any_space = pl.BlockSpec(memory_space=pl.ANY)
    shape = jax.ShapeDtypeStruct
    return pl.pallas_call(
        functools.partial(middle_kernel, n, nr, m, hop, cuts),
        out_shape=[
            shape(attn_head.shape, low),
            shape((half, width_all), low),
            shape((half, width_all), wide),
            shape((4 * RANK, width_all), wide),
            shape((RANK, a_out.shape[1]), wide),
            shape((2, RANK, hidden), wide),
            shape((RANK, hidden), wide),
        ],
        in_specs=[any_space, any_space, any_space, VM, any_space, any_space, any_space] + [VM] * 4,
        out_specs=[any_space] * 3 + [VM] * 4,
        scratch_shapes=[
            pltpu.VMEM((half, width_all), low),
            pltpu.VMEM((half, width_all), wide),
            pltpu.VMEM(w_out.shape, low),
            pltpu.VMEM((w_gu.shape[0] * nr, w_gu.shape[1]), low),
            pltpu.VMEM((w_down.shape[0] * nr, w_down.shape[1]), low),
            pltpu.VMEM((half, width_all), low),
            pltpu.VMEM((half, width_all), low),
            pltpu.VMEM((half, width_all), wide),
            pltpu.VMEM((group, a_out.shape[1]), low),
            pltpu.VMEM((group, a_out.shape[1]), low),
            pltpu.VMEM((group, width_all), low),
            pltpu.VMEM((group, width_all), low),
            pltpu.VMEM((group, width_all), low),
            pltpu.VMEM((4, band, 2 * hidden), low),
            pltpu.VMEM((group, width_all), low),
            pltpu.VMEM((half, width_all), low),
            pltpu.VMEM((half, width_all), low),
            pltpu.VMEM((band, 2 * hidden), low),
            pltpu.VMEM((4, band, 2 * RANK), low),
            pltpu.VMEM((4, band, RANK), low),
            pltpu.VMEM((band, 2 * RANK), low),
            pltpu.VMEM((band, RANK), low),
            dma((3, 4, chunks)), dma((3, 4, chunks)),
            dma((nr - 1, n)), dma((nr - 1, n)), dma((2 * (nr - 1), 4)), dma((2 * (nr - 1), 4)), dma((n,)), dma((2, 4)),
            dma((5,)),
        ] + share_sems(cuts) + share_sems(cuts // 2),
        compiler_params=pltpu.CompilerParams(collective_id=0, has_side_effects=True, vmem_limit_bytes=67043328),
        name="middle",
    )(attn_head, x, cot_half, gains, w_out, w_gu, w_down, table, a_out, b_gu, a_down)


def per_device(
    tokens,
    cotangent,
    seg_ids,
    positions,
    parents,
    tree_sets,
    gain_q,
    gain_k,
    gain_attn,
    gain_ffn,
    query_key_value_weight,
    output_weight,
    gate_up_weight,
    down_weight,
    query_key_value_adapter_first,
    query_key_value_adapter_second,
    output_adapter_first,
    output_adapter_second,
    gate_up_adapter_first,
    gate_up_adapter_second,
    down_adapter_first,
    down_adapter_second,
):
    dp_count = lax.axis_size("dp")
    row_count = lax.axis_size("row")
    col_count = lax.axis_size("col")
    row_at = lax.axis_index("row")
    tree_tokens = seg_ids.shape[0]
    assert tree_sets.shape[0] == 1 and col_count == 4
    set_count = output_adapter_first.shape[0]
    own = tokens.shape[0] // row_count
    group = own * col_count
    width_row = tokens.shape[1]
    width_col = gain_q.shape[0]
    hidden_col = down_weight.shape[0]
    tree_set = tree_sets[0]

    tables = (
        query_key_value_adapter_first,
        query_key_value_adapter_second,
        output_adapter_first,
        output_adapter_second,
        gate_up_adapter_first,
        gate_up_adapter_second,
        down_adapter_first,
        down_adapter_second,
    )
    narrow, b_qkv, a_out, b_gu, a_down = prep(tree_sets, tables)
    gain_pair = jnp.pad(jnp.stack([gain_attn, gain_ffn]), ((0, 6), (0, 0)))
    pos_own = lax.dynamic_index_in_dim(
        positions.reshape(col_count, row_count, own), row_at, 1, keepdims=False
    ).reshape(group)
    cos2, sin2 = angles(pos_own)
    gq, gk = gain_q[None, :], gain_k[None, :]
    parent_at, branch_flag = tree_tables(seg_ids, parents)
    x, table, gains, g_half, raw, factors, qkv_head, w_qkv, w_out, w_gu = front(
        tokens,
        narrow,
        gain_pair,
        cotangent,
        query_key_value_weight.reshape(width_row, 3 * width_col),
        output_weight,
        gate_up_weight,
        b_qkv,
        gq,
        gk,
        cos2,
        sin2,
        col_count,
        row_count,
    )
    attn_head, lse = attend(qkv_head, parent_at, branch_flag)
    d_attn_head, out_half, d_h_half, full_mid, part_ao, part_bgu, part_ad = middle(
        attn_head,
        x,
        g_half,
        gains,
        w_out,
        w_gu,
        down_weight,
        table,
        a_out,
        b_gu,
        a_down,
        col_count,
        row_count,
    )
    d_qkv_head = attend_back(qkv_head, d_attn_head, parent_at, branch_flag, lse)
    hot = (tree_set == lax.broadcasted_iota(jnp.int32, (set_count, width_row), 0)).astype(wide)
    in_grad, layer, sets = rear(
        d_qkv_head,
        raw,
        factors,
        gq,
        gk,
        cos2,
        sin2,
        out_half,
        x,
        w_qkv,
        table,
        b_qkv,
        d_h_half,
        full_mid,
        part_ao,
        part_bgu,
        part_ad,
        hot,
        set_count // dp_count,
        col_count,
        row_count,
        dp_count,
    )
    return tuple(unpack(in_grad, layer, sets, RANK // col_count, RANK // row_count, hidden_col))


def solution(mesh):
    in_specs = (
        P(("dp", "col"), "row"),
        P(("dp", "col"), "row"),
        P("dp"),
        P("dp"),
        P("dp", None),
        P("dp"),
        P("col"),
        P("col"),
        P("row"),
        P("row"),
        P("row", None, "col"),
        P("col", "row"),
        P("row", None, "col"),
        P("col", "row"),
        P(None, None, None, "row"),
        P(None, None, None, "col"),
        P(None, None, "col"),
        P(None, None, "row"),
        P(None, None, None, "row"),
        P(None, None, None, "col"),
        P(None, None, "col"),
        P(None, None, "row"),
    )
    out_specs = (
        P(("dp", "col"), "row"),
        P(("dp", "col"), "row"),
        P(None, "dp", "col", "row"),
        P(None, "dp", "row", "col"),
        P("dp", "row", "col"),
        P("dp", "col", "row"),
        P(None, "dp", "col", "row"),
        P(None, "dp", "row", "col"),
        P("dp", "row", "col"),
        P("dp", "col", "row"),
    )
    return jax.shard_map(
        per_device, mesh=mesh, in_specs=in_specs, out_specs=out_specs, check_vma=False
    )
```

```python
import functools

import jax
import jax.numpy as jnp
from jax import lax
from jax.experimental import pallas as pl
from jax.experimental.pallas import tpu as pltpu
from jax.sharding import PartitionSpec as P

D = 2048
HEAD = 128
RANK = 16
SEG = 128
TRUNK = 1024
QT = 256
MESH = pl.DeviceIdType.MESH
VM = pl.BlockSpec(memory_space=pltpu.VMEM)
precise = lax.Precision.HIGHEST

epsilon = 1e-06
rope_base = 500000.0
masked_out = -1e30
low = jnp.bfloat16
wide = jnp.float32
last_last = (((1,), (1,)), ((), ()))
first_first = (((0,), (0,)), ((), ()))


def dot(left, right):
    return jnp.dot(left, right, preferred_element_type=wide)


def dot_t(left, right):
    return lax.dot_general(left, right, last_last, preferred_element_type=wide)


def t_dot(left, right):
    return lax.dot_general(left, right, first_first, preferred_element_type=wide)


def angles(positions):
    lane = jnp.arange(HEAD, dtype=jnp.int32)
    frequency = rope_base ** (-((lane % (HEAD // 2)).astype(wide) * 2.0) / HEAD)
    angle_table = positions.astype(wide)[:, None] * frequency[None, :]
    return (jnp.cos(angle_table), jnp.where(lane < HEAD // 2, -1.0, 1.0) * jnp.sin(angle_table))


def norm_factor(square_sum):
    return lax.rsqrt(square_sum * (1.0 / D) + epsilon)


def tree_tables(seg_ids, parents):
    tail_seg = seg_ids[TRUNK::SEG]
    labels = jnp.arange(parents.shape[1], dtype=jnp.int32)
    tail_parent = jnp.sum(jnp.where(tail_seg[:, None] == labels[None, :], parents[0][None, :], 0), axis=1)
    hit = (tail_seg[None, :] == tail_parent[:, None])
    at = jnp.arange(tail_seg.shape[0], dtype=jnp.int32) + TRUNK // SEG
    parent_at = jnp.sum(jnp.where(hit, at[None, :], 0), axis=1)
    bias = jnp.where(tail_parent > 0, 0.0, masked_out).astype(wide)
    return parent_at, jnp.broadcast_to(bias[:, None], (tail_seg.shape[0], SEG))


def row_sum(v): return jnp.sum(v, axis=1, keepdims=True)

def params(collective):
    return pltpu.CompilerParams(collective_id=collective, has_side_effects=True, vmem_limit_bytes=60 << 20)


def span(at, size):
    return pl.ds(pl.multiple_of(at, size), size)


def remote(src, dst, send_sem, recv_sem, to):
    return pltpu.make_async_remote_copy(
        src_ref=src, dst_ref=dst, send_sem=send_sem, recv_sem=recv_sem, device_id=to, device_id_type=MESH
    )


def greet(n, nr, extra=0):
    r, c = lax.axis_index("row"), lax.axis_index("col")
    me = r * n + c
    barrier = pltpu.get_barrier_semaphore()

    @pl.loop(1, n * nr)
    def _(d):
        peer = lax.rem(me + d, n * nr)
        pl.semaphore_signal(barrier, inc=1, device_id={"row": peer // n, "col": lax.rem(peer, n)}, device_id_type=MESH)

    pl.semaphore_wait(barrier, n * nr - 1 + extra)


def row_sums(first, second):
    ones = jnp.ones((8, first.shape[1]), wide)
    at = lax.broadcasted_iota(jnp.int32, (8, first.shape[0]), 0)
    sum_first = lax.dot_general(ones, first, last_last, preferred_element_type=wide, precision=precise)
    sum_second = lax.dot_general(ones, second, last_last, preferred_element_type=wide, precision=precise)
    return jnp.where(at < 4, sum_first, sum_second)


def down_columns(values, at):
    pick = (lax.broadcasted_iota(jnp.int32, (8, HEAD), 0) == at).astype(wide)
    return lax.dot_general(values, pick, first_first, preferred_element_type=wide, precision=precise)


def flip(v):
    return v + 1 - 2 * lax.rem(v, 2)


class Share:
    def __init__(self, src, dst, cuts, sems):
        self.send, self.recv, self.local = sems
        self.src, self.cuts = src, cuts
        g, r = lax.axis_index("dp"), lax.axis_index("row")
        size = src.shape[0]
        half = size // 2
        step = half // cuts
        far = lax.rem(r + 2, 4)
        mine = lax.rem(g, 2)
        near_to, far_to, twin_to = {"row": flip(r)}, {"row": far}, {"dp": flip(g)}

        def rows(shard, part, i):
            return pl.ds(pl.multiple_of(shard * size + part * half + i * step, step), step)

        def copy(kind, i, src, dst, to):
            return remote(src, dst, self.send.at[kind, i], self.recv.at[kind, i], to)

        def hand(kind, part, to):
            return lambda i: copy(kind, i, dst.at[rows(far, part, i)], dst.at[rows(far, part, i)], to)

        whole = span(r * size, size)
        self.own = pltpu.make_async_copy(src, dst.at[whole], self.local)
        self.near = copy(0, 0, src, dst.at[whole], near_to)
        self.far = lambda i: copy(
            1, i, src.at[pl.ds(pl.multiple_of(mine * half + i * step, step), step)], dst.at[rows(r, mine, i)], far_to
        )
        self.far_near = hand(2, mine, near_to)
        self.far_twin = hand(3, mine, twin_to)
        self.twin_near = hand(4, 1 - mine, near_to)

    def start_far(self):
        for i in range(self.cuts):
            self.far(i).start()

    def start_near(self):
        self.own.start()
        self.near.start()

    def pass_far(self, i):
        self.far(i).wait_recv()
        self.far_twin(i).start()
        self.far_near(i).start()

    def pass_twin(self, i):
        self.far_twin(i).wait_recv()
        self.twin_near(i).start()

    def wait_all(self):
        self.own.wait()
        self.near.wait_recv()
        for i in range(self.cuts):
            self.far_near(i).wait_recv()
            self.twin_near(i).wait_recv()

    def drain(self):
        self.near.wait_send()
        for i in range(self.cuts):
            self.far(i).wait_send()
            self.far_near(i).wait_send()
            self.far_twin(i).wait_send()
            self.twin_near(i).wait_send()


def share_sems(cuts):
    dma = pltpu.SemaphoreType.DMA
    return [dma((5, cuts)), dma((5, cuts)), dma]


def prep_kernel(set_ref, fq_ref, sq_ref, fo_ref, so_ref, fg_ref, sg_ref, fd_ref, sd_ref,
                narrow_ref, bq_ref, ao_ref, bg_ref, ad_ref):
    for j in range(3):
        narrow_ref[j * RANK:(j + 1) * RANK, :] = fq_ref[j, 0].astype(low)
        bq_ref[j * RANK:(j + 1) * RANK, :] = sq_ref[j, 0].astype(low)
    for j in range(2):
        narrow_ref[(3 + j) * RANK:(4 + j) * RANK, :] = fg_ref[j, 0].astype(low)
        bg_ref[j] = sg_ref[j, 0].astype(low)
    narrow_ref[5 * RANK:6 * RANK, :] = so_ref[0].astype(low)
    narrow_ref[6 * RANK:, :] = sd_ref[0].astype(low)
    ao_ref[...] = fo_ref[0].astype(low)
    ad_ref[...] = fd_ref[0].astype(low)


def prep(tree_sets, tables):
    fq, sq, fo, so, fg, sg, fd, sd = tables

    def pick(table):
        if table.ndim == 4:
            return pl.BlockSpec((table.shape[0], 1) + table.shape[2:], lambda i, s: (0, s[0], 0, 0))
        return pl.BlockSpec((1,) + table.shape[1:], lambda i, s: (s[0], 0, 0))

    def out(*shape):
        return pl.BlockSpec(shape, lambda i, s: (0,) * len(shape)), jax.ShapeDtypeStruct(shape, low)

    outs = [
        out(7 * RANK, fq.shape[-1]), out(3 * RANK, sq.shape[-1]), out(RANK, fo.shape[-1]),
        out(2, RANK, sg.shape[-1]), out(RANK, fd.shape[-1]),
    ]
    return pl.pallas_call(
        prep_kernel,
        grid_spec=pltpu.PrefetchScalarGridSpec(
            num_scalar_prefetch=1, grid=(1,), in_specs=[pick(t) for t in tables], out_specs=[o[0] for o in outs]
        ),
        out_shape=[o[1] for o in outs],
        name="prep",
    )(tree_sets, *tables)


def lower_mask(size):
    return lax.broadcasted_iota(jnp.int32, (size, size), 1) <= lax.broadcasted_iota(jnp.int32, (size, size), 0)


def softmax_parts(parts):
    top = jnp.max(parts[0], axis=1, keepdims=True)
    for s in parts[1:]:
        top = jnp.maximum(top, jnp.max(s, axis=1, keepdims=True))
    raised = [jnp.exp(s - top) for s in parts]
    total = jnp.sum(raised[0], axis=1, keepdims=True)
    for e in raised[1:]:
        total = total + jnp.sum(e, axis=1, keepdims=True)
    inverse = 1.0 / total
    return raised, inverse, top + jnp.log(total)


def tail_spans(parent_ref, pair):
    at = [pl.multiple_of(TRUNK + (2 * pair + side) * SEG, SEG) for side in range(2)]
    parent = [pl.multiple_of(parent_ref[2 * pair + side] * SEG, SEG) for side in range(2)]
    return pl.ds(at[0], 2 * SEG), [pl.ds(v, SEG) for v in at], [pl.ds(v, SEG) for v in parent]


def by_side(product, left, rights):
    return jnp.concatenate([product(left[i * SEG:(i + 1) * SEG], right) for i, right in enumerate(rights)], axis=0)


def tail_parts(q, qkv, own, parents, flags):
    scale = HEAD ** -0.5
    k_lanes = slice(HEAD, 2 * HEAD)
    trunk = dot_t(q, qkv[:TRUNK, k_lanes]) * scale
    branch = by_side(dot_t, q, [qkv[rows, k_lanes] for rows in parents]) * scale
    branch = branch + jnp.concatenate([jnp.broadcast_to(flag, (SEG, SEG)) for flag in flags], axis=0)
    mask = jnp.concatenate([lower_mask(SEG)] * 2, axis=0)
    own = jnp.where(mask, by_side(dot_t, q, [qkv[rows, k_lanes] for rows in own]) * scale, masked_out)
    return [trunk, branch, own]


def trunk_parts(q, qkv, i):
    scale = HEAD ** -0.5
    k_lanes = slice(HEAD, 2 * HEAD)
    own = dot_t(q, qkv[i * QT:(i + 1) * QT, k_lanes]) * scale
    parts = [jnp.where(lower_mask(QT), own, masked_out)]
    if i:
        parts.append(dot_t(q, qkv[:i * QT, k_lanes]) * scale)
    return parts


def attend_body(parent_ref, flag_ref, qkv, o_ref, lse_ref):
    v_lanes = slice(2 * HEAD, 3 * HEAD)
    for i in range(TRUNK // QT):
        at = slice(i * QT, (i + 1) * QT)
        p, inverse, lse = softmax_parts(trunk_parts(qkv[at, :HEAD], qkv, i))
        o = dot(p[0].astype(low), qkv[at, v_lanes])
        if i:
            o = o + dot(p[1].astype(low), qkv[:i * QT, v_lanes])
        o_ref[at, :] = (o * inverse).astype(low)
        lse_ref[at, :] = lse

    @pl.loop(0, (qkv.shape[0] - TRUNK) // (2 * SEG), unroll=3)
    def _(j):
        rows, own, parents = tail_spans(parent_ref, j)
        flags = [flag_ref[pl.ds(2 * j + side, 1), :] for side in range(2)]
        p, inverse, lse = softmax_parts(tail_parts(qkv[rows, :HEAD], qkv, own, parents, flags))
        o = dot(p[0].astype(low), qkv[:TRUNK, v_lanes])
        o = o + by_side(dot, p[1].astype(low), [qkv[at, v_lanes] for at in parents])
        o = o + by_side(dot, p[2].astype(low), [qkv[at, v_lanes] for at in own])
        o_ref[rows, :] = (o * inverse).astype(low)
        lse_ref[rows, :] = lse


def back_parts(scores, lse, d_out, keys, values):
    probs = [jnp.exp(s - lse) for s in scores]
    grads = [dot_t(d_out, v) for v in values]
    inner = sum(jnp.sum(p * g, axis=1, keepdims=True) for p, g in zip(probs, grads))
    d_scores = [(p * (g - inner)).astype(low) for p, g in zip(probs, grads)]
    dq = sum(dot(d, k) for d, k in zip(d_scores, keys))
    return d_scores, [p.astype(low) for p in probs], dq


def attend_back_kernel(parent_ref, flag_ref, qkv, do_ref, lse_ref, d_ref, dk_acc, dv_acc):
    scale = HEAD ** -0.5
    k_lanes = slice(HEAD, 2 * HEAD)
    v_lanes = slice(2 * HEAD, 3 * HEAD)
    dk_acc[...] = jnp.zeros_like(dk_acc)
    dv_acc[...] = jnp.zeros_like(dv_acc)
    for i in range(TRUNK // QT):
        at = slice(i * QT, (i + 1) * QT)
        spans = [at] + ([slice(0, i * QT)] if i else [])
        q, d_out = qkv[at, :HEAD], do_ref[at, :]
        d_scores, probs, dq = back_parts(
            trunk_parts(q, qkv, i), lse_ref[at, :], d_out, [qkv[s, k_lanes] for s in spans], [qkv[s, v_lanes] for s in spans]
        )
        d_ref[at, :HEAD] = (dq * scale).astype(low)
        for s, d, p in zip(spans, d_scores, probs):
            dk_acc[s, :] += t_dot(d, q)
            dv_acc[s, :] += t_dot(p, d_out)

    @pl.loop(0, (qkv.shape[0] - TRUNK) // (2 * SEG), unroll=2)
    def _(j):
        rows, own, parents = tail_spans(parent_ref, j)
        flags = [flag_ref[pl.ds(2 * j + side, 1), :] for side in range(2)]
        q, d_out, lse = qkv[rows, :HEAD], do_ref[rows, :], lse_ref[rows, :]
        probs = [jnp.exp(s - lse) for s in tail_parts(q, qkv, own, parents, flags)]
        grads = [
            dot_t(d_out, qkv[:TRUNK, v_lanes]),
            by_side(dot_t, d_out, [qkv[at, v_lanes] for at in parents]),
            by_side(dot_t, d_out, [qkv[at, v_lanes] for at in own]),
        ]
        inner = sum(jnp.sum(p * g, axis=1, keepdims=True) for p, g in zip(probs, grads))
        d_scores = [(p * (g - inner)).astype(low) for p, g in zip(probs, grads)]
        probs = [p.astype(low) for p in probs]
        dq = dot(d_scores[0], qkv[:TRUNK, k_lanes])
        dq = dq + by_side(dot, d_scores[1], [qkv[at, k_lanes] for at in parents])
        dq = dq + by_side(dot, d_scores[2], [qkv[at, k_lanes] for at in own])
        d_ref[rows, :HEAD] = (dq * scale).astype(low)
        dk_acc[:TRUNK, :] += t_dot(d_scores[0], q)
        dv_acc[:TRUNK, :] += t_dot(probs[0], d_out)
        for part, spans in ((1, parents), (2, own)):
            for side, at in enumerate(spans):
                half = slice(side * SEG, (side + 1) * SEG)
                dk_acc[at, :] += t_dot(d_scores[part][half], q[half])
                dv_acc[at, :] += t_dot(probs[part][half], d_out[half])

    d_ref[:, k_lanes] = (dk_acc[...] * scale).astype(low)
    d_ref[:, v_lanes] = dv_acc[...].astype(low)


def attend(qkv, parent_at, flag):
    n = qkv.shape[0]

    def whole(*shape):
        return pl.BlockSpec(shape, lambda i, *_: (0, 0))

    return pl.pallas_call(
        attend_body,
        grid_spec=pltpu.PrefetchScalarGridSpec(
            num_scalar_prefetch=1,
            grid=(1,),
            in_specs=[whole(*flag.shape), whole(n, 3 * HEAD)],
            out_specs=[whole(n, HEAD), whole(n, 1)],
        ),
        out_shape=[jax.ShapeDtypeStruct((n, HEAD), low), jax.ShapeDtypeStruct((n, 1), wide)],
        name="attend",
    )(parent_at, flag, qkv)


def attend_back(qkv, d_o, parent_at, flag, lse):
    n = qkv.shape[0]

    def whole(*shape):
        return pl.BlockSpec(shape, lambda i, *_: (0, 0))

    return pl.pallas_call(
        attend_back_kernel,
        grid_spec=pltpu.PrefetchScalarGridSpec(
            num_scalar_prefetch=1,
            grid=(1,),
            in_specs=[whole(*flag.shape), whole(n, 3 * HEAD), whole(n, HEAD), whole(n, 1)],
            out_specs=whole(n, 3 * HEAD),
            scratch_shapes=[pltpu.VMEM((n, HEAD), wide), pltpu.VMEM((n, HEAD), wide)],
        ),
        out_shape=jax.ShapeDtypeStruct((n, 3 * HEAD), low),
        name="attend_back",
    )(parent_at, flag, qkv, d_o, lse)


def front_kernel(n, nr, m, mh, tok_ref, table_ref, gain_ref, cot_ref, wq_hbm, wo_hbm, gu_hbm, bq_ref, gq_ref, gk_ref,
                 cos_ref, sin_ref,
                 x_out, table_all, gain_all, half_ref, raw_out, factor_ref, qkv_ref, wq_out, wo_out, gu_out,
                 x_ref, raw_ref, gu_pair, gu_flat, wq, wo, stats, buf, fq, fk, red, cot_own,
                 send_a, recv_a, send_z, recv_z, send_t, recv_t, local_sem,
                 send_s, recv_s, send_h, recv_h, send_g, recv_g, local_h, local_g, send_e, recv_e,
                 send_q, recv_q, local_q, send_o, recv_o, local_o, out_sems):
    g, r, c = lax.axis_index("dp"), lax.axis_index("row"), lax.axis_index("col")
    own = tok_ref.shape[0] // nr
    width = tok_ref.shape[1]
    rows_all = own * n
    heads = width // HEAD
    tree_part = own * nr
    chunks = own // m
    left = {"col": jnp.maximum(c - 1, 0)}
    right = {"col": jnp.minimum(c + 1, n - 1)}
    share_q = Share(wq_hbm, wq, 2, (send_q, recv_q, local_q))
    share_o = Share(wo_hbm, wo, 2, (send_o, recv_o, local_o))

    def piece(d, j):
        peer = lax.rem(r + d, nr)
        return remote(
            tok_ref.at[span(peer * own + j * m, m)],
            x_ref.at[span(c * own + j * m, m), span(r * width, width)],
            send_a.at[d - 1, j], recv_a.at[d - 1, j], {"row": peer},
        )

    def block(kind, s, at, j, to):
        rows = span(at * own + j * m, m)
        return remote(x_ref.at[rows], x_ref.at[rows], send_z.at[kind, s, j], recv_z.at[kind, s, j], to)

    def table_piece(d, kind):
        src, dst = ((table_ref, table_all), (gain_ref, gain_all))[kind]
        to = {"row": lax.rem(r + d, nr)}
        return remote(src, dst.at[:, span(r * width, width)], send_t.at[kind, d - 1], recv_t.at[kind, d - 1], to)

    keep = pltpu.make_async_copy(
        tok_ref.at[span(r * own, own)], x_ref.at[span(c * own, own), span(r * width, width)], local_sem.at[0]
    )
    keep_table = pltpu.make_async_copy(table_ref, table_all.at[:, span(r * width, width)], local_sem.at[1])
    keep_gain = pltpu.make_async_copy(gain_ref, gain_all.at[:, span(r * width, width)], local_sem.at[2])
    keep.start()
    keep_table.start()
    keep_gain.start()
    barrier = pltpu.get_barrier_semaphore()
    pl.semaphore_signal(barrier, inc=1, device_id={"dp": flip(g)}, device_id_type=MESH)
    greet(n, nr, 1)

    @pl.loop(0, chunks)
    def _(j):
        for d in range(1, nr):
            piece(d, j).start()


    load_gu = pltpu.make_async_copy(gu_hbm, gu_pair, out_sems.at[4])
    copy_gu = pltpu.make_async_copy(gu_flat, gu_out, out_sems.at[5])
    gu_step = gu_flat.shape[0] // 8

    def flatten(i):
        @pl.when(i == 0)
        def _():
            load_gu.wait()

        rows = span(i * gu_step, gu_step)
        gu_flat[rows, :] = gu_pair[rows].reshape(gu_step, gu_flat.shape[1])

    middle_at = n // 2
    owner = jnp.where(c < middle_at, 0, n - 1)
    at_owner = jnp.where(c < middle_at, c, c - middle_at)
    is_owner = owner == c

    def cot_piece(d):
        peer = lax.rem(r + d, nr)
        return remote(
            cot_ref.at[span(peer * own, own)], cot_own.at[:, span(r * width, width)], send_g.at[d - 1], recv_g.at[d - 1], {"row": peer}
        )

    cot_local = pltpu.make_async_copy(cot_ref.at[span(r * own, own)], cot_own.at[:, span(r * width, width)], local_g.at[0])
    cot_keep = pltpu.make_async_copy(cot_own, half_ref.at[span(at_owner * own, own)], local_g.at[1])

    def cot_move(b):
        return remote(cot_own, half_ref.at[span(b * own, own)], send_e, recv_e.at[b], {"col": owner})

    share_q.start_far()
    share_q.start_near()
    for d in range(1, nr):
        table_piece(d, 0).start()
        table_piece(d, 1).start()
    share_o.start_far()
    share_o.start_near()
    cot_local.start()
    for d in range(1, nr):
        cot_piece(d).start()
    load_gu.start()
    keep.wait()

    def head_rows(i):
        block_at = i // (own // mh)
        inside = lax.rem(i, own // mh)
        return span(block_at * tree_part + r * own + inside * mh, mh)

    def head_piece(d, i):
        peer = lax.rem(r + d, nr)
        return remote(
            buf.at[peer, span(i * mh, mh)], qkv_ref.at[head_rows(i)], send_h.at[d - 1, i], recv_h.at[d - 1, i], {"row": peer}
        )

    def head_local(i):
        return pltpu.make_async_copy(buf.at[r, span(i * mh, mh)], qkv_ref.at[head_rows(i)], local_h.at[i])

    def stat_copy(b, d):
        peer = lax.rem(c + d, n)
        return remote(stats.at[c, b], stats.at[c, b], send_s.at[b, d - 1], recv_s.at[b, d - 1], {"col": peer})

    def product_block(b):
        rows = span(b * own, own)
        x_rows = x_ref[rows, :]
        red[...] = dot_t(x_rows, table_all[:3 * RANK, :]).astype(low)
        for j in range(3):
            lanes = slice(j * width, (j + 1) * width)
            raw_ref[rows, lanes] = dot(x_rows, wq[:, lanes]) + dot(
                red[:, j * RANK:(j + 1) * RANK], bq_ref[j * RANK:(j + 1) * RANK, :]
            )
        q_rows = raw_ref[rows, :width]
        k_rows = raw_ref[rows, width:2 * width]
        stats[c, b] = row_sums(q_rows * q_rows, k_rows * k_rows)
        for d in range(1, n):
            stat_copy(b, d).start()

    per = own // mh

    def head_block(b):
        for d in range(1, n):
            stat_copy(b, d).wait()
        total = stats[0, b]
        for s in range(1, n):
            total = total + stats[s, b]
        factor = lax.rsqrt(total * (1.0 / D) + epsilon)
        factor_ref[b] = factor
        fq[...] = down_columns(factor, 0)
        fk[...] = down_columns(factor, 4)

        @pl.loop(0, per)
        def _(i):
            rows = span(b * own + i * mh, mh)
            inside = span(i * mh, mh)
            cosine = cos_ref[rows, :]
            sine = sin_ref[rows, :]
            for h in range(heads):
                lanes = slice(h * HEAD, (h + 1) * HEAD)
                u = raw_ref[rows, lanes] * fq[inside, :] * gq_ref[:, lanes]
                buf[h, rows, :HEAD] = (u * cosine + pltpu.roll(u, HEAD // 2, 1) * sine).astype(low)
                k_lanes = slice(width + h * HEAD, width + (h + 1) * HEAD)
                u = raw_ref[rows, k_lanes] * fk[inside, :] * gk_ref[:, lanes]
                buf[h, rows, HEAD:2 * HEAD] = (u * cosine + pltpu.roll(u, HEAD // 2, 1) * sine).astype(low)
                v_lanes = slice(2 * width + h * HEAD, 2 * width + (h + 1) * HEAD)
                buf[h, rows, 2 * HEAD:] = raw_ref[rows, v_lanes].astype(low)
            for d in range(1, nr):
                head_piece(d, b * per + i).start()
            head_local(b * per + i).start()

    def both_phases(last_step):
        for d in range(1, nr):
            table_piece(d, 0).wait_recv()
            table_piece(d, 1).wait_recv()
        keep_table.wait()
        keep_gain.wait()
        share_q.wait_all()
        copy_wq.start()

        @pl.loop(0, 2)
        def _(phase):
            def at(i):
                return jnp.where(phase == 0, 1 + i, i * (n - 1))

            pl.when(phase == 1)(last_step)

            @pl.loop(0, 2)
            def _(i):
                product_block(at(i))

            @pl.when(phase == 0)
            def _():
                @pl.when(jnp.logical_not(is_owner))
                def _():
                    cot_move(at_owner).start()

                @pl.when(is_owner)
                def _():
                    cot_keep.start()

            @pl.when(phase == 1)
            def _():
                copy_x.start()
                copy_raw.start()
                for i in range(2):
                    share_o.pass_twin(i)

            @pl.loop(0, 2)
            def _(i):
                head_block(at(i))

    copy_wq = pltpu.make_async_copy(wq, wq_out, out_sems.at[0])
    copy_x = pltpu.make_async_copy(x_ref, x_out, out_sems.at[2])
    copy_raw = pltpu.make_async_copy(raw_ref, raw_out, out_sems.at[3])

    def ring_step(s):
        @pl.loop(0, chunks)
        def _(j):
            if s == 0:
                for d in range(1, nr):
                    piece(d, j).wait_recv()

            @pl.when(c - s >= 0)
            def _():
                if s > 0:
                    block(0, s - 1, jnp.maximum(c - s, 0), j, right).wait_recv()
                if s < n - 1:
                    @pl.when(c < n - 1)
                    def _():
                        block(0, s, jnp.maximum(c - s, 0), j, right).start()

            @pl.when(c + s <= n - 1)
            def _():
                if s > 0:
                    block(1, s - 1, jnp.minimum(c + s, n - 1), j, left).wait_recv()
                if s < n - 1:
                    @pl.when(c > 0)
                    def _():
                        block(1, s, jnp.minimum(c + s, n - 1), j, left).start()

            if 0 < s < n - 1:
                @pl.when(j < 8 // (n - 2))
                def _():
                    flatten((s - 1) * (8 // (n - 2)) + j)

        if s == 1:
            for i in range(2):
                share_q.pass_far(i)
        if s == n - 2:
            copy_gu.start()
        if s == n - 2:
            for i in range(2):
                share_o.pass_far(i)
                share_q.pass_twin(i)
            cot_local.wait()
            for d in range(1, nr):
                cot_piece(d).wait_recv()
    steps = rows_all // mh

    for s in range(n - 1):
        ring_step(s)
    both_phases(lambda: ring_step(n - 1))

    share_o.wait_all()
    copy_wo = pltpu.make_async_copy(wo, wo_out, out_sems.at[1])
    copy_wo.start()

    @pl.loop(0, steps)
    def _(i):
        for d in range(1, nr):
            head_piece(d, i).wait()
        head_local(i).wait()

    for d in range(1, nr):
        cot_piece(d).wait_send()

    @pl.when(jnp.logical_not(is_owner))
    def _():
        cot_move(at_owner).wait_send()

    @pl.when(is_owner)
    def _():
        cot_keep.wait()
        for b in range(middle_at):
            @pl.when(b != at_owner)
            def _():
                remote(cot_own, half_ref.at[span(b * own, own)], send_e, recv_e.at[b], {"row": flip(r)}).wait_recv()

    @pl.loop(0, chunks)
    def _(j):
        for d in range(1, nr):
            piece(d, j).wait_send()
        for s in range(n - 1):
            @pl.when(jnp.logical_and(c - s >= 0, c < n - 1))
            def _():
                block(0, s, jnp.maximum(c - s, 0), j, right).wait_send()

            @pl.when(jnp.logical_and(c + s <= n - 1, c > 0))
            def _():
                block(1, s, jnp.minimum(c + s, n - 1), j, left).wait_send()

    for d in range(1, nr):
        table_piece(d, 0).wait_send()
        table_piece(d, 1).wait_send()
    share_q.drain()
    share_o.drain()
    copy_wq.wait()
    copy_wo.wait()
    copy_x.wait()
    copy_raw.wait()
    copy_gu.wait()


def front(tokens, table, gain, cot, w_qkv, w_out, w_gu, b_qkv, gain_q, gain_k, cos2, sin2, n, nr, m=32, mh=160):
    own = tokens.shape[0] // nr
    width = tokens.shape[1]
    rows_all = own * n
    tree = own * n * nr
    chunks = own // m
    steps = rows_all // mh
    dma = pltpu.SemaphoreType.DMA
    shape = jax.ShapeDtypeStruct
    any_space = pl.BlockSpec(memory_space=pl.ANY)
    return pl.pallas_call(
        functools.partial(front_kernel, n, nr, m, mh),
        out_shape=[
            shape((rows_all, width * nr), low),
            shape((table.shape[0], width * nr), low),
            shape((gain.shape[0], width * nr), wide),
            shape((rows_all // 2, width * nr), low),
            shape((rows_all, 3 * width), wide),
            shape((n, 8, own), wide),
            shape((tree, 3 * HEAD), low),
            shape((w_qkv.shape[0] * nr, w_qkv.shape[1]), low),
            shape((w_out.shape[0] * nr, w_out.shape[1]), low),
            shape((w_gu.shape[0], 2 * w_gu.shape[2]), low),
        ],
        in_specs=[any_space, VM, VM] + [any_space] * 4 + [VM] * 5,
        out_specs=[any_space, VM, VM, any_space, any_space, VM, any_space, any_space, any_space, any_space],
        scratch_shapes=[
            pltpu.VMEM((rows_all, width * nr), low),
            pltpu.VMEM((rows_all, 3 * width), wide),
            pltpu.VMEM(w_gu.shape, low),
            pltpu.VMEM((w_gu.shape[0], 2 * w_gu.shape[2]), low),
            pltpu.VMEM((w_qkv.shape[0] * nr, w_qkv.shape[1]), low),
            pltpu.VMEM((w_out.shape[0] * nr, w_out.shape[1]), low),
            pltpu.VMEM((n, n, 8, own), wide),
            pltpu.VMEM((width // HEAD, rows_all, 3 * HEAD), low),
            pltpu.VMEM((own, HEAD), wide),
            pltpu.VMEM((own, HEAD), wide),
            pltpu.VMEM((own, 3 * RANK), low),
            pltpu.VMEM((own, width * nr), low),
            dma((nr - 1, chunks)), dma((nr - 1, chunks)), dma((2, n - 1, chunks)), dma((2, n - 1, chunks)),
            dma((2, nr - 1)), dma((2, nr - 1)), dma((3,)),
            dma((n, n - 1)), dma((n, n - 1)), dma((nr - 1, steps)), dma((nr - 1, steps)),
            dma((nr - 1,)), dma((nr - 1,)), dma((steps,)), dma((2,)), dma, dma((n // 2,)),
        ] + share_sems(2) + share_sems(2) + [dma((6,))],
        compiler_params=params(3),
        name="front",
    )(tokens, table, gain, cot, w_qkv, w_out, w_gu, b_qkv, gain_q, gain_k, cos2, sin2)


def one_hot_rows(out_rows, in_rows, source):
    at = lax.broadcasted_iota(jnp.int32, (out_rows, in_rows), 0)
    return (lax.broadcasted_iota(jnp.int32, (out_rows, in_rows), 1) == source(at)).astype(low)


def rear_kernel(n, nr, ndp, m, d_ref, raw_hbm, factor_ref, gq_ref, gk_ref, cos_ref, sin_ref, res_ref, x_hbm, wq_hbm,
                table_ref, bq_ref, dh_hbm, full_hbm, co_hbm, cg_hbm, cd_hbm, hot_ref,
                grad_ref, layer_ref, sets_ref,
                raw_ref, x_ref, dh_ref, full_ref, co_ref, cg_ref, cd_ref, wq, stats, buf, nq, nk, pq, pk, fq, fk, d_raw, part, recv_right, recv_left, own_buf, layer_own,
                back, red, full, cols, col_stack, full_recv, full_sum, full_last, col_recv, owned, hot_all,
                send_s, recv_s, send_h, recv_h, local_h, send_o, recv_o, local_o, load,
                send_z, recv_z, send_w, recv_w, local_w, send_v, recv_v, local_v,
                send_f, recv_f, send_c, recv_c, send_l, recv_l, send_d, recv_d, send_k, recv_k):
    g, r, c = lax.axis_index("dp"), lax.axis_index("row"), lax.axis_index("col")
    rows_all, width_all = part.shape
    own = rows_all // n
    width = gq_ref.shape[1]
    heads = width // HEAD
    tree_part = own * nr
    middle_at = n // 2
    chunks = own // m
    hop = 1
    ahead = 2
    left = {"col": jnp.maximum(c - 1, 0)}
    right = {"col": jnp.minimum(c + 1, n - 1)}
    load_raw = pltpu.make_async_copy(raw_hbm, raw_ref, load.at[0])
    load_x = pltpu.make_async_copy(x_hbm, x_ref, load.at[1])
    load_w = pltpu.make_async_copy(wq_hbm, wq, load.at[2])
    loads = [
        pltpu.make_async_copy(src, dst, load.at[3 + i])
        for i, (src, dst) in enumerate(
            ((dh_hbm, dh_ref), (full_hbm, full_ref), (co_hbm, co_ref), (cg_hbm, cg_ref), (cd_hbm, cd_ref))
        )
    ]

    def piece(d, b):
        peer = lax.rem(r + d, nr)
        return remote(
            d_ref.at[span(b * tree_part + peer * own, own)], buf.at[r, span(b * own, own)],
            send_h.at[d - 1, b], recv_h.at[d - 1, b], {"row": peer},
        )

    def local(b):
        return pltpu.make_async_copy(
            d_ref.at[span(b * tree_part + r * own, own)], buf.at[r, span(b * own, own)], local_h.at[b]
        )

    is_owner = jnp.logical_or(c == 0, c == n - 1)
    base = jnp.where(c == 0, 0, middle_at)

    def result_piece(b):
        return remote(res_ref.at[span(b * own, own)], layer_own, send_o.at[b], recv_o, {"col": base + b})

    def result_local(b):
        return pltpu.make_async_copy(res_ref.at[span(b * own, own)], layer_own, local_o)

    def width_piece(src, dst, send_sem, recv_sem, d, j, size):
        peer = lax.rem(r + d, nr)
        return remote(
            src.at[span(j * size, size), span(peer * width, width)], dst.at[span(r * own + j * size, size)],
            send_sem.at[d - 1, j], recv_sem.at[d - 1, j], {"row": peer},
        )

    def width_local(src, dst, sem, j, size):
        return pltpu.make_async_copy(
            src.at[span(j * size, size), span(r * width, width)], dst.at[span(r * own + j * size, size)], sem.at[j]
        )

    for b in range(n):
        local(b).start()
    load_raw.start()
    load_x.start()
    load_w.start()
    for copy in loads:
        copy.start()
    me = r * n + c
    barrier = pltpu.get_barrier_semaphore()
    for d in range(1, ndp):
        pl.semaphore_signal(barrier, inc=1, device_id={"dp": lax.rem(g + d, ndp)}, device_id_type=MESH)
    greet(n, nr, ndp - 1)
    for b in (0, n - 1) + tuple(range(1, n - 1)):
        for d in range(1, nr):
            piece(d, b).start()

    @pl.when(is_owner)
    def _():
        for b in range(middle_at):
            @pl.when(base + b == c)
            def _():
                result_local(b).start()

            @pl.when(base + b != c)
            def _():
                result_piece(b).start()

    hot_all[g] = hot_ref[...]
    load_x.wait()
    red[...] = dot_t(x_ref[...], table_ref[:3 * RANK, :]).astype(low)
    load_raw.wait()

    def stat_copy(b, d):
        peer = lax.rem(c + d, n)
        return remote(stats.at[c, b], stats.at[c, b], send_s.at[b, d - 1], recv_s.at[b, d - 1], {"col": peer})

    def norm_block(b):
        for d in range(1, nr):
            piece(d, b).wait_recv()
        local(b).wait()
        rows = span(b * own, own)
        fq[rows, :] = down_columns(factor_ref[b], 0)
        fk[rows, :] = down_columns(factor_ref[b], 4)
        cosine = cos_ref[rows, :]
        sine = sin_ref[rows, :]
        for h in range(heads):
            lanes = slice(h * HEAD, (h + 1) * HEAD)
            k_lanes = slice(width + h * HEAD, width + (h + 1) * HEAD)
            v_lanes = slice(2 * width + h * HEAD, 2 * width + (h + 1) * HEAD)
            u = buf[h, rows, :HEAD].astype(wide)
            u = (u * cosine - pltpu.roll(u, HEAD // 2, 1) * sine) * gq_ref[:, lanes]
            nq[rows, lanes] = u
            pq[rows, lanes] = u * raw_ref[rows, lanes] * fq[rows, :]
            u = buf[h, rows, HEAD:2 * HEAD].astype(wide)
            u = (u * cosine - pltpu.roll(u, HEAD // 2, 1) * sine) * gk_ref[:, lanes]
            nk[rows, lanes] = u
            pk[rows, lanes] = u * raw_ref[rows, k_lanes] * fk[rows, :]
            d_raw[rows, v_lanes] = buf[h, rows, 2 * HEAD:]
        stats[c, b] = row_sums(pq[rows, :], pk[rows, :])
        for d in range(1, n):
            stat_copy(b, d).start()

    def mean_block(b):
        for d in range(1, n):
            stat_copy(b, d).wait()
        total = stats[0, b]
        for s in range(1, n):
            total = total + stats[s, b]
        mean = total * (1.0 / D) * factor_ref[b]
        rows = span(b * own, own)
        pq[rows, :HEAD] = down_columns(mean, 0)
        pk[rows, :HEAD] = down_columns(mean, 4)

    def back_block(b):
        rows = span(b * own, own)
        for h in range(heads):
            lanes = slice(h * HEAD, (h + 1) * HEAD)
            k_lanes = slice(width + h * HEAD, width + (h + 1) * HEAD)
            d_raw[rows, lanes] = (fq[rows, :] * (nq[rows, lanes] - raw_ref[rows, lanes] * pq[rows, :HEAD])).astype(low)
            d_raw[rows, k_lanes] = (fk[rows, :] * (nk[rows, lanes] - raw_ref[rows, k_lanes] * pk[rows, :HEAD])).astype(low)
        for j in range(3):
            back[rows, j * RANK:(j + 1) * RANK] = dot_t(
                d_raw[rows, j * width:(j + 1) * width], bq_ref[j * RANK:(j + 1) * RANK, :]
            ).astype(low)
        mine = jnp.where(b < middle_at, c == 0, c == n - 1)
        held = span(lax.rem(b, middle_at) * own, own)
        for k in range(width_all // width):
            lanes = slice(k * width, (k + 1) * width)
            value = dot_t(d_raw[rows, :], wq[lanes, :]) + dot(back[rows, :], table_ref[:3 * RANK, lanes])
            part[rows, lanes] = (value + jnp.where(mine, dh_ref[held, lanes], 0.0)).astype(low)

    def full_piece(d):
        peer = lax.rem(r + d, nr)
        return remote(full.at[:, span(peer * width, width)], full_recv.at[r], send_f.at[d - 1], recv_f.at[d - 1], {"row": peer})

    col_rows = col_recv.shape[1]
    full_rows = full_last.shape[1]

    def col_piece(d):
        peer = lax.rem(r + d, nr)
        return remote(cols.at[span(peer * col_rows, col_rows)], col_recv.at[r], send_c.at[d - 1], recv_c.at[d - 1], {"row": peer})

    def last_piece(d):
        peer = lax.rem(c + d, n)
        return remote(full_sum.at[span(peer * full_rows, full_rows)], full_last.at[c], send_l.at[d - 1], recv_l.at[d - 1], {"col": peer})

    def tree_piece(d):
        return remote(owned.at[g], owned.at[g], send_d.at[d - 1], recv_d.at[d - 1], {"dp": lax.rem(g + d, ndp)})

    def hot_piece(d):
        return remote(hot_all.at[g], hot_all.at[g], send_k.at[d - 1], recv_k.at[d - 1], {"dp": lax.rem(g + d, ndp)})

    def reduce(kind, b, j):
        rows = span(b * own + j * m, m)
        dst, to = ((recv_right, right), (recv_left, left))[kind]
        return remote(part.at[rows], dst.at[rows], send_z.at[kind, b, j], recv_z.at[kind, b, j], to)

    def stage(s, at_edge=True, inside=True, jobs=()):
        @pl.loop(0, chunks + hop * (n - 2))
        def _(i):
            for at, job in enumerate(jobs):
                pl.when(i == at)(job)

            for kind, b, go, edge, got, j in (
                (0, n - 1 - s, n - 1 - s > c, c == 0, recv_right, i - hop * c),
                (1, s, s < c, c == n - 1, recv_left, i - hop * (n - 1 - c)),
            ):
                go = jnp.logical_and(go, jnp.logical_and(j >= 0, j < chunks))
                if at_edge:
                    @pl.when(jnp.logical_and(go, edge))
                    def _():
                        @pl.when(j >= ahead)
                        def _():
                            reduce(kind, b, j - ahead).wait_send()

                        reduce(kind, b, j).start()

                if inside:
                    @pl.when(jnp.logical_and(go, jnp.logical_not(edge)))
                    def _():
                        rows = span(b * own + j * m, m)
                        reduce(kind, b, j).wait_recv()
                        part[rows, :] = (part[rows, :].astype(wide) + got[rows, :].astype(wide)).astype(low)
                        reduce(kind, b, j).start()

    @pl.loop(0, 2)
    def _(phase):
        def at(i):
            return jnp.where(phase == 0, i * (n - 1), 1 + i)

        @pl.loop(0, 2)
        def _(i):
            norm_block(at(i))

        @pl.when(phase == 0)
        def _():
            load_w.wait()
            loads[0].wait()

        @pl.when(phase == 1)
        def _():
            stage(0)

        @pl.loop(0, 2)
        def _(i):
            mean_block(at(i))
            back_block(at(i))

    for copy in loads[1:]:
        copy.wait()

    rank_own = RANK // n
    groups = full.shape[0] // (n * rank_own) - 1
    rank_row = RANK // nr
    per_wide = cd_ref.shape[1] // width

    def full_job():
        stacked = jnp.concatenate([t_dot(back[...], x_ref[...]), full_ref[...]], axis=0).astype(low)
        order = one_hot_rows(
            full.shape[0], stacked.shape[0],
            lambda o: jnp.where(
                lax.rem(o, full_rows) < groups * rank_own,
                lax.rem(o, full_rows) // rank_own * RANK + o // full_rows * rank_own + lax.rem(o, rank_own), -1
            ),
        )
        full[...] = dot(order, stacked).astype(low)

    def raw_job():
        for j in range(3):
            col_stack[j * RANK:(j + 1) * RANK, :] = t_dot(
                red[:, j * RANK:(j + 1) * RANK], d_raw[:, j * width:(j + 1) * width]
            ).astype(low)
        col_stack[3 * RANK:4 * RANK, :] = co_ref[...].astype(low)

    def wide_job():
        for k in range(per_wide):
            lanes = slice(k * width, (k + 1) * width)
            for j, value in enumerate((cg_ref[0, :, lanes], cg_ref[1, :, lanes], cd_ref[:, lanes])):
                at = (4 + j * per_wide + k) * RANK
                col_stack[at:at + RANK, :] = value.astype(low)

    def col_job():
        order = one_hot_rows(
            cols.shape[0], cols.shape[0],
            lambda o: lax.rem(o, col_rows) // rank_row * RANK + o // col_rows * rank_row + lax.rem(o, rank_row),
        )
        cols[...] = dot(order, col_stack[...]).astype(low)

    stage(1, jobs=(wide_job, raw_job, col_job, full_job))
    for d in range(1, nr):
        full_piece(d).start()
        col_piece(d).start()

    @pl.when(is_owner)
    def _():
        for b in range(middle_at):
            @pl.when(base + b == c)
            def _():
                result_local(b).wait()

            @pl.when(base + b != c)
            def _():
                result_piece(b).wait_send()

    @pl.when(jnp.logical_not(is_owner))
    def _():
        remote(res_ref.at[span(0, own)], layer_own, send_o.at[0], recv_o, right).wait_recv()

    for d in range(1, nr):
        width_piece(layer_own, layer_ref, send_v, recv_v, d, 0, own).start()
    width_local(layer_own, layer_ref, local_v, 0, own).start()
    def row_job():
        for d in range(1, nr):
            full_piece(d).wait_recv()
            col_piece(d).wait_recv()
        total = full[:, span(r * width, width)].astype(wide)
        col_total = cols[span(r * col_rows, col_rows), :].astype(wide)
        for d in range(1, nr):
            peer = lax.rem(r + d, nr)
            total = total + full_recv[peer].astype(wide)
            col_total = col_total + col_recv[peer].astype(wide)
        full_sum[...] = total.astype(low)
        owned[g, full_rows:, :] = col_total.astype(low)
        for d in range(1, n):
            last_piece(d).start()

    stage(2, jobs=(lambda: None, row_job))
    for d in range(1, n):
        last_piece(d).wait_recv()
    last = full_sum[span(c * full_rows, full_rows), :].astype(wide)
    for d in range(1, n):
        last = last + full_last[lax.rem(c + d, n)].astype(wide)
    owned[g, :full_rows, :] = last.astype(low)
    for d in range(1, ndp):
        tree_piece(d).start()
        hot_piece(d).start()

    @pl.loop(0, chunks)
    def _(j):
        rows = span(c * own + j * m, m)
        at = span(j * m, m)
        own_buf[at, :] = part[rows, :]

        @pl.when(c > 0)
        def _():
            reduce(0, c, j).wait_recv()
            own_buf[at, :] = (own_buf[at, :].astype(wide) + recv_right[rows, :].astype(wide)).astype(low)

        @pl.when(c < n - 1)
        def _():
            reduce(1, c, j).wait_recv()
            own_buf[at, :] = (own_buf[at, :].astype(wide) + recv_left[rows, :].astype(wide)).astype(low)

        for d in range(1, nr):
            width_piece(own_buf, grad_ref, send_w, recv_w, d, j, m).start()
        width_local(own_buf, grad_ref, local_w, j, m).start()

    for d in range(1, ndp):
        tree_piece(d).wait_recv()
        hot_piece(d).wait_recv()
    sets_own = sets_ref.shape[0]
    for s in range(sets_own):
        total = owned[0].astype(wide) * hot_all[0, pl.ds(g * sets_own + s, 1), :]
        for t in range(1, ndp):
            total = total + owned[t].astype(wide) * hot_all[t, pl.ds(g * sets_own + s, 1), :]
        sets_ref[s] = total

    @pl.loop(0, chunks)
    def _(j):
        for d in range(1, nr):
            width_piece(own_buf, grad_ref, send_w, recv_w, d, j, m).wait()
        width_local(own_buf, grad_ref, local_w, j, m).wait()

    for d in range(1, nr):
        width_piece(layer_own, layer_ref, send_v, recv_v, d, 0, own).wait()
        full_piece(d).wait_send()
        col_piece(d).wait_send()
        for b in range(n):
            piece(d, b).wait_send()
    width_local(layer_own, layer_ref, local_v, 0, own).wait()
    for d in range(1, n):
        last_piece(d).wait_send()
    for d in range(1, ndp):
        tree_piece(d).wait_send()
        hot_piece(d).wait_send()
    for s in range(n - 1):
        @pl.loop(0, chunks)
        def _(j):
            late = j >= chunks - ahead

            @pl.when(jnp.logical_and(n - 1 - s > c, jnp.logical_or(c > 0, late)))
            def _():
                reduce(0, n - 1 - s, j).wait_send()

            @pl.when(jnp.logical_and(s < c, jnp.logical_or(c < n - 1, late)))
            def _():
                reduce(1, s, j).wait_send()


def rear(d_head, raw, factor, gain_q, gain_k, cos2, sin2, result, x, w_qkv, table, b_qkv, d_h, full_mid, part_ao,
         part_bgu, part_ad, hot, sets_own, n, nr, ndp, m=32):
    rows_all, wide3 = raw.shape
    width = wide3 // 3
    width_all = x.shape[1]
    own = rows_all // n
    chunks = own // m
    full_rows = 8 * RANK // n
    col_blocks = 4 + 3 * part_ad.shape[1] // width
    col_rows = col_blocks * RANK // nr
    dma = pltpu.SemaphoreType.DMA
    shape = jax.ShapeDtypeStruct
    any_space = pl.BlockSpec(memory_space=pl.ANY)
    square = pltpu.VMEM((rows_all, width), wide)
    lane = pltpu.VMEM((rows_all, HEAD), wide)
    big = pltpu.VMEM((rows_all, width_all), low)
    return pl.pallas_call(
        functools.partial(rear_kernel, n, nr, ndp, m),
        out_shape=[
            shape((own * nr, width), low),
            shape((own * nr, width), low),
            shape((sets_own, full_rows + col_rows, width), wide),
        ],
        in_specs=[any_space] * 2 + [VM] * 5 + [any_space] * 3 + [VM] * 2 + [any_space] * 5 + [VM],
        out_specs=[VM] * 3,
        scratch_shapes=[
            pltpu.VMEM(raw.shape, wide),
            pltpu.VMEM(x.shape, low),
            pltpu.VMEM(d_h.shape, wide),
            pltpu.VMEM(full_mid.shape, wide),
            pltpu.VMEM(part_ao.shape, wide),
            pltpu.VMEM(part_bgu.shape, wide),
            pltpu.VMEM(part_ad.shape, wide),
            pltpu.VMEM(w_qkv.shape, low),
            pltpu.VMEM((n, n, 8, own), wide),
            pltpu.VMEM((nr, rows_all, 3 * HEAD), low),
            square, square, square, square, lane, lane,
            pltpu.VMEM((rows_all, wide3), low),
            big, big, big,
            pltpu.VMEM((own, width_all), low),
            pltpu.VMEM((own, width_all), low),
            pltpu.VMEM((rows_all, 3 * RANK), low),
            pltpu.VMEM((rows_all, 3 * RANK), low),
            pltpu.VMEM((n * full_rows, width_all), low),
            pltpu.VMEM((nr * col_rows, width), low),
            pltpu.VMEM((nr * col_rows, width), low),
            pltpu.VMEM((nr, n * full_rows, width), low),
            pltpu.VMEM((n * full_rows, width), low),
            pltpu.VMEM((n, full_rows, width), low),
            pltpu.VMEM((nr, col_rows, width), low),
            pltpu.VMEM((ndp, full_rows + col_rows, width), low),
            pltpu.VMEM((ndp,) + hot.shape, wide),
            dma((n, n - 1)), dma((n, n - 1)), dma((nr - 1, n)), dma((nr - 1, n)), dma((n,)),
            dma((n // 2,)), dma, dma, dma((8,)),
            dma((2, n, chunks)), dma((2, n, chunks)), dma((nr - 1, chunks)), dma((nr - 1, chunks)), dma((chunks,)),
            dma((nr - 1, 1)), dma((nr - 1, 1)), dma((1,)),
            dma((nr - 1,)), dma((nr - 1,)), dma((nr - 1,)), dma((nr - 1,)), dma((n - 1,)), dma((n - 1,)),
            dma((ndp - 1,)), dma((ndp - 1,)), dma((ndp - 1,)), dma((ndp - 1,)),
        ],
        compiler_params=params(5),
        name="rear",
    )(d_head, raw, factor, gain_q, gain_k, cos2, sin2, result, x, w_qkv, table, b_qkv, d_h, full_mid, part_ao, part_bgu, part_ad, hot)


def unpack_kernel(rank_own, rank_row, grad_ref, layer_ref, sets_ref, layer_out, input_grad, a_qkv, b_qkv, a_out, b_out, a_gu, b_gu, a_down, b_down):
    layer_out[...] = layer_ref[...]
    input_grad[...] = grad_ref[...].astype(wide)
    width = grad_ref.shape[1]
    first = 8 * rank_own

    def column(s, at):
        return sets_ref[s, first + at * rank_row:first + (at + 1) * rank_row, :]

    for s in range(sets_ref.shape[0]):
        for j in range(3):
            a_qkv[j, s] = sets_ref[s, j * rank_own:(j + 1) * rank_own, :]
            b_qkv[j, s] = column(s, j)
        for j in range(2):
            a_gu[j, s] = sets_ref[s, (3 + j) * rank_own:(4 + j) * rank_own, :]
        b_out[s] = sets_ref[s, 5 * rank_own:6 * rank_own, :]
        b_down[s] = sets_ref[s, 6 * rank_own:7 * rank_own, :]
        a_out[s] = column(s, 3)
        per = a_down.shape[2] // width
        for k in range(per):
            lanes = slice(k * width, (k + 1) * width)
            b_gu[0, s, :, lanes] = column(s, 4 + k)
            b_gu[1, s, :, lanes] = column(s, 4 + per + k)
            a_down[s, :, lanes] = column(s, 4 + 2 * per + k)


def unpack(grad, layer, sets, rank_own, rank_row, hidden):
    sets_own = sets.shape[0]
    width = grad.shape[1]
    shape = jax.ShapeDtypeStruct
    return pl.pallas_call(
        functools.partial(unpack_kernel, rank_own, rank_row),
        out_shape=[
            shape(layer.shape, low),
            shape(grad.shape, wide),
            shape((3, sets_own, rank_own, width), wide),
            shape((3, sets_own, rank_row, width), wide),
            shape((sets_own, rank_row, width), wide),
            shape((sets_own, rank_own, width), wide),
            shape((2, sets_own, rank_own, width), wide),
            shape((2, sets_own, rank_row, hidden), wide),
            shape((sets_own, rank_row, hidden), wide),
            shape((sets_own, rank_own, width), wide),
        ],
        in_specs=[VM] * 3,
        out_specs=[VM] * 10,
        name="unpack",
    )(grad, layer, sets)


def middle_kernel(n, nr, m, hop, cuts, head_ref, x_hbm, cot_hbm, gain_ref, wo_hbm, wg_hbm, wd_hbm,
                  table_ref, ao_ref, bg_ref, ad_ref,
                  dhead_ref, out_hbm, grad_hbm, full_ref, co_ref, cg_ref, cd_ref,
                  out_half, grad_half, wo, wg, wd, x_half, cot_half, raw, attn, d_attn, h_all, df_all, da_all, gu, part,
                  recv_right, recv_left, hid, red_gu, red_down, back_gu, back_down,
                  sems_send, sems_recv, send_in, recv_in, send_out, recv_out, local_in, local_out, load,
                  send_g, recv_g, local_g, send_d, recv_d, local_d):
    g, r, c = lax.axis_index("dp"), lax.axis_index("row"), lax.axis_index("col")
    ag_ref = table_ref.at[3 * RANK:5 * RANK]
    bo_ref = table_ref.at[5 * RANK:6 * RANK]
    bd_ref = table_ref.at[6 * RANK:]
    rows_all, width_all = part.shape
    half = rows_all // 2
    own = rows_all // n
    tree_part = own * nr
    chunks = half // m
    blocks = 4
    band = half // blocks
    hidden = ad_ref.shape[1]
    width = width_all // nr
    left = {"col": jnp.maximum(c - 1, 0)}
    right = {"col": jnp.minimum(c + 1, n - 1)}
    first = c == 0
    last = c == n - 1
    inner = jnp.logical_and(c > 0, c < n - 1)

    base = jnp.where(last, half, 0)
    a_cut = hidden // 4
    share_g = Share(wg_hbm, wg, cuts, (send_g, recv_g, local_g))
    share_d = Share(wd_hbm, wd, cuts // 2, (send_d, recv_d, local_d))
    loads = [pltpu.make_async_copy(wo_hbm, wo, load.at[0])]
    load_x = pltpu.make_async_copy(x_hbm.at[span(base, half)], x_half, load.at[1])
    load_cot = pltpu.make_async_copy(cot_hbm, cot_half, load.at[2])
    store_out = pltpu.make_async_copy(out_half, out_hbm, load.at[3])
    store_grad = pltpu.make_async_copy(grad_half, grad_hbm, load.at[4])
    is_owner = jnp.logical_or(first, last)
    loads[0].start()

    def piece_in(d, b):
        peer = lax.rem(r + d, nr)
        return remote(
            head_ref.at[span(b * tree_part + peer * own, own)],
            attn.at[span(b * own, own), span(r * HEAD, HEAD)],
            send_in.at[d - 1, b], recv_in.at[d - 1, b], {"row": peer},
        )

    def local_piece_in(b):
        return pltpu.make_async_copy(
            head_ref.at[span(b * tree_part + r * own, own)],
            attn.at[span(b * own, own), span(r * HEAD, HEAD)], local_in.at[b]
        )

    per_block = blocks // (n // 2)

    def out_rows(b, side):
        at = side * (n // 2) + b // per_block
        inside = lax.rem(b, per_block) * band
        return span(at * own + inside, band), span(at * tree_part + r * own + inside, band)

    def piece_out(d, b, side):
        peer = lax.rem(r + d, nr)
        here, there = out_rows(b, side)
        return remote(
            d_attn.at[here, span(peer * HEAD, HEAD)], dhead_ref.at[there],
            send_out.at[side * (nr - 1) + d - 1, b], recv_out.at[side * (nr - 1) + d - 1, b], {"row": peer},
        )

    def local_piece_out(b, side):
        here, there = out_rows(b, side)
        return pltpu.make_async_copy(d_attn.at[here, span(r * HEAD, HEAD)], dhead_ref.at[there], local_out.at[side, b])

    for b in range(n):
        local_piece_in(b).start()
    barrier = pltpu.get_barrier_semaphore()
    for d in range(1, nr):
        pl.semaphore_signal(barrier, inc=1, device_id={"row": lax.rem(r + d, nr)}, device_id_type=MESH)

    @pl.when(c > 0)
    def _():
        pl.semaphore_signal(barrier, inc=1, device_id=left, device_id_type=MESH)

    @pl.when(c < n - 1)
    def _():
        pl.semaphore_signal(barrier, inc=1, device_id=right, device_id_type=MESH)

    pl.semaphore_signal(barrier, inc=1, device_id={"dp": flip(g)}, device_id_type=MESH)
    full_ref[...] = jnp.zeros_like(full_ref)
    co_ref[...] = jnp.zeros_like(co_ref)
    cg_ref[...] = jnp.zeros_like(cg_ref)
    cd_ref[...] = jnp.zeros_like(cd_ref)

    @pl.when(inner)
    def _():
        pl.semaphore_wait(barrier, nr + 2)

    @pl.when(jnp.logical_not(inner))
    def _():
        pl.semaphore_wait(barrier, nr + 1)

    middle = n // 2
    for b in range(middle):
        for block in (b, middle + b):
            for d in range(1, nr):
                piece_in(d, block).start()
    load_x.start()
    load_cot.start()
    share_g.start_far()
    share_d.start_far()
    share_g.start_near()
    share_d.start_near()

    def rows(j, start=0):
        return span(start + j * m, m)

    def band_rows(b):
        return span(b * band, band), span(half + b * band, band)

    def take(ref, b):
        low_rows, high_rows = band_rows(b)
        return jnp.concatenate([ref[low_rows, :], ref[high_rows, :]], axis=0)

    def put(b, lanes, value):
        low_rows, high_rows = band_rows(b)
        part[low_rows, lanes] = value[:band].astype(low)
        part[high_rows, lanes] = value[band:].astype(low)

    around = hop * 2 * (n - 1)
    each = chunks // blocks

    def relay_stage(stage, owner_step, all_ref):
        def send(kind, j, src, dst, to):
            return remote(src, dst, sems_send.at[stage, kind, j], sems_recv.at[stage, kind, j], to)

        def reduce_right(j):
            return send(0, j, part.at[rows(j, half)], recv_right.at[rows(j)], right)

        def reduce_left(j):
            return send(1, j, part.at[rows(j)], recv_left.at[rows(j)], left)

        def spread_left(j):
            return send(2, j, all_ref.at[rows(j, half)], all_ref.at[rows(j, half)], left)

        def spread_right(j):
            return send(3, j, all_ref.at[rows(j)], all_ref.at[rows(j)], right)

        def step(i):
            def on(offset, who, run):
                j = i - offset

                @pl.when(jnp.logical_and(who, jnp.logical_and(j >= 0, j < chunks)))
                def _():
                    run(j)

            def mid_right(j):
                reduce_right(j).wait_recv()
                at = rows(j, half)
                part[at, :] = (part[at, :].astype(wide) + recv_right[rows(j), :].astype(wide)).astype(low)
                reduce_right(j).start()

            def mid_left(j):
                reduce_left(j).wait_recv()
                at = rows(j)
                part[at, :] = (part[at, :].astype(wide) + recv_left[at, :].astype(wide)).astype(low)
                reduce_left(j).start()

            def end_right(j):
                reduce_right(j).wait_recv()
                total = part[rows(j, half), :].astype(wide) + recv_right[rows(j), :].astype(wide)
                all_ref[rows(j, half), :] = owner_step(total, rows(j))
                spread_left(j).start()

            def end_left(j):
                reduce_left(j).wait_recv()
                total = part[rows(j), :].astype(wide) + recv_left[rows(j), :].astype(wide)
                all_ref[rows(j), :] = owner_step(total, rows(j))
                spread_right(j).start()

            def pass_left(j):
                spread_left(j).wait_recv()
                spread_left(j).start()

            def pass_right(j):
                spread_right(j).wait_recv()
                spread_right(j).start()

            def arrived(j):
                @pl.when(first)
                def _():
                    reduce_right(j).wait_send()
                    spread_left(j).wait_recv()

                @pl.when(last)
                def _():
                    reduce_left(j).wait_send()
                    spread_right(j).wait_recv()

                @pl.when(inner)
                def _():
                    reduce_right(j).wait_send()
                    reduce_left(j).wait_send()

            on(0, first, lambda j: reduce_right(j).start())
            on(0, last, lambda j: reduce_left(j).start())
            on(hop * c, inner, mid_right)
            on(hop * (n - 1 - c), inner, mid_left)
            on(hop * (n - 1), last, end_right)
            on(hop * (n - 1), first, end_left)
            on(hop * (2 * (n - 1) - c), inner, pass_left)
            on(hop * (n - 1 + c), inner, pass_right)
            on(around, True, arrived)

        def rest():
            @pl.loop(0, chunks)
            def _(j):
                @pl.when(first)
                def _():
                    spread_right(j).wait_send()

                @pl.when(last)
                def _():
                    spread_left(j).wait_send()

                @pl.when(inner)
                def _():
                    spread_left(j).wait_send()
                    spread_right(j).wait_send()

        return step, rest

    def slices(before, i, per, work):
        @pl.loop(before(i), before(i + 1))
        def _(t):
            work(t // per, lax.rem(t, per))

    def paced(per):
        def before(i):
            late = per + (jnp.maximum(i - per, 0) * per) // each
            return jnp.minimum(jnp.where(i < per, i, late), per * blocks)

        return before

    def shard(j, ref):
        return slice(j * (ref.shape[0] // nr), (j + 1) * (ref.shape[0] // nr))

    def out_work(b, k):
        @pl.when(b == 0)
        def _():
            loads[0].wait()

        @pl.when(lax.rem(b, blocks // middle) == 0)
        def _():
            at = b // (blocks // middle)
            for block in (at, middle + at):
                for d in range(1, nr):
                    piece_in(d, block).wait_recv()
                local_piece_in(block).wait()

        rows_in = take(attn, b)
        red = dot_t(rows_in, ao_ref[...]).astype(low)
        for j in range(nr):
            lanes = slice(j * width, (j + 1) * width)
            put(b, lanes, dot(rows_in, wo[shard(j, wo), :]) + dot(red, bo_ref[:, lanes]))

    gain_a = gain_ref[0:1, :]
    gain_f = gain_ref[1:2, :]

    def attn_owner(total, at):
        raw[at, :] = total
        flat = total * norm_factor(row_sum(total * total))
        return (x_half[at, :].astype(wide) + flat * gain_a).astype(low)

    first_pass = 4
    apart = 2
    late = 3
    passes = cuts + cuts // 2

    def pump(ii):
        at = ii - first_pass

        @pl.when(jnp.logical_and(at >= 0, lax.rem(at, apart) == 0))
        def _():
            t = at // apart

            @pl.when(t < cuts)
            def _():
                share_g.pass_far(t)

            @pl.when(jnp.logical_and(t >= cuts, t < passes))
            def _():
                share_d.pass_far(t - cuts)

            t = t - late

            @pl.when(jnp.logical_and(t >= 0, t < cuts))
            def _():
                share_g.pass_twin(t)

            @pl.when(jnp.logical_and(t >= cuts, t < passes))
            def _():
                share_d.pass_twin(t - cuts)

    load_x.wait()
    in_loop = 1 + chunks + around
    step, rest = relay_stage(0, attn_owner, h_all)
    out_pace = paced(1)

    @pl.loop(0, in_loop)
    def _(ii):
        step(ii - 1)
        slices(out_pace, ii, 1, out_work)
        pump(ii)

    rest()

    share_g.wait_all()

    def gate_slice(b, k):
        rows_in = take(h_all, b)

        @pl.when(k == 0)
        def _():
            red_gu[b] = dot_t(rows_in, ag_ref[...]).astype(low)

        at = pl.multiple_of(k * a_cut, a_cut)
        lanes = pl.ds(at, a_cut)
        up_lanes = pl.ds(pl.multiple_of(hidden + at, a_cut), a_cut)
        red = red_gu[b]
        gate = dot(rows_in, wg[:, lanes]) + dot(red[:, :RANK], bg_ref[0, :, lanes])
        up = dot(rows_in, wg[:, up_lanes]) + dot(red[:, RANK:], bg_ref[1, :, lanes])
        gu[b, :, lanes] = gate.astype(low)
        gu[b, :, up_lanes] = up.astype(low)
        hid[:, lanes] = (gate * jax.nn.sigmoid(gate) * up).astype(low)

    def down_slice(b, k):
        @pl.when(jnp.logical_and(b == 0, k == 0))
        def _():
            @pl.loop(in_loop, jnp.maximum(in_loop, first_pass + apart * (passes + late)))
            def _(ii):
                pump(ii)

            share_d.wait_all()

        rows_in = hid[:, :hidden]

        @pl.when(k == 0)
        def _():
            red_down[b] = dot_t(rows_in, ad_ref[...]).astype(low)

        for s in range(nr // 2):
            j = k * (nr // 2) + s
            lanes = span(j * width, width)
            down_rows = pl.ds(pl.multiple_of(j * hidden, hidden), hidden)
            put(b, lanes, dot(rows_in, wd[down_rows, :]) + dot(red_down[b], bd_ref[:, lanes]))

    def ffn_work(b, k):
        @pl.when(k < 4)
        def _():
            gate_slice(b, k)

        @pl.when(k >= 4)
        def _():
            down_slice(b, k - 4)

    def ffn_owner(total, at):
        a_raw = raw[at, :]
        h = x_half[at, :].astype(wide) + a_raw * norm_factor(row_sum(a_raw * a_raw)) * gain_a
        factor = norm_factor(row_sum(total * total))
        flat = total * factor
        out_half[at, :] = (h + flat * gain_f).astype(low)
        scaled = cot_half[at, :].astype(wide) * gain_f
        return (factor * (scaled - flat * (row_sum(scaled * flat) * (1.0 / D)))).astype(low)

    b_cut = hidden // 2

    def hidden_back(b, k):
        rows_in = take(df_all, b)

        @pl.when(k == 0)
        def _():
            back_down[...] = dot_t(rows_in, bd_ref[...]).astype(low)

        at = pl.multiple_of(k * b_cut, b_cut)
        lanes = pl.ds(at, b_cut)
        up_lanes = pl.ds(pl.multiple_of(hidden + at, b_cut), b_cut)
        back = back_down[...]
        grad = dot(back, ad_ref[:, lanes])
        for j in range(nr):
            down_rows = pl.ds(pl.multiple_of(j * hidden + at, b_cut), b_cut)
            grad = grad + dot_t(rows_in[:, j * width:(j + 1) * width], wd[down_rows, :])
        gate = gu[b, :, lanes].astype(wide)
        up = gu[b, :, up_lanes].astype(wide)
        sigma = jax.nn.sigmoid(gate)
        silu = gate * sigma
        d_gate = (grad * up * sigma * (1.0 + gate * (1.0 - sigma))).astype(low)
        d_up = (grad * silu).astype(low)
        hid[:, lanes] = d_gate
        hid[:, up_lanes] = d_up
        cd_ref[:, lanes] += t_dot(back, (silu * up).astype(low))
        red = red_gu[b]
        cg_ref[0, :, lanes] += t_dot(red[:, :RANK], d_gate)
        cg_ref[1, :, lanes] += t_dot(red[:, RANK:], d_up)

    o_cut = width_all // 4

    def gate_back(b, k):
        @pl.when(k == 0)
        def _():
            back_gu[:, :RANK] = dot_t(hid[:, :hidden], bg_ref[0]).astype(low)
            back_gu[:, RANK:] = dot_t(hid[:, hidden:], bg_ref[1]).astype(low)

        lanes = span(k * o_cut, o_cut)
        put(b, lanes, dot_t(hid[...], wg[lanes, :]) + dot(back_gu[...], ag_ref[:, lanes]))

        @pl.when(k == 3)
        def _():
            full_ref[:2 * RANK, :] += t_dot(back_gu[...], take(h_all, b))
            full_ref[3 * RANK:, :] += t_dot(red_down[b], take(df_all, b))

    def back_work(b, k):
        @pl.when(k < 2)
        def _():
            hidden_back(b, k)

        @pl.when(k >= 2)
        def _():
            gate_back(b, k - 2)

    def back_owner(total, at):
        grad = cot_half[at, :].astype(wide) + total
        grad_half[at, :] = grad
        a_raw = raw[at, :]
        factor = norm_factor(row_sum(a_raw * a_raw))
        flat = a_raw * factor
        scaled = grad * gain_a
        return (factor * (scaled - flat * (row_sum(scaled * flat) * (1.0 / D)))).astype(low)

    def out_back(b, k):
        rows_in = take(da_all, b)
        back = dot_t(rows_in, bo_ref[...]).astype(low)
        grad = dot(back, ao_ref[...])
        for j in range(nr):
            grad = grad + dot_t(rows_in[:, j * width:(j + 1) * width], wo[shard(j, wo), :])
        for side in range(2):
            d_attn[out_rows(b, side)[0], :] = grad[side * band:(side + 1) * band].astype(low)
            for d in range(1, nr):
                piece_out(d, b, side).start()
            local_piece_out(b, side).start()
        attn_rows = take(attn, b)
        co_ref[...] += t_dot(back, attn_rows)
        red = dot_t(attn_rows, ao_ref[...]).astype(low)
        full_ref[2 * RANK:3 * RANK, :] += t_dot(red, rows_in)

    begin = around + each

    def back_before(i):
        return jnp.clip(i - begin, 0, 6 * blocks)

    def out_before(i):
        return jnp.clip((i - around - 1) // each, 0, blocks)

    load_cot.wait()
    step_f, rest_f = relay_stage(1, ffn_owner, df_all)
    step_b, rest_b = relay_stage(2, back_owner, da_all)
    ffn_pace = paced(6)
    period = 26

    @pl.loop(0, 6 + period + chunks + around + 1)
    def _(ii):
        i = ii - 6
        step_f(i)
        step_b(i - period)
        slices(ffn_pace, ii, 6, ffn_work)
        slices(back_before, i, 6, back_work)
        slices(out_before, i - period, 1, out_back)

    pl.when(is_owner)(store_out.start)
    rest_f()
    rest_b()
    pl.when(is_owner)(store_grad.start)

    @pl.loop(0, n)
    def _(b):
        for d in range(1, nr):
            piece_in(d, b).wait_send()

    @pl.loop(0, blocks)
    def _(b):
        for side in range(2):
            for d in range(1, nr):
                piece_out(d, b, side).wait()
            local_piece_out(b, side).wait()

    share_g.drain()
    share_d.drain()

    @pl.when(is_owner)
    def _():
        store_out.wait()
        store_grad.wait()


def middle(attn_head, x, cot_half, gains, w_out, w_gu, w_down, table, a_out, b_gu, a_down, n, nr, m=16, hop=2, cuts=8):
    group, width_all = x.shape
    half = group // 2
    width = width_all // nr
    hidden = a_down.shape[1]
    chunks = half // m
    band = group // 4
    dma = pltpu.SemaphoreType.DMA
    any_space = pl.BlockSpec(memory_space=pl.ANY)
    shape = jax.ShapeDtypeStruct
    return pl.pallas_call(
        functools.partial(middle_kernel, n, nr, m, hop, cuts),
        out_shape=[
            shape(attn_head.shape, low),
            shape((half, width_all), low),
            shape((half, width_all), wide),
            shape((4 * RANK, width_all), wide),
            shape((RANK, a_out.shape[1]), wide),
            shape((2, RANK, hidden), wide),
            shape((RANK, hidden), wide),
        ],
        in_specs=[any_space, any_space, any_space, VM, any_space, any_space, any_space] + [VM] * 4,
        out_specs=[any_space] * 3 + [VM] * 4,
        scratch_shapes=[
            pltpu.VMEM((half, width_all), low),
            pltpu.VMEM((half, width_all), wide),
            pltpu.VMEM(w_out.shape, low),
            pltpu.VMEM((w_gu.shape[0] * nr, w_gu.shape[1]), low),
            pltpu.VMEM((w_down.shape[0] * nr, w_down.shape[1]), low),
            pltpu.VMEM((half, width_all), low),
            pltpu.VMEM((half, width_all), low),
            pltpu.VMEM((half, width_all), wide),
            pltpu.VMEM((group, a_out.shape[1]), low),
            pltpu.VMEM((group, a_out.shape[1]), low),
            pltpu.VMEM((group, width_all), low),
            pltpu.VMEM((group, width_all), low),
            pltpu.VMEM((group, width_all), low),
            pltpu.VMEM((4, band, 2 * hidden), low),
            pltpu.VMEM((group, width_all), low),
            pltpu.VMEM((half, width_all), low),
            pltpu.VMEM((half, width_all), low),
            pltpu.VMEM((band, 2 * hidden), low),
            pltpu.VMEM((4, band, 2 * RANK), low),
            pltpu.VMEM((4, band, RANK), low),
            pltpu.VMEM((band, 2 * RANK), low),
            pltpu.VMEM((band, RANK), low),
            dma((3, 4, chunks)), dma((3, 4, chunks)),
            dma((nr - 1, n)), dma((nr - 1, n)), dma((2 * (nr - 1), 4)), dma((2 * (nr - 1), 4)), dma((n,)), dma((2, 4)),
            dma((5,)),
        ] + share_sems(cuts) + share_sems(cuts // 2),
        compiler_params=pltpu.CompilerParams(collective_id=0, has_side_effects=True, vmem_limit_bytes=67043328),
        name="middle",
    )(attn_head, x, cot_half, gains, w_out, w_gu, w_down, table, a_out, b_gu, a_down)


def per_device(
    tokens,
    cotangent,
    seg_ids,
    positions,
    parents,
    tree_sets,
    gain_q,
    gain_k,
    gain_attn,
    gain_ffn,
    query_key_value_weight,
    output_weight,
    gate_up_weight,
    down_weight,
    query_key_value_adapter_first,
    query_key_value_adapter_second,
    output_adapter_first,
    output_adapter_second,
    gate_up_adapter_first,
    gate_up_adapter_second,
    down_adapter_first,
    down_adapter_second,
):
    dp_count = lax.axis_size("dp")
    row_count = lax.axis_size("row")
    col_count = lax.axis_size("col")
    row_at = lax.axis_index("row")
    tree_tokens = seg_ids.shape[0]
    assert tree_sets.shape[0] == 1 and col_count == 4
    set_count = output_adapter_first.shape[0]
    own = tokens.shape[0] // row_count
    group = own * col_count
    width_row = tokens.shape[1]
    width_col = gain_q.shape[0]
    hidden_col = down_weight.shape[0]
    tree_set = tree_sets[0]

    tables = (
        query_key_value_adapter_first,
        query_key_value_adapter_second,
        output_adapter_first,
        output_adapter_second,
        gate_up_adapter_first,
        gate_up_adapter_second,
        down_adapter_first,
        down_adapter_second,
    )
    narrow, b_qkv, a_out, b_gu, a_down = prep(tree_sets, tables)
    gain_pair = jnp.pad(jnp.stack([gain_attn, gain_ffn]), ((0, 6), (0, 0)))
    pos_own = lax.dynamic_index_in_dim(
        positions.reshape(col_count, row_count, own), row_at, 1, keepdims=False
    ).reshape(group)
    cos2, sin2 = angles(pos_own)
    gq, gk = gain_q[None, :], gain_k[None, :]
    parent_at, branch_flag = tree_tables(seg_ids, parents)
    x, table, gains, g_half, raw, factors, qkv_head, w_qkv, w_out, w_gu = front(
        tokens,
        narrow,
        gain_pair,
        cotangent,
        query_key_value_weight.reshape(width_row, 3 * width_col),
        output_weight,
        gate_up_weight,
        b_qkv,
        gq,
        gk,
        cos2,
        sin2,
        col_count,
        row_count,
    )
    attn_head, lse = attend(qkv_head, parent_at, branch_flag)
    d_attn_head, out_half, d_h_half, full_mid, part_ao, part_bgu, part_ad = middle(
        attn_head,
        x,
        g_half,
        gains,
        w_out,
        w_gu,
        down_weight,
        table,
        a_out,
        b_gu,
        a_down,
        col_count,
        row_count,
    )
    d_qkv_head = attend_back(qkv_head, d_attn_head, parent_at, branch_flag, lse)
    hot = (tree_set == lax.broadcasted_iota(jnp.int32, (set_count, width_row), 0)).astype(wide)
    in_grad, layer, sets = rear(
        d_qkv_head,
        raw,
        factors,
        gq,
        gk,
        cos2,
        sin2,
        out_half,
        x,
        w_qkv,
        table,
        b_qkv,
        d_h_half,
        full_mid,
        part_ao,
        part_bgu,
        part_ad,
        hot,
        set_count // dp_count,
        col_count,
        row_count,
        dp_count,
    )
    return tuple(unpack(in_grad, layer, sets, RANK // col_count, RANK // row_count, hidden_col))


def solution(mesh):
    in_specs = (
        P(("dp", "col"), "row"),
        P(("dp", "col"), "row"),
        P("dp"),
        P("dp"),
        P("dp", None),
        P("dp"),
        P("col"),
        P("col"),
        P("row"),
        P("row"),
        P("row", None, "col"),
        P("col", "row"),
        P("row", None, "col"),
        P("col", "row"),
        P(None, None, None, "row"),
        P(None, None, None, "col"),
        P(None, None, "col"),
        P(None, None, "row"),
        P(None, None, None, "row"),
        P(None, None, None, "col"),
        P(None, None, "col"),
        P(None, None, "row"),
    )
    out_specs = (
        P(("dp", "col"), "row"),
        P(("dp", "col"), "row"),
        P(None, "dp", "col", "row"),
        P(None, "dp", "row", "col"),
        P("dp", "row", "col"),
        P("dp", "col", "row"),
        P(None, "dp", "col", "row"),
        P(None, "dp", "row", "col"),
        P("dp", "row", "col"),
        P("dp", "col", "row"),
    )
    return jax.shard_map(
        per_device, mesh=mesh, in_specs=in_specs, out_specs=out_specs, check_vma=False
    )
```

```python
import functools

import jax
import jax.numpy as jnp
from jax import lax
from jax.experimental import pallas as pl
from jax.experimental.pallas import tpu as pltpu
from jax.sharding import PartitionSpec as P

D = 2048
HEAD = 128
RANK = 16
SEG = 128
TRUNK = 1024
QT = 256
MESH = pl.DeviceIdType.MESH
VM = pl.BlockSpec(memory_space=pltpu.VMEM)
precise = lax.Precision.HIGHEST

epsilon = 1e-06
rope_base = 500000.0
masked_out = -1e30
low = jnp.bfloat16
wide = jnp.float32
last_last = (((1,), (1,)), ((), ()))
first_first = (((0,), (0,)), ((), ()))


def dot(left, right):
    return jnp.dot(left, right, preferred_element_type=wide)


def dot_t(left, right):
    return lax.dot_general(left, right, last_last, preferred_element_type=wide)


def t_dot(left, right):
    return lax.dot_general(left, right, first_first, preferred_element_type=wide)


def angles(positions):
    lane = jnp.arange(HEAD, dtype=jnp.int32)
    frequency = rope_base ** (-((lane % (HEAD // 2)).astype(wide) * 2.0) / HEAD)
    angle_table = positions.astype(wide)[:, None] * frequency[None, :]
    return (jnp.cos(angle_table), jnp.where(lane < HEAD // 2, -1.0, 1.0) * jnp.sin(angle_table))


def norm_factor(square_sum):
    return lax.rsqrt(square_sum * (1.0 / D) + epsilon)


def row_sum(v): return jnp.sum(v, axis=1, keepdims=True)

def params(collective):
    return pltpu.CompilerParams(collective_id=collective, has_side_effects=True, vmem_limit_bytes=60 << 20)


def span(at, size):
    return pl.ds(pl.multiple_of(at, size), size)


def remote(src, dst, send_sem, recv_sem, to):
    return pltpu.make_async_remote_copy(
        src_ref=src, dst_ref=dst, send_sem=send_sem, recv_sem=recv_sem, device_id=to, device_id_type=MESH
    )


def greet(n, nr, extra=0):
    r, c = lax.axis_index("row"), lax.axis_index("col")
    me = r * n + c
    barrier = pltpu.get_barrier_semaphore()

    @pl.loop(1, n * nr)
    def _(d):
        peer = lax.rem(me + d, n * nr)
        pl.semaphore_signal(barrier, inc=1, device_id={"row": peer // n, "col": lax.rem(peer, n)}, device_id_type=MESH)

    pl.semaphore_wait(barrier, n * nr - 1 + extra)


def row_sums(first, second):
    ones = jnp.ones((8, first.shape[1]), wide)
    at = lax.broadcasted_iota(jnp.int32, (8, first.shape[0]), 0)
    sum_first = lax.dot_general(ones, first, last_last, preferred_element_type=wide, precision=precise)
    sum_second = lax.dot_general(ones, second, last_last, preferred_element_type=wide, precision=precise)
    return jnp.where(at < 4, sum_first, sum_second)


def down_columns(values, at):
    pick = (lax.broadcasted_iota(jnp.int32, (8, HEAD), 0) == at).astype(wide)
    return lax.dot_general(values, pick, first_first, preferred_element_type=wide, precision=precise)


def flip(v):
    return v + 1 - 2 * lax.rem(v, 2)


class Share:
    def __init__(self, src, dst, cuts, sems):
        self.send, self.recv, self.local = sems
        self.src, self.cuts = src, cuts
        g, r = lax.axis_index("dp"), lax.axis_index("row")
        size = src.shape[0]
        half = size // 2
        step = half // cuts
        far = lax.rem(r + 2, 4)
        mine = lax.rem(g, 2)
        near_to, far_to, twin_to = {"row": flip(r)}, {"row": far}, {"dp": flip(g)}

        def rows(shard, part, i):
            return pl.ds(pl.multiple_of(shard * size + part * half + i * step, step), step)

        def copy(kind, i, src, dst, to):
            return remote(src, dst, self.send.at[kind, i], self.recv.at[kind, i], to)

        def hand(kind, part, to):
            return lambda i: copy(kind, i, dst.at[rows(far, part, i)], dst.at[rows(far, part, i)], to)

        whole = span(r * size, size)
        self.own = pltpu.make_async_copy(src, dst.at[whole], self.local)
        self.near = copy(0, 0, src, dst.at[whole], near_to)
        self.far = lambda i: copy(
            1, i, src.at[pl.ds(pl.multiple_of(mine * half + i * step, step), step)], dst.at[rows(r, mine, i)], far_to
        )
        self.far_near = hand(2, mine, near_to)
        self.far_twin = hand(3, mine, twin_to)
        self.twin_near = hand(4, 1 - mine, near_to)

    def start_far(self):
        for i in range(self.cuts):
            self.far(i).start()

    def start_near(self):
        self.own.start()
        self.near.start()

    def pass_far(self, i):
        self.far(i).wait_recv()
        self.far_twin(i).start()
        self.far_near(i).start()

    def pass_twin(self, i):
        self.far_twin(i).wait_recv()
        self.twin_near(i).start()

    def wait_all(self):
        self.own.wait()
        self.near.wait_recv()
        for i in range(self.cuts):
            self.far_near(i).wait_recv()
            self.twin_near(i).wait_recv()

    def drain(self):
        self.near.wait_send()
        for i in range(self.cuts):
            self.far(i).wait_send()
            self.far_near(i).wait_send()
            self.far_twin(i).wait_send()
            self.twin_near(i).wait_send()


def share_sems(cuts):
    dma = pltpu.SemaphoreType.DMA
    return [dma((5, cuts)), dma((5, cuts)), dma]


def prep_kernel(set_ref, seg_ref, parents_ref, ga_ref, gf_ref, fq_ref, sq_ref, fo_ref, so_ref, fg_ref, sg_ref, fd_ref, sd_ref,
                narrow_ref, bq_ref, ao_ref, bg_ref, ad_ref, gain_ref, hot_ref, flag_ref, at_ref):
    for j in range(3):
        narrow_ref[j * RANK:(j + 1) * RANK, :] = fq_ref[j, 0].astype(low)
        bq_ref[j * RANK:(j + 1) * RANK, :] = sq_ref[j, 0].astype(low)
    for j in range(2):
        narrow_ref[(3 + j) * RANK:(4 + j) * RANK, :] = fg_ref[j, 0].astype(low)
        bg_ref[j] = sg_ref[j, 0].astype(low)
    narrow_ref[5 * RANK:6 * RANK, :] = so_ref[0].astype(low)
    narrow_ref[6 * RANK:, :] = sd_ref[0].astype(low)
    ao_ref[...] = fo_ref[0].astype(low)
    ad_ref[...] = fd_ref[0].astype(low)
    gain_ref[...] = jnp.zeros_like(gain_ref)
    gain_ref[0:1, :] = ga_ref[...]
    gain_ref[1:2, :] = gf_ref[...]
    hot_ref[...] = (lax.broadcasted_iota(jnp.int32, hot_ref.shape, 0) == set_ref[0]).astype(wide)
    tails = flag_ref.shape[0]
    segments = [seg_ref[TRUNK + j * SEG] for j in range(tails)]
    for j in range(tails):
        parent = parents_ref[0, segments[j]]
        at = jnp.int32(0)
        for k in range(tails):
            at = jnp.where(segments[k] == parent, k + TRUNK // SEG, at)
        at_ref[j] = at
        flag_ref[j:j + 1, :] = jnp.full((1, SEG), jnp.where(parent > 0, 0.0, masked_out), wide)


def prep(tree_sets, seg_ids, parents, gain_a, gain_f, tables):
    fq, sq, fo, so, fg, sg, fd, sd = tables

    def pick(table):
        if table.ndim == 4:
            return pl.BlockSpec((table.shape[0], 1) + table.shape[2:], lambda i, s, *_: (0, s[0], 0, 0))
        return pl.BlockSpec((1,) + table.shape[1:], lambda i, s, *_: (s[0], 0, 0))

    def out(*shape, kind=low):
        return pl.BlockSpec(shape, lambda i, *_: (0,) * len(shape)), jax.ShapeDtypeStruct(shape, kind)

    tails = (seg_ids.shape[0] - TRUNK) // SEG
    width = gain_a.shape[1]
    gain_spec = pl.BlockSpec((1, width), lambda i, *_: (0, 0))

    outs = [
        out(7 * RANK, fq.shape[-1]), out(3 * RANK, sq.shape[-1]), out(RANK, fo.shape[-1]),
        out(2, RANK, sg.shape[-1]), out(RANK, fd.shape[-1]),
        out(8, width, kind=wide), out(fo.shape[0], width, kind=wide), out(tails, SEG, kind=wide),
        (pl.BlockSpec(memory_space=pltpu.SMEM), jax.ShapeDtypeStruct((tails,), jnp.int32)),
    ]
    return pl.pallas_call(
        prep_kernel,
        grid_spec=pltpu.PrefetchScalarGridSpec(
            num_scalar_prefetch=3,
            grid=(1,),
            in_specs=[gain_spec, gain_spec] + [pick(t) for t in tables],
            out_specs=[o[0] for o in outs],
        ),
        out_shape=[o[1] for o in outs],
        name="prep",
    )(tree_sets, seg_ids, parents, gain_a, gain_f, *tables)


def lower_mask(size):
    return lax.broadcasted_iota(jnp.int32, (size, size), 1) <= lax.broadcasted_iota(jnp.int32, (size, size), 0)


def softmax_parts(parts):
    top = jnp.max(parts[0], axis=1, keepdims=True)
    for s in parts[1:]:
        top = jnp.maximum(top, jnp.max(s, axis=1, keepdims=True))
    raised = [jnp.exp(s - top) for s in parts]
    total = jnp.sum(raised[0], axis=1, keepdims=True)
    for e in raised[1:]:
        total = total + jnp.sum(e, axis=1, keepdims=True)
    inverse = 1.0 / total
    return raised, inverse, top + jnp.log(total)


def tail_spans(parent_ref, pair):
    at = [pl.multiple_of(TRUNK + (2 * pair + side) * SEG, SEG) for side in range(2)]
    parent = [pl.multiple_of(parent_ref[2 * pair + side] * SEG, SEG) for side in range(2)]
    return pl.ds(at[0], 2 * SEG), [pl.ds(v, SEG) for v in at], [pl.ds(v, SEG) for v in parent]


def by_side(product, left, rights):
    return jnp.concatenate([product(left[i * SEG:(i + 1) * SEG], right) for i, right in enumerate(rights)], axis=0)


def tail_parts(q, qkv, own, parents, flags):
    scale = HEAD ** -0.5
    k_lanes = slice(HEAD, 2 * HEAD)
    trunk = dot_t(q, qkv[:TRUNK, k_lanes]) * scale
    branch = by_side(dot_t, q, [qkv[rows, k_lanes] for rows in parents]) * scale
    branch = branch + jnp.concatenate([jnp.broadcast_to(flag, (SEG, SEG)) for flag in flags], axis=0)
    mask = jnp.concatenate([lower_mask(SEG)] * 2, axis=0)
    own = jnp.where(mask, by_side(dot_t, q, [qkv[rows, k_lanes] for rows in own]) * scale, masked_out)
    return [trunk, branch, own]


def trunk_parts(q, qkv, i):
    scale = HEAD ** -0.5
    k_lanes = slice(HEAD, 2 * HEAD)
    own = dot_t(q, qkv[i * QT:(i + 1) * QT, k_lanes]) * scale
    parts = [jnp.where(lower_mask(QT), own, masked_out)]
    if i:
        parts.append(dot_t(q, qkv[:i * QT, k_lanes]) * scale)
    return parts


def attend_body(parent_ref, flag_ref, qkv, o_ref, lse_ref):
    v_lanes = slice(2 * HEAD, 3 * HEAD)
    for i in range(TRUNK // QT):
        at = slice(i * QT, (i + 1) * QT)
        p, inverse, lse = softmax_parts(trunk_parts(qkv[at, :HEAD], qkv, i))
        o = dot(p[0].astype(low), qkv[at, v_lanes])
        if i:
            o = o + dot(p[1].astype(low), qkv[:i * QT, v_lanes])
        o_ref[at, :] = (o * inverse).astype(low)
        lse_ref[at, :] = lse

    @pl.loop(0, (qkv.shape[0] - TRUNK) // (2 * SEG), unroll=3)
    def _(j):
        rows, own, parents = tail_spans(parent_ref, j)
        flags = [flag_ref[pl.ds(2 * j + side, 1), :] for side in range(2)]
        p, inverse, lse = softmax_parts(tail_parts(qkv[rows, :HEAD], qkv, own, parents, flags))
        o = dot(p[0].astype(low), qkv[:TRUNK, v_lanes])
        o = o + by_side(dot, p[1].astype(low), [qkv[at, v_lanes] for at in parents])
        o = o + by_side(dot, p[2].astype(low), [qkv[at, v_lanes] for at in own])
        o_ref[rows, :] = (o * inverse).astype(low)
        lse_ref[rows, :] = lse


def back_parts(scores, lse, d_out, keys, values):
    probs = [jnp.exp(s - lse) for s in scores]
    grads = [dot_t(d_out, v) for v in values]
    inner = sum(jnp.sum(p * g, axis=1, keepdims=True) for p, g in zip(probs, grads))
    d_scores = [(p * (g - inner)).astype(low) for p, g in zip(probs, grads)]
    dq = sum(dot(d, k) for d, k in zip(d_scores, keys))
    return d_scores, [p.astype(low) for p in probs], dq


def attend_back_kernel(parent_ref, flag_ref, qkv, do_ref, lse_ref, d_ref, dk_acc, dv_acc):
    scale = HEAD ** -0.5
    k_lanes = slice(HEAD, 2 * HEAD)
    v_lanes = slice(2 * HEAD, 3 * HEAD)
    dk_acc[...] = jnp.zeros_like(dk_acc)
    dv_acc[...] = jnp.zeros_like(dv_acc)
    for i in range(TRUNK // QT):
        at = slice(i * QT, (i + 1) * QT)
        spans = [at] + ([slice(0, i * QT)] if i else [])
        q, d_out = qkv[at, :HEAD], do_ref[at, :]
        d_scores, probs, dq = back_parts(
            trunk_parts(q, qkv, i), lse_ref[at, :], d_out, [qkv[s, k_lanes] for s in spans], [qkv[s, v_lanes] for s in spans]
        )
        d_ref[at, :HEAD] = (dq * scale).astype(low)
        for s, d, p in zip(spans, d_scores, probs):
            dk_acc[s, :] += t_dot(d, q)
            dv_acc[s, :] += t_dot(p, d_out)

    @pl.loop(0, (qkv.shape[0] - TRUNK) // (2 * SEG), unroll=2)
    def _(j):
        rows, own, parents = tail_spans(parent_ref, j)
        flags = [flag_ref[pl.ds(2 * j + side, 1), :] for side in range(2)]
        q, d_out, lse = qkv[rows, :HEAD], do_ref[rows, :], lse_ref[rows, :]
        probs = [jnp.exp(s - lse) for s in tail_parts(q, qkv, own, parents, flags)]
        grads = [
            dot_t(d_out, qkv[:TRUNK, v_lanes]),
            by_side(dot_t, d_out, [qkv[at, v_lanes] for at in parents]),
            by_side(dot_t, d_out, [qkv[at, v_lanes] for at in own]),
        ]
        inner = sum(jnp.sum(p * g, axis=1, keepdims=True) for p, g in zip(probs, grads))
        d_scores = [(p * (g - inner)).astype(low) for p, g in zip(probs, grads)]
        probs = [p.astype(low) for p in probs]
        dq = dot(d_scores[0], qkv[:TRUNK, k_lanes])
        dq = dq + by_side(dot, d_scores[1], [qkv[at, k_lanes] for at in parents])
        dq = dq + by_side(dot, d_scores[2], [qkv[at, k_lanes] for at in own])
        d_ref[rows, :HEAD] = (dq * scale).astype(low)
        dk_acc[:TRUNK, :] += t_dot(d_scores[0], q)
        dv_acc[:TRUNK, :] += t_dot(probs[0], d_out)
        for part, spans in ((1, parents), (2, own)):
            for side, at in enumerate(spans):
                half = slice(side * SEG, (side + 1) * SEG)
                dk_acc[at, :] += t_dot(d_scores[part][half], q[half])
                dv_acc[at, :] += t_dot(probs[part][half], d_out[half])

    d_ref[:, k_lanes] = (dk_acc[...] * scale).astype(low)
    d_ref[:, v_lanes] = dv_acc[...].astype(low)


def attend(qkv, parent_at, flag):
    n = qkv.shape[0]

    def whole(*shape):
        return pl.BlockSpec(shape, lambda i, *_: (0, 0))

    return pl.pallas_call(
        attend_body,
        grid_spec=pltpu.PrefetchScalarGridSpec(
            num_scalar_prefetch=1,
            grid=(1,),
            in_specs=[whole(*flag.shape), whole(n, 3 * HEAD)],
            out_specs=[whole(n, HEAD), whole(n, 1)],
        ),
        out_shape=[jax.ShapeDtypeStruct((n, HEAD), low), jax.ShapeDtypeStruct((n, 1), wide)],
        name="attend",
    )(parent_at, flag, qkv)


def attend_back(qkv, d_o, parent_at, flag, lse):
    n = qkv.shape[0]

    def whole(*shape):
        return pl.BlockSpec(shape, lambda i, *_: (0, 0))

    return pl.pallas_call(
        attend_back_kernel,
        grid_spec=pltpu.PrefetchScalarGridSpec(
            num_scalar_prefetch=1,
            grid=(1,),
            in_specs=[whole(*flag.shape), whole(n, 3 * HEAD), whole(n, HEAD), whole(n, 1)],
            out_specs=whole(n, 3 * HEAD),
            scratch_shapes=[pltpu.VMEM((n, HEAD), wide), pltpu.VMEM((n, HEAD), wide)],
        ),
        out_shape=jax.ShapeDtypeStruct((n, 3 * HEAD), low),
        name="attend_back",
    )(parent_at, flag, qkv, d_o, lse)


def front_kernel(n, nr, m, mh, tok_ref, table_ref, gain_ref, cot_ref, wq_hbm, wo_hbm, gu_hbm, bq_ref, gq_ref, gk_ref,
                 cos_ref, sin_ref,
                 x_out, table_all, gain_all, half_ref, raw_out, factor_ref, qkv_ref, wq_out, wo_out, gu_out,
                 x_ref, raw_ref, gu_pair, gu_flat, wq, wo, stats, buf, fq, fk, red, cot_own,
                 send_a, recv_a, send_z, recv_z, send_t, recv_t, local_sem,
                 send_s, recv_s, send_h, recv_h, send_g, recv_g, local_h, local_g, send_e, recv_e,
                 send_q, recv_q, local_q, send_o, recv_o, local_o, out_sems):
    g, r, c = lax.axis_index("dp"), lax.axis_index("row"), lax.axis_index("col")
    own = tok_ref.shape[0] // nr
    width = tok_ref.shape[1]
    rows_all = own * n
    heads = width // HEAD
    tree_part = own * nr
    chunks = own // m
    left = {"col": jnp.maximum(c - 1, 0)}
    right = {"col": jnp.minimum(c + 1, n - 1)}
    share_q = Share(wq_hbm, wq, 2, (send_q, recv_q, local_q))
    share_o = Share(wo_hbm, wo, 2, (send_o, recv_o, local_o))

    def piece(d, j):
        peer = lax.rem(r + d, nr)
        return remote(
            tok_ref.at[span(peer * own + j * m, m)],
            x_ref.at[span(c * own + j * m, m), span(r * width, width)],
            send_a.at[d - 1, j], recv_a.at[d - 1, j], {"row": peer},
        )

    def block(kind, s, at, j, to):
        rows = span(at * own + j * m, m)
        return remote(x_ref.at[rows], x_ref.at[rows], send_z.at[kind, s, j], recv_z.at[kind, s, j], to)

    def table_piece(d, kind):
        src, dst = ((table_ref, table_all), (gain_ref, gain_all))[kind]
        to = {"row": lax.rem(r + d, nr)}
        return remote(src, dst.at[:, span(r * width, width)], send_t.at[kind, d - 1], recv_t.at[kind, d - 1], to)

    keep = pltpu.make_async_copy(
        tok_ref.at[span(r * own, own)], x_ref.at[span(c * own, own), span(r * width, width)], local_sem.at[0]
    )
    keep_table = pltpu.make_async_copy(table_ref, table_all.at[:, span(r * width, width)], local_sem.at[1])
    keep_gain = pltpu.make_async_copy(gain_ref, gain_all.at[:, span(r * width, width)], local_sem.at[2])
    keep.start()
    keep_table.start()
    keep_gain.start()
    barrier = pltpu.get_barrier_semaphore()
    pl.semaphore_signal(barrier, inc=1, device_id={"dp": flip(g)}, device_id_type=MESH)
    greet(n, nr, 1)

    @pl.loop(0, chunks)
    def _(j):
        for d in range(1, nr):
            piece(d, j).start()


    load_gu = pltpu.make_async_copy(gu_hbm, gu_pair, out_sems.at[4])
    copy_gu = pltpu.make_async_copy(gu_flat, gu_out, out_sems.at[5])
    gu_step = gu_flat.shape[0] // 8

    def flatten(i):
        @pl.when(i == 0)
        def _():
            load_gu.wait()

        rows = span(i * gu_step, gu_step)
        gu_flat[rows, :] = gu_pair[rows].reshape(gu_step, gu_flat.shape[1])

    middle_at = n // 2
    owner = jnp.where(c < middle_at, 0, n - 1)
    at_owner = jnp.where(c < middle_at, c, c - middle_at)
    is_owner = owner == c

    def cot_piece(d):
        peer = lax.rem(r + d, nr)
        return remote(
            cot_ref.at[span(peer * own, own)], cot_own.at[:, span(r * width, width)], send_g.at[d - 1], recv_g.at[d - 1], {"row": peer}
        )

    cot_local = pltpu.make_async_copy(cot_ref.at[span(r * own, own)], cot_own.at[:, span(r * width, width)], local_g.at[0])
    cot_keep = pltpu.make_async_copy(cot_own, half_ref.at[span(at_owner * own, own)], local_g.at[1])

    def cot_move(b):
        return remote(cot_own, half_ref.at[span(b * own, own)], send_e, recv_e.at[b], {"col": owner})

    share_q.start_far()
    share_q.start_near()
    for d in range(1, nr):
        table_piece(d, 0).start()
        table_piece(d, 1).start()
    share_o.start_far()
    share_o.start_near()
    cot_local.start()
    for d in range(1, nr):
        cot_piece(d).start()
    load_gu.start()
    keep.wait()

    def head_rows(i):
        block_at = i // (own // mh)
        inside = lax.rem(i, own // mh)
        return span(block_at * tree_part + r * own + inside * mh, mh)

    def head_piece(d, i):
        peer = lax.rem(r + d, nr)
        return remote(
            buf.at[peer, span(i * mh, mh)], qkv_ref.at[head_rows(i)], send_h.at[d - 1, i], recv_h.at[d - 1, i], {"row": peer}
        )

    def head_local(i):
        return pltpu.make_async_copy(buf.at[r, span(i * mh, mh)], qkv_ref.at[head_rows(i)], local_h.at[i])

    def stat_copy(b, d):
        peer = lax.rem(c + d, n)
        return remote(stats.at[c, b], stats.at[c, b], send_s.at[b, d - 1], recv_s.at[b, d - 1], {"col": peer})

    def product_block(b):
        rows = span(b * own, own)
        x_rows = x_ref[rows, :]
        red[...] = dot_t(x_rows, table_all[:3 * RANK, :]).astype(low)
        for j in range(3):
            lanes = slice(j * width, (j + 1) * width)
            raw_ref[rows, lanes] = dot(x_rows, wq[:, lanes]) + dot(
                red[:, j * RANK:(j + 1) * RANK], bq_ref[j * RANK:(j + 1) * RANK, :]
            )
        q_rows = raw_ref[rows, :width]
        k_rows = raw_ref[rows, width:2 * width]
        stats[c, b] = row_sums(q_rows * q_rows, k_rows * k_rows)
        for d in range(1, n):
            stat_copy(b, d).start()

    per = own // mh

    def head_block(b):
        for d in range(1, n):
            stat_copy(b, d).wait()
        total = stats[0, b]
        for s in range(1, n):
            total = total + stats[s, b]
        factor = lax.rsqrt(total * (1.0 / D) + epsilon)
        factor_ref[b] = factor
        fq[...] = down_columns(factor, 0)
        fk[...] = down_columns(factor, 4)

        @pl.loop(0, per)
        def _(i):
            rows = span(b * own + i * mh, mh)
            inside = span(i * mh, mh)
            cosine = cos_ref[rows, :]
            sine = sin_ref[rows, :]
            for h in range(heads):
                lanes = slice(h * HEAD, (h + 1) * HEAD)
                u = raw_ref[rows, lanes] * fq[inside, :] * gq_ref[:, lanes]
                buf[h, rows, :HEAD] = (u * cosine + pltpu.roll(u, HEAD // 2, 1) * sine).astype(low)
                k_lanes = slice(width + h * HEAD, width + (h + 1) * HEAD)
                u = raw_ref[rows, k_lanes] * fk[inside, :] * gk_ref[:, lanes]
                buf[h, rows, HEAD:2 * HEAD] = (u * cosine + pltpu.roll(u, HEAD // 2, 1) * sine).astype(low)
                v_lanes = slice(2 * width + h * HEAD, 2 * width + (h + 1) * HEAD)
                buf[h, rows, 2 * HEAD:] = raw_ref[rows, v_lanes].astype(low)
            for d in range(1, nr):
                head_piece(d, b * per + i).start()
            head_local(b * per + i).start()

    def both_phases(last_step):
        for d in range(1, nr):
            table_piece(d, 0).wait_recv()
            table_piece(d, 1).wait_recv()
        keep_table.wait()
        keep_gain.wait()
        share_q.wait_all()
        copy_wq.start()

        @pl.loop(0, 2)
        def _(phase):
            def at(i):
                return jnp.where(phase == 0, 1 + i, i * (n - 1))

            pl.when(phase == 1)(last_step)

            @pl.loop(0, 2)
            def _(i):
                product_block(at(i))

            @pl.when(phase == 0)
            def _():
                @pl.when(jnp.logical_not(is_owner))
                def _():
                    cot_move(at_owner).start()

                @pl.when(is_owner)
                def _():
                    cot_keep.start()

            @pl.when(phase == 1)
            def _():
                copy_x.start()
                copy_raw.start()
                for i in range(2):
                    share_o.pass_twin(i)

            @pl.loop(0, 2)
            def _(i):
                head_block(at(i))

    copy_wq = pltpu.make_async_copy(wq, wq_out, out_sems.at[0])
    copy_x = pltpu.make_async_copy(x_ref, x_out, out_sems.at[2])
    copy_raw = pltpu.make_async_copy(raw_ref, raw_out, out_sems.at[3])

    def ring_step(s):
        @pl.loop(0, chunks)
        def _(j):
            if s == 0:
                for d in range(1, nr):
                    piece(d, j).wait_recv()

            @pl.when(c - s >= 0)
            def _():
                if s > 0:
                    block(0, s - 1, jnp.maximum(c - s, 0), j, right).wait_recv()
                if s < n - 1:
                    @pl.when(c < n - 1)
                    def _():
                        block(0, s, jnp.maximum(c - s, 0), j, right).start()

            @pl.when(c + s <= n - 1)
            def _():
                if s > 0:
                    block(1, s - 1, jnp.minimum(c + s, n - 1), j, left).wait_recv()
                if s < n - 1:
                    @pl.when(c > 0)
                    def _():
                        block(1, s, jnp.minimum(c + s, n - 1), j, left).start()

            if 0 < s < n - 1:
                @pl.when(j < 8 // (n - 2))
                def _():
                    flatten((s - 1) * (8 // (n - 2)) + j)

        if s == 1:
            for i in range(2):
                share_q.pass_far(i)
        if s == n - 2:
            copy_gu.start()
        if s == n - 2:
            for i in range(2):
                share_o.pass_far(i)
                share_q.pass_twin(i)
            cot_local.wait()
            for d in range(1, nr):
                cot_piece(d).wait_recv()
    steps = rows_all // mh

    for s in range(n - 1):
        ring_step(s)
    both_phases(lambda: ring_step(n - 1))

    share_o.wait_all()
    copy_wo = pltpu.make_async_copy(wo, wo_out, out_sems.at[1])
    copy_wo.start()

    @pl.loop(0, steps)
    def _(i):
        for d in range(1, nr):
            head_piece(d, i).wait()
        head_local(i).wait()

    for d in range(1, nr):
        cot_piece(d).wait_send()

    @pl.when(jnp.logical_not(is_owner))
    def _():
        cot_move(at_owner).wait_send()

    @pl.when(is_owner)
    def _():
        cot_keep.wait()
        for b in range(middle_at):
            @pl.when(b != at_owner)
            def _():
                remote(cot_own, half_ref.at[span(b * own, own)], send_e, recv_e.at[b], {"row": flip(r)}).wait_recv()

    @pl.loop(0, chunks)
    def _(j):
        for d in range(1, nr):
            piece(d, j).wait_send()
        for s in range(n - 1):
            @pl.when(jnp.logical_and(c - s >= 0, c < n - 1))
            def _():
                block(0, s, jnp.maximum(c - s, 0), j, right).wait_send()

            @pl.when(jnp.logical_and(c + s <= n - 1, c > 0))
            def _():
                block(1, s, jnp.minimum(c + s, n - 1), j, left).wait_send()

    for d in range(1, nr):
        table_piece(d, 0).wait_send()
        table_piece(d, 1).wait_send()
    share_q.drain()
    share_o.drain()
    copy_wq.wait()
    copy_wo.wait()
    copy_x.wait()
    copy_raw.wait()
    copy_gu.wait()


def front(tokens, table, gain, cot, w_qkv, w_out, w_gu, b_qkv, gain_q, gain_k, cos2, sin2, n, nr, m=32, mh=160):
    own = tokens.shape[0] // nr
    width = tokens.shape[1]
    rows_all = own * n
    tree = own * n * nr
    chunks = own // m
    steps = rows_all // mh
    dma = pltpu.SemaphoreType.DMA
    shape = jax.ShapeDtypeStruct
    any_space = pl.BlockSpec(memory_space=pl.ANY)
    return pl.pallas_call(
        functools.partial(front_kernel, n, nr, m, mh),
        out_shape=[
            shape((rows_all, width * nr), low),
            shape((table.shape[0], width * nr), low),
            shape((gain.shape[0], width * nr), wide),
            shape((rows_all // 2, width * nr), low),
            shape((rows_all, 3 * width), wide),
            shape((n, 8, own), wide),
            shape((tree, 3 * HEAD), low),
            shape((w_qkv.shape[0] * nr, w_qkv.shape[1]), low),
            shape((w_out.shape[0] * nr, w_out.shape[1]), low),
            shape((w_gu.shape[0], 2 * w_gu.shape[2]), low),
        ],
        in_specs=[any_space, VM, VM] + [any_space] * 4 + [VM] * 5,
        out_specs=[any_space, VM, VM, any_space, any_space, VM, any_space, any_space, any_space, any_space],
        scratch_shapes=[
            pltpu.VMEM((rows_all, width * nr), low),
            pltpu.VMEM((rows_all, 3 * width), wide),
            pltpu.VMEM(w_gu.shape, low),
            pltpu.VMEM((w_gu.shape[0], 2 * w_gu.shape[2]), low),
            pltpu.VMEM((w_qkv.shape[0] * nr, w_qkv.shape[1]), low),
            pltpu.VMEM((w_out.shape[0] * nr, w_out.shape[1]), low),
            pltpu.VMEM((n, n, 8, own), wide),
            pltpu.VMEM((width // HEAD, rows_all, 3 * HEAD), low),
            pltpu.VMEM((own, HEAD), wide),
            pltpu.VMEM((own, HEAD), wide),
            pltpu.VMEM((own, 3 * RANK), low),
            pltpu.VMEM((own, width * nr), low),
            dma((nr - 1, chunks)), dma((nr - 1, chunks)), dma((2, n - 1, chunks)), dma((2, n - 1, chunks)),
            dma((2, nr - 1)), dma((2, nr - 1)), dma((3,)),
            dma((n, n - 1)), dma((n, n - 1)), dma((nr - 1, steps)), dma((nr - 1, steps)),
            dma((nr - 1,)), dma((nr - 1,)), dma((steps,)), dma((2,)), dma, dma((n // 2,)),
        ] + share_sems(2) + share_sems(2) + [dma((6,))],
        compiler_params=params(3),
        name="front",
    )(tokens, table, gain, cot, w_qkv, w_out, w_gu, b_qkv, gain_q, gain_k, cos2, sin2)


def one_hot_rows(out_rows, in_rows, source):
    at = lax.broadcasted_iota(jnp.int32, (out_rows, in_rows), 0)
    return (lax.broadcasted_iota(jnp.int32, (out_rows, in_rows), 1) == source(at)).astype(low)


def rear_kernel(n, nr, ndp, m, d_ref, raw_hbm, factor_ref, gq_ref, gk_ref, cos_ref, sin_ref, res_ref, x_hbm, wq_hbm,
                table_ref, bq_ref, dh_hbm, full_hbm, co_hbm, cg_hbm, cd_hbm, hot_ref,
                grad_ref, layer_ref, sets_ref,
                raw_ref, x_ref, dh_ref, full_ref, co_ref, cg_ref, cd_ref, wq, stats, buf, nq, nk, pq, pk, fq, fk, d_raw, part, recv_right, recv_left, own_buf, layer_own,
                back, red, full, cols, col_stack, full_recv, full_sum, full_last, col_recv, owned, hot_all,
                send_s, recv_s, send_h, recv_h, local_h, send_o, recv_o, local_o, load,
                send_z, recv_z, send_w, recv_w, local_w, send_v, recv_v, local_v,
                send_f, recv_f, send_c, recv_c, send_l, recv_l, send_d, recv_d, send_k, recv_k):
    g, r, c = lax.axis_index("dp"), lax.axis_index("row"), lax.axis_index("col")
    rows_all, width_all = part.shape
    own = rows_all // n
    width = gq_ref.shape[1]
    heads = width // HEAD
    tree_part = own * nr
    middle_at = n // 2
    chunks = own // m
    hop = 1
    ahead = 2
    left = {"col": jnp.maximum(c - 1, 0)}
    right = {"col": jnp.minimum(c + 1, n - 1)}
    load_raw = pltpu.make_async_copy(raw_hbm, raw_ref, load.at[0])
    load_x = pltpu.make_async_copy(x_hbm, x_ref, load.at[1])
    load_w = pltpu.make_async_copy(wq_hbm, wq, load.at[2])
    loads = [
        pltpu.make_async_copy(src, dst, load.at[3 + i])
        for i, (src, dst) in enumerate(
            ((dh_hbm, dh_ref), (full_hbm, full_ref), (co_hbm, co_ref), (cg_hbm, cg_ref), (cd_hbm, cd_ref))
        )
    ]

    def piece(d, b):
        peer = lax.rem(r + d, nr)
        return remote(
            d_ref.at[span(b * tree_part + peer * own, own)], buf.at[r, span(b * own, own)],
            send_h.at[d - 1, b], recv_h.at[d - 1, b], {"row": peer},
        )

    def local(b):
        return pltpu.make_async_copy(
            d_ref.at[span(b * tree_part + r * own, own)], buf.at[r, span(b * own, own)], local_h.at[b]
        )

    is_owner = jnp.logical_or(c == 0, c == n - 1)
    base = jnp.where(c == 0, 0, middle_at)

    def result_piece(b):
        return remote(res_ref.at[span(b * own, own)], layer_own, send_o.at[b], recv_o, {"col": base + b})

    def result_local(b):
        return pltpu.make_async_copy(res_ref.at[span(b * own, own)], layer_own, local_o)

    def width_piece(src, dst, send_sem, recv_sem, d, j, size):
        peer = lax.rem(r + d, nr)
        return remote(
            src.at[span(j * size, size), span(peer * width, width)], dst.at[span(r * own + j * size, size)],
            send_sem.at[d - 1, j], recv_sem.at[d - 1, j], {"row": peer},
        )

    def width_local(src, dst, sem, j, size):
        return pltpu.make_async_copy(
            src.at[span(j * size, size), span(r * width, width)], dst.at[span(r * own + j * size, size)], sem.at[j]
        )

    for b in range(n):
        local(b).start()
    load_raw.start()
    load_x.start()
    load_w.start()
    for copy in loads:
        copy.start()
    me = r * n + c
    barrier = pltpu.get_barrier_semaphore()
    for d in range(1, ndp):
        pl.semaphore_signal(barrier, inc=1, device_id={"dp": lax.rem(g + d, ndp)}, device_id_type=MESH)
    greet(n, nr, ndp - 1)
    for b in (0, n - 1) + tuple(range(1, n - 1)):
        for d in range(1, nr):
            piece(d, b).start()

    @pl.when(is_owner)
    def _():
        for b in range(middle_at):
            @pl.when(base + b == c)
            def _():
                result_local(b).start()

            @pl.when(base + b != c)
            def _():
                result_piece(b).start()

    hot_all[g] = hot_ref[...]
    load_x.wait()
    red[...] = dot_t(x_ref[...], table_ref[:3 * RANK, :]).astype(low)
    load_raw.wait()

    def stat_copy(b, d):
        peer = lax.rem(c + d, n)
        return remote(stats.at[c, b], stats.at[c, b], send_s.at[b, d - 1], recv_s.at[b, d - 1], {"col": peer})

    def norm_block(b):
        for d in range(1, nr):
            piece(d, b).wait_recv()
        local(b).wait()
        rows = span(b * own, own)
        fq[rows, :] = down_columns(factor_ref[b], 0)
        fk[rows, :] = down_columns(factor_ref[b], 4)
        cosine = cos_ref[rows, :]
        sine = sin_ref[rows, :]
        for h in range(heads):
            lanes = slice(h * HEAD, (h + 1) * HEAD)
            k_lanes = slice(width + h * HEAD, width + (h + 1) * HEAD)
            v_lanes = slice(2 * width + h * HEAD, 2 * width + (h + 1) * HEAD)
            u = buf[h, rows, :HEAD].astype(wide)
            u = (u * cosine - pltpu.roll(u, HEAD // 2, 1) * sine) * gq_ref[:, lanes]
            nq[rows, lanes] = u
            pq[rows, lanes] = u * raw_ref[rows, lanes] * fq[rows, :]
            u = buf[h, rows, HEAD:2 * HEAD].astype(wide)
            u = (u * cosine - pltpu.roll(u, HEAD // 2, 1) * sine) * gk_ref[:, lanes]
            nk[rows, lanes] = u
            pk[rows, lanes] = u * raw_ref[rows, k_lanes] * fk[rows, :]
            d_raw[rows, v_lanes] = buf[h, rows, 2 * HEAD:]
        stats[c, b] = row_sums(pq[rows, :], pk[rows, :])
        for d in range(1, n):
            stat_copy(b, d).start()

    def mean_block(b):
        for d in range(1, n):
            stat_copy(b, d).wait()
        total = stats[0, b]
        for s in range(1, n):
            total = total + stats[s, b]
        mean = total * (1.0 / D) * factor_ref[b]
        rows = span(b * own, own)
        pq[rows, :HEAD] = down_columns(mean, 0)
        pk[rows, :HEAD] = down_columns(mean, 4)

    def back_block(b):
        rows = span(b * own, own)
        for h in range(heads):
            lanes = slice(h * HEAD, (h + 1) * HEAD)
            k_lanes = slice(width + h * HEAD, width + (h + 1) * HEAD)
            d_raw[rows, lanes] = (fq[rows, :] * (nq[rows, lanes] - raw_ref[rows, lanes] * pq[rows, :HEAD])).astype(low)
            d_raw[rows, k_lanes] = (fk[rows, :] * (nk[rows, lanes] - raw_ref[rows, k_lanes] * pk[rows, :HEAD])).astype(low)
        for j in range(3):
            back[rows, j * RANK:(j + 1) * RANK] = dot_t(
                d_raw[rows, j * width:(j + 1) * width], bq_ref[j * RANK:(j + 1) * RANK, :]
            ).astype(low)
        mine = jnp.where(b < middle_at, c == 0, c == n - 1)
        held = span(lax.rem(b, middle_at) * own, own)
        for k in range(width_all // width):
            lanes = slice(k * width, (k + 1) * width)
            value = dot_t(d_raw[rows, :], wq[lanes, :]) + dot(back[rows, :], table_ref[:3 * RANK, lanes])
            part[rows, lanes] = (value + jnp.where(mine, dh_ref[held, lanes], 0.0)).astype(low)

    def full_piece(d):
        peer = lax.rem(r + d, nr)
        return remote(full.at[:, span(peer * width, width)], full_recv.at[r], send_f.at[d - 1], recv_f.at[d - 1], {"row": peer})

    col_rows = col_recv.shape[1]
    full_rows = full_last.shape[1]

    def col_piece(d):
        peer = lax.rem(r + d, nr)
        return remote(cols.at[span(peer * col_rows, col_rows)], col_recv.at[r], send_c.at[d - 1], recv_c.at[d - 1], {"row": peer})

    def last_piece(d):
        peer = lax.rem(c + d, n)
        return remote(full_sum.at[span(peer * full_rows, full_rows)], full_last.at[c], send_l.at[d - 1], recv_l.at[d - 1], {"col": peer})

    def tree_piece(d):
        return remote(owned.at[g], owned.at[g], send_d.at[d - 1], recv_d.at[d - 1], {"dp": lax.rem(g + d, ndp)})

    def hot_piece(d):
        return remote(hot_all.at[g], hot_all.at[g], send_k.at[d - 1], recv_k.at[d - 1], {"dp": lax.rem(g + d, ndp)})

    def reduce(kind, b, j):
        rows = span(b * own + j * m, m)
        dst, to = ((recv_right, right), (recv_left, left))[kind]
        return remote(part.at[rows], dst.at[rows], send_z.at[kind, b, j], recv_z.at[kind, b, j], to)

    def stage(s, at_edge=True, inside=True, jobs=()):
        @pl.loop(0, chunks + hop * (n - 2))
        def _(i):
            for at, job in enumerate(jobs):
                pl.when(i == at)(job)

            for kind, b, go, edge, got, j in (
                (0, n - 1 - s, n - 1 - s > c, c == 0, recv_right, i - hop * c),
                (1, s, s < c, c == n - 1, recv_left, i - hop * (n - 1 - c)),
            ):
                go = jnp.logical_and(go, jnp.logical_and(j >= 0, j < chunks))
                if at_edge:
                    @pl.when(jnp.logical_and(go, edge))
                    def _():
                        @pl.when(j >= ahead)
                        def _():
                            reduce(kind, b, j - ahead).wait_send()

                        reduce(kind, b, j).start()

                if inside:
                    @pl.when(jnp.logical_and(go, jnp.logical_not(edge)))
                    def _():
                        rows = span(b * own + j * m, m)
                        reduce(kind, b, j).wait_recv()
                        part[rows, :] = (part[rows, :].astype(wide) + got[rows, :].astype(wide)).astype(low)
                        reduce(kind, b, j).start()

    @pl.loop(0, 2)
    def _(phase):
        def at(i):
            return jnp.where(phase == 0, i * (n - 1), 1 + i)

        @pl.loop(0, 2)
        def _(i):
            norm_block(at(i))

        @pl.when(phase == 0)
        def _():
            load_w.wait()
            loads[0].wait()

        @pl.when(phase == 1)
        def _():
            stage(0)

        @pl.loop(0, 2)
        def _(i):
            mean_block(at(i))
            back_block(at(i))

    for copy in loads[1:]:
        copy.wait()

    rank_own = RANK // n
    groups = full.shape[0] // (n * rank_own) - 1
    rank_row = RANK // nr
    per_wide = cd_ref.shape[1] // width

    def full_job():
        stacked = jnp.concatenate([t_dot(back[...], x_ref[...]), full_ref[...]], axis=0).astype(low)
        order = one_hot_rows(
            full.shape[0], stacked.shape[0],
            lambda o: jnp.where(
                lax.rem(o, full_rows) < groups * rank_own,
                lax.rem(o, full_rows) // rank_own * RANK + o // full_rows * rank_own + lax.rem(o, rank_own), -1
            ),
        )
        full[...] = dot(order, stacked).astype(low)

    def raw_job():
        for j in range(3):
            col_stack[j * RANK:(j + 1) * RANK, :] = t_dot(
                red[:, j * RANK:(j + 1) * RANK], d_raw[:, j * width:(j + 1) * width]
            ).astype(low)
        col_stack[3 * RANK:4 * RANK, :] = co_ref[...].astype(low)

    def wide_job():
        for k in range(per_wide):
            lanes = slice(k * width, (k + 1) * width)
            for j, value in enumerate((cg_ref[0, :, lanes], cg_ref[1, :, lanes], cd_ref[:, lanes])):
                at = (4 + j * per_wide + k) * RANK
                col_stack[at:at + RANK, :] = value.astype(low)

    def col_job():
        order = one_hot_rows(
            cols.shape[0], cols.shape[0],
            lambda o: lax.rem(o, col_rows) // rank_row * RANK + o // col_rows * rank_row + lax.rem(o, rank_row),
        )
        cols[...] = dot(order, col_stack[...]).astype(low)

    stage(1, jobs=(wide_job, raw_job, col_job, full_job))
    for d in range(1, nr):
        full_piece(d).start()
        col_piece(d).start()

    @pl.when(is_owner)
    def _():
        for b in range(middle_at):
            @pl.when(base + b == c)
            def _():
                result_local(b).wait()

            @pl.when(base + b != c)
            def _():
                result_piece(b).wait_send()

    @pl.when(jnp.logical_not(is_owner))
    def _():
        remote(res_ref.at[span(0, own)], layer_own, send_o.at[0], recv_o, right).wait_recv()

    for d in range(1, nr):
        width_piece(layer_own, layer_ref, send_v, recv_v, d, 0, own).start()
    width_local(layer_own, layer_ref, local_v, 0, own).start()
    def row_job():
        for d in range(1, nr):
            full_piece(d).wait_recv()
            col_piece(d).wait_recv()
        total = full[:, span(r * width, width)].astype(wide)
        col_total = cols[span(r * col_rows, col_rows), :].astype(wide)
        for d in range(1, nr):
            peer = lax.rem(r + d, nr)
            total = total + full_recv[peer].astype(wide)
            col_total = col_total + col_recv[peer].astype(wide)
        full_sum[...] = total.astype(low)
        owned[g, full_rows:, :] = col_total.astype(low)
        for d in range(1, n):
            last_piece(d).start()

    stage(2, jobs=(lambda: None, row_job))
    for d in range(1, n):
        last_piece(d).wait_recv()
    last = full_sum[span(c * full_rows, full_rows), :].astype(wide)
    for d in range(1, n):
        last = last + full_last[lax.rem(c + d, n)].astype(wide)
    owned[g, :full_rows, :] = last.astype(low)
    for d in range(1, ndp):
        tree_piece(d).start()
        hot_piece(d).start()

    @pl.loop(0, chunks)
    def _(j):
        rows = span(c * own + j * m, m)
        at = span(j * m, m)
        own_buf[at, :] = part[rows, :]

        @pl.when(c > 0)
        def _():
            reduce(0, c, j).wait_recv()
            own_buf[at, :] = (own_buf[at, :].astype(wide) + recv_right[rows, :].astype(wide)).astype(low)

        @pl.when(c < n - 1)
        def _():
            reduce(1, c, j).wait_recv()
            own_buf[at, :] = (own_buf[at, :].astype(wide) + recv_left[rows, :].astype(wide)).astype(low)

        for d in range(1, nr):
            width_piece(own_buf, grad_ref, send_w, recv_w, d, j, m).start()
        width_local(own_buf, grad_ref, local_w, j, m).start()

    for d in range(1, ndp):
        tree_piece(d).wait_recv()
        hot_piece(d).wait_recv()
    sets_own = sets_ref.shape[0]
    for s in range(sets_own):
        total = owned[0].astype(wide) * hot_all[0, pl.ds(g * sets_own + s, 1), :]
        for t in range(1, ndp):
            total = total + owned[t].astype(wide) * hot_all[t, pl.ds(g * sets_own + s, 1), :]
        sets_ref[s] = total

    @pl.loop(0, chunks)
    def _(j):
        for d in range(1, nr):
            width_piece(own_buf, grad_ref, send_w, recv_w, d, j, m).wait()
        width_local(own_buf, grad_ref, local_w, j, m).wait()

    for d in range(1, nr):
        width_piece(layer_own, layer_ref, send_v, recv_v, d, 0, own).wait()
        full_piece(d).wait_send()
        col_piece(d).wait_send()
        for b in range(n):
            piece(d, b).wait_send()
    width_local(layer_own, layer_ref, local_v, 0, own).wait()
    for d in range(1, n):
        last_piece(d).wait_send()
    for d in range(1, ndp):
        tree_piece(d).wait_send()
        hot_piece(d).wait_send()
    for s in range(n - 1):
        @pl.loop(0, chunks)
        def _(j):
            late = j >= chunks - ahead

            @pl.when(jnp.logical_and(n - 1 - s > c, jnp.logical_or(c > 0, late)))
            def _():
                reduce(0, n - 1 - s, j).wait_send()

            @pl.when(jnp.logical_and(s < c, jnp.logical_or(c < n - 1, late)))
            def _():
                reduce(1, s, j).wait_send()


def rear(d_head, raw, factor, gain_q, gain_k, cos2, sin2, result, x, w_qkv, table, b_qkv, d_h, full_mid, part_ao,
         part_bgu, part_ad, hot, sets_own, n, nr, ndp, m=32):
    rows_all, wide3 = raw.shape
    width = wide3 // 3
    width_all = x.shape[1]
    own = rows_all // n
    chunks = own // m
    full_rows = 8 * RANK // n
    col_blocks = 4 + 3 * part_ad.shape[1] // width
    col_rows = col_blocks * RANK // nr
    dma = pltpu.SemaphoreType.DMA
    shape = jax.ShapeDtypeStruct
    any_space = pl.BlockSpec(memory_space=pl.ANY)
    square = pltpu.VMEM((rows_all, width), wide)
    lane = pltpu.VMEM((rows_all, HEAD), wide)
    big = pltpu.VMEM((rows_all, width_all), low)
    return pl.pallas_call(
        functools.partial(rear_kernel, n, nr, ndp, m),
        out_shape=[
            shape((own * nr, width), low),
            shape((own * nr, width), low),
            shape((sets_own, full_rows + col_rows, width), wide),
        ],
        in_specs=[any_space] * 2 + [VM] * 5 + [any_space] * 3 + [VM] * 2 + [any_space] * 5 + [VM],
        out_specs=[VM] * 3,
        scratch_shapes=[
            pltpu.VMEM(raw.shape, wide),
            pltpu.VMEM(x.shape, low),
            pltpu.VMEM(d_h.shape, wide),
            pltpu.VMEM(full_mid.shape, wide),
            pltpu.VMEM(part_ao.shape, wide),
            pltpu.VMEM(part_bgu.shape, wide),
            pltpu.VMEM(part_ad.shape, wide),
            pltpu.VMEM(w_qkv.shape, low),
            pltpu.VMEM((n, n, 8, own), wide),
            pltpu.VMEM((nr, rows_all, 3 * HEAD), low),
            square, square, square, square, lane, lane,
            pltpu.VMEM((rows_all, wide3), low),
            big, big, big,
            pltpu.VMEM((own, width_all), low),
            pltpu.VMEM((own, width_all), low),
            pltpu.VMEM((rows_all, 3 * RANK), low),
            pltpu.VMEM((rows_all, 3 * RANK), low),
            pltpu.VMEM((n * full_rows, width_all), low),
            pltpu.VMEM((nr * col_rows, width), low),
            pltpu.VMEM((nr * col_rows, width), low),
            pltpu.VMEM((nr, n * full_rows, width), low),
            pltpu.VMEM((n * full_rows, width), low),
            pltpu.VMEM((n, full_rows, width), low),
            pltpu.VMEM((nr, col_rows, width), low),
            pltpu.VMEM((ndp, full_rows + col_rows, width), low),
            pltpu.VMEM((ndp,) + hot.shape, wide),
            dma((n, n - 1)), dma((n, n - 1)), dma((nr - 1, n)), dma((nr - 1, n)), dma((n,)),
            dma((n // 2,)), dma, dma, dma((8,)),
            dma((2, n, chunks)), dma((2, n, chunks)), dma((nr - 1, chunks)), dma((nr - 1, chunks)), dma((chunks,)),
            dma((nr - 1, 1)), dma((nr - 1, 1)), dma((1,)),
            dma((nr - 1,)), dma((nr - 1,)), dma((nr - 1,)), dma((nr - 1,)), dma((n - 1,)), dma((n - 1,)),
            dma((ndp - 1,)), dma((ndp - 1,)), dma((ndp - 1,)), dma((ndp - 1,)),
        ],
        compiler_params=params(5),
        name="rear",
    )(d_head, raw, factor, gain_q, gain_k, cos2, sin2, result, x, w_qkv, table, b_qkv, d_h, full_mid, part_ao, part_bgu, part_ad, hot)


def unpack_kernel(rank_own, rank_row, grad_ref, layer_ref, sets_ref, layer_out, input_grad, a_qkv, b_qkv, a_out, b_out, a_gu, b_gu, a_down, b_down):
    layer_out[...] = layer_ref[...]
    input_grad[...] = grad_ref[...].astype(wide)
    width = grad_ref.shape[1]
    first = 8 * rank_own

    def column(s, at):
        return sets_ref[s, first + at * rank_row:first + (at + 1) * rank_row, :]

    for s in range(sets_ref.shape[0]):
        for j in range(3):
            a_qkv[j, s] = sets_ref[s, j * rank_own:(j + 1) * rank_own, :]
            b_qkv[j, s] = column(s, j)
        for j in range(2):
            a_gu[j, s] = sets_ref[s, (3 + j) * rank_own:(4 + j) * rank_own, :]
        b_out[s] = sets_ref[s, 5 * rank_own:6 * rank_own, :]
        b_down[s] = sets_ref[s, 6 * rank_own:7 * rank_own, :]
        a_out[s] = column(s, 3)
        per = a_down.shape[2] // width
        for k in range(per):
            lanes = slice(k * width, (k + 1) * width)
            b_gu[0, s, :, lanes] = column(s, 4 + k)
            b_gu[1, s, :, lanes] = column(s, 4 + per + k)
            a_down[s, :, lanes] = column(s, 4 + 2 * per + k)


def unpack(grad, layer, sets, rank_own, rank_row, hidden):
    sets_own = sets.shape[0]
    width = grad.shape[1]
    shape = jax.ShapeDtypeStruct
    return pl.pallas_call(
        functools.partial(unpack_kernel, rank_own, rank_row),
        out_shape=[
            shape(layer.shape, low),
            shape(grad.shape, wide),
            shape((3, sets_own, rank_own, width), wide),
            shape((3, sets_own, rank_row, width), wide),
            shape((sets_own, rank_row, width), wide),
            shape((sets_own, rank_own, width), wide),
            shape((2, sets_own, rank_own, width), wide),
            shape((2, sets_own, rank_row, hidden), wide),
            shape((sets_own, rank_row, hidden), wide),
            shape((sets_own, rank_own, width), wide),
        ],
        in_specs=[VM] * 3,
        out_specs=[VM] * 10,
        name="unpack",
    )(grad, layer, sets)


def middle_kernel(n, nr, m, hop, cuts, head_ref, x_hbm, cot_hbm, gain_ref, wo_hbm, wg_hbm, wd_hbm,
                  table_ref, ao_ref, bg_ref, ad_ref,
                  dhead_ref, out_hbm, grad_hbm, full_ref, co_ref, cg_ref, cd_ref,
                  out_half, grad_half, wo, wg, wd, x_half, cot_half, raw, attn, d_attn, h_all, df_all, da_all, gu, part,
                  recv_right, recv_left, hid, red_gu, red_down, back_gu, back_down,
                  sems_send, sems_recv, send_in, recv_in, send_out, recv_out, local_in, local_out, load,
                  send_g, recv_g, local_g, send_d, recv_d, local_d):
    g, r, c = lax.axis_index("dp"), lax.axis_index("row"), lax.axis_index("col")
    ag_ref = table_ref.at[3 * RANK:5 * RANK]
    bo_ref = table_ref.at[5 * RANK:6 * RANK]
    bd_ref = table_ref.at[6 * RANK:]
    rows_all, width_all = part.shape
    half = rows_all // 2
    own = rows_all // n
    tree_part = own * nr
    chunks = half // m
    blocks = 4
    band = half // blocks
    hidden = ad_ref.shape[1]
    width = width_all // nr
    left = {"col": jnp.maximum(c - 1, 0)}
    right = {"col": jnp.minimum(c + 1, n - 1)}
    first = c == 0
    last = c == n - 1
    inner = jnp.logical_and(c > 0, c < n - 1)

    base = jnp.where(last, half, 0)
    a_cut = hidden // 4
    share_g = Share(wg_hbm, wg, cuts, (send_g, recv_g, local_g))
    share_d = Share(wd_hbm, wd, cuts // 2, (send_d, recv_d, local_d))
    loads = [pltpu.make_async_copy(wo_hbm, wo, load.at[0])]
    load_x = pltpu.make_async_copy(x_hbm.at[span(base, half)], x_half, load.at[1])
    load_cot = pltpu.make_async_copy(cot_hbm, cot_half, load.at[2])
    store_out = pltpu.make_async_copy(out_half, out_hbm, load.at[3])
    store_grad = pltpu.make_async_copy(grad_half, grad_hbm, load.at[4])
    is_owner = jnp.logical_or(first, last)
    loads[0].start()

    def piece_in(d, b):
        peer = lax.rem(r + d, nr)
        return remote(
            head_ref.at[span(b * tree_part + peer * own, own)],
            attn.at[span(b * own, own), span(r * HEAD, HEAD)],
            send_in.at[d - 1, b], recv_in.at[d - 1, b], {"row": peer},
        )

    def local_piece_in(b):
        return pltpu.make_async_copy(
            head_ref.at[span(b * tree_part + r * own, own)],
            attn.at[span(b * own, own), span(r * HEAD, HEAD)], local_in.at[b]
        )

    per_block = blocks // (n // 2)

    def out_rows(b, side):
        at = side * (n // 2) + b // per_block
        inside = lax.rem(b, per_block) * band
        return span(at * own + inside, band), span(at * tree_part + r * own + inside, band)

    def piece_out(d, b, side):
        peer = lax.rem(r + d, nr)
        here, there = out_rows(b, side)
        return remote(
            d_attn.at[here, span(peer * HEAD, HEAD)], dhead_ref.at[there],
            send_out.at[side * (nr - 1) + d - 1, b], recv_out.at[side * (nr - 1) + d - 1, b], {"row": peer},
        )

    def local_piece_out(b, side):
        here, there = out_rows(b, side)
        return pltpu.make_async_copy(d_attn.at[here, span(r * HEAD, HEAD)], dhead_ref.at[there], local_out.at[side, b])

    for b in range(n):
        local_piece_in(b).start()
    barrier = pltpu.get_barrier_semaphore()
    for d in range(1, nr):
        pl.semaphore_signal(barrier, inc=1, device_id={"row": lax.rem(r + d, nr)}, device_id_type=MESH)

    @pl.when(c > 0)
    def _():
        pl.semaphore_signal(barrier, inc=1, device_id=left, device_id_type=MESH)

    @pl.when(c < n - 1)
    def _():
        pl.semaphore_signal(barrier, inc=1, device_id=right, device_id_type=MESH)

    pl.semaphore_signal(barrier, inc=1, device_id={"dp": flip(g)}, device_id_type=MESH)
    full_ref[...] = jnp.zeros_like(full_ref)
    co_ref[...] = jnp.zeros_like(co_ref)
    cg_ref[...] = jnp.zeros_like(cg_ref)
    cd_ref[...] = jnp.zeros_like(cd_ref)

    @pl.when(inner)
    def _():
        pl.semaphore_wait(barrier, nr + 2)

    @pl.when(jnp.logical_not(inner))
    def _():
        pl.semaphore_wait(barrier, nr + 1)

    middle = n // 2
    for b in range(middle):
        for block in (b, middle + b):
            for d in range(1, nr):
                piece_in(d, block).start()
    load_x.start()
    load_cot.start()
    share_g.start_far()
    share_d.start_far()
    share_g.start_near()
    share_d.start_near()

    def rows(j, start=0):
        return span(start + j * m, m)

    def band_rows(b):
        return span(b * band, band), span(half + b * band, band)

    def take(ref, b):
        low_rows, high_rows = band_rows(b)
        return jnp.concatenate([ref[low_rows, :], ref[high_rows, :]], axis=0)

    def put(b, lanes, value):
        low_rows, high_rows = band_rows(b)
        part[low_rows, lanes] = value[:band].astype(low)
        part[high_rows, lanes] = value[band:].astype(low)

    around = hop * 2 * (n - 1)
    each = chunks // blocks

    def relay_stage(stage, owner_step, all_ref):
        def send(kind, j, src, dst, to):
            return remote(src, dst, sems_send.at[stage, kind, j], sems_recv.at[stage, kind, j], to)

        def reduce_right(j):
            return send(0, j, part.at[rows(j, half)], recv_right.at[rows(j)], right)

        def reduce_left(j):
            return send(1, j, part.at[rows(j)], recv_left.at[rows(j)], left)

        def spread_left(j):
            return send(2, j, all_ref.at[rows(j, half)], all_ref.at[rows(j, half)], left)

        def spread_right(j):
            return send(3, j, all_ref.at[rows(j)], all_ref.at[rows(j)], right)

        def step(i):
            def on(offset, who, run):
                j = i - offset

                @pl.when(jnp.logical_and(who, jnp.logical_and(j >= 0, j < chunks)))
                def _():
                    run(j)

            def mid_right(j):
                reduce_right(j).wait_recv()
                at = rows(j, half)
                part[at, :] = (part[at, :].astype(wide) + recv_right[rows(j), :].astype(wide)).astype(low)
                reduce_right(j).start()

            def mid_left(j):
                reduce_left(j).wait_recv()
                at = rows(j)
                part[at, :] = (part[at, :].astype(wide) + recv_left[at, :].astype(wide)).astype(low)
                reduce_left(j).start()

            def end_right(j):
                reduce_right(j).wait_recv()
                total = part[rows(j, half), :].astype(wide) + recv_right[rows(j), :].astype(wide)
                all_ref[rows(j, half), :] = owner_step(total, rows(j))
                spread_left(j).start()

            def end_left(j):
                reduce_left(j).wait_recv()
                total = part[rows(j), :].astype(wide) + recv_left[rows(j), :].astype(wide)
                all_ref[rows(j), :] = owner_step(total, rows(j))
                spread_right(j).start()

            def pass_left(j):
                spread_left(j).wait_recv()
                spread_left(j).start()

            def pass_right(j):
                spread_right(j).wait_recv()
                spread_right(j).start()

            def arrived(j):
                @pl.when(first)
                def _():
                    reduce_right(j).wait_send()
                    spread_left(j).wait_recv()

                @pl.when(last)
                def _():
                    reduce_left(j).wait_send()
                    spread_right(j).wait_recv()

                @pl.when(inner)
                def _():
                    reduce_right(j).wait_send()
                    reduce_left(j).wait_send()

            on(0, first, lambda j: reduce_right(j).start())
            on(0, last, lambda j: reduce_left(j).start())
            on(hop * c, inner, mid_right)
            on(hop * (n - 1 - c), inner, mid_left)
            on(hop * (n - 1), last, end_right)
            on(hop * (n - 1), first, end_left)
            on(hop * (2 * (n - 1) - c), inner, pass_left)
            on(hop * (n - 1 + c), inner, pass_right)
            on(around, True, arrived)

        def rest():
            @pl.loop(0, chunks)
            def _(j):
                @pl.when(first)
                def _():
                    spread_right(j).wait_send()

                @pl.when(last)
                def _():
                    spread_left(j).wait_send()

                @pl.when(inner)
                def _():
                    spread_left(j).wait_send()
                    spread_right(j).wait_send()

        return step, rest

    def slices(before, i, per, work):
        @pl.loop(before(i), before(i + 1))
        def _(t):
            work(t // per, lax.rem(t, per))

    def paced(per):
        def before(i):
            late = per + (jnp.maximum(i - per, 0) * per) // each
            return jnp.minimum(jnp.where(i < per, i, late), per * blocks)

        return before

    def shard(j, ref):
        return slice(j * (ref.shape[0] // nr), (j + 1) * (ref.shape[0] // nr))

    def out_work(b, k):
        @pl.when(b == 0)
        def _():
            loads[0].wait()

        @pl.when(lax.rem(b, blocks // middle) == 0)
        def _():
            at = b // (blocks // middle)
            for block in (at, middle + at):
                for d in range(1, nr):
                    piece_in(d, block).wait_recv()
                local_piece_in(block).wait()

        rows_in = take(attn, b)
        red = dot_t(rows_in, ao_ref[...]).astype(low)
        for j in range(nr):
            lanes = slice(j * width, (j + 1) * width)
            put(b, lanes, dot(rows_in, wo[shard(j, wo), :]) + dot(red, bo_ref[:, lanes]))

    gain_a = gain_ref[0:1, :]
    gain_f = gain_ref[1:2, :]

    def attn_owner(total, at):
        raw[at, :] = total
        flat = total * norm_factor(row_sum(total * total))
        return (x_half[at, :].astype(wide) + flat * gain_a).astype(low)

    first_pass = 4
    apart = 2
    late = 3
    passes = cuts + cuts // 2

    def pump(ii):
        at = ii - first_pass

        @pl.when(jnp.logical_and(at >= 0, lax.rem(at, apart) == 0))
        def _():
            t = at // apart

            @pl.when(t < cuts)
            def _():
                share_g.pass_far(t)

            @pl.when(jnp.logical_and(t >= cuts, t < passes))
            def _():
                share_d.pass_far(t - cuts)

            t = t - late

            @pl.when(jnp.logical_and(t >= 0, t < cuts))
            def _():
                share_g.pass_twin(t)

            @pl.when(jnp.logical_and(t >= cuts, t < passes))
            def _():
                share_d.pass_twin(t - cuts)

    load_x.wait()
    in_loop = 1 + chunks + around
    step, rest = relay_stage(0, attn_owner, h_all)
    out_pace = paced(1)

    @pl.loop(0, in_loop)
    def _(ii):
        step(ii - 1)
        slices(out_pace, ii, 1, out_work)
        pump(ii)

    rest()

    share_g.wait_all()

    def gate_slice(b, k):
        rows_in = take(h_all, b)

        @pl.when(k == 0)
        def _():
            red_gu[b] = dot_t(rows_in, ag_ref[...]).astype(low)

        at = pl.multiple_of(k * a_cut, a_cut)
        lanes = pl.ds(at, a_cut)
        up_lanes = pl.ds(pl.multiple_of(hidden + at, a_cut), a_cut)
        red = red_gu[b]
        gate = dot(rows_in, wg[:, lanes]) + dot(red[:, :RANK], bg_ref[0, :, lanes])
        up = dot(rows_in, wg[:, up_lanes]) + dot(red[:, RANK:], bg_ref[1, :, lanes])
        gu[b, :, lanes] = gate.astype(low)
        gu[b, :, up_lanes] = up.astype(low)
        hid[:, lanes] = (gate * jax.nn.sigmoid(gate) * up).astype(low)

    def down_slice(b, k):
        @pl.when(jnp.logical_and(b == 0, k == 0))
        def _():
            @pl.loop(in_loop, jnp.maximum(in_loop, first_pass + apart * (passes + late)))
            def _(ii):
                pump(ii)

            share_d.wait_all()

        rows_in = hid[:, :hidden]

        @pl.when(k == 0)
        def _():
            red_down[b] = dot_t(rows_in, ad_ref[...]).astype(low)

        for s in range(nr // 2):
            j = k * (nr // 2) + s
            lanes = span(j * width, width)
            down_rows = pl.ds(pl.multiple_of(j * hidden, hidden), hidden)
            put(b, lanes, dot(rows_in, wd[down_rows, :]) + dot(red_down[b], bd_ref[:, lanes]))

    def ffn_work(b, k):
        @pl.when(k < 4)
        def _():
            gate_slice(b, k)

        @pl.when(k >= 4)
        def _():
            down_slice(b, k - 4)

    def ffn_owner(total, at):
        a_raw = raw[at, :]
        h = x_half[at, :].astype(wide) + a_raw * norm_factor(row_sum(a_raw * a_raw)) * gain_a
        factor = norm_factor(row_sum(total * total))
        flat = total * factor
        out_half[at, :] = (h + flat * gain_f).astype(low)
        scaled = cot_half[at, :].astype(wide) * gain_f
        return (factor * (scaled - flat * (row_sum(scaled * flat) * (1.0 / D)))).astype(low)

    b_cut = hidden // 2

    def hidden_back(b, k):
        rows_in = take(df_all, b)

        @pl.when(k == 0)
        def _():
            back_down[...] = dot_t(rows_in, bd_ref[...]).astype(low)

        at = pl.multiple_of(k * b_cut, b_cut)
        lanes = pl.ds(at, b_cut)
        up_lanes = pl.ds(pl.multiple_of(hidden + at, b_cut), b_cut)
        back = back_down[...]
        grad = dot(back, ad_ref[:, lanes])
        for j in range(nr):
            down_rows = pl.ds(pl.multiple_of(j * hidden + at, b_cut), b_cut)
            grad = grad + dot_t(rows_in[:, j * width:(j + 1) * width], wd[down_rows, :])
        gate = gu[b, :, lanes].astype(wide)
        up = gu[b, :, up_lanes].astype(wide)
        sigma = jax.nn.sigmoid(gate)
        silu = gate * sigma
        d_gate = (grad * up * sigma * (1.0 + gate * (1.0 - sigma))).astype(low)
        d_up = (grad * silu).astype(low)
        hid[:, lanes] = d_gate
        hid[:, up_lanes] = d_up
        cd_ref[:, lanes] += t_dot(back, (silu * up).astype(low))
        red = red_gu[b]
        cg_ref[0, :, lanes] += t_dot(red[:, :RANK], d_gate)
        cg_ref[1, :, lanes] += t_dot(red[:, RANK:], d_up)

    o_cut = width_all // 4

    def gate_back(b, k):
        @pl.when(k == 0)
        def _():
            back_gu[:, :RANK] = dot_t(hid[:, :hidden], bg_ref[0]).astype(low)
            back_gu[:, RANK:] = dot_t(hid[:, hidden:], bg_ref[1]).astype(low)

        lanes = span(k * o_cut, o_cut)
        put(b, lanes, dot_t(hid[...], wg[lanes, :]) + dot(back_gu[...], ag_ref[:, lanes]))

        @pl.when(k == 3)
        def _():
            full_ref[:2 * RANK, :] += t_dot(back_gu[...], take(h_all, b))
            full_ref[3 * RANK:, :] += t_dot(red_down[b], take(df_all, b))

    def back_work(b, k):
        @pl.when(k < 2)
        def _():
            hidden_back(b, k)

        @pl.when(k >= 2)
        def _():
            gate_back(b, k - 2)

    def back_owner(total, at):
        grad = cot_half[at, :].astype(wide) + total
        grad_half[at, :] = grad
        a_raw = raw[at, :]
        factor = norm_factor(row_sum(a_raw * a_raw))
        flat = a_raw * factor
        scaled = grad * gain_a
        return (factor * (scaled - flat * (row_sum(scaled * flat) * (1.0 / D)))).astype(low)

    def out_back(b, k):
        rows_in = take(da_all, b)
        back = dot_t(rows_in, bo_ref[...]).astype(low)
        grad = dot(back, ao_ref[...])
        for j in range(nr):
            grad = grad + dot_t(rows_in[:, j * width:(j + 1) * width], wo[shard(j, wo), :])
        for side in range(2):
            d_attn[out_rows(b, side)[0], :] = grad[side * band:(side + 1) * band].astype(low)
            for d in range(1, nr):
                piece_out(d, b, side).start()
            local_piece_out(b, side).start()
        attn_rows = take(attn, b)
        co_ref[...] += t_dot(back, attn_rows)
        red = dot_t(attn_rows, ao_ref[...]).astype(low)
        full_ref[2 * RANK:3 * RANK, :] += t_dot(red, rows_in)

    begin = around + each

    def back_before(i):
        return jnp.clip(i - begin, 0, 6 * blocks)

    def out_before(i):
        return jnp.clip((i - around - 1) // each, 0, blocks)

    load_cot.wait()
    step_f, rest_f = relay_stage(1, ffn_owner, df_all)
    step_b, rest_b = relay_stage(2, back_owner, da_all)
    ffn_pace = paced(6)
    period = 26

    @pl.loop(0, 6 + period + chunks + around + 1)
    def _(ii):
        i = ii - 6
        step_f(i)
        step_b(i - period)
        slices(ffn_pace, ii, 6, ffn_work)
        slices(back_before, i, 6, back_work)
        slices(out_before, i - period, 1, out_back)

    pl.when(is_owner)(store_out.start)
    rest_f()
    rest_b()
    pl.when(is_owner)(store_grad.start)

    @pl.loop(0, n)
    def _(b):
        for d in range(1, nr):
            piece_in(d, b).wait_send()

    @pl.loop(0, blocks)
    def _(b):
        for side in range(2):
            for d in range(1, nr):
                piece_out(d, b, side).wait()
            local_piece_out(b, side).wait()

    share_g.drain()
    share_d.drain()

    @pl.when(is_owner)
    def _():
        store_out.wait()
        store_grad.wait()


def middle(attn_head, x, cot_half, gains, w_out, w_gu, w_down, table, a_out, b_gu, a_down, n, nr, m=16, hop=2, cuts=8):
    group, width_all = x.shape
    half = group // 2
    width = width_all // nr
    hidden = a_down.shape[1]
    chunks = half // m
    band = group // 4
    dma = pltpu.SemaphoreType.DMA
    any_space = pl.BlockSpec(memory_space=pl.ANY)
    shape = jax.ShapeDtypeStruct
    return pl.pallas_call(
        functools.partial(middle_kernel, n, nr, m, hop, cuts),
        out_shape=[
            shape(attn_head.shape, low),
            shape((half, width_all), low),
            shape((half, width_all), wide),
            shape((4 * RANK, width_all), wide),
            shape((RANK, a_out.shape[1]), wide),
            shape((2, RANK, hidden), wide),
            shape((RANK, hidden), wide),
        ],
        in_specs=[any_space, any_space, any_space, VM, any_space, any_space, any_space] + [VM] * 4,
        out_specs=[any_space] * 3 + [VM] * 4,
        scratch_shapes=[
            pltpu.VMEM((half, width_all), low),
            pltpu.VMEM((half, width_all), wide),
            pltpu.VMEM(w_out.shape, low),
            pltpu.VMEM((w_gu.shape[0] * nr, w_gu.shape[1]), low),
            pltpu.VMEM((w_down.shape[0] * nr, w_down.shape[1]), low),
            pltpu.VMEM((half, width_all), low),
            pltpu.VMEM((half, width_all), low),
            pltpu.VMEM((half, width_all), wide),
            pltpu.VMEM((group, a_out.shape[1]), low),
            pltpu.VMEM((group, a_out.shape[1]), low),
            pltpu.VMEM((group, width_all), low),
            pltpu.VMEM((group, width_all), low),
            pltpu.VMEM((group, width_all), low),
            pltpu.VMEM((4, band, 2 * hidden), low),
            pltpu.VMEM((group, width_all), low),
            pltpu.VMEM((half, width_all), low),
            pltpu.VMEM((half, width_all), low),
            pltpu.VMEM((band, 2 * hidden), low),
            pltpu.VMEM((4, band, 2 * RANK), low),
            pltpu.VMEM((4, band, RANK), low),
            pltpu.VMEM((band, 2 * RANK), low),
            pltpu.VMEM((band, RANK), low),
            dma((3, 4, chunks)), dma((3, 4, chunks)),
            dma((nr - 1, n)), dma((nr - 1, n)), dma((2 * (nr - 1), 4)), dma((2 * (nr - 1), 4)), dma((n,)), dma((2, 4)),
            dma((5,)),
        ] + share_sems(cuts) + share_sems(cuts // 2),
        compiler_params=pltpu.CompilerParams(collective_id=0, has_side_effects=True, vmem_limit_bytes=67043328),
        name="middle",
    )(attn_head, x, cot_half, gains, w_out, w_gu, w_down, table, a_out, b_gu, a_down)


def per_device(
    tokens,
    cotangent,
    seg_ids,
    positions,
    parents,
    tree_sets,
    gain_q,
    gain_k,
    gain_attn,
    gain_ffn,
    query_key_value_weight,
    output_weight,
    gate_up_weight,
    down_weight,
    query_key_value_adapter_first,
    query_key_value_adapter_second,
    output_adapter_first,
    output_adapter_second,
    gate_up_adapter_first,
    gate_up_adapter_second,
    down_adapter_first,
    down_adapter_second,
):
    dp_count = lax.axis_size("dp")
    row_count = lax.axis_size("row")
    col_count = lax.axis_size("col")
    row_at = lax.axis_index("row")
    tree_tokens = seg_ids.shape[0]
    assert tree_sets.shape[0] == 1 and col_count == 4
    set_count = output_adapter_first.shape[0]
    own = tokens.shape[0] // row_count
    group = own * col_count
    width_row = tokens.shape[1]
    width_col = gain_q.shape[0]
    hidden_col = down_weight.shape[0]
    tree_set = tree_sets[0]

    tables = (
        query_key_value_adapter_first,
        query_key_value_adapter_second,
        output_adapter_first,
        output_adapter_second,
        gate_up_adapter_first,
        gate_up_adapter_second,
        down_adapter_first,
        down_adapter_second,
    )
    narrow, b_qkv, a_out, b_gu, a_down, gain_pair, hot, branch_flag, parent_at = prep(
        tree_sets, seg_ids, parents, gain_attn[None, :], gain_ffn[None, :], tables
    )
    pos_own = lax.dynamic_index_in_dim(
        positions.reshape(col_count, row_count, own), row_at, 1, keepdims=False
    ).reshape(group)
    cos2, sin2 = angles(pos_own)
    gq, gk = gain_q[None, :], gain_k[None, :]
    x, table, gains, g_half, raw, factors, qkv_head, w_qkv, w_out, w_gu = front(
        tokens,
        narrow,
        gain_pair,
        cotangent,
        query_key_value_weight.reshape(width_row, 3 * width_col),
        output_weight,
        gate_up_weight,
        b_qkv,
        gq,
        gk,
        cos2,
        sin2,
        col_count,
        row_count,
    )
    attn_head, lse = attend(qkv_head, parent_at, branch_flag)
    d_attn_head, out_half, d_h_half, full_mid, part_ao, part_bgu, part_ad = middle(
        attn_head,
        x,
        g_half,
        gains,
        w_out,
        w_gu,
        down_weight,
        table,
        a_out,
        b_gu,
        a_down,
        col_count,
        row_count,
    )
    d_qkv_head = attend_back(qkv_head, d_attn_head, parent_at, branch_flag, lse)
    in_grad, layer, sets = rear(
        d_qkv_head,
        raw,
        factors,
        gq,
        gk,
        cos2,
        sin2,
        out_half,
        x,
        w_qkv,
        table,
        b_qkv,
        d_h_half,
        full_mid,
        part_ao,
        part_bgu,
        part_ad,
        hot,
        set_count // dp_count,
        col_count,
        row_count,
        dp_count,
    )
    return tuple(unpack(in_grad, layer, sets, RANK // col_count, RANK // row_count, hidden_col))


def solution(mesh):
    in_specs = (
        P(("dp", "col"), "row"),
        P(("dp", "col"), "row"),
        P("dp"),
        P("dp"),
        P("dp", None),
        P("dp"),
        P("col"),
        P("col"),
        P("row"),
        P("row"),
        P("row", None, "col"),
        P("col", "row"),
        P("row", None, "col"),
        P("col", "row"),
        P(None, None, None, "row"),
        P(None, None, None, "col"),
        P(None, None, "col"),
        P(None, None, "row"),
        P(None, None, None, "row"),
        P(None, None, None, "col"),
        P(None, None, "col"),
        P(None, None, "row"),
    )
    out_specs = (
        P(("dp", "col"), "row"),
        P(("dp", "col"), "row"),
        P(None, "dp", "col", "row"),
        P(None, "dp", "row", "col"),
        P("dp", "row", "col"),
        P("dp", "col", "row"),
        P(None, "dp", "col", "row"),
        P(None, "dp", "row", "col"),
        P("dp", "row", "col"),
        P("dp", "col", "row"),
    )
    return jax.shard_map(
        per_device, mesh=mesh, in_specs=in_specs, out_specs=out_specs, check_vma=False
    )
```

```python
import functools

import jax
import jax.numpy as jnp
from jax import lax
from jax.experimental import pallas as pl
from jax.experimental.pallas import tpu as pltpu
from jax.sharding import PartitionSpec as P

D = 2048
HEAD = 128
RANK = 16
SEG = 128
TRUNK = 1024
QT = 256
MESH = pl.DeviceIdType.MESH
VM = pl.BlockSpec(memory_space=pltpu.VMEM)
precise = lax.Precision.HIGHEST

epsilon = 1e-06
rope_base = 500000.0
masked_out = -1e30
low = jnp.bfloat16
wide = jnp.float32
last_last = (((1,), (1,)), ((), ()))
first_first = (((0,), (0,)), ((), ()))


def dot(left, right):
    return jnp.dot(left, right, preferred_element_type=wide)


def dot_t(left, right):
    return lax.dot_general(left, right, last_last, preferred_element_type=wide)


def t_dot(left, right):
    return lax.dot_general(left, right, first_first, preferred_element_type=wide)


def angles(positions):
    lane = jnp.arange(HEAD, dtype=jnp.int32)
    frequency = rope_base ** (-((lane % (HEAD // 2)).astype(wide) * 2.0) / HEAD)
    angle_table = positions.astype(wide)[:, None] * frequency[None, :]
    return (jnp.cos(angle_table), jnp.where(lane < HEAD // 2, -1.0, 1.0) * jnp.sin(angle_table))


def norm_factor(square_sum):
    return lax.rsqrt(square_sum * (1.0 / D) + epsilon)


def row_sum(v): return jnp.sum(v, axis=1, keepdims=True)

def params(collective):
    return pltpu.CompilerParams(collective_id=collective, has_side_effects=True, vmem_limit_bytes=60 << 20)


def span(at, size):
    return pl.ds(pl.multiple_of(at, size), size)


def remote(src, dst, send_sem, recv_sem, to):
    return pltpu.make_async_remote_copy(
        src_ref=src, dst_ref=dst, send_sem=send_sem, recv_sem=recv_sem, device_id=to, device_id_type=MESH
    )


def greet(n, nr, extra=0):
    r, c = lax.axis_index("row"), lax.axis_index("col")
    me = r * n + c
    barrier = pltpu.get_barrier_semaphore()

    @pl.loop(1, n * nr)
    def _(d):
        peer = lax.rem(me + d, n * nr)
        pl.semaphore_signal(barrier, inc=1, device_id={"row": peer // n, "col": lax.rem(peer, n)}, device_id_type=MESH)

    pl.semaphore_wait(barrier, n * nr - 1 + extra)


def row_sums(first, second):
    ones = jnp.ones((8, first.shape[1]), wide)
    at = lax.broadcasted_iota(jnp.int32, (8, first.shape[0]), 0)
    sum_first = lax.dot_general(ones, first, last_last, preferred_element_type=wide, precision=precise)
    sum_second = lax.dot_general(ones, second, last_last, preferred_element_type=wide, precision=precise)
    return jnp.where(at < 4, sum_first, sum_second)


def down_columns(values, at):
    pick = (lax.broadcasted_iota(jnp.int32, (8, HEAD), 0) == at).astype(wide)
    return lax.dot_general(values, pick, first_first, preferred_element_type=wide, precision=precise)


def flip(v):
    return v + 1 - 2 * lax.rem(v, 2)


class Share:
    def __init__(self, src, dst, cuts, sems):
        self.send, self.recv, self.local = sems
        self.src, self.cuts = src, cuts
        g, r = lax.axis_index("dp"), lax.axis_index("row")
        size = src.shape[0]
        half = size // 2
        step = half // cuts
        far = lax.rem(r + 2, 4)
        mine = lax.rem(g, 2)
        near_to, far_to, twin_to = {"row": flip(r)}, {"row": far}, {"dp": flip(g)}

        def rows(shard, part, i):
            return pl.ds(pl.multiple_of(shard * size + part * half + i * step, step), step)

        def copy(kind, i, src, dst, to):
            return remote(src, dst, self.send.at[kind, i], self.recv.at[kind, i], to)

        def hand(kind, part, to):
            return lambda i: copy(kind, i, dst.at[rows(far, part, i)], dst.at[rows(far, part, i)], to)

        whole = span(r * size, size)
        self.own = pltpu.make_async_copy(src, dst.at[whole], self.local)
        self.near = copy(0, 0, src, dst.at[whole], near_to)
        self.far = lambda i: copy(
            1, i, src.at[pl.ds(pl.multiple_of(mine * half + i * step, step), step)], dst.at[rows(r, mine, i)], far_to
        )
        self.far_near = hand(2, mine, near_to)
        self.far_twin = hand(3, mine, twin_to)
        self.twin_near = hand(4, 1 - mine, near_to)

    def start_far(self):
        for i in range(self.cuts):
            self.far(i).start()

    def start_near(self):
        self.own.start()
        self.near.start()

    def pass_far(self, i):
        self.far(i).wait_recv()
        self.far_twin(i).start()
        self.far_near(i).start()

    def pass_twin(self, i):
        self.far_twin(i).wait_recv()
        self.twin_near(i).start()

    def wait_all(self):
        self.own.wait()
        self.near.wait_recv()
        for i in range(self.cuts):
            self.far_near(i).wait_recv()
            self.twin_near(i).wait_recv()

    def drain(self):
        self.near.wait_send()
        for i in range(self.cuts):
            self.far(i).wait_send()
            self.far_near(i).wait_send()
            self.far_twin(i).wait_send()
            self.twin_near(i).wait_send()


def share_sems(cuts):
    dma = pltpu.SemaphoreType.DMA
    return [dma((5, cuts)), dma((5, cuts)), dma]


def prep_kernel(set_ref, seg_ref, parents_ref, ga_ref, gf_ref, fq_ref, sq_ref, fo_ref, so_ref, fg_ref, sg_ref, fd_ref, sd_ref,
                narrow_ref, bq_ref, ao_ref, bg_ref, ad_ref, gain_ref, hot_ref, flag_ref, at_ref):
    for j in range(3):
        narrow_ref[j * RANK:(j + 1) * RANK, :] = fq_ref[j, 0].astype(low)
        bq_ref[j * RANK:(j + 1) * RANK, :] = sq_ref[j, 0].astype(low)
    for j in range(2):
        narrow_ref[(3 + j) * RANK:(4 + j) * RANK, :] = fg_ref[j, 0].astype(low)
        bg_ref[j] = sg_ref[j, 0].astype(low)
    narrow_ref[5 * RANK:6 * RANK, :] = so_ref[0].astype(low)
    narrow_ref[6 * RANK:, :] = sd_ref[0].astype(low)
    ao_ref[...] = fo_ref[0].astype(low)
    ad_ref[...] = fd_ref[0].astype(low)
    gain_ref[...] = jnp.zeros_like(gain_ref)
    gain_ref[0:1, :] = ga_ref[...]
    gain_ref[1:2, :] = gf_ref[...]
    hot_ref[...] = (lax.broadcasted_iota(jnp.int32, hot_ref.shape, 0) == set_ref[0]).astype(wide)
    tails = flag_ref.shape[0]
    segments = [seg_ref[TRUNK + j * SEG] for j in range(tails)]
    for j in range(tails):
        parent = parents_ref[0, segments[j]]
        at = jnp.int32(0)
        for k in range(tails):
            at = jnp.where(segments[k] == parent, k + TRUNK // SEG, at)
        at_ref[j] = at
        flag_ref[j:j + 1, :] = jnp.full((1, SEG), jnp.where(parent > 0, 0.0, masked_out), wide)


def prep(tree_sets, seg_ids, parents, gain_a, gain_f, tables):
    fq, sq, fo, so, fg, sg, fd, sd = tables

    def pick(table):
        if table.ndim == 4:
            return pl.BlockSpec((table.shape[0], 1) + table.shape[2:], lambda i, s, *_: (0, s[0], 0, 0))
        return pl.BlockSpec((1,) + table.shape[1:], lambda i, s, *_: (s[0], 0, 0))

    def out(*shape, kind=low):
        return pl.BlockSpec(shape, lambda i, *_: (0,) * len(shape)), jax.ShapeDtypeStruct(shape, kind)

    tails = (seg_ids.shape[0] - TRUNK) // SEG
    width = gain_a.shape[1]
    gain_spec = pl.BlockSpec((1, width), lambda i, *_: (0, 0))

    outs = [
        out(7 * RANK, fq.shape[-1]), out(3 * RANK, sq.shape[-1]), out(RANK, fo.shape[-1]),
        out(2, RANK, sg.shape[-1]), out(RANK, fd.shape[-1]),
        out(8, width, kind=wide), out(fo.shape[0], width, kind=wide), out(tails, SEG, kind=wide),
        (pl.BlockSpec(memory_space=pltpu.SMEM), jax.ShapeDtypeStruct((tails,), jnp.int32)),
    ]
    return pl.pallas_call(
        prep_kernel,
        grid_spec=pltpu.PrefetchScalarGridSpec(
            num_scalar_prefetch=3,
            grid=(1,),
            in_specs=[gain_spec, gain_spec] + [pick(t) for t in tables],
            out_specs=[o[0] for o in outs],
        ),
        out_shape=[o[1] for o in outs],
        name="prep",
    )(tree_sets, seg_ids, parents, gain_a, gain_f, *tables)


def lower_mask(size):
    return lax.broadcasted_iota(jnp.int32, (size, size), 1) <= lax.broadcasted_iota(jnp.int32, (size, size), 0)


def softmax_parts(parts):
    top = jnp.max(parts[0], axis=1, keepdims=True)
    for s in parts[1:]:
        top = jnp.maximum(top, jnp.max(s, axis=1, keepdims=True))
    raised = [jnp.exp(s - top) for s in parts]
    total = jnp.sum(raised[0], axis=1, keepdims=True)
    for e in raised[1:]:
        total = total + jnp.sum(e, axis=1, keepdims=True)
    inverse = 1.0 / total
    return raised, inverse, top + jnp.log(total)


def tail_spans(parent_ref, pair):
    at = [pl.multiple_of(TRUNK + (2 * pair + side) * SEG, SEG) for side in range(2)]
    parent = [pl.multiple_of(parent_ref[2 * pair + side] * SEG, SEG) for side in range(2)]
    return pl.ds(at[0], 2 * SEG), [pl.ds(v, SEG) for v in at], [pl.ds(v, SEG) for v in parent]


def by_side(product, left, rights):
    return jnp.concatenate([product(left[i * SEG:(i + 1) * SEG], right) for i, right in enumerate(rights)], axis=0)


def tail_parts(q, qkv, own, parents, flags):
    scale = HEAD ** -0.5
    k_lanes = slice(HEAD, 2 * HEAD)
    trunk = dot_t(q, qkv[:TRUNK, k_lanes]) * scale
    branch = by_side(dot_t, q, [qkv[rows, k_lanes] for rows in parents]) * scale
    branch = branch + jnp.concatenate([jnp.broadcast_to(flag, (SEG, SEG)) for flag in flags], axis=0)
    mask = jnp.concatenate([lower_mask(SEG)] * 2, axis=0)
    own = jnp.where(mask, by_side(dot_t, q, [qkv[rows, k_lanes] for rows in own]) * scale, masked_out)
    return [trunk, branch, own]


def trunk_parts(q, qkv, i):
    scale = HEAD ** -0.5
    k_lanes = slice(HEAD, 2 * HEAD)
    own = dot_t(q, qkv[i * QT:(i + 1) * QT, k_lanes]) * scale
    parts = [jnp.where(lower_mask(QT), own, masked_out)]
    if i:
        parts.append(dot_t(q, qkv[:i * QT, k_lanes]) * scale)
    return parts


def attend_body(parent_ref, flag_ref, qkv, o_ref, lse_ref):
    v_lanes = slice(2 * HEAD, 3 * HEAD)
    for i in range(TRUNK // QT):
        at = slice(i * QT, (i + 1) * QT)
        p, inverse, lse = softmax_parts(trunk_parts(qkv[at, :HEAD], qkv, i))
        o = dot(p[0].astype(low), qkv[at, v_lanes])
        if i:
            o = o + dot(p[1].astype(low), qkv[:i * QT, v_lanes])
        o_ref[at, :] = (o * inverse).astype(low)
        lse_ref[at, :] = lse

    @pl.loop(0, (qkv.shape[0] - TRUNK) // (2 * SEG), unroll=3)
    def _(j):
        rows, own, parents = tail_spans(parent_ref, j)
        flags = [flag_ref[pl.ds(2 * j + side, 1), :] for side in range(2)]
        p, inverse, lse = softmax_parts(tail_parts(qkv[rows, :HEAD], qkv, own, parents, flags))
        o = dot(p[0].astype(low), qkv[:TRUNK, v_lanes])
        o = o + by_side(dot, p[1].astype(low), [qkv[at, v_lanes] for at in parents])
        o = o + by_side(dot, p[2].astype(low), [qkv[at, v_lanes] for at in own])
        o_ref[rows, :] = (o * inverse).astype(low)
        lse_ref[rows, :] = lse


def back_parts(scores, lse, d_out, keys, values):
    probs = [jnp.exp(s - lse) for s in scores]
    grads = [dot_t(d_out, v) for v in values]
    inner = sum(jnp.sum(p * g, axis=1, keepdims=True) for p, g in zip(probs, grads))
    d_scores = [(p * (g - inner)).astype(low) for p, g in zip(probs, grads)]
    dq = sum(dot(d, k) for d, k in zip(d_scores, keys))
    return d_scores, [p.astype(low) for p in probs], dq


def attend_back_kernel(parent_ref, flag_ref, qkv, do_ref, lse_ref, d_ref, dk_acc, dv_acc):
    scale = HEAD ** -0.5
    k_lanes = slice(HEAD, 2 * HEAD)
    v_lanes = slice(2 * HEAD, 3 * HEAD)
    dk_acc[...] = jnp.zeros_like(dk_acc)
    dv_acc[...] = jnp.zeros_like(dv_acc)
    for i in range(TRUNK // QT):
        at = slice(i * QT, (i + 1) * QT)
        spans = [at] + ([slice(0, i * QT)] if i else [])
        q, d_out = qkv[at, :HEAD], do_ref[at, :]
        d_scores, probs, dq = back_parts(
            trunk_parts(q, qkv, i), lse_ref[at, :], d_out, [qkv[s, k_lanes] for s in spans], [qkv[s, v_lanes] for s in spans]
        )
        d_ref[at, :HEAD] = (dq * scale).astype(low)
        for s, d, p in zip(spans, d_scores, probs):
            dk_acc[s, :] += t_dot(d, q)
            dv_acc[s, :] += t_dot(p, d_out)

    @pl.loop(0, (qkv.shape[0] - TRUNK) // (2 * SEG), unroll=3)
    def _(j):
        rows, own, parents = tail_spans(parent_ref, j)
        flags = [flag_ref[pl.ds(2 * j + side, 1), :] for side in range(2)]
        q, d_out, lse = qkv[rows, :HEAD], do_ref[rows, :], lse_ref[rows, :]
        probs = [jnp.exp(s - lse) for s in tail_parts(q, qkv, own, parents, flags)]
        grads = [
            dot_t(d_out, qkv[:TRUNK, v_lanes]),
            by_side(dot_t, d_out, [qkv[at, v_lanes] for at in parents]),
            by_side(dot_t, d_out, [qkv[at, v_lanes] for at in own]),
        ]
        inner = sum(jnp.sum(p * g, axis=1, keepdims=True) for p, g in zip(probs, grads))
        d_scores = [(p * (g - inner)).astype(low) for p, g in zip(probs, grads)]
        probs = [p.astype(low) for p in probs]
        dq = dot(d_scores[0], qkv[:TRUNK, k_lanes])
        dq = dq + by_side(dot, d_scores[1], [qkv[at, k_lanes] for at in parents])
        dq = dq + by_side(dot, d_scores[2], [qkv[at, k_lanes] for at in own])
        d_ref[rows, :HEAD] = (dq * scale).astype(low)
        dk_acc[:TRUNK, :] += t_dot(d_scores[0], q)
        dv_acc[:TRUNK, :] += t_dot(probs[0], d_out)
        for part, spans in ((1, parents), (2, own)):
            for side, at in enumerate(spans):
                half = slice(side * SEG, (side + 1) * SEG)
                dk_acc[at, :] += t_dot(d_scores[part][half], q[half])
                dv_acc[at, :] += t_dot(probs[part][half], d_out[half])

    d_ref[:, k_lanes] = (dk_acc[...] * scale).astype(low)
    d_ref[:, v_lanes] = dv_acc[...].astype(low)


def attend(qkv, parent_at, flag):
    n = qkv.shape[0]

    def whole(*shape):
        return pl.BlockSpec(shape, lambda i, *_: (0, 0))

    return pl.pallas_call(
        attend_body,
        grid_spec=pltpu.PrefetchScalarGridSpec(
            num_scalar_prefetch=1,
            grid=(1,),
            in_specs=[whole(*flag.shape), whole(n, 3 * HEAD)],
            out_specs=[whole(n, HEAD), whole(n, 1)],
        ),
        out_shape=[jax.ShapeDtypeStruct((n, HEAD), low), jax.ShapeDtypeStruct((n, 1), wide)],
        name="attend",
    )(parent_at, flag, qkv)


def attend_back(qkv, d_o, parent_at, flag, lse):
    n = qkv.shape[0]

    def whole(*shape):
        return pl.BlockSpec(shape, lambda i, *_: (0, 0))

    return pl.pallas_call(
        attend_back_kernel,
        grid_spec=pltpu.PrefetchScalarGridSpec(
            num_scalar_prefetch=1,
            grid=(1,),
            in_specs=[whole(*flag.shape), whole(n, 3 * HEAD), whole(n, HEAD), whole(n, 1)],
            out_specs=whole(n, 3 * HEAD),
            scratch_shapes=[pltpu.VMEM((n, HEAD), wide), pltpu.VMEM((n, HEAD), wide)],
        ),
        out_shape=jax.ShapeDtypeStruct((n, 3 * HEAD), low),
        name="attend_back",
    )(parent_at, flag, qkv, d_o, lse)


def front_kernel(n, nr, m, mh, tok_ref, table_ref, gain_ref, cot_ref, wq_hbm, wo_hbm, gu_hbm, bq_ref, gq_ref, gk_ref,
                 cos_ref, sin_ref,
                 x_out, table_all, gain_all, half_ref, raw_out, factor_ref, qkv_ref, wq_out, wo_out, gu_out,
                 x_ref, raw_ref, gu_pair, gu_flat, wq, wo, stats, buf, fq, fk, red, cot_own,
                 send_a, recv_a, send_z, recv_z, send_t, recv_t, local_sem,
                 send_s, recv_s, send_h, recv_h, send_g, recv_g, local_h, local_g, send_e, recv_e,
                 send_q, recv_q, local_q, send_o, recv_o, local_o, out_sems):
    g, r, c = lax.axis_index("dp"), lax.axis_index("row"), lax.axis_index("col")
    own = tok_ref.shape[0] // nr
    width = tok_ref.shape[1]
    rows_all = own * n
    heads = width // HEAD
    tree_part = own * nr
    chunks = own // m
    left = {"col": jnp.maximum(c - 1, 0)}
    right = {"col": jnp.minimum(c + 1, n - 1)}
    share_q = Share(wq_hbm, wq, 2, (send_q, recv_q, local_q))
    share_o = Share(wo_hbm, wo, 2, (send_o, recv_o, local_o))

    def piece(d, j):
        peer = lax.rem(r + d, nr)
        return remote(
            tok_ref.at[span(peer * own + j * m, m)],
            x_ref.at[span(c * own + j * m, m), span(r * width, width)],
            send_a.at[d - 1, j], recv_a.at[d - 1, j], {"row": peer},
        )

    def block(kind, s, at, j, to):
        rows = span(at * own + j * m, m)
        return remote(x_ref.at[rows], x_ref.at[rows], send_z.at[kind, s, j], recv_z.at[kind, s, j], to)

    def table_piece(d, kind):
        src, dst = ((table_ref, table_all), (gain_ref, gain_all))[kind]
        to = {"row": lax.rem(r + d, nr)}
        return remote(src, dst.at[:, span(r * width, width)], send_t.at[kind, d - 1], recv_t.at[kind, d - 1], to)

    keep = pltpu.make_async_copy(
        tok_ref.at[span(r * own, own)], x_ref.at[span(c * own, own), span(r * width, width)], local_sem.at[0]
    )
    keep_table = pltpu.make_async_copy(table_ref, table_all.at[:, span(r * width, width)], local_sem.at[1])
    keep_gain = pltpu.make_async_copy(gain_ref, gain_all.at[:, span(r * width, width)], local_sem.at[2])
    keep.start()
    keep_table.start()
    keep_gain.start()
    barrier = pltpu.get_barrier_semaphore()
    pl.semaphore_signal(barrier, inc=1, device_id={"dp": flip(g)}, device_id_type=MESH)
    greet(n, nr, 1)

    @pl.loop(0, chunks)
    def _(j):
        for d in range(1, nr):
            piece(d, j).start()


    load_gu = pltpu.make_async_copy(gu_hbm, gu_pair, out_sems.at[4])
    copy_gu = pltpu.make_async_copy(gu_flat, gu_out, out_sems.at[5])
    gu_step = gu_flat.shape[0] // 8

    def flatten(i):
        @pl.when(i == 0)
        def _():
            load_gu.wait()

        rows = span(i * gu_step, gu_step)
        gu_flat[rows, :] = gu_pair[rows].reshape(gu_step, gu_flat.shape[1])

    middle_at = n // 2
    owner = jnp.where(c < middle_at, 0, n - 1)
    at_owner = jnp.where(c < middle_at, c, c - middle_at)
    is_owner = owner == c

    def cot_piece(d):
        peer = lax.rem(r + d, nr)
        return remote(
            cot_ref.at[span(peer * own, own)], cot_own.at[:, span(r * width, width)], send_g.at[d - 1], recv_g.at[d - 1], {"row": peer}
        )

    cot_local = pltpu.make_async_copy(cot_ref.at[span(r * own, own)], cot_own.at[:, span(r * width, width)], local_g.at[0])
    cot_keep = pltpu.make_async_copy(cot_own, half_ref.at[span(at_owner * own, own)], local_g.at[1])

    def cot_move(b):
        return remote(cot_own, half_ref.at[span(b * own, own)], send_e, recv_e.at[b], {"col": owner})

    share_q.start_far()
    share_q.start_near()
    for d in range(1, nr):
        table_piece(d, 0).start()
        table_piece(d, 1).start()
    share_o.start_far()
    share_o.start_near()
    cot_local.start()
    for d in range(1, nr):
        cot_piece(d).start()
    load_gu.start()
    keep.wait()

    def head_rows(i):
        block_at = i // (own // mh)
        inside = lax.rem(i, own // mh)
        return span(block_at * tree_part + r * own + inside * mh, mh)

    def head_piece(d, i):
        peer = lax.rem(r + d, nr)
        return remote(
            buf.at[peer, span(i * mh, mh)], qkv_ref.at[head_rows(i)], send_h.at[d - 1, i], recv_h.at[d - 1, i], {"row": peer}
        )

    def head_local(i):
        return pltpu.make_async_copy(buf.at[r, span(i * mh, mh)], qkv_ref.at[head_rows(i)], local_h.at[i])

    def stat_copy(b, d):
        peer = lax.rem(c + d, n)
        return remote(stats.at[c, b], stats.at[c, b], send_s.at[b, d - 1], recv_s.at[b, d - 1], {"col": peer})

    def product_block(b):
        rows = span(b * own, own)
        x_rows = x_ref[rows, :]
        red[...] = dot_t(x_rows, table_all[:3 * RANK, :]).astype(low)
        for j in range(3):
            lanes = slice(j * width, (j + 1) * width)
            raw_ref[rows, lanes] = dot(x_rows, wq[:, lanes]) + dot(
                red[:, j * RANK:(j + 1) * RANK], bq_ref[j * RANK:(j + 1) * RANK, :]
            )
        q_rows = raw_ref[rows, :width]
        k_rows = raw_ref[rows, width:2 * width]
        stats[c, b] = row_sums(q_rows * q_rows, k_rows * k_rows)
        for d in range(1, n):
            stat_copy(b, d).start()

    per = own // mh

    def head_block(b):
        for d in range(1, n):
            stat_copy(b, d).wait()
        total = stats[0, b]
        for s in range(1, n):
            total = total + stats[s, b]
        factor = lax.rsqrt(total * (1.0 / D) + epsilon)
        factor_ref[b] = factor
        fq[...] = down_columns(factor, 0)
        fk[...] = down_columns(factor, 4)

        @pl.loop(0, per)
        def _(i):
            rows = span(b * own + i * mh, mh)
            inside = span(i * mh, mh)
            cosine = cos_ref[rows, :]
            sine = sin_ref[rows, :]
            for h in range(heads):
                lanes = slice(h * HEAD, (h + 1) * HEAD)
                u = raw_ref[rows, lanes] * fq[inside, :] * gq_ref[:, lanes]
                buf[h, rows, :HEAD] = (u * cosine + pltpu.roll(u, HEAD // 2, 1) * sine).astype(low)
                k_lanes = slice(width + h * HEAD, width + (h + 1) * HEAD)
                u = raw_ref[rows, k_lanes] * fk[inside, :] * gk_ref[:, lanes]
                buf[h, rows, HEAD:2 * HEAD] = (u * cosine + pltpu.roll(u, HEAD // 2, 1) * sine).astype(low)
                v_lanes = slice(2 * width + h * HEAD, 2 * width + (h + 1) * HEAD)
                buf[h, rows, 2 * HEAD:] = raw_ref[rows, v_lanes].astype(low)
            for d in range(1, nr):
                head_piece(d, b * per + i).start()
            head_local(b * per + i).start()

    def both_phases(last_step):
        for d in range(1, nr):
            table_piece(d, 0).wait_recv()
            table_piece(d, 1).wait_recv()
        keep_table.wait()
        keep_gain.wait()
        share_q.wait_all()
        copy_wq.start()

        @pl.loop(0, 2)
        def _(phase):
            def at(i):
                return jnp.where(phase == 0, 1 + i, i * (n - 1))

            pl.when(phase == 1)(last_step)

            @pl.loop(0, 2)
            def _(i):
                product_block(at(i))

            @pl.when(phase == 0)
            def _():
                @pl.when(jnp.logical_not(is_owner))
                def _():
                    cot_move(at_owner).start()

                @pl.when(is_owner)
                def _():
                    cot_keep.start()

            @pl.when(phase == 1)
            def _():
                copy_x.start()
                copy_raw.start()
                for i in range(2):
                    share_o.pass_twin(i)

            @pl.loop(0, 2)
            def _(i):
                head_block(at(i))

    copy_wq = pltpu.make_async_copy(wq, wq_out, out_sems.at[0])
    copy_x = pltpu.make_async_copy(x_ref, x_out, out_sems.at[2])
    copy_raw = pltpu.make_async_copy(raw_ref, raw_out, out_sems.at[3])

    def ring_step(s):
        @pl.loop(0, chunks)
        def _(j):
            if s == 0:
                for d in range(1, nr):
                    piece(d, j).wait_recv()

            @pl.when(c - s >= 0)
            def _():
                if s > 0:
                    block(0, s - 1, jnp.maximum(c - s, 0), j, right).wait_recv()
                if s < n - 1:
                    @pl.when(c < n - 1)
                    def _():
                        block(0, s, jnp.maximum(c - s, 0), j, right).start()

            @pl.when(c + s <= n - 1)
            def _():
                if s > 0:
                    block(1, s - 1, jnp.minimum(c + s, n - 1), j, left).wait_recv()
                if s < n - 1:
                    @pl.when(c > 0)
                    def _():
                        block(1, s, jnp.minimum(c + s, n - 1), j, left).start()

            if 0 < s < n - 1:
                @pl.when(j < 8 // (n - 2))
                def _():
                    flatten((s - 1) * (8 // (n - 2)) + j)

        if s == 1:
            for i in range(2):
                share_q.pass_far(i)
        if s == n - 2:
            copy_gu.start()
        if s == n - 2:
            for i in range(2):
                share_o.pass_far(i)
                share_q.pass_twin(i)
            cot_local.wait()
            for d in range(1, nr):
                cot_piece(d).wait_recv()
    steps = rows_all // mh

    for s in range(n - 1):
        ring_step(s)
    both_phases(lambda: ring_step(n - 1))

    share_o.wait_all()
    copy_wo = pltpu.make_async_copy(wo, wo_out, out_sems.at[1])
    copy_wo.start()

    @pl.loop(0, steps)
    def _(i):
        for d in range(1, nr):
            head_piece(d, i).wait()
        head_local(i).wait()

    for d in range(1, nr):
        cot_piece(d).wait_send()

    @pl.when(jnp.logical_not(is_owner))
    def _():
        cot_move(at_owner).wait_send()

    @pl.when(is_owner)
    def _():
        cot_keep.wait()
        for b in range(middle_at):
            @pl.when(b != at_owner)
            def _():
                remote(cot_own, half_ref.at[span(b * own, own)], send_e, recv_e.at[b], {"row": flip(r)}).wait_recv()

    @pl.loop(0, chunks)
    def _(j):
        for d in range(1, nr):
            piece(d, j).wait_send()
        for s in range(n - 1):
            @pl.when(jnp.logical_and(c - s >= 0, c < n - 1))
            def _():
                block(0, s, jnp.maximum(c - s, 0), j, right).wait_send()

            @pl.when(jnp.logical_and(c + s <= n - 1, c > 0))
            def _():
                block(1, s, jnp.minimum(c + s, n - 1), j, left).wait_send()

    for d in range(1, nr):
        table_piece(d, 0).wait_send()
        table_piece(d, 1).wait_send()
    share_q.drain()
    share_o.drain()
    copy_wq.wait()
    copy_wo.wait()
    copy_x.wait()
    copy_raw.wait()
    copy_gu.wait()


def front(tokens, table, gain, cot, w_qkv, w_out, w_gu, b_qkv, gain_q, gain_k, cos2, sin2, n, nr, m=32, mh=160):
    own = tokens.shape[0] // nr
    width = tokens.shape[1]
    rows_all = own * n
    tree = own * n * nr
    chunks = own // m
    steps = rows_all // mh
    dma = pltpu.SemaphoreType.DMA
    shape = jax.ShapeDtypeStruct
    any_space = pl.BlockSpec(memory_space=pl.ANY)
    return pl.pallas_call(
        functools.partial(front_kernel, n, nr, m, mh),
        out_shape=[
            shape((rows_all, width * nr), low),
            shape((table.shape[0], width * nr), low),
            shape((gain.shape[0], width * nr), wide),
            shape((rows_all // 2, width * nr), low),
            shape((rows_all, 3 * width), wide),
            shape((n, 8, own), wide),
            shape((tree, 3 * HEAD), low),
            shape((w_qkv.shape[0] * nr, w_qkv.shape[1]), low),
            shape((w_out.shape[0] * nr, w_out.shape[1]), low),
            shape((w_gu.shape[0], 2 * w_gu.shape[2]), low),
        ],
        in_specs=[any_space, VM, VM] + [any_space] * 4 + [VM] * 5,
        out_specs=[any_space, VM, VM, any_space, any_space, VM, any_space, any_space, any_space, any_space],
        scratch_shapes=[
            pltpu.VMEM((rows_all, width * nr), low),
            pltpu.VMEM((rows_all, 3 * width), wide),
            pltpu.VMEM(w_gu.shape, low),
            pltpu.VMEM((w_gu.shape[0], 2 * w_gu.shape[2]), low),
            pltpu.VMEM((w_qkv.shape[0] * nr, w_qkv.shape[1]), low),
            pltpu.VMEM((w_out.shape[0] * nr, w_out.shape[1]), low),
            pltpu.VMEM((n, n, 8, own), wide),
            pltpu.VMEM((width // HEAD, rows_all, 3 * HEAD), low),
            pltpu.VMEM((own, HEAD), wide),
            pltpu.VMEM((own, HEAD), wide),
            pltpu.VMEM((own, 3 * RANK), low),
            pltpu.VMEM((own, width * nr), low),
            dma((nr - 1, chunks)), dma((nr - 1, chunks)), dma((2, n - 1, chunks)), dma((2, n - 1, chunks)),
            dma((2, nr - 1)), dma((2, nr - 1)), dma((3,)),
            dma((n, n - 1)), dma((n, n - 1)), dma((nr - 1, steps)), dma((nr - 1, steps)),
            dma((nr - 1,)), dma((nr - 1,)), dma((steps,)), dma((2,)), dma, dma((n // 2,)),
        ] + share_sems(2) + share_sems(2) + [dma((6,))],
        compiler_params=params(3),
        name="front",
    )(tokens, table, gain, cot, w_qkv, w_out, w_gu, b_qkv, gain_q, gain_k, cos2, sin2)


def one_hot_rows(out_rows, in_rows, source):
    at = lax.broadcasted_iota(jnp.int32, (out_rows, in_rows), 0)
    return (lax.broadcasted_iota(jnp.int32, (out_rows, in_rows), 1) == source(at)).astype(low)


def rear_kernel(n, nr, ndp, m, d_ref, raw_hbm, factor_ref, gq_ref, gk_ref, cos_ref, sin_ref, res_ref, x_hbm, wq_hbm,
                table_ref, bq_ref, dh_hbm, full_hbm, co_hbm, cg_hbm, cd_hbm, hot_ref,
                grad_ref, layer_ref, sets_ref,
                raw_ref, x_ref, dh_ref, full_ref, co_ref, cg_ref, cd_ref, wq, stats, buf, nq, nk, pq, pk, fq, fk, d_raw, part, recv_right, recv_left, own_buf, layer_own,
                back, red, full, cols, col_stack, full_recv, full_sum, full_last, col_recv, owned, hot_all,
                send_s, recv_s, send_h, recv_h, local_h, send_o, recv_o, local_o, load,
                send_z, recv_z, send_w, recv_w, local_w, send_v, recv_v, local_v,
                send_f, recv_f, send_c, recv_c, send_l, recv_l, send_d, recv_d, send_k, recv_k):
    g, r, c = lax.axis_index("dp"), lax.axis_index("row"), lax.axis_index("col")
    rows_all, width_all = part.shape
    own = rows_all // n
    width = gq_ref.shape[1]
    heads = width // HEAD
    tree_part = own * nr
    middle_at = n // 2
    chunks = own // m
    hop = 1
    ahead = 3
    left = {"col": jnp.maximum(c - 1, 0)}
    right = {"col": jnp.minimum(c + 1, n - 1)}
    load_raw = pltpu.make_async_copy(raw_hbm, raw_ref, load.at[0])
    load_x = pltpu.make_async_copy(x_hbm, x_ref, load.at[1])
    load_w = pltpu.make_async_copy(wq_hbm, wq, load.at[2])
    loads = [
        pltpu.make_async_copy(src, dst, load.at[3 + i])
        for i, (src, dst) in enumerate(
            ((dh_hbm, dh_ref), (full_hbm, full_ref), (co_hbm, co_ref), (cg_hbm, cg_ref), (cd_hbm, cd_ref))
        )
    ]

    def piece(d, b):
        peer = lax.rem(r + d, nr)
        return remote(
            d_ref.at[span(b * tree_part + peer * own, own)], buf.at[r, span(b * own, own)],
            send_h.at[d - 1, b], recv_h.at[d - 1, b], {"row": peer},
        )

    def local(b):
        return pltpu.make_async_copy(
            d_ref.at[span(b * tree_part + r * own, own)], buf.at[r, span(b * own, own)], local_h.at[b]
        )

    is_owner = jnp.logical_or(c == 0, c == n - 1)
    base = jnp.where(c == 0, 0, middle_at)

    def result_piece(b):
        return remote(res_ref.at[span(b * own, own)], layer_own, send_o.at[b], recv_o, {"col": base + b})

    def result_local(b):
        return pltpu.make_async_copy(res_ref.at[span(b * own, own)], layer_own, local_o)

    def width_piece(src, dst, send_sem, recv_sem, d, j, size):
        peer = lax.rem(r + d, nr)
        return remote(
            src.at[span(j * size, size), span(peer * width, width)], dst.at[span(r * own + j * size, size)],
            send_sem.at[d - 1, j], recv_sem.at[d - 1, j], {"row": peer},
        )

    def width_local(src, dst, sem, j, size):
        return pltpu.make_async_copy(
            src.at[span(j * size, size), span(r * width, width)], dst.at[span(r * own + j * size, size)], sem.at[j]
        )

    for b in range(n):
        local(b).start()
    load_raw.start()
    load_x.start()
    load_w.start()
    for copy in loads:
        copy.start()
    me = r * n + c
    barrier = pltpu.get_barrier_semaphore()
    for d in range(1, ndp):
        pl.semaphore_signal(barrier, inc=1, device_id={"dp": lax.rem(g + d, ndp)}, device_id_type=MESH)
    greet(n, nr, ndp - 1)
    for b in (0, n - 1) + tuple(range(1, n - 1)):
        for d in range(1, nr):
            piece(d, b).start()

    @pl.when(is_owner)
    def _():
        for b in range(middle_at):
            @pl.when(base + b == c)
            def _():
                result_local(b).start()

            @pl.when(base + b != c)
            def _():
                result_piece(b).start()

    hot_all[g] = hot_ref[...]
    load_x.wait()
    red[...] = dot_t(x_ref[...], table_ref[:3 * RANK, :]).astype(low)
    load_raw.wait()

    def stat_copy(b, d):
        peer = lax.rem(c + d, n)
        return remote(stats.at[c, b], stats.at[c, b], send_s.at[b, d - 1], recv_s.at[b, d - 1], {"col": peer})

    def norm_block(b):
        for d in range(1, nr):
            piece(d, b).wait_recv()
        local(b).wait()
        rows = span(b * own, own)
        fq[rows, :] = down_columns(factor_ref[b], 0)
        fk[rows, :] = down_columns(factor_ref[b], 4)
        cosine = cos_ref[rows, :]
        sine = sin_ref[rows, :]
        for h in range(heads):
            lanes = slice(h * HEAD, (h + 1) * HEAD)
            k_lanes = slice(width + h * HEAD, width + (h + 1) * HEAD)
            v_lanes = slice(2 * width + h * HEAD, 2 * width + (h + 1) * HEAD)
            u = buf[h, rows, :HEAD].astype(wide)
            u = (u * cosine - pltpu.roll(u, HEAD // 2, 1) * sine) * gq_ref[:, lanes]
            nq[rows, lanes] = u
            pq[rows, lanes] = u * raw_ref[rows, lanes] * fq[rows, :]
            u = buf[h, rows, HEAD:2 * HEAD].astype(wide)
            u = (u * cosine - pltpu.roll(u, HEAD // 2, 1) * sine) * gk_ref[:, lanes]
            nk[rows, lanes] = u
            pk[rows, lanes] = u * raw_ref[rows, k_lanes] * fk[rows, :]
            d_raw[rows, v_lanes] = buf[h, rows, 2 * HEAD:]
        stats[c, b] = row_sums(pq[rows, :], pk[rows, :])
        for d in range(1, n):
            stat_copy(b, d).start()

    def mean_block(b):
        for d in range(1, n):
            stat_copy(b, d).wait()
        total = stats[0, b]
        for s in range(1, n):
            total = total + stats[s, b]
        mean = total * (1.0 / D) * factor_ref[b]
        rows = span(b * own, own)
        pq[rows, :HEAD] = down_columns(mean, 0)
        pk[rows, :HEAD] = down_columns(mean, 4)

    def back_block(b):
        rows = span(b * own, own)
        for h in range(heads):
            lanes = slice(h * HEAD, (h + 1) * HEAD)
            k_lanes = slice(width + h * HEAD, width + (h + 1) * HEAD)
            d_raw[rows, lanes] = (fq[rows, :] * (nq[rows, lanes] - raw_ref[rows, lanes] * pq[rows, :HEAD])).astype(low)
            d_raw[rows, k_lanes] = (fk[rows, :] * (nk[rows, lanes] - raw_ref[rows, k_lanes] * pk[rows, :HEAD])).astype(low)
        for j in range(3):
            back[rows, j * RANK:(j + 1) * RANK] = dot_t(
                d_raw[rows, j * width:(j + 1) * width], bq_ref[j * RANK:(j + 1) * RANK, :]
            ).astype(low)
        mine = jnp.where(b < middle_at, c == 0, c == n - 1)
        held = span(lax.rem(b, middle_at) * own, own)
        for k in range(width_all // width):
            lanes = slice(k * width, (k + 1) * width)
            value = dot_t(d_raw[rows, :], wq[lanes, :]) + dot(back[rows, :], table_ref[:3 * RANK, lanes])
            part[rows, lanes] = (value + jnp.where(mine, dh_ref[held, lanes], 0.0)).astype(low)

    def full_piece(d):
        peer = lax.rem(r + d, nr)
        return remote(full.at[:, span(peer * width, width)], full_recv.at[r], send_f.at[d - 1], recv_f.at[d - 1], {"row": peer})

    col_rows = col_recv.shape[1]
    full_rows = full_last.shape[1]

    def col_piece(d):
        peer = lax.rem(r + d, nr)
        return remote(cols.at[span(peer * col_rows, col_rows)], col_recv.at[r], send_c.at[d - 1], recv_c.at[d - 1], {"row": peer})

    def last_piece(d):
        peer = lax.rem(c + d, n)
        return remote(full_sum.at[span(peer * full_rows, full_rows)], full_last.at[c], send_l.at[d - 1], recv_l.at[d - 1], {"col": peer})

    def tree_piece(d):
        return remote(owned.at[g], owned.at[g], send_d.at[d - 1], recv_d.at[d - 1], {"dp": lax.rem(g + d, ndp)})

    def hot_piece(d):
        return remote(hot_all.at[g], hot_all.at[g], send_k.at[d - 1], recv_k.at[d - 1], {"dp": lax.rem(g + d, ndp)})

    def reduce(kind, b, j):
        rows = span(b * own + j * m, m)
        dst, to = ((recv_right, right), (recv_left, left))[kind]
        return remote(part.at[rows], dst.at[rows], send_z.at[kind, b, j], recv_z.at[kind, b, j], to)

    def stage(s, at_edge=True, inside=True, jobs=()):
        @pl.loop(0, chunks + hop * (n - 2))
        def _(i):
            for at, job in enumerate(jobs):
                pl.when(i == at)(job)

            for kind, b, go, edge, got, j in (
                (0, n - 1 - s, n - 1 - s > c, c == 0, recv_right, i - hop * c),
                (1, s, s < c, c == n - 1, recv_left, i - hop * (n - 1 - c)),
            ):
                go = jnp.logical_and(go, jnp.logical_and(j >= 0, j < chunks))
                if at_edge:
                    @pl.when(jnp.logical_and(go, edge))
                    def _():
                        @pl.when(j >= ahead)
                        def _():
                            reduce(kind, b, j - ahead).wait_send()

                        reduce(kind, b, j).start()

                if inside:
                    @pl.when(jnp.logical_and(go, jnp.logical_not(edge)))
                    def _():
                        rows = span(b * own + j * m, m)
                        reduce(kind, b, j).wait_recv()
                        part[rows, :] = (part[rows, :].astype(wide) + got[rows, :].astype(wide)).astype(low)
                        reduce(kind, b, j).start()

    @pl.loop(0, 2)
    def _(phase):
        def at(i):
            return jnp.where(phase == 0, i * (n - 1), 1 + i)

        @pl.loop(0, 2)
        def _(i):
            norm_block(at(i))

        @pl.when(phase == 0)
        def _():
            load_w.wait()
            loads[0].wait()

        @pl.when(phase == 1)
        def _():
            stage(0)

        @pl.loop(0, 2)
        def _(i):
            mean_block(at(i))
            back_block(at(i))

    for copy in loads[1:]:
        copy.wait()

    rank_own = RANK // n
    groups = full.shape[0] // (n * rank_own) - 1
    rank_row = RANK // nr
    per_wide = cd_ref.shape[1] // width

    def full_job():
        stacked = jnp.concatenate([t_dot(back[...], x_ref[...]), full_ref[...]], axis=0).astype(low)
        order = one_hot_rows(
            full.shape[0], stacked.shape[0],
            lambda o: jnp.where(
                lax.rem(o, full_rows) < groups * rank_own,
                lax.rem(o, full_rows) // rank_own * RANK + o // full_rows * rank_own + lax.rem(o, rank_own), -1
            ),
        )
        full[...] = dot(order, stacked).astype(low)

    def raw_job():
        for j in range(3):
            col_stack[j * RANK:(j + 1) * RANK, :] = t_dot(
                red[:, j * RANK:(j + 1) * RANK], d_raw[:, j * width:(j + 1) * width]
            ).astype(low)
        col_stack[3 * RANK:4 * RANK, :] = co_ref[...].astype(low)

    def wide_job():
        for k in range(per_wide):
            lanes = slice(k * width, (k + 1) * width)
            for j, value in enumerate((cg_ref[0, :, lanes], cg_ref[1, :, lanes], cd_ref[:, lanes])):
                at = (4 + j * per_wide + k) * RANK
                col_stack[at:at + RANK, :] = value.astype(low)

    def col_job():
        order = one_hot_rows(
            cols.shape[0], cols.shape[0],
            lambda o: lax.rem(o, col_rows) // rank_row * RANK + o // col_rows * rank_row + lax.rem(o, rank_row),
        )
        cols[...] = dot(order, col_stack[...]).astype(low)

    stage(1, jobs=(wide_job, raw_job, col_job, full_job))
    for d in range(1, nr):
        full_piece(d).start()
        col_piece(d).start()

    @pl.when(is_owner)
    def _():
        for b in range(middle_at):
            @pl.when(base + b == c)
            def _():
                result_local(b).wait()

            @pl.when(base + b != c)
            def _():
                result_piece(b).wait_send()

    @pl.when(jnp.logical_not(is_owner))
    def _():
        remote(res_ref.at[span(0, own)], layer_own, send_o.at[0], recv_o, right).wait_recv()

    for d in range(1, nr):
        width_piece(layer_own, layer_ref, send_v, recv_v, d, 0, own).start()
    width_local(layer_own, layer_ref, local_v, 0, own).start()
    def row_job():
        for d in range(1, nr):
            full_piece(d).wait_recv()
            col_piece(d).wait_recv()
        total = full[:, span(r * width, width)].astype(wide)
        col_total = cols[span(r * col_rows, col_rows), :].astype(wide)
        for d in range(1, nr):
            peer = lax.rem(r + d, nr)
            total = total + full_recv[peer].astype(wide)
            col_total = col_total + col_recv[peer].astype(wide)
        full_sum[...] = total.astype(low)
        owned[g, full_rows:, :] = col_total.astype(low)
        for d in range(1, n):
            last_piece(d).start()

    stage(2, jobs=(lambda: None, row_job))
    for d in range(1, n):
        last_piece(d).wait_recv()
    last = full_sum[span(c * full_rows, full_rows), :].astype(wide)
    for d in range(1, n):
        last = last + full_last[lax.rem(c + d, n)].astype(wide)
    owned[g, :full_rows, :] = last.astype(low)
    for d in range(1, ndp):
        tree_piece(d).start()
        hot_piece(d).start()

    @pl.loop(0, chunks)
    def _(j):
        rows = span(c * own + j * m, m)
        at = span(j * m, m)
        own_buf[at, :] = part[rows, :]

        @pl.when(c > 0)
        def _():
            reduce(0, c, j).wait_recv()
            own_buf[at, :] = (own_buf[at, :].astype(wide) + recv_right[rows, :].astype(wide)).astype(low)

        @pl.when(c < n - 1)
        def _():
            reduce(1, c, j).wait_recv()
            own_buf[at, :] = (own_buf[at, :].astype(wide) + recv_left[rows, :].astype(wide)).astype(low)

        for d in range(1, nr):
            width_piece(own_buf, grad_ref, send_w, recv_w, d, j, m).start()
        width_local(own_buf, grad_ref, local_w, j, m).start()

    for d in range(1, ndp):
        tree_piece(d).wait_recv()
        hot_piece(d).wait_recv()
    sets_own = sets_ref.shape[0]
    for s in range(sets_own):
        total = owned[0].astype(wide) * hot_all[0, pl.ds(g * sets_own + s, 1), :]
        for t in range(1, ndp):
            total = total + owned[t].astype(wide) * hot_all[t, pl.ds(g * sets_own + s, 1), :]
        sets_ref[s] = total

    @pl.loop(0, chunks)
    def _(j):
        for d in range(1, nr):
            width_piece(own_buf, grad_ref, send_w, recv_w, d, j, m).wait()
        width_local(own_buf, grad_ref, local_w, j, m).wait()

    for d in range(1, nr):
        width_piece(layer_own, layer_ref, send_v, recv_v, d, 0, own).wait()
        full_piece(d).wait_send()
        col_piece(d).wait_send()
        for b in range(n):
            piece(d, b).wait_send()
    width_local(layer_own, layer_ref, local_v, 0, own).wait()
    for d in range(1, n):
        last_piece(d).wait_send()
    for d in range(1, ndp):
        tree_piece(d).wait_send()
        hot_piece(d).wait_send()
    for s in range(n - 1):
        @pl.loop(0, chunks)
        def _(j):
            late = j >= chunks - ahead

            @pl.when(jnp.logical_and(n - 1 - s > c, jnp.logical_or(c > 0, late)))
            def _():
                reduce(0, n - 1 - s, j).wait_send()

            @pl.when(jnp.logical_and(s < c, jnp.logical_or(c < n - 1, late)))
            def _():
                reduce(1, s, j).wait_send()


def rear(d_head, raw, factor, gain_q, gain_k, cos2, sin2, result, x, w_qkv, table, b_qkv, d_h, full_mid, part_ao,
         part_bgu, part_ad, hot, sets_own, n, nr, ndp, m=32):
    rows_all, wide3 = raw.shape
    width = wide3 // 3
    width_all = x.shape[1]
    own = rows_all // n
    chunks = own // m
    full_rows = 8 * RANK // n
    col_blocks = 4 + 3 * part_ad.shape[1] // width
    col_rows = col_blocks * RANK // nr
    dma = pltpu.SemaphoreType.DMA
    shape = jax.ShapeDtypeStruct
    any_space = pl.BlockSpec(memory_space=pl.ANY)
    square = pltpu.VMEM((rows_all, width), wide)
    lane = pltpu.VMEM((rows_all, HEAD), wide)
    big = pltpu.VMEM((rows_all, width_all), low)
    return pl.pallas_call(
        functools.partial(rear_kernel, n, nr, ndp, m),
        out_shape=[
            shape((own * nr, width), low),
            shape((own * nr, width), low),
            shape((sets_own, full_rows + col_rows, width), wide),
        ],
        in_specs=[any_space] * 2 + [VM] * 5 + [any_space] * 3 + [VM] * 2 + [any_space] * 5 + [VM],
        out_specs=[VM] * 3,
        scratch_shapes=[
            pltpu.VMEM(raw.shape, wide),
            pltpu.VMEM(x.shape, low),
            pltpu.VMEM(d_h.shape, wide),
            pltpu.VMEM(full_mid.shape, wide),
            pltpu.VMEM(part_ao.shape, wide),
            pltpu.VMEM(part_bgu.shape, wide),
            pltpu.VMEM(part_ad.shape, wide),
            pltpu.VMEM(w_qkv.shape, low),
            pltpu.VMEM((n, n, 8, own), wide),
            pltpu.VMEM((nr, rows_all, 3 * HEAD), low),
            square, square, square, square, lane, lane,
            pltpu.VMEM((rows_all, wide3), low),
            big, big, big,
            pltpu.VMEM((own, width_all), low),
            pltpu.VMEM((own, width_all), low),
            pltpu.VMEM((rows_all, 3 * RANK), low),
            pltpu.VMEM((rows_all, 3 * RANK), low),
            pltpu.VMEM((n * full_rows, width_all), low),
            pltpu.VMEM((nr * col_rows, width), low),
            pltpu.VMEM((nr * col_rows, width), low),
            pltpu.VMEM((nr, n * full_rows, width), low),
            pltpu.VMEM((n * full_rows, width), low),
            pltpu.VMEM((n, full_rows, width), low),
            pltpu.VMEM((nr, col_rows, width), low),
            pltpu.VMEM((ndp, full_rows + col_rows, width), low),
            pltpu.VMEM((ndp,) + hot.shape, wide),
            dma((n, n - 1)), dma((n, n - 1)), dma((nr - 1, n)), dma((nr - 1, n)), dma((n,)),
            dma((n // 2,)), dma, dma, dma((8,)),
            dma((2, n, chunks)), dma((2, n, chunks)), dma((nr - 1, chunks)), dma((nr - 1, chunks)), dma((chunks,)),
            dma((nr - 1, 1)), dma((nr - 1, 1)), dma((1,)),
            dma((nr - 1,)), dma((nr - 1,)), dma((nr - 1,)), dma((nr - 1,)), dma((n - 1,)), dma((n - 1,)),
            dma((ndp - 1,)), dma((ndp - 1,)), dma((ndp - 1,)), dma((ndp - 1,)),
        ],
        compiler_params=params(5),
        name="rear",
    )(d_head, raw, factor, gain_q, gain_k, cos2, sin2, result, x, w_qkv, table, b_qkv, d_h, full_mid, part_ao, part_bgu, part_ad, hot)


def unpack_kernel(rank_own, rank_row, grad_ref, layer_ref, sets_ref, layer_out, input_grad, a_qkv, b_qkv, a_out, b_out, a_gu, b_gu, a_down, b_down):
    layer_out[...] = layer_ref[...]
    input_grad[...] = grad_ref[...].astype(wide)
    width = grad_ref.shape[1]
    first = 8 * rank_own

    def column(s, at):
        return sets_ref[s, first + at * rank_row:first + (at + 1) * rank_row, :]

    for s in range(sets_ref.shape[0]):
        for j in range(3):
            a_qkv[j, s] = sets_ref[s, j * rank_own:(j + 1) * rank_own, :]
            b_qkv[j, s] = column(s, j)
        for j in range(2):
            a_gu[j, s] = sets_ref[s, (3 + j) * rank_own:(4 + j) * rank_own, :]
        b_out[s] = sets_ref[s, 5 * rank_own:6 * rank_own, :]
        b_down[s] = sets_ref[s, 6 * rank_own:7 * rank_own, :]
        a_out[s] = column(s, 3)
        per = a_down.shape[2] // width
        for k in range(per):
            lanes = slice(k * width, (k + 1) * width)
            b_gu[0, s, :, lanes] = column(s, 4 + k)
            b_gu[1, s, :, lanes] = column(s, 4 + per + k)
            a_down[s, :, lanes] = column(s, 4 + 2 * per + k)


def unpack(grad, layer, sets, rank_own, rank_row, hidden):
    sets_own = sets.shape[0]
    width = grad.shape[1]
    shape = jax.ShapeDtypeStruct
    return pl.pallas_call(
        functools.partial(unpack_kernel, rank_own, rank_row),
        out_shape=[
            shape(layer.shape, low),
            shape(grad.shape, wide),
            shape((3, sets_own, rank_own, width), wide),
            shape((3, sets_own, rank_row, width), wide),
            shape((sets_own, rank_row, width), wide),
            shape((sets_own, rank_own, width), wide),
            shape((2, sets_own, rank_own, width), wide),
            shape((2, sets_own, rank_row, hidden), wide),
            shape((sets_own, rank_row, hidden), wide),
            shape((sets_own, rank_own, width), wide),
        ],
        in_specs=[VM] * 3,
        out_specs=[VM] * 10,
        name="unpack",
    )(grad, layer, sets)


def middle_kernel(n, nr, m, hop, cuts, head_ref, x_hbm, cot_hbm, gain_ref, wo_hbm, wg_hbm, wd_hbm,
                  table_ref, ao_ref, bg_ref, ad_ref,
                  dhead_ref, out_hbm, grad_hbm, full_ref, co_ref, cg_ref, cd_ref,
                  out_half, grad_half, wo, wg, wd, x_half, cot_half, raw, attn, d_attn, h_all, df_all, da_all, gu, part,
                  recv_right, recv_left, hid, red_gu, red_down, back_gu, back_down,
                  sems_send, sems_recv, send_in, recv_in, send_out, recv_out, local_in, local_out, load,
                  send_g, recv_g, local_g, send_d, recv_d, local_d):
    g, r, c = lax.axis_index("dp"), lax.axis_index("row"), lax.axis_index("col")
    ag_ref = table_ref.at[3 * RANK:5 * RANK]
    bo_ref = table_ref.at[5 * RANK:6 * RANK]
    bd_ref = table_ref.at[6 * RANK:]
    rows_all, width_all = part.shape
    half = rows_all // 2
    own = rows_all // n
    tree_part = own * nr
    chunks = half // m
    blocks = 4
    band = half // blocks
    hidden = ad_ref.shape[1]
    width = width_all // nr
    left = {"col": jnp.maximum(c - 1, 0)}
    right = {"col": jnp.minimum(c + 1, n - 1)}
    first = c == 0
    last = c == n - 1
    inner = jnp.logical_and(c > 0, c < n - 1)

    base = jnp.where(last, half, 0)
    a_cut = hidden // 4
    share_g = Share(wg_hbm, wg, cuts, (send_g, recv_g, local_g))
    share_d = Share(wd_hbm, wd, cuts // 2, (send_d, recv_d, local_d))
    loads = [pltpu.make_async_copy(wo_hbm, wo, load.at[0])]
    load_x = pltpu.make_async_copy(x_hbm.at[span(base, half)], x_half, load.at[1])
    load_cot = pltpu.make_async_copy(cot_hbm, cot_half, load.at[2])
    store_out = pltpu.make_async_copy(out_half, out_hbm, load.at[3])
    store_grad = pltpu.make_async_copy(grad_half, grad_hbm, load.at[4])
    is_owner = jnp.logical_or(first, last)
    loads[0].start()

    def piece_in(d, b):
        peer = lax.rem(r + d, nr)
        return remote(
            head_ref.at[span(b * tree_part + peer * own, own)],
            attn.at[span(b * own, own), span(r * HEAD, HEAD)],
            send_in.at[d - 1, b], recv_in.at[d - 1, b], {"row": peer},
        )

    def local_piece_in(b):
        return pltpu.make_async_copy(
            head_ref.at[span(b * tree_part + r * own, own)],
            attn.at[span(b * own, own), span(r * HEAD, HEAD)], local_in.at[b]
        )

    per_block = blocks // (n // 2)

    def out_rows(b, side):
        at = side * (n // 2) + b // per_block
        inside = lax.rem(b, per_block) * band
        return span(at * own + inside, band), span(at * tree_part + r * own + inside, band)

    def piece_out(d, b, side):
        peer = lax.rem(r + d, nr)
        here, there = out_rows(b, side)
        return remote(
            d_attn.at[here, span(peer * HEAD, HEAD)], dhead_ref.at[there],
            send_out.at[side * (nr - 1) + d - 1, b], recv_out.at[side * (nr - 1) + d - 1, b], {"row": peer},
        )

    def local_piece_out(b, side):
        here, there = out_rows(b, side)
        return pltpu.make_async_copy(d_attn.at[here, span(r * HEAD, HEAD)], dhead_ref.at[there], local_out.at[side, b])

    for b in range(n):
        local_piece_in(b).start()
    barrier = pltpu.get_barrier_semaphore()
    for d in range(1, nr):
        pl.semaphore_signal(barrier, inc=1, device_id={"row": lax.rem(r + d, nr)}, device_id_type=MESH)

    @pl.when(c > 0)
    def _():
        pl.semaphore_signal(barrier, inc=1, device_id=left, device_id_type=MESH)

    @pl.when(c < n - 1)
    def _():
        pl.semaphore_signal(barrier, inc=1, device_id=right, device_id_type=MESH)

    pl.semaphore_signal(barrier, inc=1, device_id={"dp": flip(g)}, device_id_type=MESH)
    full_ref[...] = jnp.zeros_like(full_ref)
    co_ref[...] = jnp.zeros_like(co_ref)
    cg_ref[...] = jnp.zeros_like(cg_ref)
    cd_ref[...] = jnp.zeros_like(cd_ref)

    @pl.when(inner)
    def _():
        pl.semaphore_wait(barrier, nr + 2)

    @pl.when(jnp.logical_not(inner))
    def _():
        pl.semaphore_wait(barrier, nr + 1)

    middle = n // 2
    for b in range(middle):
        for block in (b, middle + b):
            for d in range(1, nr):
                piece_in(d, block).start()
    load_x.start()
    load_cot.start()
    share_g.start_far()
    share_d.start_far()
    share_g.start_near()
    share_d.start_near()

    def rows(j, start=0):
        return span(start + j * m, m)

    def band_rows(b):
        return span(b * band, band), span(half + b * band, band)

    def take(ref, b):
        low_rows, high_rows = band_rows(b)
        return jnp.concatenate([ref[low_rows, :], ref[high_rows, :]], axis=0)

    def put(b, lanes, value):
        low_rows, high_rows = band_rows(b)
        part[low_rows, lanes] = value[:band].astype(low)
        part[high_rows, lanes] = value[band:].astype(low)

    around = hop * 2 * (n - 1)
    each = chunks // blocks

    def relay_stage(stage, owner_step, all_ref):
        def send(kind, j, src, dst, to):
            return remote(src, dst, sems_send.at[stage, kind, j], sems_recv.at[stage, kind, j], to)

        def reduce_right(j):
            return send(0, j, part.at[rows(j, half)], recv_right.at[rows(j)], right)

        def reduce_left(j):
            return send(1, j, part.at[rows(j)], recv_left.at[rows(j)], left)

        def spread_left(j):
            return send(2, j, all_ref.at[rows(j, half)], all_ref.at[rows(j, half)], left)

        def spread_right(j):
            return send(3, j, all_ref.at[rows(j)], all_ref.at[rows(j)], right)

        def step(i):
            def on(offset, who, run):
                j = i - offset

                @pl.when(jnp.logical_and(who, jnp.logical_and(j >= 0, j < chunks)))
                def _():
                    run(j)

            def mid_right(j):
                reduce_right(j).wait_recv()
                at = rows(j, half)
                part[at, :] = (part[at, :].astype(wide) + recv_right[rows(j), :].astype(wide)).astype(low)
                reduce_right(j).start()

            def mid_left(j):
                reduce_left(j).wait_recv()
                at = rows(j)
                part[at, :] = (part[at, :].astype(wide) + recv_left[at, :].astype(wide)).astype(low)
                reduce_left(j).start()

            def end_right(j):
                reduce_right(j).wait_recv()
                total = part[rows(j, half), :].astype(wide) + recv_right[rows(j), :].astype(wide)
                all_ref[rows(j, half), :] = owner_step(total, rows(j))
                spread_left(j).start()

            def end_left(j):
                reduce_left(j).wait_recv()
                total = part[rows(j), :].astype(wide) + recv_left[rows(j), :].astype(wide)
                all_ref[rows(j), :] = owner_step(total, rows(j))
                spread_right(j).start()

            def pass_left(j):
                spread_left(j).wait_recv()
                spread_left(j).start()

            def pass_right(j):
                spread_right(j).wait_recv()
                spread_right(j).start()

            def arrived(j):
                @pl.when(first)
                def _():
                    reduce_right(j).wait_send()
                    spread_left(j).wait_recv()

                @pl.when(last)
                def _():
                    reduce_left(j).wait_send()
                    spread_right(j).wait_recv()

                @pl.when(inner)
                def _():
                    reduce_right(j).wait_send()
                    reduce_left(j).wait_send()

            on(0, first, lambda j: reduce_right(j).start())
            on(0, last, lambda j: reduce_left(j).start())
            on(hop * c, inner, mid_right)
            on(hop * (n - 1 - c), inner, mid_left)
            on(hop * (n - 1), last, end_right)
            on(hop * (n - 1), first, end_left)
            on(hop * (2 * (n - 1) - c), inner, pass_left)
            on(hop * (n - 1 + c), inner, pass_right)
            on(around, True, arrived)

        def rest():
            @pl.loop(0, chunks)
            def _(j):
                @pl.when(first)
                def _():
                    spread_right(j).wait_send()

                @pl.when(last)
                def _():
                    spread_left(j).wait_send()

                @pl.when(inner)
                def _():
                    spread_left(j).wait_send()
                    spread_right(j).wait_send()

        return step, rest

    def slices(before, i, per, work):
        @pl.loop(before(i), before(i + 1))
        def _(t):
            work(t // per, lax.rem(t, per))

    def paced(per):
        def before(i):
            late = per + (jnp.maximum(i - per, 0) * per) // each
            return jnp.minimum(jnp.where(i < per, i, late), per * blocks)

        return before

    def shard(j, ref):
        return slice(j * (ref.shape[0] // nr), (j + 1) * (ref.shape[0] // nr))

    def out_work(b, k):
        @pl.when(b == 0)
        def _():
            loads[0].wait()

        @pl.when(lax.rem(b, blocks // middle) == 0)
        def _():
            at = b // (blocks // middle)
            for block in (at, middle + at):
                for d in range(1, nr):
                    piece_in(d, block).wait_recv()
                local_piece_in(block).wait()

        rows_in = take(attn, b)
        red = dot_t(rows_in, ao_ref[...]).astype(low)
        for j in range(nr):
            lanes = slice(j * width, (j + 1) * width)
            put(b, lanes, dot(rows_in, wo[shard(j, wo), :]) + dot(red, bo_ref[:, lanes]))

    gain_a = gain_ref[0:1, :]
    gain_f = gain_ref[1:2, :]

    def attn_owner(total, at):
        raw[at, :] = total
        flat = total * norm_factor(row_sum(total * total))
        return (x_half[at, :].astype(wide) + flat * gain_a).astype(low)

    first_pass = 4
    apart = 2
    late = 3
    passes = cuts + cuts // 2

    def pump(ii):
        at = ii - first_pass

        @pl.when(jnp.logical_and(at >= 0, lax.rem(at, apart) == 0))
        def _():
            t = at // apart

            @pl.when(t < cuts)
            def _():
                share_g.pass_far(t)

            @pl.when(jnp.logical_and(t >= cuts, t < passes))
            def _():
                share_d.pass_far(t - cuts)

            t = t - late

            @pl.when(jnp.logical_and(t >= 0, t < cuts))
            def _():
                share_g.pass_twin(t)

            @pl.when(jnp.logical_and(t >= cuts, t < passes))
            def _():
                share_d.pass_twin(t - cuts)

    load_x.wait()
    in_loop = 1 + chunks + around
    step, rest = relay_stage(0, attn_owner, h_all)
    out_pace = paced(1)

    @pl.loop(0, in_loop)
    def _(ii):
        step(ii - 1)
        slices(out_pace, ii, 1, out_work)
        pump(ii)

    rest()

    share_g.wait_all()

    def gate_slice(b, k):
        rows_in = take(h_all, b)

        @pl.when(k == 0)
        def _():
            red_gu[b] = dot_t(rows_in, ag_ref[...]).astype(low)

        at = pl.multiple_of(k * a_cut, a_cut)
        lanes = pl.ds(at, a_cut)
        up_lanes = pl.ds(pl.multiple_of(hidden + at, a_cut), a_cut)
        red = red_gu[b]
        gate = dot(rows_in, wg[:, lanes]) + dot(red[:, :RANK], bg_ref[0, :, lanes])
        up = dot(rows_in, wg[:, up_lanes]) + dot(red[:, RANK:], bg_ref[1, :, lanes])
        gu[b, :, lanes] = gate.astype(low)
        gu[b, :, up_lanes] = up.astype(low)
        hid[:, lanes] = (gate * jax.nn.sigmoid(gate) * up).astype(low)

    def down_slice(b, k):
        @pl.when(jnp.logical_and(b == 0, k == 0))
        def _():
            @pl.loop(in_loop, jnp.maximum(in_loop, first_pass + apart * (passes + late)))
            def _(ii):
                pump(ii)

            share_d.wait_all()

        rows_in = hid[:, :hidden]

        @pl.when(k == 0)
        def _():
            red_down[b] = dot_t(rows_in, ad_ref[...]).astype(low)

        for s in range(nr // 2):
            j = k * (nr // 2) + s
            lanes = span(j * width, width)
            down_rows = pl.ds(pl.multiple_of(j * hidden, hidden), hidden)
            put(b, lanes, dot(rows_in, wd[down_rows, :]) + dot(red_down[b], bd_ref[:, lanes]))

    def ffn_work(b, k):
        @pl.when(k < 4)
        def _():
            gate_slice(b, k)

        @pl.when(k >= 4)
        def _():
            down_slice(b, k - 4)

    def ffn_owner(total, at):
        a_raw = raw[at, :]
        h = x_half[at, :].astype(wide) + a_raw * norm_factor(row_sum(a_raw * a_raw)) * gain_a
        factor = norm_factor(row_sum(total * total))
        flat = total * factor
        out_half[at, :] = (h + flat * gain_f).astype(low)
        scaled = cot_half[at, :].astype(wide) * gain_f
        return (factor * (scaled - flat * (row_sum(scaled * flat) * (1.0 / D)))).astype(low)

    b_cut = hidden // 2

    def hidden_back(b, k):
        rows_in = take(df_all, b)

        @pl.when(k == 0)
        def _():
            back_down[...] = dot_t(rows_in, bd_ref[...]).astype(low)

        at = pl.multiple_of(k * b_cut, b_cut)
        lanes = pl.ds(at, b_cut)
        up_lanes = pl.ds(pl.multiple_of(hidden + at, b_cut), b_cut)
        back = back_down[...]
        grad = dot(back, ad_ref[:, lanes])
        for j in range(nr):
            down_rows = pl.ds(pl.multiple_of(j * hidden + at, b_cut), b_cut)
            grad = grad + dot_t(rows_in[:, j * width:(j + 1) * width], wd[down_rows, :])
        gate = gu[b, :, lanes].astype(wide)
        up = gu[b, :, up_lanes].astype(wide)
        sigma = jax.nn.sigmoid(gate)
        silu = gate * sigma
        d_gate = (grad * up * sigma * (1.0 + gate * (1.0 - sigma))).astype(low)
        d_up = (grad * silu).astype(low)
        hid[:, lanes] = d_gate
        hid[:, up_lanes] = d_up
        cd_ref[:, lanes] += t_dot(back, (silu * up).astype(low))
        red = red_gu[b]
        cg_ref[0, :, lanes] += t_dot(red[:, :RANK], d_gate)
        cg_ref[1, :, lanes] += t_dot(red[:, RANK:], d_up)

    o_cut = width_all // 4

    def gate_back(b, k):
        @pl.when(k == 0)
        def _():
            back_gu[:, :RANK] = dot_t(hid[:, :hidden], bg_ref[0]).astype(low)
            back_gu[:, RANK:] = dot_t(hid[:, hidden:], bg_ref[1]).astype(low)

        lanes = span(k * o_cut, o_cut)
        put(b, lanes, dot_t(hid[...], wg[lanes, :]) + dot(back_gu[...], ag_ref[:, lanes]))

        @pl.when(k == 3)
        def _():
            full_ref[:2 * RANK, :] += t_dot(back_gu[...], take(h_all, b))
            full_ref[3 * RANK:, :] += t_dot(red_down[b], take(df_all, b))

    def back_work(b, k):
        @pl.when(k < 2)
        def _():
            hidden_back(b, k)

        @pl.when(k >= 2)
        def _():
            gate_back(b, k - 2)

    def back_owner(total, at):
        grad = cot_half[at, :].astype(wide) + total
        grad_half[at, :] = grad
        a_raw = raw[at, :]
        factor = norm_factor(row_sum(a_raw * a_raw))
        flat = a_raw * factor
        scaled = grad * gain_a
        return (factor * (scaled - flat * (row_sum(scaled * flat) * (1.0 / D)))).astype(low)

    def out_back(b, k):
        rows_in = take(da_all, b)
        back = dot_t(rows_in, bo_ref[...]).astype(low)
        grad = dot(back, ao_ref[...])
        for j in range(nr):
            grad = grad + dot_t(rows_in[:, j * width:(j + 1) * width], wo[shard(j, wo), :])
        for side in range(2):
            d_attn[out_rows(b, side)[0], :] = grad[side * band:(side + 1) * band].astype(low)
            for d in range(1, nr):
                piece_out(d, b, side).start()
            local_piece_out(b, side).start()
        attn_rows = take(attn, b)
        co_ref[...] += t_dot(back, attn_rows)
        red = dot_t(attn_rows, ao_ref[...]).astype(low)
        full_ref[2 * RANK:3 * RANK, :] += t_dot(red, rows_in)

    begin = around + each

    def back_before(i):
        return jnp.clip(i - begin, 0, 6 * blocks)

    def out_before(i):
        return jnp.clip((i - around - 1) // each, 0, blocks)

    load_cot.wait()
    step_f, rest_f = relay_stage(1, ffn_owner, df_all)
    step_b, rest_b = relay_stage(2, back_owner, da_all)
    ffn_pace = paced(6)
    period = 26

    @pl.loop(0, 6 + period + chunks + around + 1)
    def _(ii):
        i = ii - 6
        step_f(i)
        step_b(i - period)
        slices(ffn_pace, ii, 6, ffn_work)
        slices(back_before, i, 6, back_work)
        slices(out_before, i - period, 1, out_back)

    pl.when(is_owner)(store_out.start)
    rest_f()
    rest_b()
    pl.when(is_owner)(store_grad.start)

    @pl.loop(0, n)
    def _(b):
        for d in range(1, nr):
            piece_in(d, b).wait_send()

    @pl.loop(0, blocks)
    def _(b):
        for side in range(2):
            for d in range(1, nr):
                piece_out(d, b, side).wait()
            local_piece_out(b, side).wait()

    share_g.drain()
    share_d.drain()

    @pl.when(is_owner)
    def _():
        store_out.wait()
        store_grad.wait()


def middle(attn_head, x, cot_half, gains, w_out, w_gu, w_down, table, a_out, b_gu, a_down, n, nr, m=16, hop=2, cuts=8):
    group, width_all = x.shape
    half = group // 2
    width = width_all // nr
    hidden = a_down.shape[1]
    chunks = half // m
    band = group // 4
    dma = pltpu.SemaphoreType.DMA
    any_space = pl.BlockSpec(memory_space=pl.ANY)
    shape = jax.ShapeDtypeStruct
    return pl.pallas_call(
        functools.partial(middle_kernel, n, nr, m, hop, cuts),
        out_shape=[
            shape(attn_head.shape, low),
            shape((half, width_all), low),
            shape((half, width_all), wide),
            shape((4 * RANK, width_all), wide),
            shape((RANK, a_out.shape[1]), wide),
            shape((2, RANK, hidden), wide),
            shape((RANK, hidden), wide),
        ],
        in_specs=[any_space, any_space, any_space, VM, any_space, any_space, any_space] + [VM] * 4,
        out_specs=[any_space] * 3 + [VM] * 4,
        scratch_shapes=[
            pltpu.VMEM((half, width_all), low),
            pltpu.VMEM((half, width_all), wide),
            pltpu.VMEM(w_out.shape, low),
            pltpu.VMEM((w_gu.shape[0] * nr, w_gu.shape[1]), low),
            pltpu.VMEM((w_down.shape[0] * nr, w_down.shape[1]), low),
            pltpu.VMEM((half, width_all), low),
            pltpu.VMEM((half, width_all), low),
            pltpu.VMEM((half, width_all), wide),
            pltpu.VMEM((group, a_out.shape[1]), low),
            pltpu.VMEM((group, a_out.shape[1]), low),
            pltpu.VMEM((group, width_all), low),
            pltpu.VMEM((group, width_all), low),
            pltpu.VMEM((group, width_all), low),
            pltpu.VMEM((4, band, 2 * hidden), low),
            pltpu.VMEM((group, width_all), low),
            pltpu.VMEM((half, width_all), low),
            pltpu.VMEM((half, width_all), low),
            pltpu.VMEM((band, 2 * hidden), low),
            pltpu.VMEM((4, band, 2 * RANK), low),
            pltpu.VMEM((4, band, RANK), low),
            pltpu.VMEM((band, 2 * RANK), low),
            pltpu.VMEM((band, RANK), low),
            dma((3, 4, chunks)), dma((3, 4, chunks)),
            dma((nr - 1, n)), dma((nr - 1, n)), dma((2 * (nr - 1), 4)), dma((2 * (nr - 1), 4)), dma((n,)), dma((2, 4)),
            dma((5,)),
        ] + share_sems(cuts) + share_sems(cuts // 2),
        compiler_params=pltpu.CompilerParams(collective_id=0, has_side_effects=True, vmem_limit_bytes=67043328),
        name="middle",
    )(attn_head, x, cot_half, gains, w_out, w_gu, w_down, table, a_out, b_gu, a_down)


def per_device(
    tokens,
    cotangent,
    seg_ids,
    positions,
    parents,
    tree_sets,
    gain_q,
    gain_k,
    gain_attn,
    gain_ffn,
    query_key_value_weight,
    output_weight,
    gate_up_weight,
    down_weight,
    query_key_value_adapter_first,
    query_key_value_adapter_second,
    output_adapter_first,
    output_adapter_second,
    gate_up_adapter_first,
    gate_up_adapter_second,
    down_adapter_first,
    down_adapter_second,
):
    dp_count = lax.axis_size("dp")
    row_count = lax.axis_size("row")
    col_count = lax.axis_size("col")
    row_at = lax.axis_index("row")
    tree_tokens = seg_ids.shape[0]
    assert tree_sets.shape[0] == 1 and col_count == 4
    set_count = output_adapter_first.shape[0]
    own = tokens.shape[0] // row_count
    group = own * col_count
    width_row = tokens.shape[1]
    width_col = gain_q.shape[0]
    hidden_col = down_weight.shape[0]
    tree_set = tree_sets[0]

    tables = (
        query_key_value_adapter_first,
        query_key_value_adapter_second,
        output_adapter_first,
        output_adapter_second,
        gate_up_adapter_first,
        gate_up_adapter_second,
        down_adapter_first,
        down_adapter_second,
    )
    narrow, b_qkv, a_out, b_gu, a_down, gain_pair, hot, branch_flag, parent_at = prep(
        tree_sets, seg_ids, parents, gain_attn[None, :], gain_ffn[None, :], tables
    )
    pos_own = lax.dynamic_index_in_dim(
        positions.reshape(col_count, row_count, own), row_at, 1, keepdims=False
    ).reshape(group)
    cos2, sin2 = angles(pos_own)
    gq, gk = gain_q[None, :], gain_k[None, :]
    x, table, gains, g_half, raw, factors, qkv_head, w_qkv, w_out, w_gu = front(
        tokens,
        narrow,
        gain_pair,
        cotangent,
        query_key_value_weight.reshape(width_row, 3 * width_col),
        output_weight,
        gate_up_weight,
        b_qkv,
        gq,
        gk,
        cos2,
        sin2,
        col_count,
        row_count,
    )
    attn_head, lse = attend(qkv_head, parent_at, branch_flag)
    d_attn_head, out_half, d_h_half, full_mid, part_ao, part_bgu, part_ad = middle(
        attn_head,
        x,
        g_half,
        gains,
        w_out,
        w_gu,
        down_weight,
        table,
        a_out,
        b_gu,
        a_down,
        col_count,
        row_count,
    )
    d_qkv_head = attend_back(qkv_head, d_attn_head, parent_at, branch_flag, lse)
    in_grad, layer, sets = rear(
        d_qkv_head,
        raw,
        factors,
        gq,
        gk,
        cos2,
        sin2,
        out_half,
        x,
        w_qkv,
        table,
        b_qkv,
        d_h_half,
        full_mid,
        part_ao,
        part_bgu,
        part_ad,
        hot,
        set_count // dp_count,
        col_count,
        row_count,
        dp_count,
    )
    return tuple(unpack(in_grad, layer, sets, RANK // col_count, RANK // row_count, hidden_col))


def solution(mesh):
    in_specs = (
        P(("dp", "col"), "row"),
        P(("dp", "col"), "row"),
        P("dp"),
        P("dp"),
        P("dp", None),
        P("dp"),
        P("col"),
        P("col"),
        P("row"),
        P("row"),
        P("row", None, "col"),
        P("col", "row"),
        P("row", None, "col"),
        P("col", "row"),
        P(None, None, None, "row"),
        P(None, None, None, "col"),
        P(None, None, "col"),
        P(None, None, "row"),
        P(None, None, None, "row"),
        P(None, None, None, "col"),
        P(None, None, "col"),
        P(None, None, "row"),
    )
    out_specs = (
        P(("dp", "col"), "row"),
        P(("dp", "col"), "row"),
        P(None, "dp", "col", "row"),
        P(None, "dp", "row", "col"),
        P("dp", "row", "col"),
        P("dp", "col", "row"),
        P(None, "dp", "col", "row"),
        P(None, "dp", "row", "col"),
        P("dp", "row", "col"),
        P("dp", "col", "row"),
    )
    return jax.shard_map(
        per_device, mesh=mesh, in_specs=in_specs, out_specs=out_specs, check_vma=False
    )
```
